32 devices in a mesh: batch: 16 (over z, y, x), tensor: 2 (over core).
Axes of the slice: x: 2, y: 2, z: 4, core: 2. Of those that a mesh axis runs over, the one named last changes fastest.
Arguments:
- tokens: bfloat16 [16, 768, 1152], P('batch'), may hold values from -6 to 6
- segment_ids: int32 [16, 768], P('batch'), may hold values from 0 to 7, never falling along the last dimension, each value on 1 to 256 neighbouring positions
- conditions: bfloat16 [16, 8, 1152], P('batch'), may hold values from -6 to 6
- condition_segment: int32 [16, 8], P('batch'), may hold values from 0 to 7, each once within a row
- qkv_weight: bfloat16 [1152, 3, 1152], P(None, None, 'tensor'), may hold values from -0.1875 to 0.1875
- qv_bias: float32 [2, 1152], P(None, 'tensor'), may hold values from -3 to 3
- proj_weight: bfloat16 [1152, 1152], P('tensor'), may hold values from -0.875 to 0.875
- proj_bias: float32 [1152], replicated, may hold values from -3 to 3
- up_weight: bfloat16 [1152, 4608], P(None, 'tensor'), may hold values from -0.1875 to 0.1875
- up_bias: float32 [4608], P('tensor'), may hold values from -3 to 3
- down_weight: bfloat16 [4608, 1152], P('tensor'), may hold values from -0.09375 to 0.09375
- down_bias: float32 [1152], replicated, may hold values from -3 to 3
- mod_weight: bfloat16 [1152, 6, 1152], P(None, None, 'tensor'), may hold values from -0.1875 to 0.1875
- mod_bias: float32 [6, 1152], P(None, 'tensor'), may hold values from -3 to 3
- out_grad: bfloat16 [16, 768, 1152], P('batch'), may hold values from -6 to 6
Outputs:
- layer_out: bfloat16 [16, 768, 1152], P('batch')
- token_grad: float32 [16, 768, 1152], P('batch', None, 'tensor')
- condition_grad: float32 [16, 8, 1152], P('batch')
- qkv_grad: float32 [1152, 3, 1152], P('batch', None, 'tensor')
- qvbias_grad: float32 [2, 1152], P(None, 'tensor')
- proj_grad: float32 [1152, 1152], P('tensor', 'batch')
- projbias_grad: float32 [1152], replicated
- up_grad: float32 [1152, 4608], P('batch', 'tensor')
- upbias_grad: float32 [4608], P('tensor')
- down_grad: float32 [4608, 1152], P('tensor', 'batch')
- downbias_grad: float32 [1152], replicated
- mod_grad: float32 [1152, 6, 1152], P('batch', None, 'tensor')
- modbias_grad: float32 [6, 1152], P(None, 'tensor')
The draws below stay inside these ranges and needn't reach their ends.
Inputs may be any that keep to these rules, and one draw needn't show every extreme that they name: `segment_ids`: along each row the ids never fall; each of the 8 segments of a row holds 1 to 256 positions, and some row has a segment of exactly 256 positions. `condition_segment`: each row is a permutation of 0 to 7.
All inputs are finite; a program needn't handle non-finite values.
Results may differ from the reference program's by a relative error of at most 0.022.
The reference program's roundings to bfloat16 on the way count: a program that leaves them out, or rounds other values in their place, can miss the bound.
Values may be sent and summed in bfloat16 or wider, within the bound.
No kernel may reach another device: no remote copies, remote signals or barrier semaphores. Data moves between devices by JAX's collectives and lax.ppermute only.
A program may use at most 256 MiB of HBM per device.

```python
import math
import jax
import jax.numpy as jnp
import numpy as np
from jax import lax

D = 1152
HEADS = 16
HEAD_DIM = 72
FF = 4608
LEN = 768
SEGS = 8
MOST = 256
ROWS_DEV = 1
ROWS = 16
N_TENSOR = 2


def block_scale(own_key, dims, shards, low, largest):
    def one(axis_at, blocks):
        heights = jax.random.uniform(jax.random.fold_in(jax.random.fold_in(own_key, 6), axis_at), (blocks,), jnp.float32, low / len(shards), largest / len(shards))
        return jnp.repeat(jnp.exp(heights), dims[axis_at] // blocks).reshape((-1,) + (1,) * (len(dims) - axis_at - 1))

    loudness = one(*shards[0])
    for cut in shards[1:]:
        loudness = loudness * one(*cut)
    return loudness


def profile(count, total, most, skew):
    weights = [(1 << 20) // math.isqrt(grade ** skew) + 1 for grade in range(2, count + 1)]
    surplus, holding = total - most - (count - 1), [1] * (count - 1)
    while surplus > 0:
        free = [i for i in range(count - 1) if holding[i] < most]
        whole, remaining = sum([weights[i] for i in free]), surplus
        for i in free:
            extra = min(most - holding[i], max(1, remaining * weights[i] // whole), surplus)
            holding[i] = holding[i] + extra
            surplus = surplus - extra
    return np.array([most] + holding)


def uneven_parts(key, amount, total, most, lean):
    if amount == 2:
        one = jax.random.randint(key, (), max(1, total - most), min(most, total - 1) + 1)
        return jnp.stack([one, total - one])
    tallies = jnp.asarray(profile(amount, total, most, lean), jnp.int32)
    twos = (amount - 1) // 2
    giver, taker = tallies[1:1 + 2 * twos:2], tallies[2:2 + 2 * twos:2]
    margin = jnp.minimum(giver - 1, most - taker)
    moved = jax.random.randint(jax.random.fold_in(key, 1), (twos,), 0, 1 << 20) % (margin + 1)
    tallies = tallies.at[1:1 + 2 * twos:2].set(giver - moved).at[2:2 + 2 * twos:2].set(taker + moved)
    return tallies[jax.random.permutation(jax.random.fold_in(key, 2), amount)]


def noise(own_key, dims, width, limit, shards=(), dtype=jnp.bfloat16):
    values = jax.random.normal(own_key, dims, jnp.float32) * width
    if len(shards) > 0:
        values = block_scale(own_key, dims, shards, -0.22, 0.18) * values
    return jnp.clip(values, min=-limit, max=limit).astype(dtype)


def setup_inputs(seed: int = 0) -> dict:
    splits = jax.random.split(jax.random.key(seed), 16)
    tokens = noise(splits[0], (ROWS, LEN, D), 1.0, 6.0, ((0, 16),))
    segment_ids = jax.vmap(lambda own: jnp.searchsorted(jnp.cumsum(uneven_parts(own, SEGS, LEN, MOST, 1)), jnp.arange(LEN), side="right"))(jax.random.split(splits[1], ROWS)).reshape((ROWS, LEN)).astype(jnp.int32)
    conditions = noise(splits[2], (ROWS, SEGS, D), 1.0, 6.0, ((0, 16),))
    condition_segment = jax.vmap(lambda own: jax.random.permutation(own, SEGS))(jax.random.split(splits[3], ROWS)).reshape((ROWS, SEGS)).astype(jnp.int32)
    qkv_weight = noise(splits[4], (D, 3, D), D ** -0.5, 0.1875, ((2, 2),))
    qv_bias = noise(splits[5], (2, D), 0.5, 3.0, ((1, 2),), jnp.float32)
    proj_weight = noise(splits[6], (D, D), (max(D // 24, 4)) ** -0.5, 0.875, ((0, 2),))
    proj_bias = noise(splits[7], (D,), 0.5, 3.0, (), jnp.float32)
    up_weight = noise(splits[8], (D, FF), D ** -0.5, 0.1875, ((1, 2),))
    up_bias = noise(splits[9], (FF,), 0.5, 3.0, ((0, 2),), jnp.float32)
    down_weight = noise(splits[10], (FF, D), FF ** -0.5, 0.09375, ((0, 2),))
    down_bias = noise(splits[11], (D,), 0.5, 3.0, (), jnp.float32)
    mod_weight = noise(splits[12], (D, 6, D), D ** -0.5, 0.1875, ((2, 2),))
    mod_bias = noise(splits[13], (6, D), 0.5, 3.0, ((1, 2),), jnp.float32)
    out_grad = noise(splits[14], (ROWS, LEN, D), 1.0, 6.0, ((0, 16),))
    return dict(tokens=tokens, segment_ids=segment_ids, conditions=conditions, condition_segment=condition_segment, qkv_weight=qkv_weight, qv_bias=qv_bias, proj_weight=proj_weight, proj_bias=proj_bias, up_weight=up_weight, up_bias=up_bias, down_weight=down_weight, down_bias=down_bias, mod_weight=mod_weight, mod_bias=mod_bias, out_grad=out_grad)


EPS = 1e-06
HIGHEST = lax.Precision.HIGHEST

@jax.custom_vjp
def low(v):
    return lax.optimization_barrier(v.astype(jnp.bfloat16)).astype(jnp.float32)

@jax.custom_vjp
def low_back(v):
    return v

def low_keep(v):
    return (low(v), None)

def low_pass(kept, grad):
    return (grad,)

def back_keep(v):
    return (v, None)

def back_low(kept, grad):
    return (low(grad),)
low.defvjp(low_keep, low_pass)
low_back.defvjp(back_keep, back_low)

def normalize(array):
    center = array - lax.optimization_barrier(jnp.mean(array, axis=-1, keepdims=True))
    spread = lax.optimization_barrier(jnp.mean(center * center, axis=-1, keepdims=True))
    return center * lax.rsqrt(spread + EPS)

def silu(array):
    return array / (1.0 + jnp.exp(-array))

def gelu(array):
    tanh_arg = 0.7978845608028654 * (array + 0.044715 * array * array * array)
    return 0.5 * array * (1.0 + jnp.tanh(tanh_arg))

def forward(tokens, conditions, qkv_weight, qv_bias, proj_weight, proj_bias, up_weight, up_bias, down_weight, down_bias, mod_weight, mod_bias, segment_ids, condition_segment):
    groups = tokens.shape[0]
    length = tokens.shape[1]
    cond_act = low(silu(conditions))
    modulation = low_back(jnp.einsum('gsd,djc->gsjc', cond_act, mod_weight, precision=HIGHEST) + mod_bias)
    one_hot = (segment_ids[:, :, None] == condition_segment[:, None, :]).astype(jnp.float32)
    token_mod = jnp.einsum('gls,gsjc->gljc', one_hot, modulation, precision=HIGHEST)
    attn_in = low(normalize(tokens) * (1.0 + token_mod[:, :, 1]) + token_mod[:, :, 0])
    projected = jnp.einsum('gld,djc->gljc', attn_in, qkv_weight, precision=HIGHEST)
    head_shape = (groups, length, HEADS, HEAD_DIM)
    queries = low(low_back(projected[:, :, 0] + qv_bias[0])).reshape(head_shape)
    key_vecs = low(low_back(projected[:, :, 1])).reshape(head_shape)
    values = low(low_back(projected[:, :, 2] + qv_bias[1])).reshape(head_shape)
    same_image = (segment_ids[:, :, None] == segment_ids[:, None, :])[:, None]
    scores = jnp.einsum('gqhe,gkhe->ghqk', queries, key_vecs, precision=HIGHEST) * HEAD_DIM ** (-0.5)
    scores = low_back(jnp.where(same_image, scores, -1e+30))
    shifted = jnp.exp(scores - lax.optimization_barrier(jnp.max(scores, axis=-1, keepdims=True)))
    attn_probs = shifted / lax.optimization_barrier(jnp.sum(shifted, axis=-1, keepdims=True))
    attended = low(low_back(jnp.einsum('ghqk,gkhe->gqhe', low(attn_probs), values, precision=HIGHEST)))
    attended = attended.reshape(groups, length, N_TENSOR, D // N_TENSOR)
    proj_parts = jnp.einsum('gltc,tcd->gltd', attended, proj_weight.reshape(N_TENSOR, D // N_TENSOR, D), precision=HIGHEST)
    attn_out = low_back(lax.optimization_barrier(jnp.sum(low(proj_parts), axis=2)) + proj_bias)
    middle = tokens + token_mod[:, :, 2] * attn_out
    mlp_in = low(normalize(middle) * (1.0 + token_mod[:, :, 4]) + token_mod[:, :, 3])
    hidden = low_back(jnp.einsum('gld,df->glf', mlp_in, up_weight, precision=HIGHEST) + up_bias)
    active = low(gelu(hidden)).reshape(groups, length, N_TENSOR, FF // N_TENSOR)
    down_parts = jnp.einsum('gltf,tfd->gltd', active, down_weight.reshape(N_TENSOR, FF // N_TENSOR, D), precision=HIGHEST)
    mlp_out = low_back(lax.optimization_barrier(jnp.sum(low(down_parts), axis=2)) + down_bias)
    return middle + token_mod[:, :, 5] * mlp_out

def reference(tokens, segment_ids, conditions, condition_segment, qkv_weight, qv_bias, proj_weight, proj_bias, up_weight, up_bias, down_weight, down_bias, mod_weight, mod_bias, out_grad):
    weights = tuple((weight.astype(jnp.float32) for weight in (qkv_weight, qv_bias, proj_weight, proj_bias, up_weight, up_bias, down_weight, down_bias, mod_weight, mod_bias)))
    group_count = ROWS // ROWS_DEV

    def grouped(array):
        return array.reshape((group_count, ROWS_DEV) + array.shape[1:])

    def ungroup(array):
        return array.reshape((ROWS,) + array.shape[2:])

    def one_group(totals, entries):
        tok_group, cond_group, seg_group, slot_group, grad_group = entries

        def local_fn(tok_value, cond_value, *params):
            return forward(tok_value, cond_value, *params, seg_group, slot_group)
        result, pullback = jax.vjp(local_fn, tok_group, cond_group, *weights)
        gradients = pullback(grad_group)
        totals = tuple((before + added for before, added in zip(totals, gradients[2:])))
        return (totals, (result.astype(jnp.bfloat16), gradients[0], gradients[1]))
    zero_grads = tuple((jnp.zeros(weight.shape, jnp.float32) for weight in weights))
    entries = (grouped(tokens.astype(jnp.float32)), grouped(conditions.astype(jnp.float32)), grouped(segment_ids), grouped(condition_segment), grouped(out_grad.astype(jnp.float32)))
    totals, (outputs, tok_grads, cond_grads) = lax.scan(one_group, zero_grads, entries)
    return (ungroup(outputs), ungroup(tok_grads), ungroup(cond_grads), totals[0], totals[1], totals[2], totals[3], totals[4], totals[5], totals[6], totals[7], totals[8], totals[9])
```

```python
import functools

import jax
import jax.numpy as jnp
from jax import lax
from jax.sharding import PartitionSpec as P

HEAD_DIM = 72


EPS = 1e-06
HIGHEST = lax.Precision.HIGHEST


def silu(array):
    return array / (1.0 + jnp.exp(-array))


def gelu(array):
    tanh_arg = 0.7978845608028654 * (array + 0.044715 * array * array * array)
    return 0.5 * array * (1.0 + jnp.tanh(tanh_arg))


def normalize(array):
    center = array - jnp.mean(array, axis=-1, keepdims=True)
    spread = jnp.mean(center * center, axis=-1, keepdims=True)
    inverse = lax.rsqrt(spread + EPS)
    return (center * inverse, inverse)


def segment_pick(one_hot, table):
    return jnp.einsum("rls,rsc->rlc", one_hot, table, precision=HIGHEST)


def segment_total(one_hot, array):
    return jnp.einsum("rls,rlc->rsc", one_hot, array, precision=HIGHEST)


def exchange(array, axis):
    return lax.ppermute(array, axis, [(0, 1), (1, 0)])


def tensor_sum(array, size):
    if size == 2:
        return array.astype(jnp.float32) + exchange(array, "tensor").astype(jnp.float32)
    return lax.psum(array, "tensor").astype(jnp.float32)


def tensor_join(array, size):
    if size == 2:
        other = exchange(array, "tensor")
        first = lax.axis_index("tensor") == 0
        return jnp.concatenate(
            [jnp.where(first, array, other), jnp.where(first, other, array)], axis=-1
        )
    return lax.all_gather(array, "tensor", axis=array.ndim - 1, tiled=True)


def partners(size, bit):
    return [(i, i ^ (1 << bit)) for i in range(size)]


def batch_gather(array, size):
    out = array[None]
    for bit in range(size.bit_length() - 1):
        other = lax.ppermute(out, "batch", partners(size, bit))
        out = jnp.concatenate([out, other], axis=0)
    return out


def batch_scatter(part, size, order):
    bits = size.bit_length() - 1
    index = lax.axis_index("batch")
    cube = part.reshape((2,) * bits + part.shape[1:])
    for step, bit in enumerate(order):
        axis = bits - 1 - bit
        mine = (index >> bit) & 1
        send = lax.dynamic_index_in_dim(cube, 1 - mine, axis, keepdims=True)
        keep = lax.dynamic_index_in_dim(cube, mine, axis, keepdims=True)
        got = lax.ppermute(send, "batch", partners(size, bit))
        cube = keep.astype(jnp.float32) + got.astype(jnp.float32)
        if step < bits - 1:
            cube = cube.astype(jnp.bfloat16)
    return cube.reshape(part.shape[1:])


def weight_grad(left, right, size):
    bits = size.bit_length() - 1
    depth = right.shape[-1]
    cut = depth // 256 * 128
    orders = (tuple(range(bits)), (1, 0) + tuple(range(2, bits)))
    pieces = []
    for begin, end, order in ((0, cut, orders[0]), (cut, depth, orders[1])):
        if begin == end:
            continue
        part = jnp.einsum(
            "rld,rlc->dc", left, right[:, :, begin:end], preferred_element_type=jnp.float32
        ).astype(jnp.bfloat16)
        part = part.reshape((size, part.shape[0] // size, part.shape[1]))
        pieces.append(batch_scatter(part, size, order))
    return jnp.concatenate(pieces, axis=1)


def attention_scores(queries, key_vecs, same_image, score_scale):
    scores = (
        jnp.einsum("rqhe,rkhe->rhqk", queries, key_vecs, preferred_element_type=jnp.float32)
        * score_scale
    )
    return jnp.where(same_image, scores, -1e30)


def on_device(
    n_batch,
    tokens,
    segment_ids,
    conditions,
    condition_segment,
    qkv_weight,
    qv_bias,
    proj_weight,
    proj_bias,
    up_weight,
    up_bias,
    down_weight,
    down_bias,
    mod_weight,
    mod_bias,
    out_grad,
):
    row_count = tokens.shape[0]
    length = tokens.shape[1]
    model_width = tokens.shape[2]
    local_width = qkv_weight.shape[2]
    local_heads = local_width // HEAD_DIM
    head_shape = (row_count, length, local_heads, HEAD_DIM)
    score_scale = HEAD_DIM ** (-0.5)
    offset = lax.axis_index("tensor") * local_width
    n_tensor = model_width // local_width

    def mine(array):
        return lax.dynamic_slice_in_dim(array, offset, local_width, 2)

    cond_float = conditions.astype(jnp.float32)
    cond_act = silu(cond_float).astype(jnp.bfloat16)
    mod_local = (
        jnp.einsum("rsd,djc->rsjc", cond_act, mod_weight, preferred_element_type=jnp.float32)
        + mod_bias
    )
    modulation = tensor_join(mod_local, n_tensor)
    one_hot = (segment_ids[:, :, None] == condition_segment[:, None, :]).astype(jnp.float32)
    shift_one = segment_pick(one_hot, modulation[:, :, 0])
    scale_one = segment_pick(one_hot, modulation[:, :, 1])
    gate_one = segment_pick(one_hot, modulation[:, :, 2])
    shift_two = segment_pick(one_hot, modulation[:, :, 3])
    scale_two = segment_pick(one_hot, modulation[:, :, 4])
    gate_two = segment_pick(one_hot, modulation[:, :, 5])
    tok_float = tokens.astype(jnp.float32)
    normed_one, inverse_one = normalize(tok_float)
    attn_in = (normed_one * (1.0 + scale_one) + shift_one).astype(jnp.bfloat16)
    projected = jnp.einsum("rld,djc->rljc", attn_in, qkv_weight, preferred_element_type=jnp.float32)
    queries = (projected[:, :, 0] + qv_bias[0]).astype(jnp.bfloat16).reshape(head_shape)
    key_vecs = projected[:, :, 1].astype(jnp.bfloat16).reshape(head_shape)
    values = (projected[:, :, 2] + qv_bias[1]).astype(jnp.bfloat16).reshape(head_shape)
    same_image = (segment_ids[:, :, None] == segment_ids[:, None, :])[:, None]
    scores = attention_scores(queries, key_vecs, same_image, score_scale)
    row_peak = jnp.max(scores, axis=-1, keepdims=True)
    shifted = jnp.exp(scores - row_peak)
    row_total = jnp.sum(shifted, axis=-1, keepdims=True)
    attn_probs = shifted / row_total
    log_total = row_peak + jnp.log(row_total)
    attended = jnp.einsum(
        "rhqk,rkhe->rqhe",
        attn_probs.astype(jnp.bfloat16),
        values,
        preferred_element_type=jnp.float32,
    )
    attended = attended.astype(jnp.bfloat16).reshape(row_count, length, local_width)
    proj_part = jnp.einsum("rlc,cd->rld", attended, proj_weight, preferred_element_type=jnp.float32)
    attn_out = tensor_sum(proj_part.astype(jnp.bfloat16), n_tensor) + proj_bias
    middle = tok_float + gate_one * attn_out
    normed_two, inverse_two = normalize(middle)
    mlp_in = (normed_two * (1.0 + scale_two) + shift_two).astype(jnp.bfloat16)
    hidden = (
        jnp.einsum("rld,df->rlf", mlp_in, up_weight, preferred_element_type=jnp.float32) + up_bias
    )
    active = gelu(hidden).astype(jnp.bfloat16)
    down_part = jnp.einsum("rlf,fd->rld", active, down_weight, preferred_element_type=jnp.float32)
    mlp_out = tensor_sum(down_part.astype(jnp.bfloat16), n_tensor) + down_bias
    layer_out = (middle + gate_two * mlp_out).astype(jnp.bfloat16)
    grad_float = out_grad.astype(jnp.float32)
    mlp_grad = (grad_float * gate_two).astype(jnp.bfloat16)
    gate_two_grad = grad_float * mlp_out
    down_bias_grad = jnp.sum(mlp_grad.astype(jnp.float32), axis=(0, 1))
    down_sum = weight_grad(mlp_grad, active, n_batch).T
    active_grad = jnp.einsum(
        "rld,fd->rlf", mlp_grad, down_weight, preferred_element_type=jnp.float32
    )
    gelu_pull = jax.vjp(gelu, hidden)[1]
    hidden_grad = gelu_pull(active_grad)[0].astype(jnp.bfloat16)
    up_bias_grad = jnp.sum(hidden_grad.astype(jnp.float32), axis=(0, 1))
    up_sum = weight_grad(mlp_in, hidden_grad, n_batch)
    mlp_part = jnp.einsum("rlf,df->rld", hidden_grad, up_weight, preferred_element_type=jnp.float32)
    mlp_in_grad = tensor_sum(mlp_part.astype(jnp.bfloat16), n_tensor)
    scale_two_grad = mlp_in_grad * normed_two
    scaled_two = mlp_in_grad * (1.0 + scale_two)
    middle_grad = grad_float + inverse_two * (
        scaled_two
        - jnp.mean(scaled_two, axis=-1, keepdims=True)
        - normed_two * jnp.mean(scaled_two * normed_two, axis=-1, keepdims=True)
    )
    attn_grad = (middle_grad * gate_one).astype(jnp.bfloat16)
    gate_one_grad = middle_grad * attn_out
    mlp_in_share = mine(mlp_in_grad)
    scale_two_share = mine(scale_two_grad)
    middle_share = mine(middle_grad)
    gate_one_share = mine(gate_one_grad)
    proj_bias_grad = jnp.sum(attn_grad.astype(jnp.float32), axis=(0, 1))
    proj_sum = weight_grad(attn_grad, attended, n_batch).T
    attended_grad = jnp.einsum(
        "rld,cd->rlc", attn_grad, proj_weight, preferred_element_type=jnp.float32
    )
    attended_grad = attended_grad.astype(jnp.bfloat16).reshape(head_shape)
    scores = attention_scores(queries, key_vecs, same_image, score_scale)
    attn_probs = jnp.exp(scores - log_total)
    value_grad = jnp.einsum(
        "rhqk,rqhe->rkhe",
        attn_probs.astype(jnp.bfloat16),
        attended_grad,
        preferred_element_type=jnp.float32,
    )
    prob_grad = jnp.einsum(
        "rqhe,rkhe->rhqk", attended_grad, values, preferred_element_type=jnp.float32
    )
    score_grad = attn_probs * (prob_grad - jnp.sum(prob_grad * attn_probs, axis=-1, keepdims=True))
    score_grad = score_grad.astype(jnp.bfloat16)
    query_grad = (
        jnp.einsum("rhqk,rkhe->rqhe", score_grad, key_vecs, preferred_element_type=jnp.float32)
        * score_scale
    )
    key_grad = (
        jnp.einsum("rhqk,rqhe->rkhe", score_grad, queries, preferred_element_type=jnp.float32)
        * score_scale
    )
    flat_shape = (row_count, length, local_width)
    triple_grad = jnp.stack(
        [
            query_grad.reshape(flat_shape),
            key_grad.reshape(flat_shape),
            value_grad.reshape(flat_shape),
        ],
        axis=2,
    ).astype(jnp.bfloat16)
    qv_bias_grad = jnp.sum(triple_grad[:, :, 0::2].astype(jnp.float32), axis=(0, 1))
    flat_triple = triple_grad.reshape((row_count, length, 3 * local_width))
    qkv_sum = weight_grad(attn_in, flat_triple, n_batch).reshape((-1, 3, local_width))
    attn_part = jnp.einsum(
        "rljc,djc->rld", triple_grad, qkv_weight, preferred_element_type=jnp.float32
    )
    attn_part = attn_part.astype(jnp.bfloat16)
    if n_tensor == 2:
        kept = mine(attn_part)
        sent = lax.dynamic_slice_in_dim(attn_part, local_width - offset, local_width, 2)
        attn_in_grad = kept.astype(jnp.float32) + exchange(sent, "tensor").astype(jnp.float32)
    else:
        attn_in_grad = lax.psum_scatter(
            attn_part, "tensor", scatter_dimension=2, tiled=True
        ).astype(jnp.float32)
    normed_mine = mine(normed_one)
    scaled_one = attn_in_grad * (1.0 + mine(scale_one))
    row_sums = jnp.sum(scaled_one, axis=-1)
    cross_sums = jnp.sum(scaled_one * normed_mine, axis=-1)
    token_parts = (
        attn_in_grad,
        attn_in_grad * normed_mine,
        gate_one_share,
        mlp_in_share,
        scale_two_share,
        mine(gate_two_grad),
    )
    mod_tgrad = jnp.stack([segment_total(one_hot, part) for part in token_parts], axis=2).astype(
        jnp.bfloat16
    )
    cond_all = batch_gather(cond_act, n_batch)
    tgrad_all = batch_gather(mod_tgrad, n_batch)
    block = model_width // n_batch
    cond_block = lax.dynamic_slice_in_dim(
        cond_all, lax.axis_index("batch") * block, block, cond_all.ndim - 1
    )
    mod_sum = jnp.einsum(
        "prsd,prsjc->djc", cond_block, tgrad_all, preferred_element_type=jnp.float32
    )
    modbias_sum = jnp.sum(tgrad_all.astype(jnp.float32), axis=(0, 1, 2))
    cond_part = jnp.einsum(
        "rsjc,djc->rsd", mod_tgrad, mod_weight, preferred_element_type=jnp.float32
    )
    row_whole, cross_whole, cond_act_grad = (
        tensor_sum(row_sums.astype(jnp.bfloat16), n_tensor),
        tensor_sum(cross_sums.astype(jnp.bfloat16), n_tensor),
        tensor_sum(cond_part.astype(jnp.bfloat16), n_tensor),
    )
    token_grad = middle_share + inverse_one * (
        scaled_one
        - row_whole[:, :, None] / model_width
        - normed_mine * (cross_whole[:, :, None] / model_width)
    )
    silu_pull = jax.vjp(silu, cond_float)[1]
    condition_grad = silu_pull(cond_act_grad)[0]
    widths = (2 * local_width, model_width, up_bias.shape[0], model_width)
    flat_bias = jnp.concatenate(
        [qv_bias_grad.reshape(-1), proj_bias_grad, up_bias_grad, down_bias_grad]
    )
    flat_bias = jnp.sum(batch_gather(flat_bias, n_batch), axis=0)
    pieces = []
    for width in widths:
        pieces.append(flat_bias[:width])
        flat_bias = flat_bias[width:]
    qv_sum, projbias_sum, upbias_sum, downbias_sum = pieces
    qv_sum = qv_sum.reshape((2, local_width))
    return (
        layer_out,
        token_grad,
        condition_grad,
        qkv_sum,
        qv_sum,
        proj_sum,
        projbias_sum,
        up_sum,
        upbias_sum,
        down_sum,
        downbias_sum,
        mod_sum,
        modbias_sum,
    )


def solution(mesh):
    return jax.shard_map(
        functools.partial(on_device, mesh.shape["batch"]),
        mesh=mesh,
        in_specs=(
            P("batch", None, None),
            P("batch", None),
            P("batch", None, None),
            P("batch", None),
            P(None, None, "tensor"),
            P(None, "tensor"),
            P("tensor", None),
            P(),
            P(None, "tensor"),
            P("tensor"),
            P("tensor", None),
            P(),
            P(None, None, "tensor"),
            P(None, "tensor"),
            P("batch", None, None),
        ),
        out_specs=(
            P("batch", None, None),
            P("batch", None, "tensor"),
            P("batch", None, None),
            P("batch", None, "tensor"),
            P(None, "tensor"),
            P("tensor", "batch"),
            P(),
            P("batch", "tensor"),
            P("tensor"),
            P("tensor", "batch"),
            P(),
            P("batch", None, "tensor"),
            P(None, "tensor"),
        ),
        check_vma=False,
    )
```

```python
import functools

import jax
import jax.numpy as jnp
from jax import lax
from jax.experimental import pallas as pl
from jax.experimental.pallas import tpu as pltpu
from jax.sharding import PartitionSpec as P

EPS = 1e-06
HIGHEST = lax.Precision.HIGHEST
HEAD_DIM = 72
SEGS = 8
MOST = 256
LOG2E = 1.4426950408889634
NEG = -1e30


def band(begin, width, length):
    low = max(0, (begin - MOST + 1) // 128 * 128)
    high = min(length, -(-(begin + width + MOST - 1) // 128) * 128)
    return low, high


def natural(array):
    return array.astype(jnp.float32).T.astype(jnp.bfloat16)


def marks(seg_row):
    slots = lax.broadcasted_iota(jnp.int32, (SEGS, seg_row.shape[-1]), 0)
    return (slots == seg_row[...]).astype(jnp.float32)


def fill(head, qkv, one_hot, q_aug, k_nat):
    query = jnp.concatenate([qkv[0, head].astype(jnp.float32), (1.0 - one_hot) * NEG], axis=0)
    q_aug[...] = query.astype(jnp.bfloat16)
    k_nat[...] = natural(jnp.concatenate([qkv[1, head].astype(jnp.float32), one_hot], axis=0))


def attention_forward_kernel(width, seg_row, qkv, out, stat, q_aug, k_nat):
    heads, length = qkv.shape[1], qkv.shape[3]
    factor = HEAD_DIM**-0.5 * LOG2E
    one_hot = marks(seg_row)

    def one(head, carry):
        fill(head, qkv, one_hot, q_aug, k_nat)
        for begin in range(0, length, width):
            low, high = band(begin, width, length)
            span = slice(begin, begin + width)
            scores = jnp.dot(
                k_nat[low:high, :], q_aug[:, span], preferred_element_type=jnp.float32
            )
            peak = jnp.max(scores, axis=0, keepdims=True) * factor
            shifted = jnp.exp2(scores * factor - peak)
            total = jnp.sum(shifted, axis=0, keepdims=True)
            got = jnp.dot(
                qkv[2, head, :, low:high],
                shifted.astype(jnp.bfloat16),
                preferred_element_type=jnp.float32,
            )
            out[head, :, span] = (got * (1.0 / total)).astype(jnp.bfloat16)
            stat[head, :, span] = peak + jnp.log2(total)
        return carry

    lax.fori_loop(0, heads, one, 0, unroll=2)


def attention_backward_kernel(
    width, seg_row, qkv, stat, grad, out, q_aug, k_nat, v_nat, q_nat, g_nat, p_all, s_all
):
    heads, length = qkv.shape[1], qkv.shape[3]
    scale = HEAD_DIM**-0.5
    factor = scale * LOG2E
    one_hot = marks(seg_row)

    def one(head, carry):
        fill(head, qkv, one_hot, q_aug, k_nat)
        v_nat[...] = natural(qkv[2, head])
        q_nat[...] = natural(qkv[0, head])
        g_nat[...] = natural(grad[head])
        for begin in range(0, length, width):
            low, high = band(begin, width, length)
            span = slice(begin, begin + width)
            scores = jnp.dot(
                k_nat[low:high, :], q_aug[:, span], preferred_element_type=jnp.float32
            )
            probs = jnp.exp2(scores * factor - stat[head, :, span])
            prob_grad = jnp.dot(
                v_nat[low:high, :], grad[head, :, span], preferred_element_type=jnp.float32
            )
            row = jnp.sum(prob_grad * probs, axis=0, keepdims=True)
            score_grad = (probs * (prob_grad - row)).astype(jnp.bfloat16)
            p_all[low:high, span] = probs.astype(jnp.bfloat16)
            s_all[low:high, span] = score_grad
            got = jnp.dot(
                qkv[1, head, :, low:high], score_grad, preferred_element_type=jnp.float32
            )
            out[0, head, :, span] = (got * scale).astype(jnp.bfloat16)
        for begin in range(0, length, width):
            span = slice(begin, begin + width)
            reach = [q for q in range(0, length, width) if band(q, width, length)[0] < begin + width and band(q, width, length)[1] > begin]
            low, high = reach[0], reach[-1] + width
            key_grad = jnp.dot(
                s_all[span, low:high], q_nat[low:high, :], preferred_element_type=jnp.float32
            )
            value_grad = jnp.dot(
                p_all[span, low:high], g_nat[low:high, :], preferred_element_type=jnp.float32
            )
            out[1, head, :, span] = (key_grad * scale).T.astype(jnp.bfloat16)
            out[2, head, :, span] = value_grad.T.astype(jnp.bfloat16)
        return carry

    if width < MOST:
        p_all[...] = jnp.zeros_like(p_all)
        s_all[...] = jnp.zeros_like(s_all)
    lax.fori_loop(0, heads, one, 0, unroll=2)


VMEM = pl.BlockSpec(memory_space=pltpu.VMEM)


def attention_forward(segments, qkv, width=256):
    heads, length = qkv.shape[1], qkv.shape[3]
    return pl.pallas_call(
        functools.partial(attention_forward_kernel, width),
        in_specs=[VMEM] * 2,
        out_specs=[VMEM] * 2,
        out_shape=[
            jax.ShapeDtypeStruct((heads, HEAD_DIM, length), jnp.bfloat16),
            jax.ShapeDtypeStruct((heads, 1, length), jnp.float32),
        ],
        scratch_shapes=[
            pltpu.VMEM((HEAD_DIM + SEGS, length), jnp.bfloat16),
            pltpu.VMEM((length, HEAD_DIM + SEGS), jnp.bfloat16),
        ],
        compiler_params=pltpu.CompilerParams(vmem_limit_bytes=32 << 20),
        cost_estimate=pl.CostEstimate(
            flops=4 * heads * length * length * HEAD_DIM,
            bytes_accessed=8 * heads * HEAD_DIM * length,
            transcendentals=heads * length * length,
        ),
    )(segments, qkv)


def attention_backward(segments, qkv, stat, grad, width=256):
    heads, length = qkv.shape[1], qkv.shape[3]
    return pl.pallas_call(
        functools.partial(attention_backward_kernel, width),
        in_specs=[VMEM] * 4,
        out_specs=VMEM,
        out_shape=jax.ShapeDtypeStruct(qkv.shape, jnp.bfloat16),
        scratch_shapes=[
            pltpu.VMEM((HEAD_DIM + SEGS, length), jnp.bfloat16),
            pltpu.VMEM((length, HEAD_DIM + SEGS), jnp.bfloat16),
            pltpu.VMEM((length, HEAD_DIM), jnp.bfloat16),
            pltpu.VMEM((length, HEAD_DIM), jnp.bfloat16),
            pltpu.VMEM((length, HEAD_DIM), jnp.bfloat16),
            pltpu.VMEM((length, length), jnp.bfloat16),
            pltpu.VMEM((length, length), jnp.bfloat16),
        ],
        compiler_params=pltpu.CompilerParams(vmem_limit_bytes=32 << 20),
        cost_estimate=pl.CostEstimate(
            flops=10 * heads * length * length * HEAD_DIM,
            bytes_accessed=14 * heads * HEAD_DIM * length,
            transcendentals=heads * length * length,
        ),
    )(segments, qkv, stat, grad)


def silu(array):
    return array / (1.0 + jnp.exp(-array))


def gelu(array):
    tanh_arg = 0.7978845608028654 * (array + 0.044715 * array * array * array)
    return 0.5 * array * (1.0 + jnp.tanh(tanh_arg))


def normalize(array):
    center = array - jnp.mean(array, axis=-1, keepdims=True)
    spread = jnp.mean(center * center, axis=-1, keepdims=True)
    inverse = lax.rsqrt(spread + EPS)
    return (center * inverse, inverse)


def product(spec, left, right):
    return jnp.einsum(spec, left, right, preferred_element_type=jnp.float32)


def segment_pick(one_hot, table):
    return jnp.einsum("ls,sc->lc", one_hot, table, precision=HIGHEST)


def segment_total(one_hot, array):
    return jnp.einsum("ls,lc->sc", one_hot, array, precision=HIGHEST)


def exchange(array):
    return lax.ppermute(array, "tensor", [(0, 1), (1, 0)])


def tensor_sum(array, size):
    if size == 2:
        return array.astype(jnp.float32) + exchange(array).astype(jnp.float32)
    return lax.psum(array, "tensor").astype(jnp.float32)


def tensor_join(array, size):
    if size == 2:
        other = exchange(array)
        first = lax.axis_index("tensor") == 0
        return jnp.concatenate(
            [jnp.where(first, array, other), jnp.where(first, other, array)], axis=-1
        )
    return lax.all_gather(array, "tensor", axis=array.ndim - 1, tiled=True)


def partners(size, bit):
    return [(i, i ^ (1 << bit)) for i in range(size)]


def tie(*values):
    return lax.optimization_barrier(values)


class Gather:
    def __init__(self, array, size, order):
        self.held, self.size, self.order = array[None], size, list(order)

    def step(self):
        if self.order:
            bit = self.order.pop(0)
            other = lax.ppermute(self.held, "batch", partners(self.size, bit))
            self.held = jnp.concatenate([self.held, other], axis=0)


class Halving:
    def __init__(self, halves, size):
        self.size, self.bits = size, size.bit_length() - 1
        self.cubes = [
            half.reshape((2,) * self.bits + (half.shape[0] // size, half.shape[1]))
            for half in halves
        ]
        self.stage = 0
        self.order = list(range(self.bits))
        self.keep = self.got = None

    def pieces(self):
        index = lax.axis_index("batch")
        keeps, sends, bits = [], [], []
        for at, cube in enumerate(self.cubes):
            bit = self.order[1 - self.stage if at == 1 and self.stage < 2 else self.stage]
            axis = self.bits - 1 - bit
            mine = (index >> bit) & 1
            sends.append(lax.dynamic_index_in_dim(cube, 1 - mine, axis, keepdims=True))
            keeps.append(lax.dynamic_index_in_dim(cube, mine, axis, keepdims=True))
            bits.append(bit)
        return keeps, sends, bits

    def send(self, *others):
        self.keep, sends, bits = self.pieces()
        tied = tie(*sends, *others)
        sends, others = tied[: len(sends)], tied[len(sends) :]
        self.got = [
            lax.ppermute(piece, "batch", partners(self.size, bit))
            for piece, bit in zip(sends, bits)
        ]
        return others

    def take(self, *others):
        tied = tie(*self.got, *others)
        got, others = tied[: len(self.got)], tied[len(self.got) :]
        self.stage += 1
        last = self.stage == self.bits
        self.cubes = []
        for keep, new in zip(self.keep, got):
            total = keep.astype(jnp.float32) + new.astype(jnp.float32)
            self.cubes.append(total if last else total.astype(jnp.bfloat16))
        if self.stage == 2:
            self.cubes = [jnp.concatenate(self.cubes, axis=-1)]
        return others

    def result(self):
        while self.stage < self.bits:
            self.send()
            self.take()
        return self.cubes[0].reshape(self.cubes[0].shape[-2:])


def high_low(array):
    high = array.astype(jnp.bfloat16)
    return [high, (array - high.astype(jnp.float32)).astype(jnp.bfloat16)]


def on_device(
    n_batch,
    tokens,
    segment_ids,
    conditions,
    condition_segment,
    qkv_weight,
    qv_bias,
    proj_weight,
    proj_bias,
    up_weight,
    up_bias,
    down_weight,
    down_bias,
    mod_weight,
    mod_bias,
    out_grad,
):
    bf16, f32 = jnp.bfloat16, jnp.float32
    length, model_width = tokens.shape[1:]
    local_width = qkv_weight.shape[2]
    hidden_width = up_weight.shape[1]
    heads = local_width // HEAD_DIM
    n_tensor = model_width // local_width
    offset = lax.axis_index("tensor") * local_width
    bits = list(range(n_batch.bit_length() - 1))

    def mine(array):
        return lax.dynamic_slice_in_dim(array, offset, local_width, 1)

    cond_float = conditions[0].astype(f32)
    cond_act = silu(cond_float).astype(bf16)
    mod_local = product("sd,djc->sjc", cond_act, mod_weight) + mod_bias
    modulation = tensor_join(mod_local, n_tensor)
    one_hot = (segment_ids[0][:, None] == condition_segment[0][None, :]).astype(f32)
    shift_one = segment_pick(one_hot, modulation[:, 0])
    scale_one = segment_pick(one_hot, modulation[:, 1])
    gate_one = segment_pick(one_hot, modulation[:, 2])
    shift_two = segment_pick(one_hot, modulation[:, 3])
    scale_two = segment_pick(one_hot, modulation[:, 4])
    gate_two = segment_pick(one_hot, modulation[:, 5])
    tok_float = tokens[0].astype(f32)
    normed_one, inverse_one = normalize(tok_float)
    attn_in = (normed_one * (1.0 + scale_one) + shift_one).astype(bf16)
    biases = jnp.stack([qv_bias[0], jnp.zeros_like(qv_bias[0]), qv_bias[1]])
    qkv = product("djc,ld->jcl", qkv_weight, attn_in) + biases[:, :, None]
    qkv = qkv.astype(bf16).reshape((3, heads, HEAD_DIM, length))
    attended, stat = attention_forward(segment_ids, qkv)
    attended = attended.reshape((local_width, length))
    proj_part = product("cl,cd->ld", attended, proj_weight).astype(bf16)
    attn_out = tensor_sum(proj_part, n_tensor) + proj_bias
    middle = tok_float + gate_one * attn_out
    normed_two, inverse_two = normalize(middle)
    mlp_in = (normed_two * (1.0 + scale_two) + shift_two).astype(bf16)
    hidden = product("ld,df->lf", mlp_in, up_weight) + up_bias
    active = gelu(hidden).astype(bf16)
    grad_float = out_grad[0].astype(f32)
    mlp_grad = (grad_float * gate_two).astype(bf16)
    down_bias_grad = jnp.sum(mlp_grad.astype(f32), axis=0)

    cut = hidden_width // 2

    def weight_grad(left, right):
        return product("ld,lc->dc", left, right).astype(bf16)

    down_sum = Halving([weight_grad(mlp_grad, active[:, :cut]), weight_grad(mlp_grad, active[:, cut:])], n_batch)
    (mlp_grad_then,) = down_sum.send(mlp_grad)
    active_grad = product("ld,fd->lf", mlp_grad_then, down_weight)
    hidden_grad = jax.vjp(gelu, hidden)[1](active_grad)[0].astype(bf16)
    up_bias_grad = jnp.sum(hidden_grad.astype(f32), axis=0)
    mlp_part = product("lf,df->ld", hidden_grad, up_weight).astype(bf16)
    up_halves = [weight_grad(mlp_in, hidden_grad[:, :cut]), weight_grad(mlp_in, hidden_grad[:, cut:])]
    mlp_in_grad = tensor_sum(mlp_part, n_tensor)
    up_first, up_second = down_sum.take(*up_halves)
    (mlp_in_grad,) = down_sum.send(mlp_in_grad)
    scale_two_grad = mlp_in_grad * normed_two
    scaled_two = mlp_in_grad * (1.0 + scale_two)
    middle_grad = grad_float + inverse_two * (
        scaled_two
        - jnp.mean(scaled_two, axis=-1, keepdims=True)
        - normed_two * jnp.mean(scaled_two * normed_two, axis=-1, keepdims=True)
    )
    attn_grad = (middle_grad * gate_one).astype(bf16)
    proj_bias_grad = jnp.sum(attn_grad.astype(f32), axis=0)
    attended_grad = product("ld,cd->cl", attn_grad, proj_weight).astype(bf16)
    proj_half = product("ld,cl->dc", attn_grad, attended).astype(bf16)

    (attended_grad,) = down_sum.take(attended_grad)
    up_sum = Halving([up_first, up_second], n_batch)
    (attended_grad,) = up_sum.send(attended_grad)
    (attended_grad,) = down_sum.send(attended_grad)
    triple = attention_backward(
        segment_ids, qkv, stat, attended_grad.reshape((heads, HEAD_DIM, length))
    ).reshape((3, local_width, length))
    (triple,) = up_sum.take(triple)
    (triple,) = down_sum.take(triple)
    (triple,) = up_sum.send(triple)
    (triple,) = down_sum.send(triple)
    qv_bias_grad = jnp.sum(triple[0::2].astype(f32), axis=2)
    both = triple[:2].reshape((2 * local_width, length))
    first_half = product("ld,cl->dc", attn_in, both).astype(bf16)
    value_half = product("ld,cl->dc", attn_in, triple[2]).astype(bf16)
    second_half = jnp.concatenate([value_half, proj_half], axis=1)
    first_half, second_half = up_sum.take(first_half, second_half)
    first_half, second_half = down_sum.take(first_half, second_half)
    qkv_sum = Halving([first_half, second_half], n_batch)
    (triple,) = qkv_sum.send(triple)
    (triple,) = up_sum.send(triple)
    attn_part = product("jcl,djc->ld", triple, qkv_weight).astype(bf16)
    if n_tensor == 2:
        sent = lax.dynamic_slice_in_dim(attn_part, local_width - offset, local_width, 1)
        attn_in_grad = mine(attn_part).astype(f32) + exchange(sent).astype(f32)
    else:
        attn_in_grad = lax.psum_scatter(
            attn_part, "tensor", scatter_dimension=1, tiled=True
        ).astype(f32)
    normed_mine = mine(normed_one)
    scaled_one = attn_in_grad * (1.0 + mine(scale_one))
    row_sums = jnp.sum(scaled_one, axis=-1)
    cross_sums = jnp.sum(scaled_one * normed_mine, axis=-1)

    (active_then, row_sums) = tie(active, row_sums)
    down_part = product("lf,fd->ld", active_then, down_weight).astype(bf16)
    mlp_out = tensor_sum(down_part, n_tensor) + down_bias
    layer_out = (middle + gate_two * mlp_out).astype(bf16)
    gate_two_grad = grad_float * mlp_out
    early_parts = (
        mine(middle_grad * attn_out),
        mine(mlp_in_grad),
        mine(scale_two_grad),
        mine(gate_two_grad),
    )
    early_tgrad = jnp.stack([segment_total(one_hot, part) for part in early_parts]).astype(bf16)
    late_parts = (attn_in_grad, attn_in_grad * normed_mine)
    late_tgrad = jnp.stack([segment_total(one_hot, part) for part in late_parts]).astype(bf16)
    row_whole = tensor_sum(row_sums.astype(bf16), n_tensor)
    cross_whole = tensor_sum(cross_sums.astype(bf16), n_tensor)
    token_grad = mine(middle_grad) + inverse_one * (
        scaled_one
        - row_whole[:, None] / model_width
        - normed_mine * (cross_whole[:, None] / model_width)
    )
    cond_part = product("jsc,djc->sd", jnp.concatenate([late_tgrad, early_tgrad]), mod_weight)
    cond_act_grad = tensor_sum(cond_part.astype(bf16), n_tensor)
    condition_grad = jax.vjp(silu, cond_float)[1](cond_act_grad)[0]

    early_bias = jnp.concatenate([proj_bias_grad, down_bias_grad, up_bias_grad])
    early = [early_tgrad, cond_act] + high_low(early_bias)
    late = [late_tgrad] + high_low(qv_bias_grad)

    def packed(arrays):
        return jnp.concatenate([array.reshape((-1, local_width)) for array in arrays], axis=0)

    order = bits[:1:-1] + bits[1::-1]
    early_all = Gather(packed(early), n_batch, order)
    late_all = Gather(packed(late), n_batch, order)

    (early_all.held,) = qkv_sum.take(early_all.held)
    (early_all.held,) = up_sum.take(early_all.held)
    (early_all.held,) = qkv_sum.send(early_all.held)
    (early_all.held,) = up_sum.send(early_all.held)
    early_all.step()
    early_all.step()
    late_all.step()
    late_all.step()
    (early_all.held, late_all.held) = qkv_sum.take(early_all.held, late_all.held)
    (early_all.held, late_all.held) = up_sum.take(early_all.held, late_all.held)
    (early_all.held, late_all.held) = qkv_sum.send(early_all.held, late_all.held)
    while early_all.order:
        early_all.step()
        late_all.step()
    (early_all.held, late_all.held) = qkv_sum.take(early_all.held, late_all.held)
    qkv_sum.send()
    segs = one_hot.shape[1]
    block = model_width // n_batch
    early_all, late_all = early_all.held, late_all.held
    early_tall = early_all[:, : 4 * segs].reshape((n_batch, 4, segs, local_width))
    cond_all = early_all[:, 4 * segs : (4 + n_tensor) * segs].reshape((n_batch, segs, model_width))
    bias_all = early_all[:, (4 + n_tensor) * segs :]
    late_tall = late_all[:, : 2 * segs].reshape((n_batch, 2, segs, local_width))
    late_bias = late_all[:, 2 * segs :]

    def bias_sum(held):
        return jnp.sum(held.astype(f32), axis=0).reshape((2, -1)).sum(axis=0)

    bias_all = bias_sum(bias_all)
    qv_sum = bias_sum(late_bias).reshape((2, local_width))
    projbias_sum = bias_all[:model_width]
    downbias_sum = bias_all[model_width : 2 * model_width]
    upbias_sum = bias_all[2 * model_width :]
    tgrad_all = jnp.concatenate([late_tall, early_tall], axis=1)
    cond_block = lax.dynamic_slice_in_dim(cond_all, lax.axis_index("batch") * block, block, 2)
    mod_sum = product("psd,pjsc->djc", cond_block, tgrad_all)
    modbias_sum = jnp.sum(tgrad_all.astype(f32), axis=(0, 2))

    qkv_sum.take()
    last = qkv_sum.result()
    down = down_sum.result().T
    up = up_sum.result()
    return (
        layer_out[None],
        token_grad[None],
        condition_grad[None],
        last[:, : 3 * local_width].reshape((-1, 3, local_width)),
        qv_sum,
        last[:, 3 * local_width :].T,
        projbias_sum,
        up,
        upbias_sum,
        down,
        downbias_sum,
        mod_sum,
        modbias_sum,
    )


def solution(mesh):
    return jax.shard_map(
        functools.partial(on_device, mesh.shape["batch"]),
        mesh=mesh,
        in_specs=(
            P("batch", None, None),
            P("batch", None),
            P("batch", None, None),
            P("batch", None),
            P(None, None, "tensor"),
            P(None, "tensor"),
            P("tensor", None),
            P(),
            P(None, "tensor"),
            P("tensor"),
            P("tensor", None),
            P(),
            P(None, None, "tensor"),
            P(None, "tensor"),
            P("batch", None, None),
        ),
        out_specs=(
            P("batch", None, None),
            P("batch", None, "tensor"),
            P("batch", None, None),
            P("batch", None, "tensor"),
            P(None, "tensor"),
            P("tensor", "batch"),
            P(),
            P("batch", "tensor"),
            P("tensor"),
            P("tensor", "batch"),
            P(),
            P("batch", None, "tensor"),
            P(None, "tensor"),
        ),
        check_vma=False,
    )
```

```python
import functools

import jax
import jax.numpy as jnp
from jax import lax
from jax.experimental import pallas as pl
from jax.experimental.pallas import tpu as pltpu
from jax.sharding import PartitionSpec as P

EPS = 1e-06
HEAD_DIM = 72
SEGS = 8
MOST = 256
LOG2E = 1.4426950408889634
NEG = -1e30


def band(begin, width, length):
    low = max(0, (begin - MOST + 1) // 128 * 128)
    high = min(length, -(-(begin + width + MOST - 1) // 128) * 128)
    return low, high


def natural(array):
    return array.astype(jnp.float32).T.astype(jnp.bfloat16)


def marks(seg_row):
    slots = lax.broadcasted_iota(jnp.int32, (SEGS, seg_row.shape[-1]), 0)
    return (slots == seg_row[...]).astype(jnp.float32)


def fill(head, qkv, one_hot, q_aug, k_nat):
    query = jnp.concatenate([qkv[0, head].astype(jnp.float32), (1.0 - one_hot) * NEG], axis=0)
    q_aug[...] = query.astype(jnp.bfloat16)
    k_nat[...] = natural(jnp.concatenate([qkv[1, head].astype(jnp.float32), one_hot], axis=0))


def attention_forward_kernel(width, seg_row, qkv, out, stat, q_aug, k_nat):
    heads, length = qkv.shape[1], qkv.shape[3]
    factor = HEAD_DIM**-0.5 * LOG2E
    one_hot = marks(seg_row)

    def one(head, carry):
        fill(head, qkv, one_hot, q_aug, k_nat)
        for begin in range(0, length, width):
            low, high = band(begin, width, length)
            span = slice(begin, begin + width)
            scores = jnp.dot(
                k_nat[low:high, :], q_aug[:, span], preferred_element_type=jnp.float32
            )
            peak = jnp.max(scores, axis=0, keepdims=True) * factor
            shifted = jnp.exp2(scores * factor - peak)
            total = jnp.sum(shifted, axis=0, keepdims=True)
            got = jnp.dot(
                qkv[2, head, :, low:high],
                shifted.astype(jnp.bfloat16),
                preferred_element_type=jnp.float32,
            )
            out[head, :, span] = (got * (1.0 / total)).astype(jnp.bfloat16)
            stat[head, :, span] = peak + jnp.log2(total)
        return carry

    lax.fori_loop(0, heads, one, 0, unroll=2)


def attention_backward_kernel(
    width, seg_row, qkv, stat, grad, out, q_aug, k_nat, v_nat, q_nat, g_nat, p_all, s_all
):
    heads, length = qkv.shape[1], qkv.shape[3]
    scale = HEAD_DIM**-0.5
    factor = scale * LOG2E
    one_hot = marks(seg_row)

    def one(head, carry):
        fill(head, qkv, one_hot, q_aug, k_nat)
        v_nat[...] = natural(qkv[2, head])
        q_nat[...] = natural(qkv[0, head])
        g_nat[...] = natural(grad[head])
        for begin in range(0, length, width):
            low, high = band(begin, width, length)
            span = slice(begin, begin + width)
            scores = jnp.dot(
                k_nat[low:high, :], q_aug[:, span], preferred_element_type=jnp.float32
            )
            probs = jnp.exp2(scores * factor - stat[head, :, span])
            prob_grad = jnp.dot(
                v_nat[low:high, :], grad[head, :, span], preferred_element_type=jnp.float32
            )
            row = jnp.sum(prob_grad * probs, axis=0, keepdims=True)
            score_grad = (probs * (prob_grad - row)).astype(jnp.bfloat16)
            p_all[low:high, span] = probs.astype(jnp.bfloat16)
            s_all[low:high, span] = score_grad
            got = jnp.dot(
                qkv[1, head, :, low:high], score_grad, preferred_element_type=jnp.float32
            )
            out[0, head, :, span] = (got * scale).astype(jnp.bfloat16)
        for begin in range(0, length, width):
            span = slice(begin, begin + width)
            reach = [q for q in range(0, length, width) if band(q, width, length)[0] < begin + width and band(q, width, length)[1] > begin]
            low, high = reach[0], reach[-1] + width
            key_grad = jnp.dot(
                s_all[span, low:high], q_nat[low:high, :], preferred_element_type=jnp.float32
            )
            value_grad = jnp.dot(
                p_all[span, low:high], g_nat[low:high, :], preferred_element_type=jnp.float32
            )
            out[1, head, :, span] = (key_grad * scale).T.astype(jnp.bfloat16)
            out[2, head, :, span] = value_grad.T.astype(jnp.bfloat16)
        return carry

    if width < MOST:
        p_all[...] = jnp.zeros_like(p_all)
        s_all[...] = jnp.zeros_like(s_all)
    lax.fori_loop(0, heads, one, 0, unroll=2)


VMEM = pl.BlockSpec(memory_space=pltpu.VMEM)


def attention_forward(segments, qkv, width=256):
    heads, length = qkv.shape[1], qkv.shape[3]
    return pl.pallas_call(
        functools.partial(attention_forward_kernel, width),
        in_specs=[VMEM] * 2,
        out_specs=[VMEM] * 2,
        out_shape=[
            jax.ShapeDtypeStruct((heads, HEAD_DIM, length), jnp.bfloat16),
            jax.ShapeDtypeStruct((heads, 1, length), jnp.float32),
        ],
        scratch_shapes=[
            pltpu.VMEM((HEAD_DIM + SEGS, length), jnp.bfloat16),
            pltpu.VMEM((length, HEAD_DIM + SEGS), jnp.bfloat16),
        ],
        compiler_params=pltpu.CompilerParams(vmem_limit_bytes=24 << 20),
        cost_estimate=pl.CostEstimate(
            flops=4 * heads * length * length * HEAD_DIM,
            bytes_accessed=8 * heads * HEAD_DIM * length,
            transcendentals=heads * length * length,
        ),
    )(segments, qkv)


def attention_backward(segments, qkv, stat, grad, width=256):
    heads, length = qkv.shape[1], qkv.shape[3]
    return pl.pallas_call(
        functools.partial(attention_backward_kernel, width),
        in_specs=[VMEM] * 4,
        out_specs=VMEM,
        out_shape=jax.ShapeDtypeStruct(qkv.shape, jnp.bfloat16),
        scratch_shapes=[
            pltpu.VMEM((HEAD_DIM + SEGS, length), jnp.bfloat16),
            pltpu.VMEM((length, HEAD_DIM + SEGS), jnp.bfloat16),
            pltpu.VMEM((length, HEAD_DIM), jnp.bfloat16),
            pltpu.VMEM((length, HEAD_DIM), jnp.bfloat16),
            pltpu.VMEM((length, HEAD_DIM), jnp.bfloat16),
            pltpu.VMEM((length, length), jnp.bfloat16),
            pltpu.VMEM((length, length), jnp.bfloat16),
        ],
        compiler_params=pltpu.CompilerParams(vmem_limit_bytes=24 << 20),
        cost_estimate=pl.CostEstimate(
            flops=10 * heads * length * length * HEAD_DIM,
            bytes_accessed=14 * heads * HEAD_DIM * length,
            transcendentals=heads * length * length,
        ),
    )(segments, qkv, stat, grad)


CHUNK = 128


def dot(left, right):
    return jnp.dot(left, right, preferred_element_type=jnp.float32)


def spans(length):
    return [slice(begin, begin + CHUNK) for begin in range(0, length, CHUNK)]


def wide(value):
    return value.astype(jnp.float32)


def transpose_in_order(order, source, first, second, work):
    length, width = source.shape
    count = order.shape[0]
    rows = width // count
    for span in spans(length):
        work[:, span] = wide(source[span, :]).T
    for at in range(0, count, 2):
        pair = [
            work[pl.ds(pl.multiple_of(order[at + i] * rows, 8), rows), :] for i in range(2)
        ]
        pair = jnp.concatenate(pair, axis=0).astype(jnp.bfloat16)
        quarter = at * 4 // count
        other = at + (count // 4 if quarter == 1 else -count // 4 if quarter == 2 else 0)
        first[at * rows : (at + 2) * rows, :] = pair
        second[other * rows : (other + 2) * rows, :] = pair


def own_part(side, value, width):
    part = value[:, :width]
    for at in range(1, value.shape[1] // width):
        part = jnp.where(side == at, value[:, at * width : (at + 1) * width], part)
    return part


def add_totals(marks, span, value, totals, row):
    high = value.astype(jnp.bfloat16)
    low = (value - wide(high)).astype(jnp.bfloat16)
    pick = marks[:, span]
    totals[row : row + 16, :] += dot(pick, high) + dot(pick, low)


def entry_kernel(
    order, side, picks, tables, tokens, out, mean, inverse, normed_mine, *turned
):
    length, width = tokens.shape
    for span in spans(length):
        pick = picks[span, :]
        value = wide(tokens[span, :])
        middle = jnp.sum(value, axis=1, keepdims=True) / width
        center = value - middle
        spread = jnp.sum(center * center, axis=1, keepdims=True) / width
        scale = lax.rsqrt(spread + EPS)
        mean[span, :] = middle
        inverse[span, :] = scale
        value = center * scale
        normed_mine[span, :] = own_part(side[0], value, normed_mine.shape[1])
        value = value * (1.0 + dot(pick, tables[1])) + dot(pick, tables[0])
        out[span, :] = value.astype(jnp.bfloat16)
    if turned:
        transpose_in_order(order, out, *turned)


def gate_kernel(order, picks, tables, grad, out, bias, *turned):
    length, width = grad.shape
    total = jnp.zeros((1, width), jnp.float32)
    for span in spans(length):
        value = (wide(grad[span, :]) * dot(picks[span, :], tables[5])).astype(jnp.bfloat16)
        out[span, :] = value
        total += jnp.sum(wide(value), axis=0, keepdims=True)
    bias[...] = total
    if turned:
        transpose_in_order(order, out, *turned)


def middle_kernel(
    order, picks, tables, tokens, part, other, bias, attn_out, normed, inverse, out, *turned
):
    length, width = tokens.shape
    for span in spans(length):
        pick = picks[span, :]
        value = wide(part[span, :]) + wide(other[span, :]) + bias[...]
        attn_out[span, :] = value
        value = wide(tokens[span, :]) + dot(pick, tables[2]) * value
        center = value - jnp.sum(value, axis=1, keepdims=True) / width
        spread = jnp.sum(center * center, axis=1, keepdims=True) / width
        scale = lax.rsqrt(spread + EPS)
        inverse[span, :] = scale
        value = center * scale
        normed[span, :] = value
        value = value * (1.0 + dot(pick, tables[4])) + dot(pick, tables[3])
        out[span, :] = value.astype(jnp.bfloat16)
    if turned:
        transpose_in_order(order, out, *turned)


def middle_grad_kernel(
    order, side, picks, marks, tables, part, other, normed, inverse, attn_out, grad,
    out, bias, grad_mine, totals, *turned
):
    length, width = grad.shape
    total = jnp.zeros((1, width), jnp.float32)
    totals[...] = jnp.zeros_like(totals)
    for span in spans(length):
        pick = picks[span, :]
        value = wide(part[span, :]) + wide(other[span, :])
        norm = normed[span, :]
        add_totals(marks, span, value, totals, 16)
        add_totals(marks, span, value * norm, totals, 32)
        value = value * (1.0 + dot(pick, tables[4]))
        plain = jnp.sum(value, axis=1, keepdims=True) / width
        cross = jnp.sum(value * norm, axis=1, keepdims=True) / width
        value = wide(grad[span, :]) + inverse[span, :] * (value - plain - norm * cross)
        grad_mine[span, :] = own_part(side[0], value, grad_mine.shape[1])
        add_totals(marks, span, value * attn_out[span, :], totals, 0)
        value = (value * dot(pick, tables[2])).astype(jnp.bfloat16)
        out[span, :] = value
        total += jnp.sum(wide(value), axis=0, keepdims=True)
    bias[...] = total
    if turned:
        transpose_in_order(order, out, *turned)


def halves_kernel(side, picks, tables, part, tokens, mean, inverse, kept, sent, sums):
    length, width = tokens.shape
    for span in spans(length):
        value = part[span, :]
        kept[span, :] = own_part(side[0], value, kept.shape[1])
        sent[span, :] = own_part(1 - side[0], value, sent.shape[1])
        value = wide(value) * (1.0 + dot(picks[span, :], tables[1]))
        norm = (wide(tokens[span, :]) - mean[span, :]) * inverse[span, :]
        sums[span, 0:1] = jnp.sum(value, axis=1, keepdims=True)
        sums[span, 1:2] = jnp.sum(value * norm, axis=1, keepdims=True)


def token_grad_kernel(
    width, picks, marks, tables, kept, other, sums, other_sums, normed, inverse, grad, out_t, totals
):
    totals[...] = jnp.zeros_like(totals)
    for span in spans(normed.shape[0]):
        value = wide(kept[span, :]) + wide(other[span, :])
        norm = normed[span, :]
        add_totals(marks, span, value, totals, 0)
        add_totals(marks, span, value * norm, totals, 16)
        whole = (sums[span, :] + other_sums[span, :]) / width
        value = value * (1.0 + dot(picks[span, :], tables[1]))
        value = value - whole[:, 0:1] - norm * whole[:, 1:2]
        out_t[:, span] = (grad[span, :] + inverse[span, :] * value).T


def layer_kernel(picks, marks, tables, tokens, attn_out, part, other, bias, grad, out, totals):
    totals[...] = jnp.zeros_like(totals)
    for span in spans(tokens.shape[0]):
        pick = picks[span, :]
        mlp_out = wide(part[span, :]) + wide(other[span, :]) + bias[...]
        middle = wide(tokens[span, :]) + dot(pick, tables[2]) * attn_out[span, :]
        out[span, :] = (middle + dot(pick, tables[5]) * mlp_out).astype(jnp.bfloat16)
        add_totals(marks, span, wide(grad[span, :]) * mlp_out, totals, 0)


SMEM = pl.BlockSpec(memory_space=pltpu.SMEM)


def call(kernel, scalars, arrays, outs, work=None, flops=64, mib=40):
    size = sum(a.size * a.dtype.itemsize for a in arrays)
    size += sum(o.size * o.dtype.itemsize for o in outs)
    return pl.pallas_call(
        kernel,
        in_specs=[SMEM] * len(scalars) + [VMEM] * len(arrays),
        out_specs=[VMEM] * len(outs),
        out_shape=outs,
        scratch_shapes=[] if work is None else [pltpu.VMEM(work, jnp.float32)],
        compiler_params=pltpu.CompilerParams(vmem_limit_bytes=mib << 20),
        cost_estimate=pl.CostEstimate(
            flops=flops * max(a.size for a in arrays), bytes_accessed=size, transcendentals=0
        ),
    )(*scalars, *arrays)


def shape(dims, dtype=jnp.bfloat16):
    return jax.ShapeDtypeStruct(dims, dtype)


def silu(array):
    return array / (1.0 + jnp.exp(-array))


def product(spec, left, right):
    return jnp.einsum(spec, left, right, preferred_element_type=jnp.float32)


def exchange(array):
    return lax.ppermute(array, "tensor", [(0, 1), (1, 0)])


def summands(part, size):
    if size == 2:
        return part, exchange(part)
    return lax.psum(part, "tensor"), jnp.zeros_like(part)


def tensor_join(array, size):
    if size == 2:
        other = exchange(array)
        first = lax.axis_index("tensor") == 0
        return jnp.concatenate(
            [jnp.where(first, array, other), jnp.where(first, other, array)], axis=-1
        )
    return lax.all_gather(array, "tensor", axis=array.ndim - 1, tiled=True)


def partners(size, bit):
    return [(i, i ^ (1 << bit)) for i in range(size)]


def tie(*values):
    return lax.optimization_barrier(values)


class Gather:
    def __init__(self, array, size, order):
        self.held, self.size, self.order = array[None], size, list(order)

    def step(self):
        if self.order:
            bit = self.order.pop(0)
            other = lax.ppermute(self.held, "batch", partners(self.size, bit))
            self.held = jnp.concatenate([self.held, other], axis=0)


class Sum:
    def __init__(self, sends, size):
        self.sends, self.size, self.bits = sends, size, size.bit_length() - 1
        self.keeps, self.got = None, []

    def rows(self, low, high):
        halves = [keep[low:high].astype(jnp.float32) for keep in self.keeps]
        for stage in self.got[:2]:
            halves = [half + new[low:high].astype(jnp.float32) for half, new in zip(halves, stage)]
        if len(self.got) < 2:
            return halves
        total = jnp.concatenate(halves, axis=1)
        for (new,) in self.got[2:]:
            total = total + new[low:high].astype(jnp.float32)
        return [total]

    def send(self, *others):
        stage = len(self.got)
        sends, bits = self.sends, [stage]
        if stage > 0:
            left = self.keeps[0].shape[0] >> stage
            sends = [half.astype(jnp.bfloat16) for half in self.rows(left, 2 * left)]
        if stage < 2:
            bits = [stage, 1 - stage]
        tied = tie(*sends, *others)
        self.flying = [
            lax.ppermute(piece, "batch", partners(self.size, bit))
            for piece, bit in zip(tied, bits)
        ]
        return tied[len(sends) :]

    def take(self, *others):
        tied = tie(*self.flying, *others)
        self.got.append(tied[: len(self.flying)])
        return tied[len(self.flying) :]

    def result(self):
        while len(self.got) < self.bits:
            self.send()
            self.take()
        return self.rows(0, 2 * self.keeps[0].shape[0] // self.size)[0]


def gelu_and_slope(array):
    square = array * array
    bent = jnp.tanh(0.7978845608028654 * (array + 0.044715 * array * square))
    half = 0.5 * (1.0 + bent)
    inner = 0.7978845608028654 * (1.0 + 3.0 * 0.044715 * square)
    return array * half, half + 0.5 * array * (1.0 - bent * bent) * inner


def high_low(array):
    high = lax.reduce_precision(array, 8, 7)
    return [high.astype(jnp.bfloat16), (array - high).astype(jnp.bfloat16)]


def in_three(array):
    high = lax.reduce_precision(array, 8, 7)
    middle = lax.reduce_precision(array - high, 8, 7)
    return [high, middle, array - high - middle]


def on_device(
    n_batch,
    tokens,
    segment_ids,
    conditions,
    condition_segment,
    qkv_weight,
    qv_bias,
    proj_weight,
    proj_bias,
    up_weight,
    up_bias,
    down_weight,
    down_bias,
    mod_weight,
    mod_bias,
    out_grad,
):
    bf16, f32 = jnp.bfloat16, jnp.float32
    tokens, out_grad = tokens[0], out_grad[0]
    length, model_width = tokens.shape
    local_width = qkv_weight.shape[2]
    hidden_width = up_weight.shape[1]
    heads = local_width // HEAD_DIM
    n_tensor = model_width // local_width
    bits = list(range(n_batch.bit_length() - 1))
    block = model_width // n_batch
    in_kernel = block % 8 == 0
    index = lax.axis_index("batch")
    order = jnp.array(
        [sum((p >> bit & 1) << (bits[-1] - bit) for bit in bits) for p in range(n_batch)], jnp.int32
    )
    order = order ^ index
    side = lax.axis_index("tensor")[None]

    def run(kernel, scalars, arrays, outs, mib=32):
        left = shape((model_width, length))
        if in_kernel:
            return call(kernel, scalars, arrays, outs + [left, left], (model_width, length), mib=mib)
        got = call(kernel, scalars, arrays, outs, mib=mib)
        first = got[0].T.reshape((n_batch, block, length))[order].reshape(left.shape)
        parts = jnp.split(first, 4)
        return list(got) + [first, jnp.concatenate([parts[0], parts[2], parts[1], parts[3]])]

    def lefts(first, second):
        half = model_width // 2
        return (first[half:], second[half:]), (first[:half], second[:half])

    def grads(sides, rights, spec="dl,lc->dc"):
        return [product(spec, left, right).astype(bf16) for left, right in zip(sides, rights)]

    cond_float = conditions[0].astype(f32)
    cond_act = silu(cond_float).astype(bf16)
    mod_local = product("sd,djc->jsc", cond_act, mod_weight) + mod_bias[:, None]
    modulation = tensor_join(mod_local, n_tensor)
    segs = modulation.shape[1]
    tables = jnp.concatenate(in_three(modulation) + [jnp.zeros_like(modulation)], axis=1).astype(bf16)
    tables_mine = jnp.concatenate(in_three(mod_local) + [jnp.zeros_like(mod_local)], axis=1).astype(bf16)
    slots = condition_segment[0][jnp.arange(4 * segs) % segs]
    real = jnp.arange(4 * segs) < 3 * segs
    picks = ((segment_ids[0][:, None] == slots[None]) & real[None]).astype(bf16)
    real = jnp.arange(2 * segs) < segs
    marks = ((segment_ids[0][None] == slots[: 2 * segs, None]) & real[:, None]).astype(bf16)
    full, column = (length, model_width), (length, 1)
    mine = (length, local_width)
    row = shape((1, model_width), f32)

    attn_in, mean, inverse_one, normed_mine, *in_t = run(
        entry_kernel,
        [order, side],
        [picks, tables, tokens],
        [shape(full), shape(column, f32), shape(column, f32), shape(mine, f32)],
    )
    in_sends, in_keeps = lefts(*in_t)
    biases = jnp.stack([qv_bias[0], jnp.zeros_like(qv_bias[0]), qv_bias[1]])
    qkv = product("djc,ld->jcl", qkv_weight, attn_in) + biases[:, :, None]
    qkv = qkv.astype(bf16).reshape((3, heads, HEAD_DIM, length))
    attended, stat = attention_forward(segment_ids, qkv)
    attended = attended.reshape((local_width, length))
    proj_part = product("cl,cd->ld", attended, proj_weight).astype(bf16)
    proj_part, proj_other = summands(proj_part, n_tensor)
    out_grad, proj_tied = tie(out_grad, proj_part)
    mlp_grad, down_bias_grad, *grad_t = run(
        gate_kernel, [order], [picks, tables, out_grad], [shape(full), row]
    )
    grad_sends, grad_keeps = lefts(*grad_t)
    proj_other, mlp_grad = tie(proj_other, mlp_grad)
    attn_out, normed_two, inverse_two, mlp_in, *mlp_t = run(
        middle_kernel,
        [order],
        [picks, tables, tokens, proj_tied, proj_other, proj_bias[None]],
        [shape(full, f32), shape(full, f32), shape(column, f32), shape(full)],
        40,
    )
    mlp_sends, mlp_keeps = lefts(*mlp_t)
    hidden = product("ld,df->lf", mlp_in, up_weight) + up_bias
    active, slope = gelu_and_slope(hidden)
    active, slope = tie(active.astype(bf16), slope.astype(bf16))

    cut = hidden_width // 2

    def cols(array):
        return array[:, :cut], array[:, cut:]

    down_sum = Sum(grads(grad_sends, cols(active)), n_batch)
    (mlp_grad_then, active_then) = down_sum.send(mlp_grad, active)
    active_grad = product("ld,fd->lf", mlp_grad_then, down_weight)
    hidden_grad = (active_grad * slope.astype(f32)).astype(bf16)
    mlp_part = product("lf,df->ld", hidden_grad, up_weight).astype(bf16)
    mlp_part, mlp_other = summands(mlp_part, n_tensor)
    (hidden_then, mlp_tied) = tie(hidden_grad, mlp_part)
    up_bias_grad = jnp.sum(hidden_then.astype(f32), axis=0)
    up_sum = Sum(grads(mlp_sends, cols(hidden_then)), n_batch)
    down_sum.keeps = grads(grad_keeps, cols(active_then))
    up_sum.sends[0], up_sum.sends[1], down_sum.keeps[0], down_sum.keeps[1] = down_sum.take(
        *up_sum.sends, *down_sum.keeps
    )
    (mlp_other, hidden_then) = down_sum.send(mlp_other, hidden_then)
    total = shape((6 * segs, model_width), f32)
    attn_grad, proj_bias_grad, grad_mine, early_totals, *attn_t = run(
        middle_grad_kernel,
        [order, side],
        [picks, marks, tables, mlp_tied, mlp_other, normed_two, inverse_two, attn_out, out_grad],
        [shape(full), row, shape(mine, f32), total],
        40,
    )
    attn_sends, attn_keeps = lefts(*attn_t)
    attended_grad = product("cd,ld->cl", proj_weight, attn_grad).astype(bf16)

    (attended_grad,) = down_sum.take(attended_grad)
    (attended_grad, hidden_then) = up_sum.send(attended_grad, hidden_then)
    (attended_grad, hidden_then) = down_sum.send(attended_grad, hidden_then)
    triple = attention_backward(
        segment_ids, qkv, stat, attended_grad.reshape((heads, HEAD_DIM, length))
    ).reshape((3, local_width, length))
    up_sum.keeps = grads(mlp_keeps, cols(hidden_then))
    (triple, *up_sum.keeps) = up_sum.take(triple, *up_sum.keeps)
    (triple,) = down_sum.take(triple)
    (triple,) = up_sum.send(triple)
    (triple,) = down_sum.send(triple)

    def qkv_grads(sides, others):
        both = triple[:2].reshape((2 * local_width, length))
        first, value = grads((sides[0], sides[1]), (both, triple[2]), "dl,cl->dc")
        (proj,) = grads((others[1],), (attended,), "dl,cl->dc")
        return [first, jnp.concatenate([value, proj], axis=1)]

    qkv_sum = Sum(qkv_grads(in_sends, attn_sends), n_batch)
    qkv_sum.sends[0], qkv_sum.sends[1] = up_sum.take(*qkv_sum.sends)
    qkv_sum.sends[0], qkv_sum.sends[1] = down_sum.take(*qkv_sum.sends)
    (triple,) = qkv_sum.send(triple)
    (triple,) = up_sum.send(triple)
    attn_part = product("jcl,djc->ld", triple, qkv_weight).astype(bf16)
    kept, sent, sums = call(
        halves_kernel,
        [side],
        [picks, tables, attn_part, tokens, mean, inverse_one],
        [shape(mine), shape(mine), shape((length, 2), f32)],
        mib=24,
    )
    if n_tensor == 2:
        other, other_sums = exchange(sent), exchange(sums)
    else:
        kept = lax.psum_scatter(attn_part, "tensor", scatter_dimension=1, tiled=True)
        other = jnp.zeros_like(kept)
        sums = lax.psum(sums, "tensor")
        other_sums = jnp.zeros_like(sums)
    (triple, active_then, kept) = tie(triple, active, kept)
    qv_bias_grad = jnp.sum(triple[0::2].astype(f32), axis=2)
    qkv_sum.keeps = qkv_grads(in_keeps, attn_keeps)
    down_part = product("lf,fd->ld", active_then, down_weight).astype(bf16)
    down_part, down_other = summands(down_part, n_tensor)
    token_t, late_totals = call(
        functools.partial(token_grad_kernel, model_width),
        [],
        [picks, marks, tables_mine, kept, other, sums, other_sums, normed_mine, inverse_one, grad_mine],
        [shape((local_width, length), f32), shape((4 * segs, local_width), f32)],
        mib=24,
    )
    layer_out, gate_total = call(
        layer_kernel,
        [],
        [picks, marks, tables, tokens, attn_out, down_part, down_other, down_bias[None], out_grad],
        [shape(full), shape((2 * segs, model_width), f32)],
    )
    early_totals = jnp.concatenate([early_totals, gate_total]).reshape((4, 2 * segs, model_width))
    early_tgrad = lax.dynamic_slice_in_dim(
        early_totals[:, :segs], side[0] * local_width, local_width, 2
    ).astype(bf16)
    late_tgrad = late_totals.reshape((2, 2 * segs, local_width))[:, :segs].astype(bf16)
    cond_part = product("jsc,djc->sd", jnp.concatenate([late_tgrad, early_tgrad]), mod_weight)
    cond_part, cond_other = summands(cond_part.astype(bf16), n_tensor)
    cond_act_grad = cond_part.astype(f32) + cond_other.astype(f32)
    condition_grad = jax.vjp(silu, cond_float)[1](cond_act_grad)[0]

    early_bias = jnp.concatenate([proj_bias_grad[0], down_bias_grad[0], up_bias_grad])
    early = [early_tgrad, cond_act] + high_low(early_bias)
    late = [late_tgrad] + high_low(qv_bias_grad)

    def packed(arrays):
        return jnp.concatenate([array.reshape((-1, local_width)) for array in arrays], axis=0)

    ways = bits[:1:-1] + bits[1::-1]
    early_all = Gather(packed(early), n_batch, ways)
    late_all = Gather(packed(late), n_batch, ways)

    (early_all.held, *qkv_sum.keeps) = qkv_sum.take(early_all.held, *qkv_sum.keeps)
    (early_all.held,) = up_sum.take(early_all.held)
    (early_all.held,) = qkv_sum.send(early_all.held)
    (early_all.held,) = up_sum.send(early_all.held)
    early_all.step()
    early_all.step()
    late_all.step()
    late_all.step()
    (early_all.held, late_all.held) = qkv_sum.take(early_all.held, late_all.held)
    (early_all.held, late_all.held) = up_sum.take(early_all.held, late_all.held)
    (early_all.held, late_all.held) = qkv_sum.send(early_all.held, late_all.held)
    while early_all.order:
        early_all.step()
        late_all.step()
    (early_all.held, late_all.held) = qkv_sum.take(early_all.held, late_all.held)
    qkv_sum.send()
    early_all, late_all = early_all.held, late_all.held
    early_tall = early_all[:, : 4 * segs].reshape((n_batch, 4, segs, local_width))
    cond_all = early_all[:, 4 * segs : (4 + n_tensor) * segs].reshape((n_batch, segs, model_width))
    bias_all = early_all[:, (4 + n_tensor) * segs :]
    late_tall = late_all[:, : 2 * segs].reshape((n_batch, 2, segs, local_width))
    late_bias = late_all[:, 2 * segs :]

    def bias_sum(held):
        return jnp.sum(held.astype(f32), axis=0).reshape((2, -1)).sum(axis=0)

    bias_all = bias_sum(bias_all)
    qv_sum = bias_sum(late_bias).reshape((2, local_width))
    projbias_sum = bias_all[:model_width]
    downbias_sum = bias_all[model_width : 2 * model_width]
    upbias_sum = bias_all[2 * model_width :]
    tgrad_all = jnp.concatenate([late_tall, early_tall], axis=1)
    cond_block = lax.dynamic_slice_in_dim(cond_all, index * block, block, 2)
    mod_sum = product("psd,pjsc->djc", cond_block, tgrad_all)
    modbias_sum = jnp.sum(tgrad_all.astype(f32), axis=(0, 2))

    qkv_sum.take()
    last = qkv_sum.result()
    down = down_sum.result().T
    up = up_sum.result()
    return (
        layer_out[None],
        token_t.T[None],
        condition_grad[None],
        last[:, : 3 * local_width].reshape((-1, 3, local_width)),
        qv_sum,
        last[:, 3 * local_width :].T,
        projbias_sum,
        up,
        upbias_sum,
        down,
        downbias_sum,
        mod_sum,
        modbias_sum,
    )


def solution(mesh):
    return jax.shard_map(
        functools.partial(on_device, mesh.shape["batch"]),
        mesh=mesh,
        in_specs=(
            P("batch", None, None),
            P("batch", None),
            P("batch", None, None),
            P("batch", None),
            P(None, None, "tensor"),
            P(None, "tensor"),
            P("tensor", None),
            P(),
            P(None, "tensor"),
            P("tensor"),
            P("tensor", None),
            P(),
            P(None, None, "tensor"),
            P(None, "tensor"),
            P("batch", None, None),
        ),
        out_specs=(
            P("batch", None, None),
            P("batch", None, "tensor"),
            P("batch", None, None),
            P("batch", None, "tensor"),
            P(None, "tensor"),
            P("tensor", "batch"),
            P(),
            P("batch", "tensor"),
            P("tensor"),
            P("tensor", "batch"),
            P(),
            P("batch", None, "tensor"),
            P(None, "tensor"),
        ),
        check_vma=False,
    )
```

```python
import functools

import jax
import jax.numpy as jnp
from jax import lax
from jax.experimental import pallas as pl
from jax.experimental.pallas import tpu as pltpu
from jax.sharding import PartitionSpec as P

EPS = 1e-06
HEAD_DIM = 72
SEGS = 8
MOST = 256
LOG2E = 1.4426950408889634
NEG = -1e30


def band(begin, width, length):
    low = max(0, (begin - MOST + 1) // 128 * 128)
    high = min(length, -(-(begin + width + MOST - 1) // 128) * 128)
    return low, high


def natural(array):
    return array.astype(jnp.float32).T.astype(jnp.bfloat16)


def marks(seg_row):
    slots = lax.broadcasted_iota(jnp.int32, (SEGS, seg_row.shape[-1]), 0)
    return (slots == seg_row[...]).astype(jnp.float32)


def fill(head, qkv, one_hot, q_aug, k_nat):
    query = jnp.concatenate([qkv[0, head].astype(jnp.float32), (1.0 - one_hot) * NEG], axis=0)
    q_aug[...] = query.astype(jnp.bfloat16)
    k_nat[...] = natural(jnp.concatenate([qkv[1, head].astype(jnp.float32), one_hot], axis=0))


def attention_forward_kernel(width, seg_row, qkv, out, stat, q_aug, k_nat):
    heads, length = qkv.shape[1], qkv.shape[3]
    factor = HEAD_DIM**-0.5 * LOG2E
    one_hot = marks(seg_row)

    def one(head, carry):
        fill(head, qkv, one_hot, q_aug, k_nat)
        for begin in range(0, length, width):
            low, high = band(begin, width, length)
            span = slice(begin, begin + width)
            scores = jnp.dot(
                k_nat[low:high, :], q_aug[:, span], preferred_element_type=jnp.float32
            )
            peak = jnp.max(scores, axis=0, keepdims=True) * factor
            shifted = jnp.exp2(scores * factor - peak)
            total = jnp.sum(shifted, axis=0, keepdims=True)
            got = jnp.dot(
                qkv[2, head, :, low:high],
                shifted.astype(jnp.bfloat16),
                preferred_element_type=jnp.float32,
            )
            out[head, :, span] = (got * (1.0 / total)).astype(jnp.bfloat16)
            stat[head, :, span] = peak + jnp.log2(total)
        return carry

    lax.fori_loop(0, heads, one, 0, unroll=2)


def attention_backward_kernel(
    width, seg_row, qkv, stat, grad, out, q_aug, k_nat, v_nat, q_nat, g_nat, p_all, s_all
):
    heads, length = qkv.shape[1], qkv.shape[3]
    scale = HEAD_DIM**-0.5
    factor = scale * LOG2E
    one_hot = marks(seg_row)

    def one(head, carry):
        fill(head, qkv, one_hot, q_aug, k_nat)
        v_nat[...] = natural(qkv[2, head])
        q_nat[...] = natural(qkv[0, head])
        g_nat[...] = natural(grad[head])
        for begin in range(0, length, width):
            low, high = band(begin, width, length)
            span = slice(begin, begin + width)
            scores = jnp.dot(
                k_nat[low:high, :], q_aug[:, span], preferred_element_type=jnp.float32
            )
            probs = jnp.exp2(scores * factor - stat[head, :, span])
            prob_grad = jnp.dot(
                v_nat[low:high, :], grad[head, :, span], preferred_element_type=jnp.float32
            )
            row = jnp.sum(prob_grad * probs, axis=0, keepdims=True)
            score_grad = (probs * (prob_grad - row)).astype(jnp.bfloat16)
            p_all[low:high, span] = probs.astype(jnp.bfloat16)
            s_all[low:high, span] = score_grad
            got = jnp.dot(
                qkv[1, head, :, low:high], score_grad, preferred_element_type=jnp.float32
            )
            out[0, head, :, span] = (got * scale).astype(jnp.bfloat16)
        for begin in range(0, length, width):
            span = slice(begin, begin + width)
            reach = [q for q in range(0, length, width) if band(q, width, length)[0] < begin + width and band(q, width, length)[1] > begin]
            low, high = reach[0], reach[-1] + width
            key_grad = jnp.dot(
                s_all[span, low:high], q_nat[low:high, :], preferred_element_type=jnp.float32
            )
            value_grad = jnp.dot(
                p_all[span, low:high], g_nat[low:high, :], preferred_element_type=jnp.float32
            )
            out[1, head, :, span] = (key_grad * scale).T.astype(jnp.bfloat16)
            out[2, head, :, span] = value_grad.T.astype(jnp.bfloat16)
        return carry

    if width < MOST:
        p_all[...] = jnp.zeros_like(p_all)
        s_all[...] = jnp.zeros_like(s_all)
    lax.fori_loop(0, heads, one, 0, unroll=2)


VMEM = pl.BlockSpec(memory_space=pltpu.VMEM)


def attention_forward(segments, qkv, width=256):
    heads, length = qkv.shape[1], qkv.shape[3]
    return call(
        functools.partial(attention_forward_kernel, width),
        [],
        [segments, qkv],
        [shape((heads, HEAD_DIM, length)), shape((heads, 1, length), jnp.float32)],
        [
            pltpu.VMEM((HEAD_DIM + SEGS, length), jnp.bfloat16),
            pltpu.VMEM((length, HEAD_DIM + SEGS), jnp.bfloat16),
        ],
        flops=2 * length,
        room=8,
    )


def attention_backward(segments, qkv, stat, grad, fetch, width=256):
    heads, length = qkv.shape[1], qkv.shape[3]
    tall, square = (length, HEAD_DIM), (length, length)
    return call(
        functools.partial(attention_backward_kernel, width),
        [],
        [segments, qkv, stat, grad],
        [shape(qkv.shape)],
        [
            pltpu.VMEM((HEAD_DIM + SEGS, length), jnp.bfloat16),
            pltpu.VMEM((length, HEAD_DIM + SEGS), jnp.bfloat16),
        ]
        + [pltpu.VMEM(tall, jnp.bfloat16)] * 3
        + [pltpu.VMEM(square, jnp.bfloat16)] * 2,
        flops=4 * length,
        fetch=fetch,
        room=8,
    )


CHUNK = 128


def dot(left, right):
    return jnp.dot(left, right, preferred_element_type=jnp.float32)


def sweep(length, body):
    def one(at, carry):
        body(pl.ds(pl.multiple_of(at * CHUNK, CHUNK), CHUNK))
        return carry

    lax.fori_loop(0, length // CHUNK, one, 0)


def wide(value):
    return value.astype(jnp.float32)


def transpose_in_order(order, source, first, second, work):
    length, width = source.shape
    count = order.shape[0]
    rows = width // count

    def body(span):
        work[:, span] = wide(source[span, :]).T

    sweep(length, body)
    for at in range(0, count, 2):
        pair = [
            work[pl.ds(pl.multiple_of(order[at + i] * rows, 8), rows), :] for i in range(2)
        ]
        pair = jnp.concatenate(pair, axis=0).astype(jnp.bfloat16)
        quarter = at * 4 // count
        other = at + (count // 4 if quarter == 1 else -count // 4 if quarter == 2 else 0)
        first[at * rows : (at + 2) * rows, :] = pair
        second[other * rows : (other + 2) * rows, :] = pair


def own_part(side, value, width):
    part = value[:, :width]
    for at in range(1, value.shape[1] // width):
        part = jnp.where(side == at, value[:, at * width : (at + 1) * width], part)
    return part


def add_totals(marks, span, value, totals, row):
    high = value.astype(jnp.bfloat16)
    low = (value - wide(high)).astype(jnp.bfloat16)
    pick = marks[:, span]
    totals[row : row + 16, :] += dot(pick, high) + dot(pick, low)


def entry_kernel(
    order, side, picks, tables, tokens, out, mean, inverse, normed_mine, *turned
):
    length, width = tokens.shape

    def body(span):
        pick = picks[span, :]
        value = wide(tokens[span, :])
        middle = jnp.sum(value, axis=1, keepdims=True) / width
        center = value - middle
        spread = jnp.sum(center * center, axis=1, keepdims=True) / width
        scale = lax.rsqrt(spread + EPS)
        mean[span, :] = middle
        inverse[span, :] = scale
        value = center * scale
        normed_mine[span, :] = own_part(side[0], value, normed_mine.shape[1])
        value = value * (1.0 + dot(pick, tables[1])) + dot(pick, tables[0])
        out[span, :] = value.astype(jnp.bfloat16)

    sweep(length, body)
    if turned:
        transpose_in_order(order, out, *turned)


def gate_kernel(order, picks, tables, grad, out, bias, *turned):
    length, width = grad.shape
    bias[...] = jnp.zeros_like(bias)

    def body(span):
        value = (wide(grad[span, :]) * dot(picks[span, :], tables[5])).astype(jnp.bfloat16)
        out[span, :] = value
        bias[...] += jnp.sum(wide(value), axis=0, keepdims=True)

    sweep(length, body)
    if turned:
        transpose_in_order(order, out, *turned)


def middle_kernel(
    order, picks, tables, tokens, part, other, bias, attn_out, normed, inverse, out, *turned
):
    length, width = tokens.shape

    def body(span):
        pick = picks[span, :]
        value = wide(part[span, :]) + wide(other[span, :]) + bias[...]
        attn_out[span, :] = value
        value = wide(tokens[span, :]) + dot(pick, tables[2]) * value
        center = value - jnp.sum(value, axis=1, keepdims=True) / width
        spread = jnp.sum(center * center, axis=1, keepdims=True) / width
        scale = lax.rsqrt(spread + EPS)
        inverse[span, :] = scale
        value = center * scale
        normed[span, :] = value
        value = value * (1.0 + dot(pick, tables[4])) + dot(pick, tables[3])
        out[span, :] = value.astype(jnp.bfloat16)

    sweep(length, body)
    if turned:
        transpose_in_order(order, out, *turned)


def middle_grad_kernel(
    order, side, picks, marks, tables, part, other, normed, inverse, attn_out, grad,
    out, bias, grad_mine, totals, *turned
):
    length, width = grad.shape
    bias[...] = jnp.zeros_like(bias)
    totals[...] = jnp.zeros_like(totals)

    def body(span):
        pick = picks[span, :]
        value = wide(part[span, :]) + wide(other[span, :])
        norm = normed[span, :]
        add_totals(marks, span, value, totals, 16)
        add_totals(marks, span, value * norm, totals, 32)
        value = value * (1.0 + dot(pick, tables[4]))
        plain = jnp.sum(value, axis=1, keepdims=True) / width
        cross = jnp.sum(value * norm, axis=1, keepdims=True) / width
        value = wide(grad[span, :]) + inverse[span, :] * (value - plain - norm * cross)
        grad_mine[span, :] = own_part(side[0], value, grad_mine.shape[1])
        add_totals(marks, span, value * attn_out[span, :], totals, 0)
        value = (value * dot(pick, tables[2])).astype(jnp.bfloat16)
        out[span, :] = value
        bias[...] += jnp.sum(wide(value), axis=0, keepdims=True)

    sweep(length, body)
    if turned:
        transpose_in_order(order, out, *turned)


def halves_kernel(side, picks, tables, part, tokens, mean, inverse, kept, sent, sums):
    length, width = tokens.shape

    def body(span):
        value = part[span, :]
        kept[span, :] = own_part(side[0], value, kept.shape[1])
        sent[span, :] = own_part(1 - side[0], value, sent.shape[1])
        value = wide(value) * (1.0 + dot(picks[span, :], tables[1]))
        norm = (wide(tokens[span, :]) - mean[span, :]) * inverse[span, :]
        sums[span, 0:1] = jnp.sum(value, axis=1, keepdims=True)
        sums[span, 1:2] = jnp.sum(value * norm, axis=1, keepdims=True)

    sweep(length, body)


def token_grad_kernel(
    width, picks, marks, tables, kept, other, sums, other_sums, normed, inverse, grad, out_t, totals
):
    totals[...] = jnp.zeros_like(totals)

    def body(span):
        value = wide(kept[span, :]) + wide(other[span, :])
        norm = normed[span, :]
        add_totals(marks, span, value, totals, 0)
        add_totals(marks, span, value * norm, totals, 16)
        whole = (sums[span, :] + other_sums[span, :]) / width
        value = value * (1.0 + dot(picks[span, :], tables[1]))
        value = value - whole[:, 0:1] - norm * whole[:, 1:2]
        out_t[:, span] = (grad[span, :] + inverse[span, :] * value).T

    sweep(normed.shape[0], body)


def layer_kernel(picks, marks, tables, tokens, attn_out, part, other, bias, grad, out, totals):
    totals[...] = jnp.zeros_like(totals)

    def body(span):
        pick = picks[span, :]
        mlp_out = wide(part[span, :]) + wide(other[span, :]) + bias[...]
        middle = wide(tokens[span, :]) + dot(pick, tables[2]) * attn_out[span, :]
        out[span, :] = (middle + dot(pick, tables[5]) * mlp_out).astype(jnp.bfloat16)
        add_totals(marks, span, wide(grad[span, :]) * mlp_out, totals, 0)

    sweep(tokens.shape[0], body)


SMEM = pl.BlockSpec(memory_space=pltpu.SMEM)


def fetch_kernel(body, counts, *refs):
    groups, at = [], 0
    for count in counts:
        groups.append(refs[at : at + count])
        at += count
    given, sources, outs, targets, work, sems = groups
    copies = [
        pltpu.make_async_copy(source, target, sems[0].at[at])
        for at, (source, target) in enumerate(zip(sources, targets))
    ]
    for copy in copies:
        copy.start()
    body(*given, *outs, *work)
    for copy in copies:
        copy.wait()


def call(kernel, scalars, arrays, outs, work=None, flops=64, fetch=(), room=5):
    used = sum(o.size * o.dtype.itemsize for o in outs)
    size = used + sum(a.size * a.dtype.itemsize for a in arrays)
    work = () if work is None else work if isinstance(work, list) else [pltpu.VMEM(work, jnp.float32)]
    used += sum(w.shape[0] * w.shape[1] * w.dtype.itemsize for w in work)
    counts = (len(scalars) + len(arrays), len(fetch), len(outs), len(fetch), len(work), min(1, len(fetch)))
    return pl.pallas_call(
        functools.partial(fetch_kernel, kernel, counts),
        in_specs=[SMEM] * len(scalars)
        + [VMEM] * len(arrays)
        + [pl.BlockSpec(memory_space=pl.ANY)] * len(fetch),
        out_specs=[VMEM] * (len(outs) + len(fetch)),
        out_shape=list(outs) + [pltpu.VMEM(a.shape, a.dtype) for a in fetch],
        scratch_shapes=list(work) + [pltpu.SemaphoreType.DMA((len(fetch),))] * min(1, len(fetch)),
        compiler_params=pltpu.CompilerParams(vmem_limit_bytes=used + (room << 20)),
        cost_estimate=pl.CostEstimate(
            flops=flops * max(a.size for a in arrays), bytes_accessed=size, transcendentals=0
        ),
    )(*scalars, *arrays, *fetch)


def shape(dims, dtype=jnp.bfloat16):
    return jax.ShapeDtypeStruct(dims, dtype)


def silu(array):
    return array / (1.0 + jnp.exp(-array))


def product(spec, left, right):
    return jnp.einsum(spec, left, right, preferred_element_type=jnp.float32)


def exchange(array):
    return lax.ppermute(array, "tensor", [(0, 1), (1, 0)])


def summands(part, size):
    if size == 2:
        return part, exchange(part)
    return lax.psum(part, "tensor"), jnp.zeros_like(part)


def tensor_join(array, size):
    if size == 2:
        other = exchange(array)
        first = lax.axis_index("tensor") == 0
        return jnp.concatenate(
            [jnp.where(first, array, other), jnp.where(first, other, array)], axis=-1
        )
    return lax.all_gather(array, "tensor", axis=array.ndim - 1, tiled=True)


def partners(size, bit):
    return [(i, i ^ (1 << bit)) for i in range(size)]


def tie(*values):
    return lax.optimization_barrier(values)


class Gather:
    def __init__(self, array, size, order):
        self.held, self.size, self.order = array[None], size, list(order)

    def step(self):
        if self.order:
            bit = self.order.pop(0)
            other = lax.ppermute(self.held, "batch", partners(self.size, bit))
            self.held = jnp.concatenate([self.held, other], axis=0)


class Sum:
    def __init__(self, sends, size):
        self.sends, self.size, self.bits = sends, size, size.bit_length() - 1
        self.keeps, self.got = None, []

    def rows(self, low, high):
        halves = [keep[low:high].astype(jnp.float32) for keep in self.keeps]
        for stage in self.got[:2]:
            halves = [half + new[low:high].astype(jnp.float32) for half, new in zip(halves, stage)]
        if len(self.got) < 2:
            return halves
        total = jnp.concatenate(halves, axis=1)
        for (new,) in self.got[2:]:
            total = total + new[low:high].astype(jnp.float32)
        return [total]

    def send(self, *others):
        stage = len(self.got)
        sends, bits = self.sends, [stage]
        if stage > 0:
            left = self.keeps[0].shape[0] >> stage
            sends = [half.astype(jnp.bfloat16) for half in self.rows(left, 2 * left)]
        if stage < 2:
            bits = [stage, 1 - stage]
        tied = tie(*sends, *others)
        self.flying = [
            lax.ppermute(piece, "batch", partners(self.size, bit))
            for piece, bit in zip(tied, bits)
        ]
        return tied[len(sends) :]

    def take(self, *others):
        tied = tie(*self.flying, *others)
        self.got.append(tied[: len(self.flying)])
        return tied[len(self.flying) :]

    def result(self):
        while len(self.got) < self.bits:
            self.send()
            self.take()
        return self.rows(0, 2 * self.keeps[0].shape[0] // self.size)[0]


def gelu_and_slope(array):
    square = array * array
    bent = jnp.tanh(0.7978845608028654 * (array + 0.044715 * array * square))
    half = 0.5 * (1.0 + bent)
    inner = 0.7978845608028654 * (1.0 + 3.0 * 0.044715 * square)
    return array * half, half + 0.5 * array * (1.0 - bent * bent) * inner


def high_low(array):
    high = lax.reduce_precision(array, 8, 7)
    return [high.astype(jnp.bfloat16), (array - high).astype(jnp.bfloat16)]


def in_three(array):
    high = lax.reduce_precision(array, 8, 7)
    middle = lax.reduce_precision(array - high, 8, 7)
    return [high, middle, array - high - middle]


def on_device(
    n_batch,
    tokens,
    segment_ids,
    conditions,
    condition_segment,
    qkv_weight,
    qv_bias,
    proj_weight,
    proj_bias,
    up_weight,
    up_bias,
    down_weight,
    down_bias,
    mod_weight,
    mod_bias,
    out_grad,
):
    bf16, f32 = jnp.bfloat16, jnp.float32
    tokens, out_grad = tokens[0], out_grad[0]
    length, model_width = tokens.shape
    local_width = qkv_weight.shape[2]
    hidden_width = up_weight.shape[1]
    heads = local_width // HEAD_DIM
    n_tensor = model_width // local_width
    bits = list(range(n_batch.bit_length() - 1))
    block = model_width // n_batch
    in_kernel = block % 8 == 0
    index = lax.axis_index("batch")
    order = jnp.array(
        [sum((p >> bit & 1) << (bits[-1] - bit) for bit in bits) for p in range(n_batch)], jnp.int32
    )
    order = order ^ index
    side = lax.axis_index("tensor")[None]

    def run(kernel, scalars, arrays, outs, fetch=()):
        left = shape((model_width, length))
        if in_kernel:
            return call(
                kernel, scalars, arrays, outs + [left, left], (model_width, length), fetch=fetch
            )
        got = call(kernel, scalars, arrays, outs)
        first = got[0].T.reshape((n_batch, block, length))[order].reshape(left.shape)
        parts = jnp.split(first, 4)
        return list(got) + [first, jnp.concatenate([parts[0], parts[2], parts[1], parts[3]]), *fetch]

    def lefts(first, second):
        half = model_width // 2
        return (first[half:], second[half:]), (first[:half], second[:half])

    def grads(sides, rights, spec="dl,lc->dc"):
        return [product(spec, left, right).astype(bf16) for left, right in zip(sides, rights)]

    cond_float = conditions[0].astype(f32)
    cond_act = silu(cond_float).astype(bf16)
    mod_local = product("sd,djc->jsc", cond_act, mod_weight) + mod_bias[:, None]
    modulation = tensor_join(mod_local, n_tensor)
    segs = modulation.shape[1]
    tables = jnp.concatenate(in_three(modulation) + [jnp.zeros_like(modulation)], axis=1).astype(bf16)
    tables_mine = jnp.concatenate(in_three(mod_local) + [jnp.zeros_like(mod_local)], axis=1).astype(bf16)
    slots = condition_segment[0][jnp.arange(4 * segs) % segs]
    real = jnp.arange(4 * segs) < 3 * segs
    picks = ((segment_ids[0][:, None] == slots[None]) & real[None]).astype(bf16)
    real = jnp.arange(2 * segs) < segs
    marks = ((segment_ids[0][None] == slots[: 2 * segs, None]) & real[:, None]).astype(bf16)
    full, column = (length, model_width), (length, 1)
    mine = (length, local_width)
    row = shape((1, model_width), f32)

    qkv_weight = qkv_weight.transpose((1, 2, 0))
    attn_in, mean, inverse_one, normed_mine, *in_t, qkv_held = run(
        entry_kernel,
        [order, side],
        [picks, tables, tokens],
        [shape(full), shape(column, f32), shape(column, f32), shape(mine, f32)],
        [qkv_weight],
    )
    in_sends, in_keeps = lefts(*in_t)
    biases = jnp.stack([qv_bias[0], jnp.zeros_like(qv_bias[0]), qv_bias[1]])
    qkv = product("jcd,ld->jcl", qkv_held, attn_in) + biases[:, :, None]
    qkv = qkv.astype(bf16).reshape((3, heads, HEAD_DIM, length))
    attended, stat = attention_forward(segment_ids, qkv)
    attended = attended.reshape((local_width, length))
    proj_part = product("cl,cd->ld", attended, proj_weight).astype(bf16)
    proj_part, proj_other = summands(proj_part, n_tensor)
    out_grad, proj_tied = tie(out_grad, proj_part)
    mlp_grad, down_bias_grad, *grad_t = run(
        gate_kernel, [order], [picks, tables, out_grad], [shape(full), row]
    )
    grad_sends, grad_keeps = lefts(*grad_t)
    proj_other, mlp_grad = tie(proj_other, mlp_grad)
    attn_out, normed_two, inverse_two, mlp_in, *mlp_t, up_held, down_held = run(
        middle_kernel,
        [order],
        [picks, tables, tokens, proj_tied, proj_other, proj_bias[None]],
        [shape(full, f32), shape(full, f32), shape(column, f32), shape(full)],
        [up_weight, down_weight],
    )
    mlp_sends, mlp_keeps = lefts(*mlp_t)
    hidden = product("ld,df->lf", mlp_in, up_held) + up_bias
    active, slope = gelu_and_slope(hidden)
    active, slope = tie(active.astype(bf16), slope.astype(bf16))

    cut = hidden_width // 2

    def cols(array):
        return array[:, :cut], array[:, cut:]

    down_sum = Sum(grads(grad_sends, cols(active)), n_batch)
    (mlp_grad_then, active_then) = down_sum.send(mlp_grad, active)
    active_grad = product("ld,fd->lf", mlp_grad_then, down_held)
    hidden_grad = (active_grad * slope.astype(f32)).astype(bf16)
    mlp_part = product("lf,df->ld", hidden_grad, up_held).astype(bf16)
    mlp_part, mlp_other = summands(mlp_part, n_tensor)
    (hidden_then, mlp_tied) = tie(hidden_grad, mlp_part)
    up_bias_grad = jnp.sum(hidden_then.astype(f32), axis=0)
    up_sum = Sum(grads(mlp_sends, cols(hidden_then)), n_batch)
    down_sum.keeps = grads(grad_keeps, cols(active_then))
    up_sum.sends[0], up_sum.sends[1], down_sum.keeps[0], down_sum.keeps[1] = down_sum.take(
        *up_sum.sends, *down_sum.keeps
    )
    (mlp_other, hidden_then) = down_sum.send(mlp_other, hidden_then)
    total = shape((6 * segs, model_width), f32)
    attn_grad, proj_bias_grad, grad_mine, early_totals, *attn_t = run(
        middle_grad_kernel,
        [order, side],
        [picks, marks, tables, mlp_tied, mlp_other, normed_two, inverse_two, attn_out, out_grad],
        [shape(full), row, shape(mine, f32), total],
    )
    attn_sends, attn_keeps = lefts(*attn_t)
    attended_grad = product("cd,ld->cl", proj_weight, attn_grad).astype(bf16)

    (attended_grad,) = down_sum.take(attended_grad)
    (attended_grad, hidden_then) = up_sum.send(attended_grad, hidden_then)
    (attended_grad, hidden_then) = down_sum.send(attended_grad, hidden_then)
    triple, qkv_held = attention_backward(
        segment_ids, qkv, stat, attended_grad.reshape((heads, HEAD_DIM, length)), [qkv_weight]
    )
    triple = triple.reshape((3, local_width, length))
    up_sum.keeps = grads(mlp_keeps, cols(hidden_then))
    (triple, *up_sum.keeps) = up_sum.take(triple, *up_sum.keeps)
    (triple,) = down_sum.take(triple)
    (triple,) = up_sum.send(triple)
    (triple,) = down_sum.send(triple)

    def qkv_grads(sides, others):
        both = triple[:2].reshape((2 * local_width, length))
        first, value = grads((sides[0], sides[1]), (both, triple[2]), "dl,cl->dc")
        (proj,) = grads((others[1],), (attended,), "dl,cl->dc")
        return [first, jnp.concatenate([value, proj], axis=1)]

    qkv_sum = Sum(qkv_grads(in_sends, attn_sends), n_batch)
    qkv_sum.sends[0], qkv_sum.sends[1] = up_sum.take(*qkv_sum.sends)
    qkv_sum.sends[0], qkv_sum.sends[1] = down_sum.take(*qkv_sum.sends)
    (triple,) = qkv_sum.send(triple)
    (triple,) = up_sum.send(triple)
    attn_part = product("jcl,jcd->ld", triple, qkv_held).astype(bf16)
    kept, sent, sums, down_held = call(
        halves_kernel,
        [side],
        [picks, tables, attn_part, tokens, mean, inverse_one],
        [shape(mine), shape(mine), shape((length, 2), f32)],
        fetch=[down_weight],
    )
    if n_tensor == 2:
        other, other_sums = exchange(sent), exchange(sums)
    else:
        kept = lax.psum_scatter(attn_part, "tensor", scatter_dimension=1, tiled=True)
        other = jnp.zeros_like(kept)
        sums = lax.psum(sums, "tensor")
        other_sums = jnp.zeros_like(sums)
    (triple, active_then, kept) = tie(triple, active, kept)
    qv_bias_grad = jnp.sum(triple[0::2].astype(f32), axis=2)
    qkv_sum.keeps = qkv_grads(in_keeps, attn_keeps)
    down_part = product("lf,fd->ld", active_then, down_held).astype(bf16)
    down_part, down_other = summands(down_part, n_tensor)
    token_t, late_totals = call(
        functools.partial(token_grad_kernel, model_width),
        [],
        [picks, marks, tables_mine, kept, other, sums, other_sums, normed_mine, inverse_one, grad_mine],
        [shape((local_width, length), f32), shape((4 * segs, local_width), f32)],
    )
    layer_out, gate_total = call(
        layer_kernel,
        [],
        [picks, marks, tables, tokens, attn_out, down_part, down_other, down_bias[None], out_grad],
        [shape(full), shape((2 * segs, model_width), f32)],
    )
    early_totals = jnp.concatenate([early_totals, gate_total]).reshape((4, 2 * segs, model_width))
    early_tgrad = lax.dynamic_slice_in_dim(
        early_totals[:, :segs], side[0] * local_width, local_width, 2
    ).astype(bf16)
    late_tgrad = late_totals.reshape((2, 2 * segs, local_width))[:, :segs].astype(bf16)
    cond_part = product("jsc,djc->sd", jnp.concatenate([late_tgrad, early_tgrad]), mod_weight)
    cond_part, cond_other = summands(cond_part.astype(bf16), n_tensor)
    cond_act_grad = cond_part.astype(f32) + cond_other.astype(f32)
    condition_grad = jax.vjp(silu, cond_float)[1](cond_act_grad)[0]

    early_bias = jnp.concatenate([proj_bias_grad[0], down_bias_grad[0], up_bias_grad])
    early = [early_tgrad, cond_act] + high_low(early_bias)
    late = [late_tgrad] + high_low(qv_bias_grad)

    def packed(arrays):
        return jnp.concatenate([array.reshape((-1, local_width)) for array in arrays], axis=0)

    ways = bits[:1:-1] + bits[1::-1]
    early_all = Gather(packed(early), n_batch, ways)
    late_all = Gather(packed(late), n_batch, ways)

    (early_all.held, *qkv_sum.keeps) = qkv_sum.take(early_all.held, *qkv_sum.keeps)
    (early_all.held,) = up_sum.take(early_all.held)
    (early_all.held,) = qkv_sum.send(early_all.held)
    (early_all.held,) = up_sum.send(early_all.held)
    early_all.step()
    early_all.step()
    late_all.step()
    late_all.step()
    (early_all.held, late_all.held) = qkv_sum.take(early_all.held, late_all.held)
    (early_all.held, late_all.held) = up_sum.take(early_all.held, late_all.held)
    (early_all.held, late_all.held) = qkv_sum.send(early_all.held, late_all.held)
    while early_all.order:
        early_all.step()
        late_all.step()
    (early_all.held, late_all.held) = qkv_sum.take(early_all.held, late_all.held)
    qkv_sum.send()
    early_all, late_all = early_all.held, late_all.held
    early_tall = early_all[:, : 4 * segs].reshape((n_batch, 4, segs, local_width))
    cond_all = early_all[:, 4 * segs : (4 + n_tensor) * segs].reshape((n_batch, segs, model_width))
    bias_all = early_all[:, (4 + n_tensor) * segs :]
    late_tall = late_all[:, : 2 * segs].reshape((n_batch, 2, segs, local_width))
    late_bias = late_all[:, 2 * segs :]

    def bias_sum(held):
        return jnp.sum(held.astype(f32), axis=0).reshape((2, -1)).sum(axis=0)

    bias_all = bias_sum(bias_all)
    qv_sum = bias_sum(late_bias).reshape((2, local_width))
    projbias_sum = bias_all[:model_width]
    downbias_sum = bias_all[model_width : 2 * model_width]
    upbias_sum = bias_all[2 * model_width :]
    tgrad_all = jnp.concatenate([late_tall, early_tall], axis=1)
    cond_block = lax.dynamic_slice_in_dim(cond_all, index * block, block, 2)
    mod_sum = product("psd,pjsc->djc", cond_block, tgrad_all)
    modbias_sum = jnp.sum(tgrad_all.astype(f32), axis=(0, 2))

    qkv_sum.take()
    last = qkv_sum.result()
    down = down_sum.result().T
    up = up_sum.result()
    return (
        layer_out[None],
        token_t.T[None],
        condition_grad[None],
        last[:, : 3 * local_width].reshape((-1, 3, local_width)),
        qv_sum,
        last[:, 3 * local_width :].T,
        projbias_sum,
        up,
        upbias_sum,
        down,
        downbias_sum,
        mod_sum,
        modbias_sum,
    )


def solution(mesh):
    return jax.shard_map(
        functools.partial(on_device, mesh.shape["batch"]),
        mesh=mesh,
        in_specs=(
            P("batch", None, None),
            P("batch", None),
            P("batch", None, None),
            P("batch", None),
            P(None, None, "tensor"),
            P(None, "tensor"),
            P("tensor", None),
            P(),
            P(None, "tensor"),
            P("tensor"),
            P("tensor", None),
            P(),
            P(None, None, "tensor"),
            P(None, "tensor"),
            P("batch", None, None),
        ),
        out_specs=(
            P("batch", None, None),
            P("batch", None, "tensor"),
            P("batch", None, None),
            P("batch", None, "tensor"),
            P(None, "tensor"),
            P("tensor", "batch"),
            P(),
            P("batch", "tensor"),
            P("tensor"),
            P("tensor", "batch"),
            P(),
            P("batch", None, "tensor"),
            P(None, "tensor"),
        ),
        check_vma=False,
    )
```

```python
import functools

import jax
import jax.numpy as jnp
from jax import lax
from jax.experimental import pallas as pl
from jax.experimental.pallas import tpu as pltpu
from jax.sharding import PartitionSpec as P

EPS = 1e-06
HEAD_DIM = 72
SEGS = 8
MOST = 256
LOG2E = 1.4426950408889634
NEG = -1e30


def band(begin, width, length):
    low = max(0, (begin - MOST + 1) // 128 * 128)
    high = min(length, -(-(begin + width + MOST - 1) // 128) * 128)
    return low, high


def natural(array):
    return array.astype(jnp.float32).T.astype(jnp.bfloat16)


def marks(seg_row):
    slots = lax.broadcasted_iota(jnp.int32, (SEGS, seg_row.shape[-1]), 0)
    return (slots == seg_row[...]).astype(jnp.float32)


def fill(head, qkv, one_hot, q_aug, k_nat):
    query = jnp.concatenate([qkv[0, head].astype(jnp.float32), (1.0 - one_hot) * NEG], axis=0)
    q_aug[...] = query.astype(jnp.bfloat16)
    k_nat[...] = natural(jnp.concatenate([qkv[1, head].astype(jnp.float32), one_hot], axis=0))


def attention_forward_kernel(width, seg_row, qkv, out, stat, q_aug, k_nat):
    heads, length = qkv.shape[1], qkv.shape[3]
    factor = HEAD_DIM**-0.5 * LOG2E
    one_hot = marks(seg_row)

    def one(head, carry):
        fill(head, qkv, one_hot, q_aug, k_nat)
        for begin in range(0, length, width):
            low, high = band(begin, width, length)
            span = slice(begin, begin + width)
            scores = jnp.dot(
                k_nat[low:high, :], q_aug[:, span], preferred_element_type=jnp.float32
            )
            peak = jnp.max(scores, axis=0, keepdims=True) * factor
            shifted = jnp.exp2(scores * factor - peak)
            total = jnp.sum(shifted, axis=0, keepdims=True)
            got = jnp.dot(
                qkv[2, head, :, low:high],
                shifted.astype(jnp.bfloat16),
                preferred_element_type=jnp.float32,
            )
            out[head, :, span] = (got * (1.0 / total)).astype(jnp.bfloat16)
            stat[head, :, span] = peak + jnp.log2(total)
        return carry

    lax.fori_loop(0, heads, one, 0, unroll=2)


def attention_backward_kernel(
    width, seg_row, qkv, stat, grad, out, q_aug, k_nat, v_nat, q_nat, g_nat, p_all, s_all
):
    heads, length = qkv.shape[1], qkv.shape[3]
    scale = HEAD_DIM**-0.5
    factor = scale * LOG2E
    one_hot = marks(seg_row)

    def one(head, carry):
        fill(head, qkv, one_hot, q_aug, k_nat)
        v_nat[...] = natural(qkv[2, head])
        q_nat[...] = natural(qkv[0, head])
        g_nat[...] = natural(grad[head])
        for begin in range(0, length, width):
            low, high = band(begin, width, length)
            span = slice(begin, begin + width)
            scores = jnp.dot(
                k_nat[low:high, :], q_aug[:, span], preferred_element_type=jnp.float32
            )
            probs = jnp.exp2(scores * factor - stat[head, :, span])
            prob_grad = jnp.dot(
                v_nat[low:high, :], grad[head, :, span], preferred_element_type=jnp.float32
            )
            row = jnp.sum(prob_grad * probs, axis=0, keepdims=True)
            score_grad = (probs * (prob_grad - row)).astype(jnp.bfloat16)
            p_all[low:high, span] = probs.astype(jnp.bfloat16)
            s_all[low:high, span] = score_grad
            got = jnp.dot(
                qkv[1, head, :, low:high], score_grad, preferred_element_type=jnp.float32
            )
            out[0, head, :, span] = (got * scale).astype(jnp.bfloat16)
        for begin in range(0, length, width):
            span = slice(begin, begin + width)
            reach = [q for q in range(0, length, width) if band(q, width, length)[0] < begin + width and band(q, width, length)[1] > begin]
            low, high = reach[0], reach[-1] + width
            key_grad = jnp.dot(
                s_all[span, low:high], q_nat[low:high, :], preferred_element_type=jnp.float32
            )
            value_grad = jnp.dot(
                p_all[span, low:high], g_nat[low:high, :], preferred_element_type=jnp.float32
            )
            out[1, head, :, span] = (key_grad * scale).T.astype(jnp.bfloat16)
            out[2, head, :, span] = value_grad.T.astype(jnp.bfloat16)
        return carry

    if width < MOST:
        p_all[...] = jnp.zeros_like(p_all)
        s_all[...] = jnp.zeros_like(s_all)
    lax.fori_loop(0, heads, one, 0, unroll=2)


VMEM = pl.BlockSpec(memory_space=pltpu.VMEM)


CHUNK = 128


def dot(left, right):
    return jnp.dot(left, right, preferred_element_type=jnp.float32)


def dot_nt(left, right):
    return lax.dot_general(
        left, right, (((1,), (1,)), ((), ())), preferred_element_type=jnp.float32
    )


def wide(value):
    return value.astype(jnp.float32)


def turn(order, value, out, work):
    count = order.shape[0]
    rows = value.shape[1] // count
    work[...] = wide(value).T
    for at in range(0, count, 2):
        pair = [
            work[pl.ds(pl.multiple_of(order[at + i] * rows, 8), rows), :] for i in range(2)
        ]
        pair = jnp.concatenate(pair, axis=0).astype(jnp.bfloat16)
        out[at * rows : (at + 2) * rows, :] = pair


def own_part(side, value, width):
    part = value[:, :width]
    for at in range(1, value.shape[1] // width):
        part = jnp.where(side == at, value[:, at * width : (at + 1) * width], part)
    return part


def accumulate(total, value):
    @pl.when(pl.program_id(0) == 0)
    def _():
        total[...] = value

    @pl.when(pl.program_id(0) > 0)
    def _():
        total[...] += value


def segment_sums(marks, *values):
    sums = []
    for value in values:
        high = value.astype(jnp.bfloat16)
        low = (value - wide(high)).astype(jnp.bfloat16)
        sums.append(dot(marks, high) + dot(marks, low))
    return jnp.concatenate(sums, axis=0)


def norm_parts(value):
    width = value.shape[1]
    mean = jnp.sum(value, axis=1, keepdims=True) / width
    center = value - mean
    spread = jnp.sum(center * center, axis=1, keepdims=True) / width
    return mean, center, lax.rsqrt(spread + EPS)


def entry_kernel(order, side, picks, tables, tokens, out, mean, inverse, normed_mine, *turned):
    pick = picks[...]
    middle, center, scale = norm_parts(wide(tokens[...]))
    mean[...] = middle
    inverse[...] = scale
    value = center * scale
    normed_mine[...] = own_part(side[0], value, normed_mine.shape[1])
    value = (value * (1.0 + dot(pick, tables[1])) + dot(pick, tables[0])).astype(jnp.bfloat16)
    out[...] = value
    if turned:
        turn(order, value, *turned)


def gate_kernel(order, picks, tables, grad, out, bias, *turned):
    value = (wide(grad[...]) * dot(picks[...], tables[5])).astype(jnp.bfloat16)
    out[...] = value
    accumulate(bias, jnp.sum(wide(value), axis=0, keepdims=True))
    if turned:
        turn(order, value, *turned)


def middle_of(pick, tables, tokens, part, other, bias):
    attn_out = wide(part[...]) + wide(other[...]) + bias[...]
    return attn_out, wide(tokens[...]) + dot(pick, tables[2]) * attn_out


def middle_kernel(order, picks, tables, tokens, part, other, bias, out, mean, inverse, *turned):
    pick = picks[...]
    value = middle_of(pick, tables, tokens, part, other, bias)[1]
    middle, center, scale = norm_parts(value)
    mean[...] = middle
    inverse[...] = scale
    value = center * scale * (1.0 + dot(pick, tables[4])) + dot(pick, tables[3])
    value = value.astype(jnp.bfloat16)
    out[...] = value
    if turned:
        turn(order, value, *turned)


def middle_grad_kernel(
    order, side, picks, marks, tables, tokens, part, other, bias, mean, inverse, mlp, mlp_other, grad,
    out, bias_sum, grad_mine, totals, *turned
):
    pick = picks[...]
    width = grad.shape[1]
    attn_out, value = middle_of(pick, tables, tokens, part, other, bias)
    norm = (value - mean[...]) * inverse[...]
    in_grad = wide(mlp[...]) + wide(mlp_other[...])
    value = in_grad * (1.0 + dot(pick, tables[4]))
    plain = jnp.sum(value, axis=1, keepdims=True) / width
    cross = jnp.sum(value * norm, axis=1, keepdims=True) / width
    value = wide(grad[...]) + inverse[...] * (value - plain - norm * cross)
    grad_mine[...] = own_part(side[0], value, grad_mine.shape[1])
    accumulate(totals, segment_sums(marks[...], value * attn_out, in_grad, in_grad * norm))
    value = (value * dot(pick, tables[2])).astype(jnp.bfloat16)
    out[...] = value
    accumulate(bias_sum, jnp.sum(wide(value), axis=0, keepdims=True))
    if turned:
        turn(order, value, *turned)


def halves_kernel(side, picks, tables, part, tokens, mean, inverse, kept, sent, sums):
    value = part[...]
    kept[...] = own_part(side[0], value, kept.shape[1])
    sent[...] = own_part(1 - side[0], value, sent.shape[1])
    value = wide(value) * (1.0 + dot(picks[...], tables[1]))
    norm = (wide(tokens[...]) - mean[...]) * inverse[...]
    sums[:, 0:1] = jnp.sum(value, axis=1, keepdims=True)
    sums[:, 1:2] = jnp.sum(value * norm, axis=1, keepdims=True)


def token_grad_kernel(
    width, picks, marks, tables, kept, other, sums, other_sums, normed, inverse, grad, out_t, totals
):
    value = wide(kept[...]) + wide(other[...])
    norm = normed[...]
    accumulate(totals, segment_sums(marks[...], value, value * norm))
    whole = (sums[...] + other_sums[...]) / width
    value = value * (1.0 + dot(picks[...], tables[1]))
    value = value - whole[:, 0:1] - norm * whole[:, 1:2]
    out_t[...] = (grad[...] + inverse[...] * value).T


def layer_kernel(
    picks, marks, tables, tokens, part, other, bias, down, down_other, down_bias, grad, out, totals
):
    pick = picks[...]
    mlp_out = wide(down[...]) + wide(down_other[...]) + down_bias[...]
    middle = middle_of(pick, tables, tokens, part, other, bias)[1]
    out[...] = (middle + dot(pick, tables[5]) * mlp_out).astype(jnp.bfloat16)
    accumulate(totals, segment_sums(marks[...], wide(grad[...]) * mlp_out))


def row_parts(sent, first):
    if first:
        return (2, 3) if sent else (0, 1)
    return (1, 3) if sent else (0, 2)


def put_rows(left, right, out, parts, product):
    quarter = left.shape[0] // 4
    columns = slice(0, right.shape[0] if product is dot_nt else right.shape[1])
    if parts[1] == parts[0] + 1:
        rows = slice(parts[0] * quarter, (parts[1] + 1) * quarter)
        out[:, columns] = product(left[rows, :], right[...]).astype(jnp.bfloat16)
        return
    for at, part in enumerate(parts):
        rows = slice(part * quarter, (part + 1) * quarter)
        value = product(left[rows, :], right[...]).astype(jnp.bfloat16)
        out[at * quarter : (at + 1) * quarter, columns] = value


def mlp_grads_kernel(sent, left, right, first, second):
    step, half = pl.program_id(0), pl.num_programs(0) // 2

    @pl.when(step < half)
    def _():
        put_rows(left, right, first, row_parts(sent, True), dot)

    @pl.when(step >= half)
    def _():
        put_rows(left, right, second, row_parts(sent, False), dot)


def qkv_grads_kernel(sent, left, proj_left, both, value, attended, first, second):
    step = pl.program_id(0)

    @pl.when(step < 3)
    def _():
        put_rows(left, both, first, row_parts(sent, True), dot_nt)

    @pl.when(step == 3)
    def _():
        second[...] = jnp.zeros_like(second)
        put_rows(left, value, second, row_parts(sent, False), dot_nt)

    @pl.when(step == 4)
    def _():
        second[...] = jnp.zeros_like(second)
        put_rows(proj_left, attended, second, row_parts(sent, False), dot_nt)


SMEM = pl.BlockSpec(memory_space=pltpu.SMEM)
FREE = pl.CostEstimate(flops=1, bytes_accessed=1, transcendentals=0)


def micros(time):
    return pl.CostEstimate(flops=time * 10**9, bytes_accessed=time * 10**6, transcendentals=0)


def shape(dims, dtype=jnp.bfloat16):
    return jax.ShapeDtypeStruct(dims, dtype)


def room(mib):
    return pltpu.CompilerParams(vmem_limit_bytes=mib << 20)


def spec(dims, kind):
    if kind == "v":
        return VMEM
    if kind == "r":
        return pl.BlockSpec((CHUNK, dims[1]), lambda i: (i, 0))
    if kind == "c":
        return pl.BlockSpec((dims[0], CHUNK), lambda i: (0, i))
    return pl.BlockSpec(tuple(dims), lambda i: (0,) * len(dims))


def sweep(kernel, length, scalars, arrays, outs, work=(), mib=16, cost=200):
    return pl.pallas_call(
        kernel,
        grid=(length // CHUNK,),
        in_specs=[SMEM] * len(scalars) + [spec(a.shape, kind) for a, kind in arrays],
        out_specs=[spec(o.shape, kind) for o, kind in outs],
        out_shape=[o for o, _ in outs],
        scratch_shapes=[pltpu.VMEM(dims, jnp.float32) for dims in work],
        compiler_params=room(mib),
        cost_estimate=micros(cost),
    )(*scalars, *[a for a, _ in arrays])


def mlp_grads(sent, left, right):
    width, length = left.shape
    hidden = right.shape[1]
    half, block = hidden // 2, hidden // 6
    return pl.pallas_call(
        functools.partial(mlp_grads_kernel, sent),
        grid=(6,),
        in_specs=[
            spec(left.shape, "w"),
            pl.BlockSpec((length, block), lambda j: (0, j)),
        ],
        out_specs=[
            pl.BlockSpec((width // 2, block), lambda j: (0, jnp.minimum(j, 2))),
            pl.BlockSpec((width // 2, block), lambda j: (0, jnp.maximum(j - 3, 0))),
        ],
        out_shape=[shape((width // 2, half))] * 2,
        compiler_params=room(16),
        cost_estimate=FREE,
    )(left, right)


def padded(width):
    return -(-width // 128) * 128


def qkv_grads(sent, left, proj_left, triple, attended):
    width, length = left.shape
    local = attended.shape[0]
    block, wide_block = 2 * local // 3, padded(local)
    return pl.pallas_call(
        functools.partial(qkv_grads_kernel, sent),
        grid=(5,),
        in_specs=[
            spec(left.shape, "w"),
            spec(left.shape, "w"),
            pl.BlockSpec((block, length), lambda j: (jnp.minimum(j, 2), 0)),
            pl.BlockSpec((local, length), lambda j: (2, 0)),
            spec(attended.shape, "w"),
        ],
        out_specs=[
            pl.BlockSpec((width // 2, block), lambda j: (0, jnp.minimum(j, 2))),
            pl.BlockSpec((width // 2, wide_block), lambda j: (0, jnp.maximum(j - 3, 0))),
        ],
        out_shape=[shape((width // 2, 2 * local)), shape((width // 2, 2 * wide_block))],
        compiler_params=room(24),
        cost_estimate=FREE,
    )(left, proj_left, triple, triple, attended)


def attention_forward(segments, qkv, width=256):
    heads, length = qkv.shape[1], qkv.shape[3]
    return pl.pallas_call(
        functools.partial(attention_forward_kernel, width),
        in_specs=[VMEM] * 2,
        out_specs=[VMEM] * 2,
        out_shape=[shape((heads, HEAD_DIM, length)), shape((heads, 1, length), jnp.float32)],
        scratch_shapes=[
            pltpu.VMEM((HEAD_DIM + SEGS, length), jnp.bfloat16),
            pltpu.VMEM((length, HEAD_DIM + SEGS), jnp.bfloat16),
        ],
        compiler_params=room(12),
        cost_estimate=micros(15),
    )(segments, qkv)


def attention_backward(segments, qkv, stat, grad, width=256):
    heads, length = qkv.shape[1], qkv.shape[3]
    return pl.pallas_call(
        functools.partial(attention_backward_kernel, width),
        in_specs=[VMEM] * 4,
        out_specs=VMEM,
        out_shape=shape(qkv.shape),
        scratch_shapes=[
            pltpu.VMEM((HEAD_DIM + SEGS, length), jnp.bfloat16),
            pltpu.VMEM((length, HEAD_DIM + SEGS), jnp.bfloat16),
        ]
        + [pltpu.VMEM((length, HEAD_DIM), jnp.bfloat16)] * 3
        + [pltpu.VMEM((length, length), jnp.bfloat16)] * 2,
        compiler_params=room(16),
        cost_estimate=micros(15),
    )(segments, qkv, stat, grad)


def silu(array):
    return array / (1.0 + jnp.exp(-array))


def product(spec, left, right):
    return jnp.einsum(spec, left, right, preferred_element_type=jnp.float32)


def exchange(array):
    return lax.ppermute(array, "tensor", [(0, 1), (1, 0)])


def summands(part, size):
    if size == 2:
        return part, exchange(part)
    return lax.psum(part, "tensor"), jnp.zeros_like(part)


def tensor_join(array, size):
    if size == 2:
        other = exchange(array)
        first = lax.axis_index("tensor") == 0
        return jnp.concatenate(
            [jnp.where(first, array, other), jnp.where(first, other, array)], axis=-1
        )
    return lax.all_gather(array, "tensor", axis=array.ndim - 1, tiled=True)


def partners(size, bit):
    return [(i, i ^ (1 << bit)) for i in range(size)]


def tie(*values):
    return lax.optimization_barrier(values)


class Gather:
    def __init__(self, array, size, order):
        self.held, self.size, self.order = array[None], size, list(order)

    def step(self):
        if self.order:
            bit = self.order.pop(0)
            other = lax.ppermute(self.held, "batch", partners(self.size, bit))
            self.held = jnp.concatenate([self.held, other], axis=0)


class Sum:
    def __init__(self, sends, size):
        self.sends, self.size, self.bits = sends, size, size.bit_length() - 1
        self.keeps, self.got = None, []

    def rows(self, low, high):
        halves = [keep[low:high].astype(jnp.float32) for keep in self.keeps]
        for stage in self.got[:2]:
            halves = [half + new[low:high].astype(jnp.float32) for half, new in zip(halves, stage)]
        if len(self.got) < 2:
            return halves
        total = jnp.concatenate(halves, axis=1)
        for (new,) in self.got[2:]:
            total = total + new[low:high].astype(jnp.float32)
        return [total]

    def send(self, *others):
        stage = len(self.got)
        sends, bits = self.sends, [stage]
        if stage > 0:
            left = self.keeps[0].shape[0] >> stage
            sends = [half.astype(jnp.bfloat16) for half in self.rows(left, 2 * left)]
        if stage < 2:
            bits = [stage, 1 - stage]
        tied = tie(*sends, *others)
        self.flying = [
            lax.ppermute(piece, "batch", partners(self.size, bit))
            for piece, bit in zip(tied, bits)
        ]
        return tied[len(sends) :]

    def take(self, *others):
        tied = tie(*self.flying, *others)
        self.got.append(tied[: len(self.flying)])
        return tied[len(self.flying) :]

    def result(self):
        while len(self.got) < self.bits:
            self.send()
            self.take()
        return self.rows(0, 2 * self.keeps[0].shape[0] // self.size)[0]


def gelu_and_slope(array):
    square = array * array
    bent = jnp.tanh(0.7978845608028654 * (array + 0.044715 * array * square))
    half = 0.5 * (1.0 + bent)
    inner = 0.7978845608028654 * (1.0 + 3.0 * 0.044715 * square)
    return array * half, half + 0.5 * array * (1.0 - bent * bent) * inner


def high_low(array):
    high = lax.reduce_precision(array, 8, 7)
    return [high.astype(jnp.bfloat16), (array - high).astype(jnp.bfloat16)]


def in_three(array):
    high = lax.reduce_precision(array, 8, 7)
    middle = lax.reduce_precision(array - high, 8, 7)
    return [high, middle, array - high - middle]


def on_device(
    n_batch,
    tokens,
    segment_ids,
    conditions,
    condition_segment,
    qkv_weight,
    qv_bias,
    proj_weight,
    proj_bias,
    up_weight,
    up_bias,
    down_weight,
    down_bias,
    mod_weight,
    mod_bias,
    out_grad,
):
    bf16, f32 = jnp.bfloat16, jnp.float32
    tokens, out_grad = tokens[0], out_grad[0]
    length, model_width = tokens.shape
    local_width = qkv_weight.shape[2]
    hidden_width = up_weight.shape[1]
    heads = local_width // HEAD_DIM
    n_tensor = model_width // local_width
    bits = list(range(n_batch.bit_length() - 1))
    block = model_width // n_batch
    in_kernel = block % 8 == 0
    index = lax.axis_index("batch")
    order = jnp.array(
        [sum((p >> bit & 1) << (bits[-1] - bit) for bit in bits) for p in range(n_batch)], jnp.int32
    )
    order = order ^ index
    side = lax.axis_index("tensor")[None]

    def run(kernel, scalars, arrays, outs):
        turned = shape((model_width, length))
        if in_kernel:
            chunk = (model_width, CHUNK)
            return sweep(kernel, length, scalars, arrays, outs + [(turned, "c")], [chunk])
        got = sweep(kernel, length, scalars, arrays, outs)
        return list(got) + [got[0].T.reshape((n_batch, block, length))[order].reshape(turned.shape)]

    def part_rows(left, sent, first):
        quarter = model_width // 4
        rows = [left[at * quarter : (at + 1) * quarter] for at in row_parts(sent, first)]
        return jnp.concatenate(rows)

    def hidden_grads(sent, left, right):
        if in_kernel:
            return mlp_grads(sent, left, right)
        cut = right.shape[1] // 2
        return [
            product("dl,lc->dc", part_rows(left, sent, True), right[:, :cut]).astype(bf16),
            product("dl,lc->dc", part_rows(left, sent, False), right[:, cut:]).astype(bf16),
        ]

    def attention_grads(sent, left, proj_left, triple, attended):
        if in_kernel:
            return qkv_grads(sent, left, proj_left, triple, attended)
        cut, extra = 2 * local_width, ((0, 0), (0, padded(local_width) - local_width))
        halves = [
            (part_rows(left, sent, True), triple[:cut]),
            (part_rows(left, sent, False), triple[cut:]),
            (part_rows(proj_left, sent, False), attended),
        ]
        first, value, proj = [product("dl,cl->dc", *pair).astype(bf16) for pair in halves]
        return [first, jnp.concatenate([jnp.pad(value, extra), jnp.pad(proj, extra)], axis=1)]

    cond_float = conditions[0].astype(f32)
    cond_act = silu(cond_float).astype(bf16)
    mod_local = product("sd,djc->jsc", cond_act, mod_weight) + mod_bias[:, None]
    modulation = tensor_join(mod_local, n_tensor)
    segs = modulation.shape[1]
    tables = jnp.concatenate(in_three(modulation) + [jnp.zeros_like(modulation)], axis=1).astype(bf16)
    tables_mine = jnp.concatenate(in_three(mod_local) + [jnp.zeros_like(mod_local)], axis=1).astype(bf16)
    slots = condition_segment[0][jnp.arange(4 * segs) % segs]
    real = jnp.arange(4 * segs) < 3 * segs
    picks = ((segment_ids[0][:, None] == slots[None]) & real[None]).astype(bf16)
    real = jnp.arange(2 * segs) < segs
    marks = ((segment_ids[0][None] == slots[: 2 * segs, None]) & real[:, None]).astype(bf16)
    full, column = (length, model_width), shape((length, 1), f32)
    mine = (length, local_width)
    row = shape((1, model_width), f32)

    qkv_weight = qkv_weight.transpose((1, 2, 0))
    attn_in, mean_one, inverse_one, normed_mine, in_t = run(
        entry_kernel,
        [order, side],
        [(picks, "r"), (tables, "v"), (tokens, "r")],
        [(shape(full), "r"), (column, "r"), (column, "r"), (shape(mine, f32), "r")],
    )
    biases = jnp.stack([qv_bias[0], jnp.zeros_like(qv_bias[0]), qv_bias[1]])
    qkv = product("jcd,ld->jcl", qkv_weight, attn_in) + biases[:, :, None]
    qkv = qkv.astype(bf16).reshape((3, heads, HEAD_DIM, length))
    attended, stat = attention_forward(segment_ids, qkv)
    attended = attended.reshape((local_width, length))
    proj_part = product("cl,cd->ld", attended, proj_weight).astype(bf16)
    proj_part, proj_other = summands(proj_part, n_tensor)
    out_grad, proj_tied = tie(out_grad, proj_part)
    mlp_grad, down_bias_grad, grad_t = run(
        gate_kernel,
        [order],
        [(picks, "r"), (tables, "v"), (out_grad, "r")],
        [(shape(full), "r"), (row, "w")],
    )
    proj_other, mlp_grad = tie(proj_other, mlp_grad)
    middle_args = [
        (tables, "v"), (tokens, "r"), (proj_tied, "r"), (proj_other, "r"), (proj_bias[None], "v")
    ]
    mlp_in, mean_two, inverse_two, mlp_t = run(
        middle_kernel,
        [order],
        [(picks, "r")] + middle_args,
        [(shape(full), "r"), (column, "r"), (column, "r")],
    )
    hidden = product("ld,df->lf", mlp_in, up_weight) + up_bias
    active, slope = gelu_and_slope(hidden)
    active, slope = tie(active.astype(bf16), slope.astype(bf16))

    down_sum = Sum(hidden_grads(True, grad_t, active), n_batch)
    (mlp_grad_then, active_then) = down_sum.send(mlp_grad, active)
    active_grad = product("ld,fd->lf", mlp_grad_then, down_weight)
    hidden_grad = (active_grad * slope.astype(f32)).astype(bf16)
    mlp_part = product("lf,df->ld", hidden_grad, up_weight).astype(bf16)
    mlp_part, mlp_other = summands(mlp_part, n_tensor)
    (hidden_then, mlp_tied) = tie(hidden_grad, mlp_part)
    up_bias_grad = jnp.sum(hidden_then.astype(f32), axis=0)
    up_sum = Sum(hidden_grads(True, mlp_t, hidden_then), n_batch)
    down_sum.keeps = hidden_grads(False, grad_t, active_then)
    first, second, *down_sum.keeps = down_sum.take(*up_sum.sends, *down_sum.keeps)
    up_sum.sends = [first, second]
    (mlp_other, hidden_then) = down_sum.send(mlp_other, hidden_then)
    (mlp_other, hidden_then) = up_sum.send(mlp_other, hidden_then)
    attn_grad, proj_bias_grad, grad_mine, early_totals, attn_t = run(
        middle_grad_kernel,
        [order, side],
        [(picks, "r"), (marks, "c")]
        + middle_args
        + [(mean_two, "r"), (inverse_two, "r"), (mlp_tied, "r"), (mlp_other, "r"), (out_grad, "r")],
        [
            (shape(full), "r"),
            (row, "w"),
            (shape(mine, f32), "r"),
            (shape((6 * segs, model_width), f32), "w"),
        ],
    )
    attended_grad = product("cd,ld->cl", proj_weight, attn_grad).astype(bf16)

    def packed(arrays):
        return jnp.concatenate([array.reshape((-1, local_width)) for array in arrays], axis=0)

    def tgrad(totals, count):
        kept = totals.reshape((count, 2 * segs, -1))[:, :segs]
        if kept.shape[2] > local_width:
            kept = lax.dynamic_slice_in_dim(kept, side[0] * local_width, local_width, 2)
        return kept.astype(bf16)

    ways = bits[:1:-1] + bits[1::-1]
    early_bias = jnp.concatenate([proj_bias_grad[0], down_bias_grad[0], up_bias_grad])
    early_tgrad = tgrad(early_totals, 3)
    early_all = Gather(packed([early_tgrad, cond_act] + high_low(early_bias)), n_batch, ways)

    early_all.step()
    triple = attention_backward(
        segment_ids, qkv, stat, attended_grad.reshape((heads, HEAD_DIM, length))
    ).reshape((3 * local_width, length))
    up_sum.keeps = hidden_grads(False, mlp_t, hidden_then)
    (triple, early_all.held, *up_sum.keeps) = up_sum.take(triple, early_all.held, *up_sum.keeps)
    (triple, early_all.held) = down_sum.take(triple, early_all.held)
    (triple, early_all.held) = up_sum.send(triple, early_all.held)
    (triple, early_all.held) = down_sum.send(triple, early_all.held)
    early_all.step()
    qkv_sum = Sum(attention_grads(True, in_t, attn_t, triple, attended), n_batch)
    attn_part = product(
        "jcl,jcd->ld", triple.reshape((3, local_width, length)), qkv_weight
    ).astype(bf16)
    kept, sent, sums = sweep(
        halves_kernel,
        length,
        [side],
        [
            (picks, "r"),
            (tables, "v"),
            (attn_part, "r"),
            (tokens, "r"),
            (mean_one, "r"),
            (inverse_one, "r"),
        ],
        [(shape(mine), "r"), (shape(mine), "r"), (shape((length, 2), f32), "r")],
    )
    if n_tensor == 2:
        other, other_sums = exchange(sent), exchange(sums)
    else:
        kept = lax.psum_scatter(attn_part, "tensor", scatter_dimension=1, tiled=True)
        other = jnp.zeros_like(kept)
        sums = lax.psum(sums, "tensor")
        other_sums = jnp.zeros_like(sums)
    first, second, kept = up_sum.take(*qkv_sum.sends, kept)
    first, second, kept, early_all.held = down_sum.take(first, second, kept, early_all.held)
    qkv_sum.sends = [first, second]
    (kept, triple, active_then) = qkv_sum.send(kept, triple, active)
    (kept, triple, active_then) = up_sum.send(kept, triple, active_then)
    (kept, triple, active_then) = down_sum.send(kept, triple, active_then)
    qv_bias_grad = jnp.sum(triple.reshape((3, local_width, length))[0::2].astype(f32), axis=2)
    qkv_sum.keeps = attention_grads(False, in_t, attn_t, triple, attended)
    token_t, late_totals = sweep(
        functools.partial(token_grad_kernel, model_width),
        length,
        [],
        [
            (picks, "r"),
            (marks, "c"),
            (tables_mine, "v"),
            (kept, "r"),
            (other, "r"),
            (sums, "r"),
            (other_sums, "r"),
            (normed_mine, "r"),
            (inverse_one, "r"),
            (grad_mine, "r"),
        ],
        [(shape((local_width, length), f32), "c"), (shape((4 * segs, local_width), f32), "w")],
    )
    (active_then, late_totals) = tie(active_then, late_totals)
    down_part = product("lf,fd->ld", active_then, down_weight).astype(bf16)
    down_part, down_other = summands(down_part, n_tensor)
    layer_out, gate_total = sweep(
        layer_kernel,
        length,
        [],
        [(picks, "r"), (marks, "c")]
        + middle_args
        + [(down_part, "r"), (down_other, "r"), (down_bias[None], "v"), (out_grad, "r")],
        [(shape(full), "r"), (shape((2 * segs, model_width), f32), "w")],
    )
    late_tgrad = jnp.concatenate([tgrad(late_totals, 2), tgrad(gate_total, 1)])
    all_tgrad = jnp.concatenate([late_tgrad[:2], early_tgrad[:1], early_tgrad[1:], late_tgrad[2:]])
    cond_part = product("jsc,djc->sd", all_tgrad, mod_weight)
    cond_part, cond_other = summands(cond_part.astype(bf16), n_tensor)
    cond_act_grad = cond_part.astype(f32) + cond_other.astype(f32)
    condition_grad = jax.vjp(silu, cond_float)[1](cond_act_grad)[0]
    late_all = Gather(packed([late_tgrad] + high_low(qv_bias_grad)), n_batch, ways)

    (late_all.held, *qkv_sum.keeps) = qkv_sum.take(late_all.held, *qkv_sum.keeps)
    (late_all.held, early_all.held) = up_sum.take(late_all.held, early_all.held)
    (late_all.held, early_all.held) = down_sum.take(late_all.held, early_all.held)
    (late_all.held, early_all.held) = qkv_sum.send(late_all.held, early_all.held)
    (late_all.held, early_all.held) = up_sum.send(late_all.held, early_all.held)
    while len(early_all.order) > 1:
        early_all.step()
    while len(late_all.order) > 2:
        late_all.step()
    (late_all.held, early_all.held) = qkv_sum.take(late_all.held, early_all.held)
    (late_all.held, early_all.held) = up_sum.take(late_all.held, early_all.held)
    (late_all.held, early_all.held) = qkv_sum.send(late_all.held, early_all.held)
    early_all.step()
    late_all.step()
    (late_all.held, early_all.held) = qkv_sum.take(late_all.held, early_all.held)
    (late_all.held,) = qkv_sum.send(late_all.held)
    late_all.step()
    early_all, late_all = early_all.held, late_all.held
    early_tall = early_all[:, : 3 * segs].reshape((n_batch, 3, segs, local_width))
    cond_all = early_all[:, 3 * segs : (3 + n_tensor) * segs].reshape((n_batch, segs, model_width))
    bias_all = early_all[:, (3 + n_tensor) * segs :]
    late_tall = late_all[:, : 3 * segs].reshape((n_batch, 3, segs, local_width))
    late_bias = late_all[:, 3 * segs :]

    def bias_sum(held):
        return jnp.sum(held.astype(f32), axis=0).reshape((2, -1)).sum(axis=0)

    bias_all = bias_sum(bias_all)
    qv_sum = bias_sum(late_bias).reshape((2, local_width))
    projbias_sum = bias_all[:model_width]
    downbias_sum = bias_all[model_width : 2 * model_width]
    upbias_sum = bias_all[2 * model_width :]
    cond_block = lax.dynamic_slice_in_dim(cond_all, index * block, block, 2)

    def mod_sums(held):
        return product("psd,pjsc->jdc", cond_block, held), jnp.sum(held.astype(f32), axis=(0, 2))

    early_mod, early_modbias = mod_sums(early_tall)
    late_mod, late_modbias = mod_sums(late_tall)
    mod_sum = jnp.concatenate([late_mod[:2], early_mod, late_mod[2:]]).transpose((1, 0, 2))
    modbias_sum = jnp.concatenate([late_modbias[:2], early_modbias, late_modbias[2:]])

    qkv_sum.take()
    last = qkv_sum.result()
    down = down_sum.result().T
    up = up_sum.result()
    begin = 2 * local_width + padded(local_width)
    return (
        layer_out[None],
        token_t.T[None],
        condition_grad[None],
        last[:, : 3 * local_width].reshape((-1, 3, local_width)),
        qv_sum,
        last[:, begin : begin + local_width].T,
        projbias_sum,
        up,
        upbias_sum,
        down,
        downbias_sum,
        mod_sum,
        modbias_sum,
    )


def solution(mesh):
    return jax.shard_map(
        functools.partial(on_device, mesh.shape["batch"]),
        mesh=mesh,
        in_specs=(
            P("batch", None, None),
            P("batch", None),
            P("batch", None, None),
            P("batch", None),
            P(None, None, "tensor"),
            P(None, "tensor"),
            P("tensor", None),
            P(),
            P(None, "tensor"),
            P("tensor"),
            P("tensor", None),
            P(),
            P(None, None, "tensor"),
            P(None, "tensor"),
            P("batch", None, None),
        ),
        out_specs=(
            P("batch", None, None),
            P("batch", None, "tensor"),
            P("batch", None, None),
            P("batch", None, "tensor"),
            P(None, "tensor"),
            P("tensor", "batch"),
            P(),
            P("batch", "tensor"),
            P("tensor"),
            P("tensor", "batch"),
            P(),
            P("batch", None, "tensor"),
            P(None, "tensor"),
        ),
        check_vma=False,
    )
```

```python
import functools

import jax
import jax.numpy as jnp
from jax import lax
from jax.experimental import pallas as pl
from jax.experimental.pallas import tpu as pltpu
from jax.sharding import PartitionSpec as P

EPS = 1e-06
HEAD_DIM = 72
SEGS = 8
MOST = 256
LOG2E = 1.4426950408889634
NEG = -1e30


def band(begin, width, length):
    low = max(0, (begin - MOST + 1) // 128 * 128)
    high = min(length, -(-(begin + width + MOST - 1) // 128) * 128)
    return low, high


def natural(array):
    return array.astype(jnp.float32).T.astype(jnp.bfloat16)


def marks(seg_row):
    slots = lax.broadcasted_iota(jnp.int32, (SEGS, seg_row.shape[-1]), 0)
    return (slots == seg_row[...]).astype(jnp.float32)


def fill(head, qkv, one_hot, q_aug, k_nat):
    query = jnp.concatenate([qkv[0, head].astype(jnp.float32), (1.0 - one_hot) * NEG], axis=0)
    q_aug[...] = query.astype(jnp.bfloat16)
    k_nat[...] = natural(jnp.concatenate([qkv[1, head].astype(jnp.float32), one_hot], axis=0))


def attention_forward_kernel(width, seg_row, qkv, out, stat, q_aug, k_nat):
    heads, length = qkv.shape[1], qkv.shape[3]
    factor = HEAD_DIM**-0.5 * LOG2E
    one_hot = marks(seg_row)

    def one(head, carry):
        fill(head, qkv, one_hot, q_aug, k_nat)
        for begin in range(0, length, width):
            low, high = band(begin, width, length)
            span = slice(begin, begin + width)
            scores = jnp.dot(
                k_nat[low:high, :], q_aug[:, span], preferred_element_type=jnp.float32
            )
            peak = jnp.max(scores, axis=0, keepdims=True) * factor
            shifted = jnp.exp2(scores * factor - peak)
            total = jnp.sum(shifted, axis=0, keepdims=True)
            got = jnp.dot(
                qkv[2, head, :, low:high],
                shifted.astype(jnp.bfloat16),
                preferred_element_type=jnp.float32,
            )
            out[head, :, span] = (got * (1.0 / total)).astype(jnp.bfloat16)
            stat[head, :, span] = peak + jnp.log2(total)
        return carry

    lax.fori_loop(0, heads, one, 0, unroll=2)


def attention_backward_kernel(
    width, seg_row, qkv, stat, grad, out, q_aug, k_nat, v_nat, q_nat, g_nat, p_all, s_all
):
    heads, length = qkv.shape[1], qkv.shape[3]
    scale = HEAD_DIM**-0.5
    factor = scale * LOG2E
    one_hot = marks(seg_row)

    def one(head, carry):
        fill(head, qkv, one_hot, q_aug, k_nat)
        v_nat[...] = natural(qkv[2, head])
        q_nat[...] = natural(qkv[0, head])
        g_nat[...] = natural(grad[head])
        for begin in range(0, length, width):
            low, high = band(begin, width, length)
            span = slice(begin, begin + width)
            scores = jnp.dot(
                k_nat[low:high, :], q_aug[:, span], preferred_element_type=jnp.float32
            )
            probs = jnp.exp2(scores * factor - stat[head, :, span])
            prob_grad = jnp.dot(
                v_nat[low:high, :], grad[head, :, span], preferred_element_type=jnp.float32
            )
            row = jnp.sum(prob_grad * probs, axis=0, keepdims=True)
            score_grad = (probs * (prob_grad - row)).astype(jnp.bfloat16)
            p_all[low:high, span] = probs.astype(jnp.bfloat16)
            s_all[low:high, span] = score_grad
            got = jnp.dot(
                qkv[1, head, :, low:high], score_grad, preferred_element_type=jnp.float32
            )
            out[0, head, :, span] = (got * scale).astype(jnp.bfloat16)
        for begin in range(0, length, width):
            span = slice(begin, begin + width)
            reach = [q for q in range(0, length, width) if band(q, width, length)[0] < begin + width and band(q, width, length)[1] > begin]
            low, high = reach[0], reach[-1] + width
            key_grad = jnp.dot(
                s_all[span, low:high], q_nat[low:high, :], preferred_element_type=jnp.float32
            )
            value_grad = jnp.dot(
                p_all[span, low:high], g_nat[low:high, :], preferred_element_type=jnp.float32
            )
            out[1, head, :, span] = (key_grad * scale).T.astype(jnp.bfloat16)
            out[2, head, :, span] = value_grad.T.astype(jnp.bfloat16)
        return carry

    if width < MOST:
        p_all[...] = jnp.zeros_like(p_all)
        s_all[...] = jnp.zeros_like(s_all)
    lax.fori_loop(0, heads, one, 0, unroll=2)


VMEM = pl.BlockSpec(memory_space=pltpu.VMEM)


CHUNK = 128


def dot(left, right):
    return jnp.dot(left, right, preferred_element_type=jnp.float32)


def dot_nt(left, right):
    return lax.dot_general(
        left, right, (((1,), (1,)), ((), ())), preferred_element_type=jnp.float32
    )


def wide(value):
    return value.astype(jnp.float32)


def turn(order, value, out, work):
    count = order.shape[0]
    rows = value.shape[1] // count
    work[...] = wide(value).T
    for at in range(0, count, 2):
        pair = [
            work[pl.ds(pl.multiple_of(order[at + i] * rows, 8), rows), :] for i in range(2)
        ]
        pair = jnp.concatenate(pair, axis=0).astype(jnp.bfloat16)
        out[at * rows : (at + 2) * rows, :] = pair


def own_part(side, value, width):
    part = value[:, :width]
    for at in range(1, value.shape[1] // width):
        part = jnp.where(side == at, value[:, at * width : (at + 1) * width], part)
    return part


def accumulate(total, value):
    @pl.when(pl.program_id(0) == 0)
    def _():
        total[...] = value

    @pl.when(pl.program_id(0) > 0)
    def _():
        total[...] += value


def segment_sums(marks, *values):
    sums = []
    for value in values:
        high = value.astype(jnp.bfloat16)
        low = (value - wide(high)).astype(jnp.bfloat16)
        sums.append(dot(marks, high) + dot(marks, low))
    return jnp.concatenate(sums, axis=0)


def norm_parts(value):
    width = value.shape[1]
    mean = jnp.sum(value, axis=1, keepdims=True) / width
    center = value - mean
    spread = jnp.sum(center * center, axis=1, keepdims=True) / width
    return mean, center, lax.rsqrt(spread + EPS)


def entry_kernel(order, side, picks, tables, tokens, out, mean, inverse, normed_mine, *turned):
    pick = picks[...]
    middle, center, scale = norm_parts(wide(tokens[...]))
    mean[...] = middle
    inverse[...] = scale
    value = center * scale
    normed_mine[...] = own_part(side[0], value, normed_mine.shape[1])
    value = (value * (1.0 + dot(pick, tables[1])) + dot(pick, tables[0])).astype(jnp.bfloat16)
    out[...] = value
    if turned:
        turn(order, value, *turned)


def gate_kernel(order, picks, tables, grad, out, bias, *turned):
    value = (wide(grad[...]) * dot(picks[...], tables[5])).astype(jnp.bfloat16)
    out[...] = value
    accumulate(bias, jnp.sum(wide(value), axis=0, keepdims=True))
    if turned:
        turn(order, value, *turned)


def middle_of(pick, tables, tokens, part, other, bias):
    attn_out = wide(part[...]) + wide(other[...]) + bias[...]
    return attn_out, wide(tokens[...]) + dot(pick, tables[2]) * attn_out


def middle_kernel(order, picks, tables, tokens, part, other, bias, out, mean, inverse, *turned):
    pick = picks[...]
    value = middle_of(pick, tables, tokens, part, other, bias)[1]
    middle, center, scale = norm_parts(value)
    mean[...] = middle
    inverse[...] = scale
    value = center * scale * (1.0 + dot(pick, tables[4])) + dot(pick, tables[3])
    value = value.astype(jnp.bfloat16)
    out[...] = value
    if turned:
        turn(order, value, *turned)


def middle_grad_kernel(
    order, side, picks, marks, tables, tokens, part, other, bias, mean, inverse, mlp, mlp_other, grad,
    out, bias_sum, grad_mine, totals, *turned
):
    pick = picks[...]
    width = grad.shape[1]
    attn_out, value = middle_of(pick, tables, tokens, part, other, bias)
    norm = (value - mean[...]) * inverse[...]
    in_grad = wide(mlp[...]) + wide(mlp_other[...])
    value = in_grad * (1.0 + dot(pick, tables[4]))
    plain = jnp.sum(value, axis=1, keepdims=True) / width
    cross = jnp.sum(value * norm, axis=1, keepdims=True) / width
    value = wide(grad[...]) + inverse[...] * (value - plain - norm * cross)
    grad_mine[...] = own_part(side[0], value, grad_mine.shape[1])
    accumulate(totals, segment_sums(marks[...], value * attn_out, in_grad, in_grad * norm))
    value = (value * dot(pick, tables[2])).astype(jnp.bfloat16)
    out[...] = value
    accumulate(bias_sum, jnp.sum(wide(value), axis=0, keepdims=True))
    if turned:
        turn(order, value, *turned)


def halves_kernel(side, picks, tables, part, tokens, mean, inverse, kept, sent, sums):
    value = part[...]
    width = kept.shape[1]
    kept[...] = own_part(side[0], value, width)
    sent[:, :width] = own_part(1 - side[0], value, width)
    value = wide(value) * (1.0 + dot(picks[...], tables[1]))
    norm = (wide(tokens[...]) - mean[...]) * inverse[...]
    for at, term in enumerate((value, value * norm)):
        total = jnp.sum(term, axis=1, keepdims=True)
        high = total.astype(jnp.bfloat16)
        sums[:, at : at + 1] = total
        sent[:, width + 2 * at : width + 2 * at + 1] = high
        sent[:, width + 2 * at + 1 : width + 2 * at + 2] = (total - wide(high)).astype(jnp.bfloat16)


def token_grad_kernel(
    width, picks, marks, tables, kept, other, sums, normed, inverse, grad, out_t, totals
):
    mine = kept.shape[1]
    value = wide(kept[...]) + wide(other[:, :mine])
    norm = normed[...]
    accumulate(totals, segment_sums(marks[...], value, value * norm))
    value = value * (1.0 + dot(picks[...], tables[1]))
    for at, factor in enumerate((1.0, norm)):
        rest = wide(other[:, mine + 2 * at : mine + 2 * at + 1])
        rest = rest + wide(other[:, mine + 2 * at + 1 : mine + 2 * at + 2])
        value = value - factor * ((sums[:, at : at + 1] + rest) / width)
    out_t[...] = (grad[...] + inverse[...] * value).T


def layer_kernel(
    picks, marks, tables, tokens, part, other, bias, down, down_other, down_bias, grad, out, totals
):
    pick = picks[...]
    mlp_out = wide(down[...]) + wide(down_other[...]) + down_bias[...]
    middle = middle_of(pick, tables, tokens, part, other, bias)[1]
    out[...] = (middle + dot(pick, tables[5]) * mlp_out).astype(jnp.bfloat16)
    accumulate(totals, segment_sums(marks[...], wide(grad[...]) * mlp_out))


def row_parts(sent, first):
    if first:
        return (2, 3) if sent else (0, 1)
    return (1, 3) if sent else (0, 2)


def put_rows(left, right, out, parts, product):
    quarter = left.shape[0] // 4
    columns = slice(0, right.shape[0] if product is dot_nt else right.shape[1])
    if parts[1] == parts[0] + 1:
        rows = slice(parts[0] * quarter, (parts[1] + 1) * quarter)
        out[:, columns] = product(left[rows, :], right[...]).astype(jnp.bfloat16)
        return
    for at, part in enumerate(parts):
        rows = slice(part * quarter, (part + 1) * quarter)
        value = product(left[rows, :], right[...]).astype(jnp.bfloat16)
        out[at * quarter : (at + 1) * quarter, columns] = value


def mlp_grads_kernel(sent, left, right, first, second):
    step, half = pl.program_id(0), pl.num_programs(0) // 2

    @pl.when(step < half)
    def _():
        put_rows(left, right, first, row_parts(sent, True), dot)

    @pl.when(step >= half)
    def _():
        put_rows(left, right, second, row_parts(sent, False), dot)


def qkv_grads_kernel(sent, left, proj_left, both, value, attended, first, second):
    step = pl.program_id(0)

    @pl.when(step < 3)
    def _():
        put_rows(left, both, first, row_parts(sent, True), dot_nt)

    @pl.when(step == 3)
    def _():
        second[...] = jnp.zeros_like(second)
        put_rows(left, value, second, row_parts(sent, False), dot_nt)

    @pl.when(step == 4)
    def _():
        second[...] = jnp.zeros_like(second)
        put_rows(proj_left, attended, second, row_parts(sent, False), dot_nt)


SMEM = pl.BlockSpec(memory_space=pltpu.SMEM)
FREE = pl.CostEstimate(flops=1, bytes_accessed=1, transcendentals=0)


def micros(time):
    if time == 0:
        return FREE
    return pl.CostEstimate(flops=time * 10**9, bytes_accessed=time * 10**6, transcendentals=0)


def shape(dims, dtype=jnp.bfloat16):
    return jax.ShapeDtypeStruct(dims, dtype)


def room(mib):
    return pltpu.CompilerParams(vmem_limit_bytes=mib << 20)


def spec(dims, kind):
    if kind == "v":
        return VMEM
    if kind == "r":
        return pl.BlockSpec((CHUNK, dims[1]), lambda i: (i, 0))
    if kind == "c":
        return pl.BlockSpec((dims[0], CHUNK), lambda i: (0, i))
    return pl.BlockSpec(tuple(dims), lambda i: (0,) * len(dims))


def sweep(kernel, length, scalars, arrays, outs, work=(), mib=16, cost=200):
    return pl.pallas_call(
        kernel,
        grid=(length // CHUNK,),
        in_specs=[SMEM] * len(scalars) + [spec(a.shape, kind) for a, kind in arrays],
        out_specs=[spec(o.shape, kind) for o, kind in outs],
        out_shape=[o for o, _ in outs],
        scratch_shapes=[pltpu.VMEM(dims, jnp.float32) for dims in work],
        compiler_params=room(mib),
        cost_estimate=micros(cost),
    )(*scalars, *[a for a, _ in arrays])


def mlp_grads(sent, left, right):
    width, length = left.shape
    hidden = right.shape[1]
    half, block = hidden // 2, hidden // 6
    return pl.pallas_call(
        functools.partial(mlp_grads_kernel, sent),
        grid=(6,),
        in_specs=[
            spec(left.shape, "w"),
            pl.BlockSpec((length, block), lambda j: (0, j)),
        ],
        out_specs=[
            pl.BlockSpec((width // 2, block), lambda j: (0, jnp.minimum(j, 2))),
            pl.BlockSpec((width // 2, block), lambda j: (0, jnp.maximum(j - 3, 0))),
        ],
        out_shape=[shape((width // 2, half))] * 2,
        compiler_params=room(16),
        cost_estimate=FREE,
    )(left, right)


def padded(width):
    return -(-width // 128) * 128


def qkv_grads(sent, left, proj_left, triple, attended):
    width, length = left.shape
    local = attended.shape[0]
    block, wide_block = 2 * local // 3, padded(local)
    return pl.pallas_call(
        functools.partial(qkv_grads_kernel, sent),
        grid=(5,),
        in_specs=[
            spec(left.shape, "w"),
            spec(left.shape, "w"),
            pl.BlockSpec((block, length), lambda j: (jnp.minimum(j, 2), 0)),
            pl.BlockSpec((local, length), lambda j: (2, 0)),
            spec(attended.shape, "w"),
        ],
        out_specs=[
            pl.BlockSpec((width // 2, block), lambda j: (0, jnp.minimum(j, 2))),
            pl.BlockSpec((width // 2, wide_block), lambda j: (0, jnp.maximum(j - 3, 0))),
        ],
        out_shape=[shape((width // 2, 2 * local)), shape((width // 2, 2 * wide_block))],
        compiler_params=room(24),
        cost_estimate=FREE,
    )(left, proj_left, triple, triple, attended)


def attention_forward(segments, qkv, width=256):
    heads, length = qkv.shape[1], qkv.shape[3]
    return pl.pallas_call(
        functools.partial(attention_forward_kernel, width),
        in_specs=[VMEM] * 2,
        out_specs=[VMEM] * 2,
        out_shape=[shape((heads, HEAD_DIM, length)), shape((heads, 1, length), jnp.float32)],
        scratch_shapes=[
            pltpu.VMEM((HEAD_DIM + SEGS, length), jnp.bfloat16),
            pltpu.VMEM((length, HEAD_DIM + SEGS), jnp.bfloat16),
        ],
        compiler_params=room(12),
        cost_estimate=micros(15),
    )(segments, qkv)


def attention_backward(segments, qkv, stat, grad, width=256):
    heads, length = qkv.shape[1], qkv.shape[3]
    return pl.pallas_call(
        functools.partial(attention_backward_kernel, width),
        in_specs=[VMEM] * 4,
        out_specs=VMEM,
        out_shape=shape(qkv.shape),
        scratch_shapes=[
            pltpu.VMEM((HEAD_DIM + SEGS, length), jnp.bfloat16),
            pltpu.VMEM((length, HEAD_DIM + SEGS), jnp.bfloat16),
        ]
        + [pltpu.VMEM((length, HEAD_DIM), jnp.bfloat16)] * 3
        + [pltpu.VMEM((length, length), jnp.bfloat16)] * 2,
        compiler_params=room(16),
        cost_estimate=micros(15),
    )(segments, qkv, stat, grad)


def silu(array):
    return array / (1.0 + jnp.exp(-array))


def product(spec, left, right):
    return jnp.einsum(spec, left, right, preferred_element_type=jnp.float32)


def exchange(array):
    return lax.ppermute(array, "tensor", [(0, 1), (1, 0)])


def summands(part, size):
    if size == 2:
        return part, exchange(part)
    return lax.psum(part, "tensor"), jnp.zeros_like(part)


def tensor_join(array, size):
    if size == 2:
        other = exchange(array)
        first = lax.axis_index("tensor") == 0
        return jnp.concatenate(
            [jnp.where(first, array, other), jnp.where(first, other, array)], axis=-1
        )
    return lax.all_gather(array, "tensor", axis=array.ndim - 1, tiled=True)


def partners(size, bit):
    return [(i, i ^ (1 << bit)) for i in range(size)]


def tie(*values):
    return lax.optimization_barrier(values)


class Gather:
    def __init__(self, array, size, order):
        self.held, self.size, self.order = array[None], size, list(order)

    def step(self):
        if self.order:
            bit = self.order.pop(0)
            other = lax.ppermute(self.held, "batch", partners(self.size, bit))
            self.held = jnp.concatenate([self.held, other], axis=0)


class Sum:
    def __init__(self, sends, size):
        self.sends, self.size, self.bits = sends, size, size.bit_length() - 1
        self.keeps, self.got = None, []

    def rows(self, low, high):
        halves = [keep[low:high].astype(jnp.float32) for keep in self.keeps]
        for stage in self.got[:2]:
            halves = [half + new[low:high].astype(jnp.float32) for half, new in zip(halves, stage)]
        if len(self.got) < 2:
            return halves
        total = jnp.concatenate(halves, axis=1)
        for (new,) in self.got[2:]:
            total = total + new[low:high].astype(jnp.float32)
        return [total]

    def send(self, *others):
        stage = len(self.got)
        sends, bits = self.sends, [stage]
        if stage > 0:
            left = self.keeps[0].shape[0] >> stage
            sends = [half.astype(jnp.bfloat16) for half in self.rows(left, 2 * left)]
        if stage < 2:
            bits = [stage, 1 - stage]
        tied = tie(*sends, *others)
        self.flying = [
            lax.ppermute(piece, "batch", partners(self.size, bit))
            for piece, bit in zip(tied, bits)
        ]
        return tied[len(sends) :]

    def take(self, *others):
        tied = tie(*self.flying, *others)
        self.got.append(tied[: len(self.flying)])
        return tied[len(self.flying) :]

    def settle(self, other):
        if len(self.got) == self.bits:
            self.keeps = list(tie(*self.keeps, other)[:2])

    def result(self):
        while len(self.got) < self.bits:
            self.send()
            self.take()
        return self.rows(0, 2 * self.keeps[0].shape[0] // self.size)[0]


def gelu_and_slope(array):
    square = array * array
    bent = jnp.tanh(0.7978845608028654 * (array + 0.044715 * array * square))
    half = 0.5 * (1.0 + bent)
    inner = 0.7978845608028654 * (1.0 + 3.0 * 0.044715 * square)
    return array * half, half + 0.5 * array * (1.0 - bent * bent) * inner


def high_low(array):
    high = lax.reduce_precision(array, 8, 7)
    return [high.astype(jnp.bfloat16), (array - high).astype(jnp.bfloat16)]


def in_three(array):
    high = lax.reduce_precision(array, 8, 7)
    middle = lax.reduce_precision(array - high, 8, 7)
    return [high, middle, array - high - middle]


def on_device(
    n_batch,
    tokens,
    segment_ids,
    conditions,
    condition_segment,
    qkv_weight,
    qv_bias,
    proj_weight,
    proj_bias,
    up_weight,
    up_bias,
    down_weight,
    down_bias,
    mod_weight,
    mod_bias,
    out_grad,
):
    bf16, f32 = jnp.bfloat16, jnp.float32
    tokens, out_grad = tokens[0], out_grad[0]
    length, model_width = tokens.shape
    local_width = qkv_weight.shape[2]
    hidden_width = up_weight.shape[1]
    heads = local_width // HEAD_DIM
    n_tensor = model_width // local_width
    bits = list(range(n_batch.bit_length() - 1))
    block = model_width // n_batch
    in_kernel = block % 8 == 0
    index = lax.axis_index("batch")
    order = jnp.array(
        [sum((p >> bit & 1) << (bits[-1] - bit) for bit in bits) for p in range(n_batch)], jnp.int32
    )
    order = order ^ index
    side = lax.axis_index("tensor")[None]

    def run(kernel, scalars, arrays, outs):
        turned = shape((model_width, length))
        if in_kernel:
            chunk = (model_width, CHUNK)
            return sweep(kernel, length, scalars, arrays, outs + [(turned, "c")], [chunk])
        got = sweep(kernel, length, scalars, arrays, outs)
        return list(got) + [got[0].T.reshape((n_batch, block, length))[order].reshape(turned.shape)]

    def part_rows(left, sent, first):
        quarter = model_width // 4
        rows = [left[at * quarter : (at + 1) * quarter] for at in row_parts(sent, first)]
        return jnp.concatenate(rows)

    def hidden_grads(sent, left, right):
        if in_kernel:
            return mlp_grads(sent, left, right)
        cut = right.shape[1] // 2
        return [
            product("dl,lc->dc", part_rows(left, sent, True), right[:, :cut]).astype(bf16),
            product("dl,lc->dc", part_rows(left, sent, False), right[:, cut:]).astype(bf16),
        ]

    def attention_grads(sent, left, proj_left, triple, attended):
        if in_kernel:
            return qkv_grads(sent, left, proj_left, triple, attended)
        cut, extra = 2 * local_width, ((0, 0), (0, padded(local_width) - local_width))
        halves = [
            (part_rows(left, sent, True), triple[:cut]),
            (part_rows(left, sent, False), triple[cut:]),
            (part_rows(proj_left, sent, False), attended),
        ]
        first, value, proj = [product("dl,cl->dc", *pair).astype(bf16) for pair in halves]
        return [first, jnp.concatenate([jnp.pad(value, extra), jnp.pad(proj, extra)], axis=1)]

    cond_float = conditions[0].astype(f32)
    cond_act = silu(cond_float).astype(bf16)
    mod_local = product("sd,djc->jsc", cond_act, mod_weight) + mod_bias[:, None]
    modulation = tensor_join(mod_local, n_tensor)
    segs = modulation.shape[1]
    tables = jnp.concatenate(in_three(modulation) + [jnp.zeros_like(modulation)], axis=1).astype(bf16)
    tables_mine = jnp.concatenate(in_three(mod_local) + [jnp.zeros_like(mod_local)], axis=1).astype(bf16)
    slots = condition_segment[0][jnp.arange(4 * segs) % segs]
    real = jnp.arange(4 * segs) < 3 * segs
    picks = ((segment_ids[0][:, None] == slots[None]) & real[None]).astype(bf16)
    real = jnp.arange(2 * segs) < segs
    marks = ((segment_ids[0][None] == slots[: 2 * segs, None]) & real[:, None]).astype(bf16)
    full, column = (length, model_width), shape((length, 1), f32)
    mine = (length, local_width)
    row = shape((1, model_width), f32)

    qkv_weight = qkv_weight.transpose((1, 2, 0))
    attn_in, mean_one, inverse_one, normed_mine, in_t = run(
        entry_kernel,
        [order, side],
        [(picks, "r"), (tables, "v"), (tokens, "r")],
        [(shape(full), "r"), (column, "r"), (column, "r"), (shape(mine, f32), "r")],
    )
    biases = jnp.stack([qv_bias[0], jnp.zeros_like(qv_bias[0]), qv_bias[1]])
    qkv = product("jcd,ld->jcl", qkv_weight, attn_in) + biases[:, :, None]
    qkv = qkv.astype(bf16).reshape((3, heads, HEAD_DIM, length))
    attended, stat = attention_forward(segment_ids, qkv)
    attended = attended.reshape((local_width, length))
    proj_part = product("cl,cd->ld", attended, proj_weight).astype(bf16)
    proj_part, proj_other = summands(proj_part, n_tensor)
    out_grad, proj_tied = tie(out_grad, proj_part)
    mlp_grad, down_bias_grad, grad_t = run(
        gate_kernel,
        [order],
        [(picks, "r"), (tables, "v"), (out_grad, "r")],
        [(shape(full), "r"), (row, "w")],
    )
    proj_other, mlp_grad = tie(proj_other, mlp_grad)
    middle_args = [
        (tables, "v"), (tokens, "r"), (proj_tied, "r"), (proj_other, "r"), (proj_bias[None], "v")
    ]
    mlp_in, mean_two, inverse_two, mlp_t = run(
        middle_kernel,
        [order],
        [(picks, "r")] + middle_args,
        [(shape(full), "r"), (column, "r"), (column, "r")],
    )
    hidden = product("ld,df->lf", mlp_in, up_weight) + up_bias
    active, slope = gelu_and_slope(hidden)
    active, slope = tie(active.astype(bf16), slope.astype(bf16))

    down_sum = Sum(hidden_grads(True, grad_t, active), n_batch)
    (mlp_grad_then, active_then) = down_sum.send(mlp_grad, active)
    active_grad = product("ld,fd->lf", mlp_grad_then, down_weight)
    hidden_grad = (active_grad * slope.astype(f32)).astype(bf16)
    mlp_part = product("lf,df->ld", hidden_grad, up_weight).astype(bf16)
    mlp_part, mlp_other = summands(mlp_part, n_tensor)
    (hidden_then, mlp_tied) = tie(hidden_grad, mlp_part)
    up_bias_grad = jnp.sum(hidden_then.astype(f32), axis=0)
    up_sum = Sum(hidden_grads(True, mlp_t, hidden_then), n_batch)
    down_sum.keeps = hidden_grads(False, grad_t, active_then)
    first, second, *down_sum.keeps = down_sum.take(*up_sum.sends, *down_sum.keeps)
    up_sum.sends = [first, second]
    (mlp_other, hidden_then) = down_sum.send(mlp_other, hidden_then)
    (mlp_other, hidden_then) = up_sum.send(mlp_other, hidden_then)
    attn_grad, proj_bias_grad, grad_mine, early_totals, attn_t = run(
        middle_grad_kernel,
        [order, side],
        [(picks, "r"), (marks, "c")]
        + middle_args
        + [(mean_two, "r"), (inverse_two, "r"), (mlp_tied, "r"), (mlp_other, "r"), (out_grad, "r")],
        [
            (shape(full), "r"),
            (row, "w"),
            (shape(mine, f32), "r"),
            (shape((6 * segs, model_width), f32), "w"),
        ],
    )
    attended_grad = product("cd,ld->cl", proj_weight, attn_grad).astype(bf16)

    def packed(arrays):
        return jnp.concatenate([array.reshape((-1, local_width)) for array in arrays], axis=0)

    def tgrad(totals, count):
        kept = totals.reshape((count, 2 * segs, -1))[:, :segs]
        if kept.shape[2] > local_width:
            kept = lax.dynamic_slice_in_dim(kept, side[0] * local_width, local_width, 2)
        return kept.astype(bf16)

    ways = bits[:1:-1] + bits[1::-1]
    early_bias = jnp.concatenate([proj_bias_grad[0], down_bias_grad[0], up_bias_grad])
    early_tgrad = tgrad(early_totals, 3)
    early_all = Gather(packed([early_tgrad, cond_act] + high_low(early_bias)), n_batch, ways)

    early_all.step()
    triple = attention_backward(
        segment_ids, qkv, stat, attended_grad.reshape((heads, HEAD_DIM, length))
    ).reshape((3 * local_width, length))
    up_sum.keeps = hidden_grads(False, mlp_t, hidden_then)
    (triple, early_all.held, *up_sum.keeps) = up_sum.take(triple, early_all.held, *up_sum.keeps)
    (triple, early_all.held) = down_sum.take(triple, early_all.held)
    (triple, early_all.held) = up_sum.send(triple, early_all.held)
    (triple, early_all.held) = down_sum.send(triple, early_all.held)
    qkv_sum = Sum(attention_grads(True, in_t, attn_t, triple, attended), n_batch)
    (triple,) = qkv_sum.send(triple)
    attn_part = product(
        "jcl,jcd->ld", triple.reshape((3, local_width, length)), qkv_weight
    ).astype(bf16)
    kept, sent, sums = sweep(
        halves_kernel,
        length,
        [side],
        [
            (picks, "r"),
            (tables, "v"),
            (attn_part, "r"),
            (tokens, "r"),
            (mean_one, "r"),
            (inverse_one, "r"),
        ],
        [
            (shape(mine), "r"),
            (shape((length, padded(local_width + 4))), "r"),
            (shape((length, 2), f32), "r"),
        ],
        cost=0,
    )
    (kept, sent, early_all.held) = up_sum.take(kept, sent, early_all.held)
    (kept, sent, early_all.held) = down_sum.take(kept, sent, early_all.held)
    (kept, sent, triple, active_then) = up_sum.send(kept, sent, triple, active)
    (kept, sent, triple, active_then) = down_sum.send(kept, sent, triple, active_then)
    if n_tensor == 2:
        other = exchange(sent)
    else:
        kept = lax.psum_scatter(attn_part, "tensor", scatter_dimension=1, tiled=True)
        other = jnp.zeros_like(sent)
        sums = lax.psum(sums, "tensor")
    qkv_sum.keeps = attention_grads(False, in_t, attn_t, triple, attended)
    qv_bias_grad = jnp.sum(triple.reshape((3, local_width, length))[0::2].astype(f32), axis=2)
    token_t, late_totals = sweep(
        functools.partial(token_grad_kernel, model_width),
        length,
        [],
        [
            (picks, "r"),
            (marks, "c"),
            (tables_mine, "v"),
            (kept, "r"),
            (other, "r"),
            (sums, "r"),
            (normed_mine, "r"),
            (inverse_one, "r"),
            (grad_mine, "r"),
        ],
        [(shape((local_width, length), f32), "c"), (shape((4 * segs, local_width), f32), "w")],
        cost=0,
    )
    (active_then, kept) = tie(active_then, kept)
    down_part = product("lf,fd->ld", active_then, down_weight).astype(bf16)
    (late_totals, down_part, *qkv_sum.keeps) = qkv_sum.take(
        late_totals, down_part, *qkv_sum.keeps
    )
    (late_totals,) = up_sum.take(late_totals)
    (late_totals,) = down_sum.take(late_totals)
    (down_part, late_totals, early_all.held) = qkv_sum.send(
        down_part, late_totals, early_all.held
    )
    (down_part, late_totals, early_all.held) = up_sum.send(
        down_part, late_totals, early_all.held
    )
    early_all.step()
    down_part, down_other = summands(down_part, n_tensor)
    layer_out, gate_total = sweep(
        layer_kernel,
        length,
        [],
        [(picks, "r"), (marks, "c")]
        + middle_args
        + [(down_part, "r"), (down_other, "r"), (down_bias[None], "v"), (out_grad, "r")],
        [(shape(full), "r"), (shape((2 * segs, model_width), f32), "w")],
        cost=0,
    )
    late_tgrad = jnp.concatenate([tgrad(late_totals, 2), tgrad(gate_total, 1)])
    all_tgrad = jnp.concatenate([late_tgrad[:2], early_tgrad[:1], early_tgrad[1:], late_tgrad[2:]])
    cond_part = product("jsc,djc->sd", all_tgrad, mod_weight)
    cond_part, cond_other = summands(cond_part.astype(bf16), n_tensor)
    cond_act_grad = cond_part.astype(f32) + cond_other.astype(f32)
    condition_grad = jax.vjp(silu, cond_float)[1](cond_act_grad)[0]
    late_all = Gather(packed([late_tgrad] + high_low(qv_bias_grad)), n_batch, ways)

    (late_all.held, early_all.held) = qkv_sum.take(late_all.held, early_all.held)
    (late_all.held, early_all.held) = up_sum.take(late_all.held, early_all.held)
    (late_all.held, early_all.held) = qkv_sum.send(late_all.held, early_all.held)
    early_all.step()
    late_all.step()
    late_all.step()
    down_sum.settle(late_all.held)
    up_sum.settle(late_all.held)
    down = down_sum.result().T
    up = up_sum.result()
    (late_all.held, early_all.held, up, down) = qkv_sum.take(
        late_all.held, early_all.held, up, down
    )
    (late_all.held, early_all.held) = qkv_sum.send(late_all.held, early_all.held)
    while early_all.order:
        early_all.step()
    while late_all.order:
        late_all.step()
    early_all, late_all = early_all.held, late_all.held
    early_tall = early_all[:, : 3 * segs].reshape((n_batch, 3, segs, local_width))
    cond_all = early_all[:, 3 * segs : (3 + n_tensor) * segs].reshape((n_batch, segs, model_width))
    bias_all = early_all[:, (3 + n_tensor) * segs :]
    late_tall = late_all[:, : 3 * segs].reshape((n_batch, 3, segs, local_width))
    late_bias = late_all[:, 3 * segs :]

    def bias_sum(held):
        return jnp.sum(held.astype(f32), axis=0).reshape((2, -1)).sum(axis=0)

    bias_all = bias_sum(bias_all)
    qv_sum = bias_sum(late_bias).reshape((2, local_width))
    projbias_sum = bias_all[:model_width]
    downbias_sum = bias_all[model_width : 2 * model_width]
    upbias_sum = bias_all[2 * model_width :]
    cond_block = lax.dynamic_slice_in_dim(cond_all, index * block, block, 2)

    def mod_sums(held):
        return product("psd,pjsc->jdc", cond_block, held), jnp.sum(held.astype(f32), axis=(0, 2))

    early_mod, early_modbias = mod_sums(early_tall)
    late_mod, late_modbias = mod_sums(late_tall)
    mod_sum = jnp.concatenate([late_mod[:2], early_mod, late_mod[2:]]).transpose((1, 0, 2))
    modbias_sum = jnp.concatenate([late_modbias[:2], early_modbias, late_modbias[2:]])

    qkv_sum.take()
    last = qkv_sum.result()
    begin = 2 * local_width + padded(local_width)
    return (
        layer_out[None],
        token_t.T[None],
        condition_grad[None],
        last[:, : 3 * local_width].reshape((-1, 3, local_width)),
        qv_sum,
        last[:, begin : begin + local_width].T,
        projbias_sum,
        up,
        upbias_sum,
        down,
        downbias_sum,
        mod_sum,
        modbias_sum,
    )


def solution(mesh):
    return jax.shard_map(
        functools.partial(on_device, mesh.shape["batch"]),
        mesh=mesh,
        in_specs=(
            P("batch", None, None),
            P("batch", None),
            P("batch", None, None),
            P("batch", None),
            P(None, None, "tensor"),
            P(None, "tensor"),
            P("tensor", None),
            P(),
            P(None, "tensor"),
            P("tensor"),
            P("tensor", None),
            P(),
            P(None, None, "tensor"),
            P(None, "tensor"),
            P("batch", None, None),
        ),
        out_specs=(
            P("batch", None, None),
            P("batch", None, "tensor"),
            P("batch", None, None),
            P("batch", None, "tensor"),
            P(None, "tensor"),
            P("tensor", "batch"),
            P(),
            P("batch", "tensor"),
            P("tensor"),
            P("tensor", "batch"),
            P(),
            P("batch", None, "tensor"),
            P(None, "tensor"),
        ),
        check_vma=False,
    )
```

```python
import functools

import jax
import jax.numpy as jnp
import numpy as np
from jax import lax
from jax.experimental import pallas as pl
from jax.experimental.pallas import tpu as pltpu
from jax.sharding import PartitionSpec as P

EPS = 1e-06
HEAD_DIM = 72
SEGS = 8
MOST = 256
LOG2E = 1.4426950408889634
NEG = -1e30


def band(begin, width, length):
    low = max(0, (begin - MOST + 1) // 128 * 128)
    high = min(length, -(-(begin + width + MOST - 1) // 128) * 128)
    return low, high


def natural(array):
    return array.astype(jnp.float32).T.astype(jnp.bfloat16)


def marks(seg_row):
    slots = lax.broadcasted_iota(jnp.int32, (SEGS, seg_row.shape[-1]), 0)
    return (slots == seg_row[...]).astype(jnp.float32)


def fill(head, qkv, one_hot, q_aug, k_nat):
    query = jnp.concatenate([qkv[0, head].astype(jnp.float32), (1.0 - one_hot) * NEG], axis=0)
    q_aug[...] = query.astype(jnp.bfloat16)
    k_nat[...] = natural(jnp.concatenate([qkv[1, head].astype(jnp.float32), one_hot], axis=0))


def attention_forward_kernel(width, seg_row, qkv, out, stat, q_aug, k_nat):
    heads, length = qkv.shape[1], qkv.shape[3]
    factor = HEAD_DIM**-0.5 * LOG2E
    one_hot = marks(seg_row)

    def one(head, carry):
        fill(head, qkv, one_hot, q_aug, k_nat)
        for begin in range(0, length, width):
            low, high = band(begin, width, length)
            span = slice(begin, begin + width)
            scores = jnp.dot(
                k_nat[low:high, :], q_aug[:, span], preferred_element_type=jnp.float32
            )
            peak = jnp.max(scores, axis=0, keepdims=True) * factor
            shifted = jnp.exp2(scores * factor - peak)
            total = jnp.sum(shifted, axis=0, keepdims=True)
            got = jnp.dot(
                qkv[2, head, :, low:high],
                shifted.astype(jnp.bfloat16),
                preferred_element_type=jnp.float32,
            )
            out[head, :, span] = (got * (1.0 / total)).astype(jnp.bfloat16)
            stat[head, :, span] = peak + jnp.log2(total)
        return carry

    lax.fori_loop(0, heads, one, 0, unroll=2)


def attention_backward_kernel(
    width, seg_row, qkv, stat, grad, out, q_aug, k_nat, v_nat, q_nat, g_nat, p_all, s_all
):
    heads, length = qkv.shape[1], qkv.shape[3]
    scale = HEAD_DIM**-0.5
    factor = scale * LOG2E
    one_hot = marks(seg_row)

    def one(head, carry):
        fill(head, qkv, one_hot, q_aug, k_nat)
        v_nat[...] = natural(qkv[2, head])
        q_nat[...] = natural(qkv[0, head])
        g_nat[...] = natural(grad[head])
        for begin in range(0, length, width):
            low, high = band(begin, width, length)
            span = slice(begin, begin + width)
            scores = jnp.dot(
                k_nat[low:high, :], q_aug[:, span], preferred_element_type=jnp.float32
            )
            probs = jnp.exp2(scores * factor - stat[head, :, span])
            prob_grad = jnp.dot(
                v_nat[low:high, :], grad[head, :, span], preferred_element_type=jnp.float32
            )
            row = jnp.sum(prob_grad * probs, axis=0, keepdims=True)
            score_grad = (probs * (prob_grad - row)).astype(jnp.bfloat16)
            p_all[low:high, span] = probs.astype(jnp.bfloat16)
            s_all[low:high, span] = score_grad
            got = jnp.dot(
                qkv[1, head, :, low:high], score_grad, preferred_element_type=jnp.float32
            )
            out[0, head, :, span] = (got * scale).astype(jnp.bfloat16)
        for begin in range(0, length, width):
            span = slice(begin, begin + width)
            reach = [q for q in range(0, length, width) if band(q, width, length)[0] < begin + width and band(q, width, length)[1] > begin]
            low, high = reach[0], reach[-1] + width
            key_grad = jnp.dot(
                s_all[span, low:high], q_nat[low:high, :], preferred_element_type=jnp.float32
            )
            value_grad = jnp.dot(
                p_all[span, low:high], g_nat[low:high, :], preferred_element_type=jnp.float32
            )
            out[1, head, :, span] = (key_grad * scale).T.astype(jnp.bfloat16)
            out[2, head, :, span] = value_grad.T.astype(jnp.bfloat16)
        return carry

    if width < MOST:
        p_all[...] = jnp.zeros_like(p_all)
        s_all[...] = jnp.zeros_like(s_all)
    lax.fori_loop(0, heads, one, 0, unroll=2)


VMEM = pl.BlockSpec(memory_space=pltpu.VMEM)


CHUNK = 128


def dot(left, right):
    return jnp.dot(left, right, preferred_element_type=jnp.float32)


def dot_nt(left, right):
    return lax.dot_general(
        left, right, (((1,), (1,)), ((), ())), preferred_element_type=jnp.float32
    )


def wide(value):
    return value.astype(jnp.float32)


def turn(order, value, out, work):
    count = order.shape[0]
    rows = value.shape[1] // count
    work[...] = wide(value).T
    for at in range(0, count, 2):
        pair = [
            work[pl.ds(pl.multiple_of(order[at + i] * rows, 8), rows), :] for i in range(2)
        ]
        pair = jnp.concatenate(pair, axis=0).astype(jnp.bfloat16)
        out[at * rows : (at + 2) * rows, :] = pair


def own_part(side, value, width):
    part = value[:, :width]
    for at in range(1, value.shape[1] // width):
        part = jnp.where(side == at, value[:, at * width : (at + 1) * width], part)
    return part


def accumulate(total, value):
    @pl.when(pl.program_id(0) == 0)
    def _():
        total[...] = value

    @pl.when(pl.program_id(0) > 0)
    def _():
        total[...] += value


def segment_sums(slots, seg, *values):
    marks = (slots[...] == seg[...]).astype(jnp.bfloat16)
    sums = []
    for value in values:
        high = value.astype(jnp.bfloat16)
        low = (value - wide(high)).astype(jnp.bfloat16)
        sums.append(dot(marks, high) + dot(marks, low))
    return jnp.concatenate(sums, axis=0)


def norm_parts(value):
    width = value.shape[1]
    mean = jnp.sum(value, axis=1, keepdims=True) / width
    center = value - mean
    spread = jnp.sum(center * center, axis=1, keepdims=True) / width
    return mean, center, lax.rsqrt(spread + EPS)


def entry_kernel(order, side, picks, tables, tokens, out, mean, inverse, normed_mine, *turned):
    pick = picks[...]
    middle, center, scale = norm_parts(wide(tokens[...]))
    mean[...] = middle
    inverse[...] = scale
    value = center * scale
    normed_mine[...] = own_part(side[0], value, normed_mine.shape[1])
    value = (value * (1.0 + dot(pick, tables[1])) + dot(pick, tables[0])).astype(jnp.bfloat16)
    out[...] = value
    if turned:
        turn(order, value, *turned)


def gate_kernel(order, picks, tables, grad, out, bias, *turned):
    value = (wide(grad[...]) * dot(picks[...], tables[5])).astype(jnp.bfloat16)
    out[...] = value
    accumulate(bias, jnp.sum(wide(value), axis=0, keepdims=True))
    if turned:
        turn(order, value, *turned)


def middle_of(pick, tables, tokens, part, other, bias):
    attn_out = wide(part[...]) + wide(other[...]) + bias[...]
    return attn_out, wide(tokens[...]) + dot(pick, tables[2]) * attn_out


def middle_kernel(order, picks, tables, tokens, part, other, bias, out, mean, inverse, *turned):
    pick = picks[...]
    value = middle_of(pick, tables, tokens, part, other, bias)[1]
    middle, center, scale = norm_parts(value)
    mean[...] = middle
    inverse[...] = scale
    value = center * scale * (1.0 + dot(pick, tables[4])) + dot(pick, tables[3])
    value = value.astype(jnp.bfloat16)
    out[...] = value
    if turned:
        turn(order, value, *turned)


def middle_grad_kernel(
    order, side, picks, marks, seg, tables, tokens, part, other, bias, mean, inverse, mlp, mlp_other, grad,
    out, bias_sum, grad_mine, totals, *turned
):
    pick = picks[...]
    width = grad.shape[1]
    attn_out, value = middle_of(pick, tables, tokens, part, other, bias)
    norm = (value - mean[...]) * inverse[...]
    in_grad = wide(mlp[...]) + wide(mlp_other[...])
    value = in_grad * (1.0 + dot(pick, tables[4]))
    plain = jnp.sum(value, axis=1, keepdims=True) / width
    cross = jnp.sum(value * norm, axis=1, keepdims=True) / width
    value = wide(grad[...]) + inverse[...] * (value - plain - norm * cross)
    grad_mine[...] = own_part(side[0], value, grad_mine.shape[1])
    accumulate(totals, segment_sums(marks, seg, value * attn_out, in_grad, in_grad * norm))
    value = (value * dot(pick, tables[2])).astype(jnp.bfloat16)
    out[...] = value
    accumulate(bias_sum, jnp.sum(wide(value), axis=0, keepdims=True))
    if turned:
        turn(order, value, *turned)


def halves_kernel(side, picks, tables, part, tokens, mean, inverse, kept, sent, sums):
    value = part[...]
    width = kept.shape[1]
    kept[...] = own_part(side[0], value, width)
    sent[:, :width] = own_part(1 - side[0], value, width)
    value = wide(value) * (1.0 + dot(picks[...], tables[1]))
    norm = (wide(tokens[...]) - mean[...]) * inverse[...]
    for at, term in enumerate((value, value * norm)):
        total = jnp.sum(term, axis=1, keepdims=True)
        high = total.astype(jnp.bfloat16)
        sums[:, at : at + 1] = total
        sent[:, width + 2 * at : width + 2 * at + 1] = high
        sent[:, width + 2 * at + 1 : width + 2 * at + 2] = (total - wide(high)).astype(jnp.bfloat16)


def token_grad_kernel(
    width, picks, marks, seg, tables, kept, other, sums, normed, inverse, grad, out_t, totals
):
    mine = kept.shape[1]
    value = wide(kept[...]) + wide(other[:, :mine])
    norm = normed[...]
    accumulate(totals, segment_sums(marks, seg, value, value * norm))
    value = value * (1.0 + dot(picks[...], tables[1]))
    for at, factor in enumerate((1.0, norm)):
        rest = wide(other[:, mine + 2 * at : mine + 2 * at + 1])
        rest = rest + wide(other[:, mine + 2 * at + 1 : mine + 2 * at + 2])
        value = value - factor * ((sums[:, at : at + 1] + rest) / width)
    out_t[...] = (grad[...] + inverse[...] * value).T


def layer_kernel(
    picks, marks, seg, tables, tokens, part, other, bias, down, down_other, down_bias, grad, out, totals
):
    pick = picks[...]
    mlp_out = wide(down[...]) + wide(down_other[...]) + down_bias[...]
    middle = middle_of(pick, tables, tokens, part, other, bias)[1]
    out[...] = (middle + dot(pick, tables[5]) * mlp_out).astype(jnp.bfloat16)
    accumulate(totals, segment_sums(marks, seg, wide(grad[...]) * mlp_out))


def row_parts(sent, first):
    if first:
        return (2, 3) if sent else (0, 1)
    return (1, 3) if sent else (0, 2)


def put_rows(left, right, out, parts, product):
    quarter = left.shape[0] // 4
    columns = slice(0, right.shape[0] if product is dot_nt else right.shape[1])
    if parts[1] == parts[0] + 1:
        rows = slice(parts[0] * quarter, (parts[1] + 1) * quarter)
        out[:, columns] = product(left[rows, :], right[...]).astype(jnp.bfloat16)
        return
    for at, part in enumerate(parts):
        rows = slice(part * quarter, (part + 1) * quarter)
        value = product(left[rows, :], right[...]).astype(jnp.bfloat16)
        out[at * quarter : (at + 1) * quarter, columns] = value


def mlp_grads_kernel(sent, left, right, first, second):
    step, half = pl.program_id(0), pl.num_programs(0) // 2

    @pl.when(step < half)
    def _():
        put_rows(left, right, first, row_parts(sent, True), dot)

    @pl.when(step >= half)
    def _():
        put_rows(left, right, second, row_parts(sent, False), dot)


def qkv_grads_kernel(sent, left, proj_left, both, value, attended, first, second):
    step = pl.program_id(0)

    @pl.when(step < 3)
    def _():
        put_rows(left, both, first, row_parts(sent, True), dot_nt)

    @pl.when(step == 3)
    def _():
        second[...] = jnp.zeros_like(second)
        put_rows(left, value, second, row_parts(sent, False), dot_nt)

    @pl.when(step == 4)
    def _():
        second[...] = jnp.zeros_like(second)
        put_rows(proj_left, attended, second, row_parts(sent, False), dot_nt)


SMEM = pl.BlockSpec(memory_space=pltpu.SMEM)
FREE = pl.CostEstimate(flops=1, bytes_accessed=1, transcendentals=0)


def micros(time):
    if time == 0:
        return FREE
    return pl.CostEstimate(flops=time * 10**9, bytes_accessed=time * 10**6, transcendentals=0)


def shape(dims, dtype=jnp.bfloat16):
    return jax.ShapeDtypeStruct(dims, dtype)


def in_hbm(array):
    return pltpu.with_memory_space_constraint(array, pltpu.HBM)


def room(mib):
    return pltpu.CompilerParams(vmem_limit_bytes=mib << 20)


def spec(dims, kind):
    if kind == "v":
        return VMEM
    if kind == "r":
        return pl.BlockSpec((CHUNK, dims[1]), lambda i: (i, 0))
    if kind == "c":
        return pl.BlockSpec((dims[0], CHUNK), lambda i: (0, i))
    return pl.BlockSpec(tuple(dims), lambda i: (0,) * len(dims))


def sweep(kernel, length, scalars, arrays, outs, work=(), mib=16, cost=200):
    return pl.pallas_call(
        kernel,
        grid=(length // CHUNK,),
        in_specs=[SMEM] * len(scalars) + [spec(a.shape, kind) for a, kind in arrays],
        out_specs=[spec(o.shape, kind) for o, kind in outs],
        out_shape=[o for o, _ in outs],
        scratch_shapes=[pltpu.VMEM(dims, jnp.float32) for dims in work],
        compiler_params=room(mib),
        cost_estimate=micros(cost),
    )(*scalars, *[a for a, _ in arrays])


def mlp_grads(sent, left, right):
    width, length = left.shape
    hidden = right.shape[1]
    half, block = hidden // 2, hidden // 6
    return pl.pallas_call(
        functools.partial(mlp_grads_kernel, sent),
        grid=(6,),
        in_specs=[
            spec(left.shape, "w"),
            pl.BlockSpec((length, block), lambda j: (0, j)),
        ],
        out_specs=[
            pl.BlockSpec((width // 2, block), lambda j: (0, jnp.minimum(j, 2))),
            pl.BlockSpec((width // 2, block), lambda j: (0, jnp.maximum(j - 3, 0))),
        ],
        out_shape=[shape((width // 2, half))] * 2,
        compiler_params=room(16),
        cost_estimate=FREE,
    )(in_hbm(left), in_hbm(right))


def padded(width):
    return -(-width // 128) * 128


def qkv_grads(sent, left, proj_left, triple, attended):
    width, length = left.shape
    local = attended.shape[0]
    block, wide_block = 2 * local // 3, padded(local)
    return pl.pallas_call(
        functools.partial(qkv_grads_kernel, sent),
        grid=(5,),
        in_specs=[
            spec(left.shape, "w"),
            spec(left.shape, "w"),
            pl.BlockSpec((block, length), lambda j: (jnp.minimum(j, 2), 0)),
            pl.BlockSpec((local, length), lambda j: (2, 0)),
            spec(attended.shape, "w"),
        ],
        out_specs=[
            pl.BlockSpec((width // 2, block), lambda j: (0, jnp.minimum(j, 2))),
            pl.BlockSpec((width // 2, wide_block), lambda j: (0, jnp.maximum(j - 3, 0))),
        ],
        out_shape=[shape((width // 2, 2 * local)), shape((width // 2, 2 * wide_block))],
        compiler_params=room(24),
        cost_estimate=FREE,
    )(in_hbm(left), in_hbm(proj_left), triple, triple, attended)


def attention_forward(segments, qkv, width=256):
    heads, length = qkv.shape[1], qkv.shape[3]
    return pl.pallas_call(
        functools.partial(attention_forward_kernel, width),
        in_specs=[VMEM] * 2,
        out_specs=[VMEM] * 2,
        out_shape=[shape((heads, HEAD_DIM, length)), shape((heads, 1, length), jnp.float32)],
        scratch_shapes=[
            pltpu.VMEM((HEAD_DIM + SEGS, length), jnp.bfloat16),
            pltpu.VMEM((length, HEAD_DIM + SEGS), jnp.bfloat16),
        ],
        compiler_params=room(12),
        cost_estimate=micros(15),
    )(segments, qkv)


def attention_backward(segments, qkv, stat, grad, width=256):
    heads, length = qkv.shape[1], qkv.shape[3]
    return pl.pallas_call(
        functools.partial(attention_backward_kernel, width),
        in_specs=[VMEM] * 4,
        out_specs=VMEM,
        out_shape=shape(qkv.shape),
        scratch_shapes=[
            pltpu.VMEM((HEAD_DIM + SEGS, length), jnp.bfloat16),
            pltpu.VMEM((length, HEAD_DIM + SEGS), jnp.bfloat16),
        ]
        + [pltpu.VMEM((length, HEAD_DIM), jnp.bfloat16)] * 3
        + [pltpu.VMEM((length, length), jnp.bfloat16)] * 2,
        compiler_params=room(16),
        cost_estimate=micros(15),
    )(segments, qkv, stat, grad)


def silu(array):
    return array / (1.0 + jnp.exp(-array))


def product(spec, left, right):
    return jnp.einsum(spec, left, right, preferred_element_type=jnp.float32)


def exchange(array):
    return lax.ppermute(array, "tensor", [(0, 1), (1, 0)])


def summands(part, size):
    if size == 2:
        return part, exchange(part)
    return lax.psum(part, "tensor"), jnp.zeros_like(part)


def tensor_join(array, size):
    if size == 2:
        other = exchange(array)
        first = lax.axis_index("tensor") == 0
        return jnp.concatenate(
            [jnp.where(first, array, other), jnp.where(first, other, array)], axis=-1
        )
    return lax.all_gather(array, "tensor", axis=array.ndim - 1, tiled=True)


def partners(size, bit):
    return [(i, i ^ (1 << bit)) for i in range(size)]


def tie(*values):
    return lax.optimization_barrier(values)


def after(value, *others):
    return tie(value, *others)[0]


class Gather:
    def __init__(self, array, size, order):
        self.held, self.size, self.order = array[None], size, list(order)

    def step(self, *others):
        if self.order:
            bit = self.order.pop(0)
            self.held = after(self.held, *others)
            other = lax.ppermute(self.held, "batch", partners(self.size, bit))
            self.held = jnp.concatenate([self.held, other], axis=0)


class Sum:
    def __init__(self, sends, size):
        self.sends, self.size, self.bits = sends, size, size.bit_length() - 1
        self.keeps, self.got = None, []

    def rows(self, low, high):
        halves = [keep[low:high].astype(jnp.float32) for keep in self.keeps]
        for stage in self.got[:2]:
            halves = [half + new[low:high].astype(jnp.float32) for half, new in zip(halves, stage)]
        if len(self.got) < 2:
            return halves
        total = jnp.concatenate(halves, axis=1)
        for (new,) in self.got[2:]:
            total = total + new[low:high].astype(jnp.float32)
        return [total]

    def send(self, *others):
        stage = len(self.got)
        sends, bits = self.sends, [stage]
        if stage > 0:
            left = self.keeps[0].shape[0] >> stage
            sends = [half.astype(jnp.bfloat16) for half in self.rows(left, 2 * left)]
        if stage < 2:
            bits = [stage, 1 - stage]
        tied = tie(*sends, *others)
        self.sent = tied[: len(sends)]
        self.flying = [
            lax.ppermute(piece, "batch", partners(self.size, bit))
            for piece, bit in zip(tied, bits)
        ]
        return tied[len(sends) :]

    def take(self, *others):
        tied = tie(*self.flying, *others)
        self.got.append(tied[: len(self.flying)])
        return tied[len(self.flying) :]

    def settle(self, other):
        if len(self.got) == self.bits:
            self.keeps = list(tie(*self.keeps, other)[:2])

    def result(self):
        while len(self.got) < self.bits:
            self.send()
            self.take()
        return self.rows(0, 2 * self.keeps[0].shape[0] // self.size)[0]


def gelu_and_slope(array):
    square = array * array
    bent = jnp.tanh(0.7978845608028654 * (array + 0.044715 * array * square))
    half = 0.5 * (1.0 + bent)
    inner = 0.7978845608028654 * (1.0 + 3.0 * 0.044715 * square)
    return array * half, half + 0.5 * array * (1.0 - bent * bent) * inner


def high_low(array):
    high = lax.reduce_precision(array, 8, 7)
    return [high.astype(jnp.bfloat16), (array - high).astype(jnp.bfloat16)]


def in_three(array):
    high = lax.reduce_precision(array, 8, 7)
    middle = lax.reduce_precision(array - high, 8, 7)
    return [high, middle, array - high - middle]


def on_device(
    n_batch,
    tokens,
    segment_ids,
    conditions,
    condition_segment,
    qkv_weight,
    qv_bias,
    proj_weight,
    proj_bias,
    up_weight,
    up_bias,
    down_weight,
    down_bias,
    mod_weight,
    mod_bias,
    out_grad,
):
    bf16, f32 = jnp.bfloat16, jnp.float32
    tokens, out_grad = tokens[0], out_grad[0]
    length, model_width = tokens.shape
    local_width = qkv_weight.shape[2]
    hidden_width = up_weight.shape[1]
    heads = local_width // HEAD_DIM
    n_tensor = model_width // local_width
    bits = list(range(n_batch.bit_length() - 1))
    block = model_width // n_batch
    in_kernel = block % 8 == 0
    index = lax.axis_index("batch")
    order = jnp.array(
        [sum((p >> bit & 1) << (bits[-1] - bit) for bit in bits) for p in range(n_batch)], jnp.int32
    )
    order = order ^ index
    side = lax.axis_index("tensor")[None]

    def run(kernel, scalars, arrays, outs):
        turned = pltpu.HBM((model_width, length), bf16)
        if in_kernel:
            chunk = (model_width, CHUNK)
            return sweep(kernel, length, scalars, arrays, outs + [(turned, "c")], [chunk])
        got = sweep(kernel, length, scalars, arrays, outs)
        return list(got) + [got[0].T.reshape((n_batch, block, length))[order].reshape(turned.shape)]

    def part_rows(left, sent, first):
        quarter = model_width // 4
        rows = [left[at * quarter : (at + 1) * quarter] for at in row_parts(sent, first)]
        return jnp.concatenate(rows)

    def hidden_grads(sent, left, right):
        if in_kernel:
            return mlp_grads(sent, left, right)
        cut = right.shape[1] // 2
        return [
            product("dl,lc->dc", part_rows(left, sent, True), right[:, :cut]).astype(bf16),
            product("dl,lc->dc", part_rows(left, sent, False), right[:, cut:]).astype(bf16),
        ]

    def attention_grads(sent, left, proj_left, triple, attended):
        if in_kernel:
            return qkv_grads(sent, left, proj_left, triple, attended)
        cut, extra = 2 * local_width, ((0, 0), (0, padded(local_width) - local_width))
        halves = [
            (part_rows(left, sent, True), triple[:cut]),
            (part_rows(left, sent, False), triple[cut:]),
            (part_rows(proj_left, sent, False), attended),
        ]
        first, value, proj = [product("dl,cl->dc", *pair).astype(bf16) for pair in halves]
        return [first, jnp.concatenate([jnp.pad(value, extra), jnp.pad(proj, extra)], axis=1)]

    cond_float = conditions[0].astype(f32)
    cond_act = silu(cond_float).astype(bf16)
    mod_local = product("sd,djc->jsc", cond_act, mod_weight) + mod_bias[:, None]
    modulation = tensor_join(mod_local, n_tensor)
    segs = modulation.shape[1]
    tables = jnp.concatenate(in_three(modulation) + [jnp.zeros_like(modulation)], axis=1).astype(bf16)
    slots = condition_segment[0][jnp.arange(4 * segs) % segs]
    real = jnp.arange(4 * segs) < 3 * segs
    picks = ((segment_ids[0][:, None] == slots[None]) & real[None]).astype(bf16)
    marks = jnp.concatenate([condition_segment[0], jnp.full((segs,), -1, jnp.int32)])[:, None]
    full, column = (length, model_width), shape((length, 1), f32)
    mine = (length, local_width)
    row = shape((1, model_width), f32)

    qkv_weight = qkv_weight.transpose((1, 2, 0))
    attn_in, mean_one, inverse_one, normed_mine, in_t = run(
        entry_kernel,
        [order, side],
        [(picks, "r"), (tables, "v"), (in_hbm(tokens), "r")],
        [(shape(full), "r"), (column, "r"), (column, "r"), (pltpu.HBM(mine, f32), "r")],
    )
    biases = jnp.stack([qv_bias[0], jnp.zeros_like(qv_bias[0]), qv_bias[1]])
    qkv = product("jcd,ld->jcl", qkv_weight, attn_in) + biases[:, :, None]
    qkv = qkv.astype(bf16).reshape((3, heads, HEAD_DIM, length))
    attended, stat = attention_forward(segment_ids, qkv)
    attended = attended.reshape((local_width, length))
    proj_part = product("cl,cd->ld", attended, proj_weight).astype(bf16)
    proj_part, proj_other = summands(proj_part, n_tensor)
    out_grad, proj_tied = tie(out_grad, proj_part)
    mlp_grad, down_bias_grad, grad_t = run(
        gate_kernel,
        [order],
        [(picks, "r"), (tables, "v"), (in_hbm(out_grad), "r")],
        [(shape(full), "r"), (row, "w")],
    )
    proj_other, mlp_grad = tie(proj_other, mlp_grad)
    middle_args = [
        (tables, "v"), (tokens, "r"), (proj_tied, "r"), (proj_other, "r"), (proj_bias[None], "v")
    ]
    mlp_in, mean_two, inverse_two, mlp_t = run(
        middle_kernel,
        [order],
        [(picks, "r")] + middle_args,
        [(shape(full), "r"), (column, "r"), (column, "r")],
    )
    hidden = product("ld,df->lf", mlp_in, up_weight) + up_bias
    active, slope = gelu_and_slope(hidden)
    active, slope = tie(active.astype(bf16), slope.astype(bf16))

    down_sum = Sum(hidden_grads(True, grad_t, active), n_batch)
    (mlp_grad_then, active_then) = down_sum.send(mlp_grad, active)
    active_grad = product("ld,fd->lf", mlp_grad_then, down_weight)
    hidden_grad = (active_grad * slope.astype(f32)).astype(bf16)
    mlp_part = product("lf,df->ld", hidden_grad, up_weight).astype(bf16)
    mlp_part, mlp_other = summands(mlp_part, n_tensor)
    (hidden_then, mlp_tied) = tie(hidden_grad, mlp_part)
    up_sum = Sum(hidden_grads(True, mlp_t, hidden_then), n_batch)
    down_sum.keeps = hidden_grads(False, grad_t, active_then)
    first, second, *down_sum.keeps = down_sum.take(*up_sum.sends, *down_sum.keeps)
    up_sum.sends = [first, second]
    (mlp_other, hidden_then) = down_sum.send(mlp_other, hidden_then)
    (mlp_other, hidden_then) = up_sum.send(mlp_other, hidden_then)
    attn_grad, proj_bias_grad, grad_mine, early_totals, attn_t = run(
        middle_grad_kernel,
        [order, side],
        [(picks, "r"), (marks, "v"), (segment_ids, "c")]
        + middle_args
        + [(mean_two, "r"), (inverse_two, "r"), (mlp_tied, "r"), (mlp_other, "r"), (out_grad, "r")],
        [
            (shape(full), "r"),
            (row, "w"),
            (pltpu.HBM(mine, f32), "r"),
            (shape((6 * segs, model_width), f32), "w"),
        ],
    )
    attended_grad = product("cd,ld->cl", proj_weight, attn_grad).astype(bf16)

    def packed(arrays):
        return jnp.concatenate([array.reshape((-1, local_width)) for array in arrays], axis=0)

    def tgrad(totals, count):
        kept = totals.reshape((count, 2 * segs, -1))[:, :segs]
        if kept.shape[2] > local_width:
            kept = lax.dynamic_slice_in_dim(kept, side[0] * local_width, local_width, 2)
        return kept.astype(bf16)

    triple = attention_backward(
        segment_ids, qkv, stat, attended_grad.reshape((heads, HEAD_DIM, length))
    ).reshape((3 * local_width, length))
    up_sum.keeps = hidden_grads(False, mlp_t, hidden_then)
    qkv_sum = Sum(attention_grads(True, in_t, attn_t, triple, attended), n_batch)
    first, second, *up_sum.keeps = up_sum.take(*qkv_sum.sends, *up_sum.keeps)
    qkv_sum.sends = [first, second]
    (triple,) = down_sum.take(triple)
    (triple,) = up_sum.send(triple)
    (triple,) = qkv_sum.send(triple)
    (triple,) = down_sum.send(triple)
    attn_part = product(
        "jcl,jcd->ld", triple.reshape((3, local_width, length)), qkv_weight
    ).astype(bf16)
    kept, sent, sums = sweep(
        halves_kernel,
        length,
        [side],
        [
            (picks, "r"),
            (tables, "v"),
            (attn_part, "r"),
            (tokens, "r"),
            (mean_one, "r"),
            (inverse_one, "r"),
        ],
        [
            (shape(mine), "r"),
            (shape((length, padded(local_width + 4))), "r"),
            (shape((length, 2), f32), "r"),
        ],
        cost=0,
    )
    (kept, sent) = up_sum.take(kept, sent)
    (kept, sent) = down_sum.take(kept, sent)
    (kept, sent, triple, active_then) = up_sum.send(kept, sent, triple, active)
    (kept, sent, triple, active_then) = down_sum.send(kept, sent, triple, active_then)
    (mod_local, kept) = tie(mod_local, kept)
    tables_mine = jnp.concatenate(in_three(mod_local) + [jnp.zeros_like(mod_local)], axis=1).astype(bf16)
    if n_tensor == 2:
        other = exchange(sent)
    else:
        kept = lax.psum_scatter(attn_part, "tensor", scatter_dimension=1, tiled=True)
        other = jnp.zeros_like(sent)
        sums = lax.psum(sums, "tensor")
    qkv_sum.keeps = attention_grads(False, in_t, attn_t, triple, attended)
    qv_bias_grad = jnp.sum(triple.reshape((3, local_width, length))[0::2].astype(f32), axis=2)
    token_t, late_totals = sweep(
        functools.partial(token_grad_kernel, model_width),
        length,
        [],
        [
            (picks, "r"),
            (marks, "v"), (segment_ids, "c"),
            (tables_mine, "v"),
            (kept, "r"),
            (other, "r"),
            (sums, "r"),
            (normed_mine, "r"),
            (inverse_one, "r"),
            (grad_mine, "r"),
        ],
        [(shape((local_width, length), f32), "c"), (shape((4 * segs, local_width), f32), "w")],
        cost=0,
    )
    (active_then, kept) = tie(active_then, kept)
    down_part = product("lf,fd->ld", active_then, down_weight).astype(bf16)
    (late_totals, down_part, *qkv_sum.keeps) = qkv_sum.take(
        late_totals, down_part, *qkv_sum.keeps
    )
    (late_totals,) = up_sum.take(late_totals)
    (down_part, late_totals) = qkv_sum.send(down_part, late_totals)
    (down_part, late_totals) = up_sum.send(down_part, late_totals)
    ways = bits[:1:-1] + bits[1::-1]
    up_bias_grad = jnp.sum(after(hidden_then, *qkv_sum.sent).astype(f32), axis=0)
    early_bias = [after(grad[0], *qkv_sum.sent) for grad in (proj_bias_grad, down_bias_grad)]
    early_bias = jnp.concatenate(early_bias + [up_bias_grad])
    early_totals = after(early_totals, *qkv_sum.sent)
    early_tgrad = tgrad(early_totals, 3)
    cond_rows = after(cond_act, *qkv_sum.sent).reshape((segs, n_tensor, local_width)).transpose((1, 0, 2))
    early_all = Gather(packed([early_tgrad, cond_rows] + high_low(early_bias)), n_batch, ways)
    early_all.step(*qkv_sum.sent)
    down_part, down_other = summands(down_part, n_tensor)
    layer_out, gate_total = sweep(
        layer_kernel,
        length,
        [],
        [(picks, "r"), (marks, "v"), (segment_ids, "c")]
        + middle_args
        + [(down_part, "r"), (down_other, "r"), (down_bias[None], "v"), (out_grad, "r")],
        [(shape(full), "r"), (shape((2 * segs, model_width), f32), "w")],
        cost=0,
    )
    (gate_total,) = qkv_sum.take(gate_total)
    (gate_total,) = up_sum.take(gate_total)
    (gate_total,) = down_sum.take(gate_total)
    early_all.step(gate_total)
    (gate_total,) = qkv_sum.send(gate_total)
    early_all.step(*qkv_sum.sent)
    late_tgrad = jnp.concatenate([tgrad(late_totals, 2), tgrad(gate_total, 1)])
    late_all = Gather(packed([late_tgrad] + high_low(qv_bias_grad)), n_batch, ways)
    late_all.step(*qkv_sum.sent)
    late_all.step()
    all_tgrad = jnp.concatenate([late_tgrad[:2], early_tgrad, late_tgrad[2:]])
    cond_part = product("jsc,djc->sd", all_tgrad, mod_weight)
    cond_part, cond_other = summands(cond_part.astype(bf16), n_tensor)
    cond_act_grad = cond_part.astype(f32) + cond_other.astype(f32)
    condition_grad = jax.vjp(silu, cond_float)[1](cond_act_grad)[0]
    down_sum.settle(gate_total)
    up_sum.settle(gate_total)
    down = down_sum.result().T
    up = up_sum.result()
    (up, down) = qkv_sum.take(up, down)
    qkv_sum.send()
    while late_all.order:
        early_all.step(*qkv_sum.sent)
        late_all.step(*qkv_sum.sent)

    part = index * block // local_width
    cond_block = lax.dynamic_slice(
        early_all.held,
        (0, (3 + part) * segs, index * block % local_width),
        (n_batch, segs, block),
    )

    def finish(held, biases):
        rows = held.shape[1]
        groups = np.arange(rows) // segs
        first = rows - 2 * biases
        marks = [(groups == j) & (np.arange(rows) < 3 * segs) for j in range(3)]
        marks += [(np.arange(rows) - first) % biases == b for b in range(biases)]
        for at in range(3, 3 + biases):
            marks[at] = marks[at] & (np.arange(rows) >= first)
        marks = jnp.asarray(np.stack(marks, axis=1), bf16)
        rest = ((0, 0), (0, rows - 3 * segs), (0, 0))
        blocks = jnp.pad(jnp.concatenate([cond_block] * 3, axis=1), rest)
        blocks = [blocks * marks[None, :, j : j + 1] for j in range(3)]
        left = jnp.concatenate(blocks + [jnp.broadcast_to(marks, (n_batch,) + marks.shape)], axis=2)
        left = left.reshape((n_batch * rows, -1))
        out = product("rk,rc->kc", left, held.reshape((n_batch * rows, local_width)))
        return out[: 3 * block].reshape((3, block, local_width)), out[3 * block :]

    early_mod, early_rows = finish(early_all.held, early_bias.shape[0] // local_width)
    late_mod, late_rows = finish(late_all.held, 2)
    qv_sum = late_rows[3:5]
    bias_all = early_rows[3:].reshape(-1)
    projbias_sum = bias_all[:model_width]
    downbias_sum = bias_all[model_width : 2 * model_width]
    upbias_sum = bias_all[2 * model_width :]
    mod_sum = jnp.concatenate([late_mod[:2], early_mod, late_mod[2:]])
    modbias_sum = jnp.concatenate([late_rows[:2], early_rows[:3], late_rows[2:3]])
    (mod_sum, modbias_sum, qv_sum, bias_all) = qkv_sum.take(mod_sum, modbias_sum, qv_sum, bias_all)
    mod_sum = mod_sum.transpose((1, 0, 2))
    last = qkv_sum.result()
    begin = 2 * local_width + padded(local_width)
    return (
        layer_out[None],
        token_t.T[None],
        condition_grad[None],
        last[:, : 3 * local_width].reshape((-1, 3, local_width)),
        qv_sum,
        last[:, begin : begin + local_width].T,
        projbias_sum,
        up,
        upbias_sum,
        down,
        downbias_sum,
        mod_sum,
        modbias_sum,
    )


def solution(mesh):
    return jax.shard_map(
        functools.partial(on_device, mesh.shape["batch"]),
        mesh=mesh,
        in_specs=(
            P("batch", None, None),
            P("batch", None),
            P("batch", None, None),
            P("batch", None),
            P(None, None, "tensor"),
            P(None, "tensor"),
            P("tensor", None),
            P(),
            P(None, "tensor"),
            P("tensor"),
            P("tensor", None),
            P(),
            P(None, None, "tensor"),
            P(None, "tensor"),
            P("batch", None, None),
        ),
        out_specs=(
            P("batch", None, None),
            P("batch", None, "tensor"),
            P("batch", None, None),
            P("batch", None, "tensor"),
            P(None, "tensor"),
            P("tensor", "batch"),
            P(),
            P("batch", "tensor"),
            P("tensor"),
            P("tensor", "batch"),
            P(),
            P("batch", None, "tensor"),
            P(None, "tensor"),
        ),
        check_vma=False,
    )
```

```python
import functools

import jax
import jax.numpy as jnp
import numpy as np
from jax import lax
from jax.experimental import pallas as pl
from jax.experimental.pallas import tpu as pltpu
from jax.sharding import PartitionSpec as P

EPS = 1e-06
HEAD_DIM = 72
SEGS = 8
MOST = 256
LOG2E = 1.4426950408889634
NEG = -1e30


def band(begin, width, length):
    low = max(0, (begin - MOST + 1) // 128 * 128)
    high = min(length, -(-(begin + width + MOST - 1) // 128) * 128)
    return low, high


def natural(array):
    return array.astype(jnp.float32).T.astype(jnp.bfloat16)


def marks(seg_row):
    slots = lax.broadcasted_iota(jnp.int32, (SEGS, seg_row.shape[-1]), 0)
    return (slots == seg_row[...]).astype(jnp.float32)


def fill(head, qkv, one_hot, q_aug, k_nat):
    query = jnp.concatenate([qkv[0, head].astype(jnp.float32), (1.0 - one_hot) * NEG], axis=0)
    q_aug[...] = query.astype(jnp.bfloat16)
    k_nat[...] = natural(jnp.concatenate([qkv[1, head].astype(jnp.float32), one_hot], axis=0))


def attention_forward_kernel(width, seg_row, qkv, out, stat, q_aug, k_nat):
    heads, length = qkv.shape[1], qkv.shape[3]
    factor = HEAD_DIM**-0.5 * LOG2E
    one_hot = marks(seg_row)

    def one(head, carry):
        fill(head, qkv, one_hot, q_aug, k_nat)
        for begin in range(0, length, width):
            low, high = band(begin, width, length)
            span = slice(begin, begin + width)
            scores = jnp.dot(
                k_nat[low:high, :], q_aug[:, span], preferred_element_type=jnp.float32
            )
            peak = jnp.max(scores, axis=0, keepdims=True) * factor
            shifted = jnp.exp2(scores * factor - peak)
            total = jnp.sum(shifted, axis=0, keepdims=True)
            got = jnp.dot(
                qkv[2, head, :, low:high],
                shifted.astype(jnp.bfloat16),
                preferred_element_type=jnp.float32,
            )
            out[head, :, span] = (got * (1.0 / total)).astype(jnp.bfloat16)
            stat[head, :, span] = peak + jnp.log2(total)
        return carry

    lax.fori_loop(0, heads, one, 0, unroll=2)


def attention_backward_kernel(
    width, seg_row, qkv, stat, grad, out, q_aug, k_nat, v_nat, q_nat, g_nat, p_all, s_all
):
    heads, length = qkv.shape[1], qkv.shape[3]
    scale = HEAD_DIM**-0.5
    factor = scale * LOG2E
    one_hot = marks(seg_row)

    def one(head, carry):
        fill(head, qkv, one_hot, q_aug, k_nat)
        v_nat[...] = natural(qkv[2, head])
        q_nat[...] = natural(qkv[0, head])
        g_nat[...] = natural(grad[head])
        for begin in range(0, length, width):
            low, high = band(begin, width, length)
            span = slice(begin, begin + width)
            scores = jnp.dot(
                k_nat[low:high, :], q_aug[:, span], preferred_element_type=jnp.float32
            )
            probs = jnp.exp2(scores * factor - stat[head, :, span])
            prob_grad = jnp.dot(
                v_nat[low:high, :], grad[head, :, span], preferred_element_type=jnp.float32
            )
            row = jnp.sum(prob_grad * probs, axis=0, keepdims=True)
            score_grad = (probs * (prob_grad - row)).astype(jnp.bfloat16)
            p_all[low:high, span] = probs.astype(jnp.bfloat16)
            s_all[low:high, span] = score_grad
            got = jnp.dot(
                qkv[1, head, :, low:high], score_grad, preferred_element_type=jnp.float32
            )
            out[0, head, :, span] = (got * scale).astype(jnp.bfloat16)
        for begin in range(0, length, width):
            span = slice(begin, begin + width)
            reach = [q for q in range(0, length, width) if band(q, width, length)[0] < begin + width and band(q, width, length)[1] > begin]
            low, high = reach[0], reach[-1] + width
            key_grad = jnp.dot(
                s_all[span, low:high], q_nat[low:high, :], preferred_element_type=jnp.float32
            )
            value_grad = jnp.dot(
                p_all[span, low:high], g_nat[low:high, :], preferred_element_type=jnp.float32
            )
            out[1, head, :, span] = (key_grad * scale).T.astype(jnp.bfloat16)
            out[2, head, :, span] = value_grad.T.astype(jnp.bfloat16)
        return carry

    if width < MOST:
        p_all[...] = jnp.zeros_like(p_all)
        s_all[...] = jnp.zeros_like(s_all)
    lax.fori_loop(0, heads, one, 0, unroll=2)


VMEM = pl.BlockSpec(memory_space=pltpu.VMEM)


CHUNK = 128


def dot(left, right):
    return jnp.dot(left, right, preferred_element_type=jnp.float32)


def dot_nt(left, right):
    return lax.dot_general(
        left, right, (((1,), (1,)), ((), ())), preferred_element_type=jnp.float32
    )


def wide(value):
    return value.astype(jnp.float32)


def turn(order, value, out, work):
    count = order.shape[0]
    rows = value.shape[1] // count
    work[...] = wide(value).T
    for at in range(0, count, 2):
        pair = [
            work[pl.ds(pl.multiple_of(order[at + i] * rows, 8), rows), :] for i in range(2)
        ]
        pair = jnp.concatenate(pair, axis=0).astype(jnp.bfloat16)
        out[at * rows : (at + 2) * rows, :] = pair


def own_part(side, value, width):
    part = value[:, :width]
    for at in range(1, value.shape[1] // width):
        part = jnp.where(side == at, value[:, at * width : (at + 1) * width], part)
    return part


def accumulate(total, value):
    @pl.when(pl.program_id(0) == 0)
    def _():
        total[...] = value

    @pl.when(pl.program_id(0) > 0)
    def _():
        total[...] += value


def segment_sums(slots, seg, *values):
    marks = (slots[...] == seg[...]).astype(jnp.bfloat16)
    sums = []
    for value in values:
        high = value.astype(jnp.bfloat16)
        low = (value - wide(high)).astype(jnp.bfloat16)
        sums.append(dot(marks, high) + dot(marks, low))
    return jnp.concatenate(sums, axis=0)


def norm_parts(value):
    width = value.shape[1]
    mean = jnp.sum(value, axis=1, keepdims=True) / width
    center = value - mean
    spread = jnp.sum(center * center, axis=1, keepdims=True) / width
    return mean, center, lax.rsqrt(spread + EPS)


def entry_kernel(order, side, picks, tables, tokens, out, mean, inverse, normed_mine, *turned):
    pick = picks[...]
    middle, center, scale = norm_parts(wide(tokens[...]))
    mean[...] = middle
    inverse[...] = scale
    value = center * scale
    normed_mine[...] = own_part(side[0], value, normed_mine.shape[1])
    value = (value * (1.0 + dot(pick, tables[1])) + dot(pick, tables[0])).astype(jnp.bfloat16)
    out[...] = value
    if turned:
        turn(order, value, *turned)


def gate_kernel(order, picks, tables, grad, out, bias, *turned):
    value = (wide(grad[...]) * dot(picks[...], tables[5])).astype(jnp.bfloat16)
    out[...] = value
    accumulate(bias, jnp.sum(wide(value), axis=0, keepdims=True))
    if turned:
        turn(order, value, *turned)


def middle_of(pick, tables, tokens, part, other, bias):
    attn_out = wide(part[...]) + wide(other[...]) + bias[...]
    return attn_out, wide(tokens[...]) + dot(pick, tables[2]) * attn_out


def middle_kernel(order, picks, tables, tokens, part, other, bias, out, mean, inverse, *turned):
    pick = picks[...]
    value = middle_of(pick, tables, tokens, part, other, bias)[1]
    middle, center, scale = norm_parts(value)
    mean[...] = middle
    inverse[...] = scale
    value = center * scale * (1.0 + dot(pick, tables[4])) + dot(pick, tables[3])
    value = value.astype(jnp.bfloat16)
    out[...] = value
    if turned:
        turn(order, value, *turned)


def middle_grad_kernel(
    order, side, picks, marks, seg, tables, tokens, part, other, bias, mean, inverse, mlp, mlp_other, grad,
    out, bias_sum, grad_mine, totals, *turned
):
    pick = picks[...]
    width = grad.shape[1]
    attn_out, value = middle_of(pick, tables, tokens, part, other, bias)
    norm = (value - mean[...]) * inverse[...]
    in_grad = wide(mlp[...]) + wide(mlp_other[...])
    value = in_grad * (1.0 + dot(pick, tables[4]))
    plain = jnp.sum(value, axis=1, keepdims=True) / width
    cross = jnp.sum(value * norm, axis=1, keepdims=True) / width
    value = wide(grad[...]) + inverse[...] * (value - plain - norm * cross)
    grad_mine[...] = own_part(side[0], value, grad_mine.shape[1])
    accumulate(totals, segment_sums(marks, seg, value * attn_out, in_grad, in_grad * norm))
    value = (value * dot(pick, tables[2])).astype(jnp.bfloat16)
    out[...] = value
    accumulate(bias_sum, jnp.sum(wide(value), axis=0, keepdims=True))
    if turned:
        turn(order, value, *turned)


def halves_kernel(side, picks, tables, part, tokens, mean, inverse, kept, sent, sums):
    value = part[...]
    width = kept.shape[1]
    kept[...] = own_part(side[0], value, width)
    sent[:, :width] = own_part(1 - side[0], value, width)
    value = wide(value) * (1.0 + dot(picks[...], tables[1]))
    norm = (wide(tokens[...]) - mean[...]) * inverse[...]
    for at, term in enumerate((value, value * norm)):
        total = jnp.sum(term, axis=1, keepdims=True)
        high = total.astype(jnp.bfloat16)
        sums[:, at : at + 1] = total
        sent[:, width + 2 * at : width + 2 * at + 1] = high
        sent[:, width + 2 * at + 1 : width + 2 * at + 2] = (total - wide(high)).astype(jnp.bfloat16)


def token_grad_kernel(
    width, picks, marks, seg, tables, kept, other, sums, normed, inverse, grad, out_t, totals
):
    mine = kept.shape[1]
    value = wide(kept[...]) + wide(other[:, :mine])
    norm = normed[...]
    accumulate(totals, segment_sums(marks, seg, value, value * norm))
    value = value * (1.0 + dot(picks[...], tables[1]))
    for at, factor in enumerate((1.0, norm)):
        rest = wide(other[:, mine + 2 * at : mine + 2 * at + 1])
        rest = rest + wide(other[:, mine + 2 * at + 1 : mine + 2 * at + 2])
        value = value - factor * ((sums[:, at : at + 1] + rest) / width)
    out_t[...] = (grad[...] + inverse[...] * value).T


def layer_kernel(
    picks, marks, seg, tables, tokens, part, other, bias, down, down_other, down_bias, grad, out, totals
):
    pick = picks[...]
    mlp_out = wide(down[...]) + wide(down_other[...]) + down_bias[...]
    middle = middle_of(pick, tables, tokens, part, other, bias)[1]
    out[...] = (middle + dot(pick, tables[5]) * mlp_out).astype(jnp.bfloat16)
    accumulate(totals, segment_sums(marks, seg, wide(grad[...]) * mlp_out))


def row_parts(sent, first):
    if first:
        return (2, 3) if sent else (0, 1)
    return (1, 3) if sent else (0, 2)


def put_rows(left, right, out, parts, product):
    quarter = left.shape[0] // 4
    columns = slice(0, right.shape[0] if product is dot_nt else right.shape[1])
    if parts[1] == parts[0] + 1:
        rows = slice(parts[0] * quarter, (parts[1] + 1) * quarter)
        out[:, columns] = product(left[rows, :], right[...]).astype(jnp.bfloat16)
        return
    for at, part in enumerate(parts):
        rows = slice(part * quarter, (part + 1) * quarter)
        value = product(left[rows, :], right[...]).astype(jnp.bfloat16)
        out[at * quarter : (at + 1) * quarter, columns] = value


def column_sums(array, product):
    return product(jnp.ones((8, array.shape[1] if product is dot_nt else array.shape[0]), jnp.bfloat16), array[...])


def mlp_grads_kernel(sent, left, right, first, second, sums):
    sums[...] = column_sums(right, dot)
    step, half = pl.program_id(0), pl.num_programs(0) // 2

    @pl.when(step < half)
    def _():
        put_rows(left, right, first, row_parts(sent, True), dot)

    @pl.when(step >= half)
    def _():
        put_rows(left, right, second, row_parts(sent, False), dot)


def qkv_grads_kernel(sent, left, proj_left, both, value, attended, first, second, sums, value_sums):
    step = pl.program_id(0)

    @pl.when(step < 3)
    def _():
        put_rows(left, both, first, row_parts(sent, True), dot_nt)
        sums[...] = column_sums(both, dot_nt)

    @pl.when(step == 3)
    def _():
        second[...] = jnp.zeros_like(second)
        put_rows(left, value, second, row_parts(sent, False), dot_nt)
        value_sums[...] = column_sums(value, dot_nt)

    @pl.when(step == 4)
    def _():
        second[...] = jnp.zeros_like(second)
        put_rows(proj_left, attended, second, row_parts(sent, False), dot_nt)


SMEM = pl.BlockSpec(memory_space=pltpu.SMEM)
FREE = pl.CostEstimate(flops=1, bytes_accessed=1, transcendentals=0)


def micros(time):
    if time == 0:
        return FREE
    return pl.CostEstimate(flops=time * 10**9, bytes_accessed=time * 10**6, transcendentals=0)


def shape(dims, dtype=jnp.bfloat16):
    return jax.ShapeDtypeStruct(dims, dtype)


def room(mib):
    return pltpu.CompilerParams(vmem_limit_bytes=mib << 20)


def spec(dims, kind):
    if kind == "v":
        return VMEM
    if kind == "r":
        return pl.BlockSpec((CHUNK, dims[1]), lambda i: (i, 0))
    if kind == "c":
        return pl.BlockSpec((dims[0], CHUNK), lambda i: (0, i))
    return pl.BlockSpec(tuple(dims), lambda i: (0,) * len(dims))


def sweep(kernel, length, scalars, arrays, outs, work=(), mib=16, cost=200):
    return pl.pallas_call(
        kernel,
        grid=(length // CHUNK,),
        in_specs=[SMEM] * len(scalars) + [spec(a.shape, kind) for a, kind in arrays],
        out_specs=[spec(o.shape, kind) for o, kind in outs],
        out_shape=[o for o, _ in outs],
        scratch_shapes=[pltpu.VMEM(dims, jnp.float32) for dims in work],
        compiler_params=room(mib),
        cost_estimate=micros(cost),
    )(*scalars, *[a for a, _ in arrays])


def mlp_grads(sent, left, right):
    width, length = left.shape
    hidden = right.shape[1]
    half, block = hidden // 2, hidden // 6
    return pl.pallas_call(
        functools.partial(mlp_grads_kernel, sent),
        grid=(6,),
        in_specs=[
            spec(left.shape, "w"),
            pl.BlockSpec((length, block), lambda j: (0, j)),
        ],
        out_specs=[
            pl.BlockSpec((width // 2, block), lambda j: (0, jnp.minimum(j, 2))),
            pl.BlockSpec((width // 2, block), lambda j: (0, jnp.maximum(j - 3, 0))),
            pl.BlockSpec((8, block), lambda j: (0, j)),
        ],
        out_shape=[shape((width // 2, half))] * 2 + [shape((8, hidden), jnp.float32)],
        compiler_params=room(16),
        cost_estimate=FREE,
    )(left, right)


def sum_kernel(counts, splits, *refs):
    halves, at = [], 0
    for count in counts[:2]:
        total = wide(refs[at][...])
        for ref in refs[at + 1 : at + count]:
            total += wide(ref[...])
        halves.append(total)
        at += count
    outs = refs[at + counts[2] :]
    for half in range(2):
        begin = 0 if half == 0 else halves[0].shape[1]
        columns = slice(begin, begin + halves[half].shape[1])
        for ref in refs[at : at + counts[2]]:
            halves[half] += wide(ref[:, columns])
    if splits is None:
        for out, total in zip(outs, halves):
            out[...] = total.astype(out.dtype)
    elif splits == ():
        for total, begin in zip(halves, (0, halves[0].shape[1])):
            outs[0][:, begin : begin + total.shape[1]] = total.astype(outs[0].dtype)
    else:
        for out, (half, begin, end) in zip(outs, splits):
            out[...] = halves[half][:, begin:end]


def sum_rows(halves, joined, at, count, outs, splits=None):
    arrays = halves[0] + halves[1] + joined

    def rows(width):
        return pl.BlockSpec((count, width), lambda i: (at, 0))

    return pl.pallas_call(
        functools.partial(sum_kernel, (len(halves[0]), len(halves[1]), len(joined)), splits),
        grid=(1,),
        in_specs=[rows(a.shape[1]) for a in arrays],
        out_specs=[pl.BlockSpec(o.shape, lambda i: (0, 0)) for o in outs],
        out_shape=outs,
        compiler_params=room(16),
        cost_estimate=FREE,
    )(*arrays)


def pack_kernel(
    side, middle, late, gate, cond, proj_bias, down_bias, up_bias, qk_bias, value_bias, out, work
):
    width = out.shape[1]
    segs = cond.shape[0]
    own = [late[:segs, :], late[2 * segs : 3 * segs, :]]
    for source, at in ((middle, 0), (middle, 1), (middle, 2), (gate, 0)):
        own.append(own_part(side[0], source[2 * at * segs : (2 * at + 1) * segs, :], width))
    own += [wide(cond[:, at : at + width]) for at in range(0, cond.shape[1], width)]
    for at, value in enumerate(own):
        work[at * segs : (at + 1) * segs, :] = value
    rows = []
    for source in (proj_bias, down_bias, up_bias):
        rows += [source[0:1, at : at + width] for at in range(0, source.shape[1], width)]
    rows += [qk_bias[0:1, :width], value_bias[0:1, :]]
    first = len(own) * segs
    for at, value in enumerate(rows):
        high = wide(value.astype(jnp.bfloat16))
        work[first + at : first + at + 1, :] = high
        work[first + len(rows) + at : first + len(rows) + at + 1, :] = value - high
    out[...] = work[: out.shape[0], :].astype(jnp.bfloat16)


def padded(width):
    return -(-width // 128) * 128


def qkv_grads(sent, left, proj_left, triple, attended):
    width, length = left.shape
    local = attended.shape[0]
    block, wide_block = 2 * local // 3, padded(local)
    return pl.pallas_call(
        functools.partial(qkv_grads_kernel, sent),
        grid=(5,),
        in_specs=[
            spec(left.shape, "w"),
            spec(left.shape, "w"),
            pl.BlockSpec((block, length), lambda j: (jnp.minimum(j, 2), 0)),
            pl.BlockSpec((local, length), lambda j: (2, 0)),
            spec(attended.shape, "w"),
        ],
        out_specs=[
            pl.BlockSpec((width // 2, block), lambda j: (0, jnp.minimum(j, 2))),
            pl.BlockSpec((width // 2, wide_block), lambda j: (0, jnp.maximum(j - 3, 0))),
            pl.BlockSpec((8, block), lambda j: (0, jnp.minimum(j, 2))),
            pl.BlockSpec((8, local), lambda j: (0, 0)),
        ],
        out_shape=[
            shape((width // 2, 2 * local)),
            shape((width // 2, 2 * wide_block)),
            shape((8, 2 * local), jnp.float32),
            shape((8, local), jnp.float32),
        ],
        compiler_params=room(24),
        cost_estimate=FREE,
    )(left, proj_left, triple, triple, attended)


def attention_forward(segments, qkv, width=256):
    heads, length = qkv.shape[1], qkv.shape[3]
    return pl.pallas_call(
        functools.partial(attention_forward_kernel, width),
        in_specs=[VMEM] * 2,
        out_specs=[VMEM] * 2,
        out_shape=[shape((heads, HEAD_DIM, length)), shape((heads, 1, length), jnp.float32)],
        scratch_shapes=[
            pltpu.VMEM((HEAD_DIM + SEGS, length), jnp.bfloat16),
            pltpu.VMEM((length, HEAD_DIM + SEGS), jnp.bfloat16),
        ],
        compiler_params=room(12),
        cost_estimate=micros(15),
    )(segments, qkv)


def attention_backward(segments, qkv, stat, grad, width=256):
    heads, length = qkv.shape[1], qkv.shape[3]
    return pl.pallas_call(
        functools.partial(attention_backward_kernel, width),
        in_specs=[VMEM] * 4,
        out_specs=VMEM,
        out_shape=shape(qkv.shape),
        scratch_shapes=[
            pltpu.VMEM((HEAD_DIM + SEGS, length), jnp.bfloat16),
            pltpu.VMEM((length, HEAD_DIM + SEGS), jnp.bfloat16),
        ]
        + [pltpu.VMEM((length, HEAD_DIM), jnp.bfloat16)] * 3
        + [pltpu.VMEM((length, length), jnp.bfloat16)] * 2,
        compiler_params=room(16),
        cost_estimate=micros(15),
    )(segments, qkv, stat, grad)


def silu(array):
    return array / (1.0 + jnp.exp(-array))


def product(spec, left, right):
    return jnp.einsum(spec, left, right, preferred_element_type=jnp.float32)


def exchange(array):
    return lax.ppermute(array, "tensor", [(0, 1), (1, 0)])


def summands(part, size):
    if size == 2:
        return part, exchange(part)
    return lax.psum(part, "tensor"), jnp.zeros_like(part)


def tensor_join(array, size):
    if size == 2:
        other = exchange(array)
        first = lax.axis_index("tensor") == 0
        return jnp.concatenate(
            [jnp.where(first, array, other), jnp.where(first, other, array)], axis=-1
        )
    return lax.all_gather(array, "tensor", axis=array.ndim - 1, tiled=True)


def partners(size, bit):
    return [(i, i ^ (1 << bit)) for i in range(size)]


def tie(*values):
    return lax.optimization_barrier(values)


def after(value, *others):
    return tie(value, *others)[0]


class Gather:
    def __init__(self, array, size, order):
        self.held, self.size, self.order = array[None], size, list(order)

    def step(self, *others):
        if self.order:
            bit = self.order.pop(0)
            self.held = after(self.held, *others)
            other = lax.ppermute(self.held, "batch", partners(self.size, bit))
            self.held = jnp.concatenate([self.held, other], axis=0)


class Sum:
    def __init__(self, sends, size, kernels):
        self.kernels = kernels
        self.sends, self.size, self.bits = sends, size, size.bit_length() - 1
        self.keeps, self.got = None, []

    def pieces(self, at, count, dtype, splits=None, outs=None):
        halves = [[self.keeps[h]] + [stage[h] for stage in self.got[:2]] for h in range(2)]
        joined = [new for (new,) in self.got[2:]]
        widths = [half[0].shape[1] for half in halves]
        if self.kernels:
            if outs is None:
                outs = [shape((count, width), dtype) for width in widths]
                if len(self.got) > 1:
                    outs, splits = [shape((count, sum(widths)), dtype)], ()
            return list(sum_rows(halves, joined, at, count, outs, splits))
        window = slice(at * count, (at + 1) * count)
        totals = [sum(a[window].astype(jnp.float32) for a in half) for half in halves]
        if len(self.got) < 2:
            return [total.astype(dtype) for total in totals]
        total = jnp.concatenate(totals, axis=1)
        total = sum((a[window].astype(jnp.float32) for a in joined), total)
        if outs is None:
            return [total.astype(dtype)]
        totals = [total[:, : widths[0]], total[:, widths[0] :]]
        return [totals[half][:, begin:end] for half, begin, end in splits]

    def send(self, *others):
        stage = len(self.got)
        sends, bits = self.sends, [stage]
        if stage > 0:
            left = self.keeps[0].shape[0] >> stage
            sends = self.pieces(1, left, jnp.bfloat16)
        if stage < 2:
            bits = [stage, 1 - stage]
        tied = tie(*sends, *others)
        self.sent = tied[: len(sends)]
        self.flying = [
            lax.ppermute(piece, "batch", partners(self.size, bit))
            for piece, bit in zip(tied, bits)
        ]
        return tied[len(sends) :]

    def take(self, *others):
        tied = tie(*self.flying, *others)
        self.got.append(tied[: len(self.flying)])
        return tied[len(self.flying) :]

    def settle(self, other):
        if len(self.got) == self.bits:
            self.keeps = list(tie(*self.keeps, other)[:2])

    def result(self, splits):
        while len(self.got) < self.bits:
            self.send()
            self.take()
        count = 2 * self.keeps[0].shape[0] // self.size
        outs = [shape((count, end - begin), jnp.float32) for _, begin, end in splits]
        return self.pieces(0, count, jnp.float32, splits, outs)


def gelu_and_slope(array):
    square = array * array
    bent = jnp.tanh(0.7978845608028654 * (array + 0.044715 * array * square))
    half = 0.5 * (1.0 + bent)
    inner = 0.7978845608028654 * (1.0 + 3.0 * 0.044715 * square)
    return array * half, half + 0.5 * array * (1.0 - bent * bent) * inner


def in_three(array):
    high = lax.reduce_precision(array, 8, 7)
    middle = lax.reduce_precision(array - high, 8, 7)
    return [high, middle, array - high - middle]


def on_device(
    n_batch,
    tokens,
    segment_ids,
    conditions,
    condition_segment,
    qkv_weight,
    qv_bias,
    proj_weight,
    proj_bias,
    up_weight,
    up_bias,
    down_weight,
    down_bias,
    mod_weight,
    mod_bias,
    out_grad,
):
    bf16, f32 = jnp.bfloat16, jnp.float32
    tokens, out_grad = tokens[0], out_grad[0]
    length, model_width = tokens.shape
    local_width = qkv_weight.shape[2]
    hidden_width = up_weight.shape[1]
    heads = local_width // HEAD_DIM
    n_tensor = model_width // local_width
    bits = list(range(n_batch.bit_length() - 1))
    block = model_width // n_batch
    in_kernel = block % 8 == 0
    index = lax.axis_index("batch")
    order = jnp.array(
        [sum((p >> bit & 1) << (bits[-1] - bit) for bit in bits) for p in range(n_batch)], jnp.int32
    )
    order = order ^ index
    side = lax.axis_index("tensor")[None]

    def run(kernel, scalars, arrays, outs):
        turned = shape((model_width, length))
        if in_kernel:
            chunk = (model_width, CHUNK)
            return sweep(kernel, length, scalars, arrays, outs + [(turned, "c")], [chunk])
        got = sweep(kernel, length, scalars, arrays, outs)
        return list(got) + [got[0].T.reshape((n_batch, block, length))[order].reshape(turned.shape)]

    def part_rows(left, sent, first):
        quarter = model_width // 4
        rows = [left[at * quarter : (at + 1) * quarter] for at in row_parts(sent, first)]
        return jnp.concatenate(rows)

    def hidden_grads(sent, left, right):
        if in_kernel:
            first, second, sums = mlp_grads(sent, left, right)
            return [first, second], sums
        sums = jnp.sum(right.astype(f32), axis=0)[None]
        cut = right.shape[1] // 2
        return [
            product("dl,lc->dc", part_rows(left, sent, True), right[:, :cut]).astype(bf16),
            product("dl,lc->dc", part_rows(left, sent, False), right[:, cut:]).astype(bf16),
        ], sums

    def attention_grads(sent, left, proj_left, triple, attended):
        if in_kernel:
            first, second, sums, value_sums = qkv_grads(sent, left, proj_left, triple, attended)
            return [first, second], (sums, value_sums)
        sums = jnp.sum(triple.astype(f32), axis=1)[None]
        sums = (sums[:, : 2 * local_width], sums[:, 2 * local_width :])
        cut, extra = 2 * local_width, ((0, 0), (0, padded(local_width) - local_width))
        halves = [
            (part_rows(left, sent, True), triple[:cut]),
            (part_rows(left, sent, False), triple[cut:]),
            (part_rows(proj_left, sent, False), attended),
        ]
        first, value, proj = [product("dl,cl->dc", *pair).astype(bf16) for pair in halves]
        return [first, jnp.concatenate([jnp.pad(value, extra), jnp.pad(proj, extra)], axis=1)], sums

    cond_float = conditions[0].astype(f32)
    cond_act = silu(cond_float).astype(bf16)
    mod_local = product("sd,djc->jsc", cond_act, mod_weight) + mod_bias[:, None]
    modulation = tensor_join(mod_local, n_tensor)
    segs = modulation.shape[1]
    tables = jnp.concatenate(in_three(modulation) + [jnp.zeros_like(modulation)], axis=1).astype(bf16)
    slots = condition_segment[0][jnp.arange(4 * segs) % segs]
    real = jnp.arange(4 * segs) < 3 * segs
    picks = ((segment_ids[0][:, None] == slots[None]) & real[None]).astype(bf16)
    marks = jnp.concatenate([condition_segment[0], jnp.full((segs,), -1, jnp.int32)])[:, None]
    full, column = (length, model_width), shape((length, 1), f32)
    mine = (length, local_width)
    row = shape((1, model_width), f32)

    qkv_weight = qkv_weight.transpose((1, 2, 0))
    attn_in, mean_one, inverse_one, normed_mine, in_t = run(
        entry_kernel,
        [order, side],
        [(picks, "r"), (tables, "v"), (tokens, "r")],
        [(shape(full), "r"), (column, "r"), (column, "r"), (shape(mine, f32), "r")],
    )
    biases = jnp.stack([qv_bias[0], jnp.zeros_like(qv_bias[0]), qv_bias[1]])
    qkv = product("jcd,ld->jcl", qkv_weight, attn_in) + biases[:, :, None]
    qkv = qkv.astype(bf16).reshape((3, heads, HEAD_DIM, length))
    attended, stat = attention_forward(segment_ids, qkv)
    attended = attended.reshape((local_width, length))
    proj_part = product("cl,cd->ld", attended, proj_weight).astype(bf16)
    proj_part, proj_other = summands(proj_part, n_tensor)
    out_grad, proj_tied = tie(out_grad, proj_part)
    mlp_grad, down_bias_grad, grad_t = run(
        gate_kernel,
        [order],
        [(picks, "r"), (tables, "v"), (out_grad, "r")],
        [(shape(full), "r"), (row, "w")],
    )
    proj_other, mlp_grad = tie(proj_other, mlp_grad)
    middle_args = [
        (tables, "v"), (tokens, "r"), (proj_tied, "r"), (proj_other, "r"), (proj_bias[None], "v")
    ]
    mlp_in, mean_two, inverse_two, mlp_t = run(
        middle_kernel,
        [order],
        [(picks, "r")] + middle_args,
        [(shape(full), "r"), (column, "r"), (column, "r")],
    )
    hidden = product("ld,df->lf", mlp_in, up_weight) + up_bias
    active, slope = gelu_and_slope(hidden)
    active, slope = tie(active.astype(bf16), slope.astype(bf16))

    sends, _ = hidden_grads(True, grad_t, active)
    down_sum = Sum(sends, n_batch, in_kernel)
    (mlp_grad_then, active_then) = down_sum.send(mlp_grad, active)
    active_grad = product("ld,fd->lf", mlp_grad_then, down_weight)
    hidden_grad = (active_grad * slope.astype(f32)).astype(bf16)
    mlp_part = product("lf,df->ld", hidden_grad, up_weight).astype(bf16)
    mlp_part, mlp_other = summands(mlp_part, n_tensor)
    (hidden_then, mlp_tied) = tie(hidden_grad, mlp_part)
    sends, up_bias_grad = hidden_grads(True, mlp_t, hidden_then)
    up_sum = Sum(sends, n_batch, in_kernel)
    down_sum.keeps, _ = hidden_grads(False, grad_t, active_then)
    first, second, *down_sum.keeps = down_sum.take(*up_sum.sends, *down_sum.keeps)
    up_sum.sends = [first, second]
    (mlp_other, hidden_then) = down_sum.send(mlp_other, hidden_then)
    (mlp_other, hidden_then) = up_sum.send(mlp_other, hidden_then)
    attn_grad, proj_bias_grad, grad_mine, early_totals, attn_t = run(
        middle_grad_kernel,
        [order, side],
        [(picks, "r"), (marks, "v"), (segment_ids, "c")]
        + middle_args
        + [(mean_two, "r"), (inverse_two, "r"), (mlp_tied, "r"), (mlp_other, "r"), (out_grad, "r")],
        [
            (shape(full), "r"),
            (row, "w"),
            (shape(mine, f32), "r"),
            (shape((6 * segs, model_width), f32), "w"),
        ],
    )
    attended_grad = product("cd,ld->cl", proj_weight, attn_grad).astype(bf16)

    triple = attention_backward(
        segment_ids, qkv, stat, attended_grad.reshape((heads, HEAD_DIM, length))
    ).reshape((3 * local_width, length))
    up_sum.keeps, _ = hidden_grads(False, mlp_t, hidden_then)
    sends, (qk_bias_grad, value_bias_grad) = attention_grads(True, in_t, attn_t, triple, attended)
    qkv_sum = Sum(sends, n_batch, in_kernel)
    first, second, *up_sum.keeps = up_sum.take(*qkv_sum.sends, *up_sum.keeps)
    qkv_sum.sends = [first, second]
    (triple,) = down_sum.take(triple)
    (triple,) = up_sum.send(triple)
    (triple,) = qkv_sum.send(triple)
    (triple,) = down_sum.send(triple)
    attn_part = product(
        "jcl,jcd->ld", triple.reshape((3, local_width, length)), qkv_weight
    ).astype(bf16)
    kept, sent, sums = sweep(
        halves_kernel,
        length,
        [side],
        [
            (picks, "r"),
            (tables, "v"),
            (attn_part, "r"),
            (tokens, "r"),
            (mean_one, "r"),
            (inverse_one, "r"),
        ],
        [
            (shape(mine), "r"),
            (shape((length, padded(local_width + 4))), "r"),
            (shape((length, 2), f32), "r"),
        ],
        cost=0,
    )
    (kept, sent) = up_sum.take(kept, sent)
    (kept, sent) = down_sum.take(kept, sent)
    (kept, sent, triple, active_then) = up_sum.send(kept, sent, triple, active)
    (kept, sent, triple, active_then) = down_sum.send(kept, sent, triple, active_then)
    (mod_local, kept) = tie(mod_local, kept)
    tables_mine = jnp.concatenate(in_three(mod_local) + [jnp.zeros_like(mod_local)], axis=1).astype(bf16)
    if n_tensor == 2:
        other = exchange(sent)
    else:
        kept = lax.psum_scatter(attn_part, "tensor", scatter_dimension=1, tiled=True)
        other = jnp.zeros_like(sent)
        sums = lax.psum(sums, "tensor")
    qkv_sum.keeps, _ = attention_grads(False, in_t, attn_t, triple, attended)
    token_t, late_totals = sweep(
        functools.partial(token_grad_kernel, model_width),
        length,
        [],
        [
            (picks, "r"),
            (marks, "v"), (segment_ids, "c"),
            (tables_mine, "v"),
            (kept, "r"),
            (other, "r"),
            (sums, "r"),
            (normed_mine, "r"),
            (inverse_one, "r"),
            (grad_mine, "r"),
        ],
        [(shape((local_width, length), f32), "c"), (shape((4 * segs, local_width), f32), "w")],
        cost=0,
    )
    (active_then, kept) = tie(active_then, kept)
    down_part = product("lf,fd->ld", active_then, down_weight).astype(bf16)
    (late_totals, down_part, *qkv_sum.keeps) = qkv_sum.take(
        late_totals, down_part, *qkv_sum.keeps
    )
    (late_totals,) = up_sum.take(late_totals)
    (down_part, late_totals) = qkv_sum.send(down_part, late_totals)
    (down_part, late_totals) = up_sum.send(down_part, late_totals)
    down_part, down_other = summands(down_part, n_tensor)
    layer_out, gate_total = sweep(
        layer_kernel,
        length,
        [],
        [(picks, "r"), (marks, "v"), (segment_ids, "c")]
        + middle_args
        + [(down_part, "r"), (down_other, "r"), (down_bias[None], "v"), (out_grad, "r")],
        [(shape(full), "r"), (shape((2 * segs, model_width), f32), "w")],
        cost=0,
    )
    (gate_total,) = qkv_sum.take(gate_total)
    (gate_total,) = up_sum.take(gate_total)
    (gate_total,) = down_sum.take(gate_total)
    (gate_total,) = qkv_sum.send(gate_total)
    bias_rows = 2 * n_tensor + hidden_width // local_width + 2
    rows = (6 + n_tensor) * segs + 2 * bias_rows
    (packed,) = pl.pallas_call(
        pack_kernel,
        in_specs=[SMEM] + [VMEM] * 9,
        out_specs=[VMEM],
        out_shape=[shape((rows, local_width))],
        scratch_shapes=[pltpu.VMEM((-(-rows // 16) * 16, local_width), f32)],
        compiler_params=room(16),
        cost_estimate=FREE,
    )(
        side,
        early_totals,
        late_totals,
        after(gate_total, *qkv_sum.sent),
        cond_act,
        proj_bias_grad,
        down_bias_grad,
        up_bias_grad,
        qk_bias_grad,
        value_bias_grad,
    )
    gathered = Gather(packed, n_batch, bits[:1:-1] + bits[1::-1])
    gathered.step()
    gathered.step()
    tgrad = packed[: 6 * segs].reshape((6, segs, local_width))
    cond_part = product("jsc,djc->sd", tgrad, mod_weight)
    cond_part, cond_other = summands(cond_part.astype(bf16), n_tensor)
    cond_act_grad = cond_part.astype(f32) + cond_other.astype(f32)
    condition_grad = jax.vjp(silu, cond_float)[1](cond_act_grad)[0]
    down_sum.settle(gate_total)
    up_sum.settle(gate_total)
    cut = hidden_width // 2
    down = down_sum.result([(0, 0, cut), (1, 0, cut)])
    up = up_sum.result([(0, 0, cut), (1, 0, cut)])
    (*up, down_first, down_second) = qkv_sum.take(*up, *down)
    qkv_sum.send()
    while gathered.order:
        gathered.step(*qkv_sum.sent)

    held = gathered.held
    part = index * block // local_width
    cond_block = lax.dynamic_slice(
        held, (0, (6 + part) * segs, index * block % local_width), (n_batch, segs, block)
    )
    places, first = np.arange(rows), (6 + n_tensor) * segs
    marked = [(places // segs == j) for j in range(6)]
    marked += [(places >= first) & ((places - first) % bias_rows == b) for b in range(bias_rows)]
    marked = jnp.asarray(np.stack(marked, axis=1), bf16)
    blocks = jnp.concatenate([cond_block] * (rows // segs + 1), axis=1)[:, :rows]
    blocks = (blocks[:, :, None, :] * marked[None, :, :6, None]).reshape((n_batch * rows, -1))
    left = jnp.concatenate([blocks, jnp.tile(marked, (n_batch, 1))], axis=1)
    out = product("rk,rc->kc", left, held.reshape((n_batch * rows, local_width)))
    mod_sum = out[: 6 * block].reshape((6, block, local_width))
    modbias_sum = out[6 * block : 6 * block + 6]
    bias_all = out[6 * block + 6 :]
    (mod_sum, modbias_sum, bias_all) = qkv_sum.take(mod_sum, modbias_sum, bias_all)
    qv_sum = bias_all[-2:]
    bias_all = bias_all[:-2].reshape(-1)
    projbias_sum = bias_all[:model_width]
    downbias_sum = bias_all[model_width : 2 * model_width]
    upbias_sum = bias_all[2 * model_width :]
    mod_sum = mod_sum.transpose((1, 0, 2))
    begin = padded(local_width)
    *last, proj_last = qkv_sum.result(
        [
            (0, 0, local_width),
            (0, local_width, 2 * local_width),
            (1, 0, local_width),
            (1, begin, begin + local_width),
        ]
    )
    last = jnp.stack(last, axis=1)
    up = jnp.concatenate(up, axis=1)
    down = jnp.concatenate([down_first, down_second], axis=1).T
    return (
        layer_out[None],
        token_t.T[None],
        condition_grad[None],
        last,
        qv_sum,
        proj_last.T,
        projbias_sum,
        up,
        upbias_sum,
        down,
        downbias_sum,
        mod_sum,
        modbias_sum,
    )


def solution(mesh):
    return jax.shard_map(
        functools.partial(on_device, mesh.shape["batch"]),
        mesh=mesh,
        in_specs=(
            P("batch", None, None),
            P("batch", None),
            P("batch", None, None),
            P("batch", None),
            P(None, None, "tensor"),
            P(None, "tensor"),
            P("tensor", None),
            P(),
            P(None, "tensor"),
            P("tensor"),
            P("tensor", None),
            P(),
            P(None, None, "tensor"),
            P(None, "tensor"),
            P("batch", None, None),
        ),
        out_specs=(
            P("batch", None, None),
            P("batch", None, "tensor"),
            P("batch", None, None),
            P("batch", None, "tensor"),
            P(None, "tensor"),
            P("tensor", "batch"),
            P(),
            P("batch", "tensor"),
            P("tensor"),
            P("tensor", "batch"),
            P(),
            P("batch", None, "tensor"),
            P(None, "tensor"),
        ),
        check_vma=False,
    )
```

```python
import functools

import jax
import jax.numpy as jnp
from jax import lax
from jax.experimental import pallas as pl
from jax.experimental.pallas import tpu as pltpu
from jax.sharding import PartitionSpec as P

EPS = 1e-06
HEAD_DIM = 72
SEGS = 8
MOST = 256
LOG2E = 1.4426950408889634
NEG = -1e30


def band(begin, width, length):
    low = max(0, (begin - MOST + 1) // 128 * 128)
    high = min(length, -(-(begin + width + MOST - 1) // 128) * 128)
    return low, high


def natural(array):
    return array.astype(jnp.float32).T.astype(jnp.bfloat16)


def marks(seg_row):
    slots = lax.broadcasted_iota(jnp.int32, (SEGS, seg_row.shape[-1]), 0)
    return (slots == seg_row[...]).astype(jnp.float32)


def fill(head, qkv, one_hot, q_aug, k_nat):
    query = jnp.concatenate([qkv[0, head].astype(jnp.float32), (1.0 - one_hot) * NEG], axis=0)
    q_aug[...] = query.astype(jnp.bfloat16)
    k_nat[...] = natural(jnp.concatenate([qkv[1, head].astype(jnp.float32), one_hot], axis=0))


def attention_forward_kernel(width, seg_row, qkv, out, stat, q_aug, k_nat):
    heads, length = qkv.shape[1], qkv.shape[3]
    factor = HEAD_DIM**-0.5 * LOG2E
    one_hot = marks(seg_row)

    def one(head, carry):
        fill(head, qkv, one_hot, q_aug, k_nat)
        for begin in range(0, length, width):
            low, high = band(begin, width, length)
            span = slice(begin, begin + width)
            scores = jnp.dot(
                k_nat[low:high, :], q_aug[:, span], preferred_element_type=jnp.float32
            )
            peak = jnp.max(scores, axis=0, keepdims=True) * factor
            shifted = jnp.exp2(scores * factor - peak)
            total = jnp.sum(shifted, axis=0, keepdims=True)
            got = jnp.dot(
                qkv[2, head, :, low:high],
                shifted.astype(jnp.bfloat16),
                preferred_element_type=jnp.float32,
            )
            out[head, :, span] = (got * (1.0 / total)).astype(jnp.bfloat16)
            stat[head, :, span] = peak + jnp.log2(total)
        return carry

    lax.fori_loop(0, heads, one, 0, unroll=2)


def attention_backward_kernel(
    width, seg_row, qkv, stat, grad, out, q_aug, k_nat, v_nat, q_nat, g_nat, p_all, s_all
):
    heads, length = qkv.shape[1], qkv.shape[3]
    scale = HEAD_DIM**-0.5
    factor = scale * LOG2E
    one_hot = marks(seg_row)

    def one(head, carry):
        fill(head, qkv, one_hot, q_aug, k_nat)
        v_nat[...] = natural(qkv[2, head])
        q_nat[...] = natural(qkv[0, head])
        g_nat[...] = natural(grad[head])
        for begin in range(0, length, width):
            low, high = band(begin, width, length)
            span = slice(begin, begin + width)
            scores = jnp.dot(
                k_nat[low:high, :], q_aug[:, span], preferred_element_type=jnp.float32
            )
            probs = jnp.exp2(scores * factor - stat[head, :, span])
            prob_grad = jnp.dot(
                v_nat[low:high, :], grad[head, :, span], preferred_element_type=jnp.float32
            )
            row = jnp.sum(prob_grad * probs, axis=0, keepdims=True)
            score_grad = (probs * (prob_grad - row)).astype(jnp.bfloat16)
            p_all[low:high, span] = probs.astype(jnp.bfloat16)
            s_all[low:high, span] = score_grad
            got = jnp.dot(
                qkv[1, head, :, low:high], score_grad, preferred_element_type=jnp.float32
            )
            out[0, head, :, span] = (got * scale).astype(jnp.bfloat16)
        for begin in range(0, length, width):
            span = slice(begin, begin + width)
            reach = [q for q in range(0, length, width) if band(q, width, length)[0] < begin + width and band(q, width, length)[1] > begin]
            low, high = reach[0], reach[-1] + width
            key_grad = jnp.dot(
                s_all[span, low:high], q_nat[low:high, :], preferred_element_type=jnp.float32
            )
            value_grad = jnp.dot(
                p_all[span, low:high], g_nat[low:high, :], preferred_element_type=jnp.float32
            )
            out[1, head, :, span] = (key_grad * scale).T.astype(jnp.bfloat16)
            out[2, head, :, span] = value_grad.T.astype(jnp.bfloat16)
        return carry

    if width < MOST:
        p_all[...] = jnp.zeros_like(p_all)
        s_all[...] = jnp.zeros_like(s_all)
    lax.fori_loop(0, heads, one, 0, unroll=2)


VMEM = pl.BlockSpec(memory_space=pltpu.VMEM)


CHUNK = 128


def dot(left, right):
    return jnp.dot(left, right, preferred_element_type=jnp.float32)


def dot_nt(left, right):
    return lax.dot_general(
        left, right, (((1,), (1,)), ((), ())), preferred_element_type=jnp.float32
    )


def wide(value):
    return value.astype(jnp.float32)


def turn(order, value, out, work):
    count = order.shape[0]
    rows = value.shape[1] // count
    work[...] = wide(value).T
    for at in range(0, count, 2):
        pair = [
            work[pl.ds(pl.multiple_of(order[at + i] * rows, 8), rows), :] for i in range(2)
        ]
        pair = jnp.concatenate(pair, axis=0).astype(jnp.bfloat16)
        out[at * rows : (at + 2) * rows, :] = pair


def own_part(side, value, width):
    part = value[:, :width]
    for at in range(1, value.shape[1] // width):
        part = jnp.where(side == at, value[:, at * width : (at + 1) * width], part)
    return part


def accumulate(total, value):
    @pl.when(pl.program_id(0) == 0)
    def _():
        total[...] = value

    @pl.when(pl.program_id(0) > 0)
    def _():
        total[...] += value


def segment_sums(slots, seg, *values):
    marks = (slots[...] == seg[...]).astype(jnp.bfloat16)
    sums = []
    for value in values:
        high = value.astype(jnp.bfloat16)
        low = (value - wide(high)).astype(jnp.bfloat16)
        sums.append(dot(marks, high) + dot(marks, low))
    return jnp.concatenate(sums, axis=0)


def norm_parts(value):
    width = value.shape[1]
    mean = jnp.sum(value, axis=1, keepdims=True) / width
    center = value - mean
    spread = jnp.sum(center * center, axis=1, keepdims=True) / width
    return mean, center, lax.rsqrt(spread + EPS)


def entry_kernel(order, side, picks, tables, tokens, out, mean, inverse, normed_mine, *turned):
    pick = picks[...]
    middle, center, scale = norm_parts(wide(tokens[...]))
    mean[...] = middle
    inverse[...] = scale
    value = center * scale
    normed_mine[...] = own_part(side[0], value, normed_mine.shape[1])
    value = (value * (1.0 + dot(pick, tables[1])) + dot(pick, tables[0])).astype(jnp.bfloat16)
    out[...] = value
    if turned:
        turn(order, value, *turned)


def gate_kernel(order, picks, tables, grad, out, bias, *turned):
    value = (wide(grad[...]) * dot(picks[...], tables[5])).astype(jnp.bfloat16)
    out[...] = value
    accumulate(bias, jnp.sum(wide(value), axis=0, keepdims=True))
    if turned:
        turn(order, value, *turned)


def middle_of(pick, tables, tokens, part, other, bias):
    attn_out = wide(part[...]) + wide(other[...]) + bias[...]
    return attn_out, wide(tokens[...]) + dot(pick, tables[2]) * attn_out


def middle_kernel(order, picks, tables, tokens, part, other, bias, out, mean, inverse, *turned):
    pick = picks[...]
    value = middle_of(pick, tables, tokens, part, other, bias)[1]
    middle, center, scale = norm_parts(value)
    mean[...] = middle
    inverse[...] = scale
    value = center * scale * (1.0 + dot(pick, tables[4])) + dot(pick, tables[3])
    value = value.astype(jnp.bfloat16)
    out[...] = value
    if turned:
        turn(order, value, *turned)


def middle_grad_kernel(
    order, side, picks, marks, seg, tables, tokens, part, other, bias, mean, inverse, mlp, mlp_other, grad,
    out, bias_sum, grad_mine, totals, *turned
):
    pick = picks[...]
    width = grad.shape[1]
    attn_out, value = middle_of(pick, tables, tokens, part, other, bias)
    norm = (value - mean[...]) * inverse[...]
    in_grad = wide(mlp[...]) + wide(mlp_other[...])
    value = in_grad * (1.0 + dot(pick, tables[4]))
    plain = jnp.sum(value, axis=1, keepdims=True) / width
    cross = jnp.sum(value * norm, axis=1, keepdims=True) / width
    value = wide(grad[...]) + inverse[...] * (value - plain - norm * cross)
    grad_mine[...] = own_part(side[0], value, grad_mine.shape[1])
    accumulate(totals, segment_sums(marks, seg, value * attn_out, in_grad, in_grad * norm))
    value = (value * dot(pick, tables[2])).astype(jnp.bfloat16)
    out[...] = value
    accumulate(bias_sum, jnp.sum(wide(value), axis=0, keepdims=True))
    if turned:
        turn(order, value, *turned)


def halves_kernel(side, picks, tables, part, tokens, mean, inverse, kept, sent, sums):
    value = part[...]
    width = kept.shape[1]
    kept[...] = own_part(side[0], value, width)
    sent[:, :width] = own_part(1 - side[0], value, width)
    value = wide(value) * (1.0 + dot(picks[...], tables[1]))
    norm = (wide(tokens[...]) - mean[...]) * inverse[...]
    for at, term in enumerate((value, value * norm)):
        total = jnp.sum(term, axis=1, keepdims=True)
        high = total.astype(jnp.bfloat16)
        sums[:, at : at + 1] = total
        sent[:, width + 2 * at : width + 2 * at + 1] = high
        sent[:, width + 2 * at + 1 : width + 2 * at + 2] = (total - wide(high)).astype(jnp.bfloat16)


def token_grad_kernel(
    width, picks, marks, seg, tables, kept, other, sums, normed, inverse, grad, out_t, totals
):
    mine = kept.shape[1]
    value = wide(kept[...]) + wide(other[:, :mine])
    norm = normed[...]
    accumulate(totals, segment_sums(marks, seg, value, value * norm))
    value = value * (1.0 + dot(picks[...], tables[1]))
    for at, factor in enumerate((1.0, norm)):
        rest = wide(other[:, mine + 2 * at : mine + 2 * at + 1])
        rest = rest + wide(other[:, mine + 2 * at + 1 : mine + 2 * at + 2])
        value = value - factor * ((sums[:, at : at + 1] + rest) / width)
    out_t[...] = (grad[...] + inverse[...] * value).T


def layer_kernel(
    picks, marks, seg, tables, tokens, part, other, bias, down, down_other, down_bias, grad, out, totals
):
    pick = picks[...]
    mlp_out = wide(down[...]) + wide(down_other[...]) + down_bias[...]
    middle = middle_of(pick, tables, tokens, part, other, bias)[1]
    out[...] = (middle + dot(pick, tables[5]) * mlp_out).astype(jnp.bfloat16)
    accumulate(totals, segment_sums(marks, seg, wide(grad[...]) * mlp_out))


def row_parts(sent, first):
    if first:
        return (2, 3) if sent else (0, 1)
    return (1, 3) if sent else (0, 2)


def put_rows(left, right, out, parts, product):
    quarter = left.shape[0] // 4
    columns = slice(0, right.shape[0] if product is dot_nt else right.shape[1])
    if parts[1] == parts[0] + 1:
        rows = slice(parts[0] * quarter, (parts[1] + 1) * quarter)
        out[:, columns] = product(left[rows, :], right[...]).astype(jnp.bfloat16)
        return
    for at, part in enumerate(parts):
        rows = slice(part * quarter, (part + 1) * quarter)
        value = product(left[rows, :], right[...]).astype(jnp.bfloat16)
        out[at * quarter : (at + 1) * quarter, columns] = value


def column_sums(array, product):
    return product(jnp.ones((8, array.shape[1] if product is dot_nt else array.shape[0]), jnp.bfloat16), array[...])


def mlp_grads_kernel(sent, left, right, first, second, sums):
    sums[...] = column_sums(right, dot)
    step, half = pl.program_id(0), pl.num_programs(0) // 2

    @pl.when(step < half)
    def _():
        put_rows(left, right, first, row_parts(sent, True), dot)

    @pl.when(step >= half)
    def _():
        put_rows(left, right, second, row_parts(sent, False), dot)


def qkv_grads_kernel(sent, left, proj_left, both, value, attended, first, second, sums, value_sums):
    step = pl.program_id(0)

    @pl.when(step < 3)
    def _():
        put_rows(left, both, first, row_parts(sent, True), dot_nt)
        sums[...] = column_sums(both, dot_nt)

    @pl.when(step == 3)
    def _():
        second[...] = jnp.zeros_like(second)
        put_rows(left, value, second, row_parts(sent, False), dot_nt)
        value_sums[...] = column_sums(value, dot_nt)

    @pl.when(step == 4)
    def _():
        second[...] = jnp.zeros_like(second)
        put_rows(proj_left, attended, second, row_parts(sent, False), dot_nt)


SMEM = pl.BlockSpec(memory_space=pltpu.SMEM)
GRADS = 10
FREE = pl.CostEstimate(flops=1, bytes_accessed=1, transcendentals=0)


def micros(time):
    if time == 0:
        return FREE
    return pl.CostEstimate(flops=time * 10**9, bytes_accessed=time * 10**6, transcendentals=0)


def shape(dims, dtype=jnp.bfloat16):
    return jax.ShapeDtypeStruct(dims, dtype)


def room(mib):
    return pltpu.CompilerParams(vmem_limit_bytes=mib << 20)


def spec(dims, kind):
    if kind == "v":
        return VMEM
    if kind == "r":
        return pl.BlockSpec((CHUNK, dims[1]), lambda i: (i, 0))
    if kind == "c":
        return pl.BlockSpec((dims[0], CHUNK), lambda i: (0, i))
    return pl.BlockSpec(tuple(dims), lambda i: (0,) * len(dims))


def sweep(kernel, length, scalars, arrays, outs, work=(), mib=16, cost=200):
    return pl.pallas_call(
        kernel,
        grid=(length // CHUNK,),
        in_specs=[SMEM] * len(scalars) + [spec(a.shape, kind) for a, kind in arrays],
        out_specs=[spec(o.shape, kind) for o, kind in outs],
        out_shape=[o for o, _ in outs],
        scratch_shapes=[pltpu.VMEM(dims, jnp.float32) for dims in work],
        compiler_params=room(mib),
        cost_estimate=micros(cost),
    )(*scalars, *[a for a, _ in arrays])


def mlp_grads(sent, left, right):
    width, length = left.shape
    hidden = right.shape[1]
    half, block = hidden // 2, hidden // 6
    return pl.pallas_call(
        functools.partial(mlp_grads_kernel, sent),
        grid=(6,),
        in_specs=[
            spec(left.shape, "w"),
            pl.BlockSpec((length, block), lambda j: (0, j)),
        ],
        out_specs=[
            pl.BlockSpec((width // 2, block), lambda j: (0, jnp.minimum(j, 2))),
            pl.BlockSpec((width // 2, block), lambda j: (0, jnp.maximum(j - 3, 0))),
            pl.BlockSpec((8, block), lambda j: (0, j)),
        ],
        out_shape=[shape((width // 2, half))] * 2 + [shape((8, hidden), jnp.float32)],
        compiler_params=room(16),
        cost_estimate=micros(GRADS),
    )(left, right)


def sum_kernel(counts, splits, *refs):
    halves, at = [], 0
    for count in counts[:2]:
        total = wide(refs[at][...])
        for ref in refs[at + 1 : at + count]:
            total += wide(ref[...])
        halves.append(total)
        at += count
    outs = refs[at + counts[2] :]
    for half in range(2):
        begin = 0 if half == 0 else halves[0].shape[1]
        columns = slice(begin, begin + halves[half].shape[1])
        for ref in refs[at : at + counts[2]]:
            halves[half] += wide(ref[:, columns])
    if splits is None:
        for out, total in zip(outs, halves):
            out[...] = total.astype(out.dtype)
    elif splits == ():
        for total, begin in zip(halves, (0, halves[0].shape[1])):
            outs[0][:, begin : begin + total.shape[1]] = total.astype(outs[0].dtype)
    else:
        for out, (half, begin, end) in zip(outs, splits):
            out[...] = halves[half][:, begin:end]


def sum_rows(halves, joined, at, count, outs, splits=None):
    arrays = halves[0] + halves[1] + joined

    def rows(width):
        return pl.BlockSpec((count, width), lambda i: (at, 0))

    return pl.pallas_call(
        functools.partial(sum_kernel, (len(halves[0]), len(halves[1]), len(joined)), splits),
        grid=(1,),
        in_specs=[rows(a.shape[1]) for a in arrays],
        out_specs=[pl.BlockSpec(o.shape, lambda i: (0, 0)) for o in outs],
        out_shape=outs,
        compiler_params=room(16),
        cost_estimate=FREE,
    )(*arrays)


def pack_kernel(
    side, middle, late, gate, cond, proj_bias, down_bias, up_bias, qk_bias, value_bias, out, work
):
    width = out.shape[1]
    segs = cond.shape[0]
    own = [late[:segs, :], late[2 * segs : 3 * segs, :]]
    for source, at in ((middle, 0), (middle, 1), (middle, 2), (gate, 0)):
        own.append(own_part(side[0], source[2 * at * segs : (2 * at + 1) * segs, :], width))
    own += [wide(cond[:, at : at + width]) for at in range(0, cond.shape[1], width)]
    for at, value in enumerate(own):
        work[at * segs : (at + 1) * segs, :] = value
    rows = []
    for source in (proj_bias, down_bias, up_bias):
        rows += [source[0:1, at : at + width] for at in range(0, source.shape[1], width)]
    rows += [qk_bias[0:1, :width], value_bias[0:1, :]]
    first = len(own) * segs
    for at, value in enumerate(rows):
        high = wide(value.astype(jnp.bfloat16))
        work[first + at : first + at + 1, :] = high
        work[first + len(rows) + at : first + len(rows) + at + 1, :] = value - high
    out[...] = work[: out.shape[0], :].astype(jnp.bfloat16)


def finish_kernel(segs, first, held, cond, mod, modbias, bias, work):
    value = wide(held[...])
    devices, rows, width = value.shape
    left = wide(cond[...]).reshape((devices * segs, cond.shape[2])).T.astype(jnp.bfloat16)
    for at in range(mod.shape[0]):
        part = value[:, at * segs : (at + 1) * segs, :].reshape((devices * segs, width))
        mod[at] = dot(left, part.astype(jnp.bfloat16))
        modbias[at : at + 1, :] = jnp.sum(part, axis=0, keepdims=True)
    work[:rows, :] = jnp.sum(value, axis=0)
    count = bias.shape[0]
    bias[...] = work[first : first + count, :] + work[first + count : first + 2 * count, :]


def padded(width):
    return -(-width // 128) * 128


def qkv_grads(sent, left, proj_left, triple, attended):
    width, length = left.shape
    local = attended.shape[0]
    block, wide_block = 2 * local // 3, padded(local)
    return pl.pallas_call(
        functools.partial(qkv_grads_kernel, sent),
        grid=(5,),
        in_specs=[
            spec(left.shape, "w"),
            spec(left.shape, "w"),
            pl.BlockSpec((block, length), lambda j: (jnp.minimum(j, 2), 0)),
            pl.BlockSpec((local, length), lambda j: (2, 0)),
            spec(attended.shape, "w"),
        ],
        out_specs=[
            pl.BlockSpec((width // 2, block), lambda j: (0, jnp.minimum(j, 2))),
            pl.BlockSpec((width // 2, wide_block), lambda j: (0, jnp.maximum(j - 3, 0))),
            pl.BlockSpec((8, block), lambda j: (0, jnp.minimum(j, 2))),
            pl.BlockSpec((8, local), lambda j: (0, 0)),
        ],
        out_shape=[
            shape((width // 2, 2 * local)),
            shape((width // 2, 2 * wide_block)),
            shape((8, 2 * local), jnp.float32),
            shape((8, local), jnp.float32),
        ],
        compiler_params=room(24),
        cost_estimate=FREE,
    )(left, proj_left, triple, triple, attended)


def attention_forward(segments, qkv, width=256):
    heads, length = qkv.shape[1], qkv.shape[3]
    return pl.pallas_call(
        functools.partial(attention_forward_kernel, width),
        in_specs=[VMEM] * 2,
        out_specs=[VMEM] * 2,
        out_shape=[shape((heads, HEAD_DIM, length)), shape((heads, 1, length), jnp.float32)],
        scratch_shapes=[
            pltpu.VMEM((HEAD_DIM + SEGS, length), jnp.bfloat16),
            pltpu.VMEM((length, HEAD_DIM + SEGS), jnp.bfloat16),
        ],
        compiler_params=room(12),
        cost_estimate=micros(15),
    )(segments, qkv)


def attention_backward(segments, qkv, stat, grad, width=256):
    heads, length = qkv.shape[1], qkv.shape[3]
    return pl.pallas_call(
        functools.partial(attention_backward_kernel, width),
        in_specs=[VMEM] * 4,
        out_specs=VMEM,
        out_shape=shape(qkv.shape),
        scratch_shapes=[
            pltpu.VMEM((HEAD_DIM + SEGS, length), jnp.bfloat16),
            pltpu.VMEM((length, HEAD_DIM + SEGS), jnp.bfloat16),
        ]
        + [pltpu.VMEM((length, HEAD_DIM), jnp.bfloat16)] * 3
        + [pltpu.VMEM((length, length), jnp.bfloat16)] * 2,
        compiler_params=room(16),
        cost_estimate=micros(15),
    )(segments, qkv, stat, grad)


def silu(array):
    return array / (1.0 + jnp.exp(-array))


def product(spec, left, right):
    return jnp.einsum(spec, left, right, preferred_element_type=jnp.float32)


def exchange(array):
    return lax.ppermute(array, "tensor", [(0, 1), (1, 0)])


def summands(part, size):
    if size == 2:
        return part, exchange(part)
    return lax.psum(part, "tensor"), jnp.zeros_like(part)


def tensor_join(array, size):
    if size == 2:
        other = exchange(array)
        first = lax.axis_index("tensor") == 0
        return jnp.concatenate(
            [jnp.where(first, array, other), jnp.where(first, other, array)], axis=-1
        )
    return lax.all_gather(array, "tensor", axis=array.ndim - 1, tiled=True)


def partners(size, bit):
    return [(i, i ^ (1 << bit)) for i in range(size)]


def tie(*values):
    return lax.optimization_barrier(values)


def after(value, *others):
    return tie(value, *others)[0]


class Gather:
    def __init__(self, array, size, order):
        self.held, self.size, self.order = array[None], size, list(order)

    def step(self, *others):
        if self.order:
            bit = self.order.pop(0)
            self.held = after(self.held, *others)
            other = lax.ppermute(self.held, "batch", partners(self.size, bit))
            self.held = jnp.concatenate([self.held, other], axis=0)


class Sum:
    def __init__(self, sends, size, kernels):
        self.kernels = kernels
        self.sends, self.size, self.bits = sends, size, size.bit_length() - 1
        self.keeps, self.got = None, []

    def pieces(self, at, count, dtype, splits=None, outs=None):
        halves = [[self.keeps[h]] + [stage[h] for stage in self.got[:2]] for h in range(2)]
        joined = [new for (new,) in self.got[2:]]
        widths = [half[0].shape[1] for half in halves]
        if self.kernels:
            if outs is None:
                outs = [shape((count, width), dtype) for width in widths]
                if len(self.got) > 1:
                    outs, splits = [shape((count, sum(widths)), dtype)], ()
            return list(sum_rows(halves, joined, at, count, outs, splits))
        window = slice(at * count, (at + 1) * count)
        totals = [sum(a[window].astype(jnp.float32) for a in half) for half in halves]
        if len(self.got) < 2:
            return [total.astype(dtype) for total in totals]
        total = jnp.concatenate(totals, axis=1)
        total = sum((a[window].astype(jnp.float32) for a in joined), total)
        if outs is None:
            return [total.astype(dtype)]
        totals = [total[:, : widths[0]], total[:, widths[0] :]]
        return [totals[half][:, begin:end] for half, begin, end in splits]

    def send(self, *others):
        stage = len(self.got)
        sends, bits = self.sends, [stage]
        if stage > 0:
            left = self.keeps[0].shape[0] >> stage
            sends = self.pieces(1, left, jnp.bfloat16)
        if stage < 2:
            bits = [stage, 1 - stage]
        tied = tie(*sends, *others)
        self.sent = tied[: len(sends)]
        self.flying = [
            lax.ppermute(piece, "batch", partners(self.size, bit))
            for piece, bit in zip(tied, bits)
        ]
        return tied[len(sends) :]

    def take(self, *others):
        tied = tie(*self.flying, *others)
        self.got.append(tied[: len(self.flying)])
        return tied[len(self.flying) :]

    def settle(self, other):
        if len(self.got) == self.bits:
            self.keeps = list(tie(*self.keeps, other)[:2])

    def result(self, splits):
        while len(self.got) < self.bits:
            self.send()
            self.take()
        count = 2 * self.keeps[0].shape[0] // self.size
        outs = [shape((count, end - begin), jnp.float32) for _, begin, end in splits]
        return self.pieces(0, count, jnp.float32, splits, outs)


def gelu_and_slope(array):
    square = array * array
    bent = jnp.tanh(0.7978845608028654 * (array + 0.044715 * array * square))
    half = 0.5 * (1.0 + bent)
    inner = 0.7978845608028654 * (1.0 + 3.0 * 0.044715 * square)
    return array * half, half + 0.5 * array * (1.0 - bent * bent) * inner


def in_three(array):
    high = lax.reduce_precision(array, 8, 7)
    middle = lax.reduce_precision(array - high, 8, 7)
    return [high, middle, array - high - middle]


def on_device(
    n_batch,
    tokens,
    segment_ids,
    conditions,
    condition_segment,
    qkv_weight,
    qv_bias,
    proj_weight,
    proj_bias,
    up_weight,
    up_bias,
    down_weight,
    down_bias,
    mod_weight,
    mod_bias,
    out_grad,
):
    bf16, f32 = jnp.bfloat16, jnp.float32
    tokens, out_grad = tokens[0], out_grad[0]
    length, model_width = tokens.shape
    local_width = qkv_weight.shape[2]
    hidden_width = up_weight.shape[1]
    heads = local_width // HEAD_DIM
    n_tensor = model_width // local_width
    bits = list(range(n_batch.bit_length() - 1))
    block = model_width // n_batch
    in_kernel = block % 8 == 0
    index = lax.axis_index("batch")
    order = jnp.array(
        [sum((p >> bit & 1) << (bits[-1] - bit) for bit in bits) for p in range(n_batch)], jnp.int32
    )
    order = order ^ index
    side = lax.axis_index("tensor")[None]

    def run(kernel, scalars, arrays, outs):
        turned = shape((model_width, length))
        if in_kernel:
            chunk = (model_width, CHUNK)
            return sweep(kernel, length, scalars, arrays, outs + [(turned, "c")], [chunk])
        got = sweep(kernel, length, scalars, arrays, outs)
        return list(got) + [got[0].T.reshape((n_batch, block, length))[order].reshape(turned.shape)]

    def part_rows(left, sent, first):
        quarter = model_width // 4
        rows = [left[at * quarter : (at + 1) * quarter] for at in row_parts(sent, first)]
        return jnp.concatenate(rows)

    def hidden_grads(sent, left, right):
        if in_kernel:
            first, second, sums = mlp_grads(sent, left, right)
            return [first, second], sums
        sums = jnp.sum(right.astype(f32), axis=0)[None]
        cut = right.shape[1] // 2
        return [
            product("dl,lc->dc", part_rows(left, sent, True), right[:, :cut]).astype(bf16),
            product("dl,lc->dc", part_rows(left, sent, False), right[:, cut:]).astype(bf16),
        ], sums

    def attention_grads(sent, left, proj_left, triple, attended):
        if in_kernel:
            first, second, sums, value_sums = qkv_grads(sent, left, proj_left, triple, attended)
            return [first, second], (sums, value_sums)
        sums = jnp.sum(triple.astype(f32), axis=1)[None]
        sums = (sums[:, : 2 * local_width], sums[:, 2 * local_width :])
        cut, extra = 2 * local_width, ((0, 0), (0, padded(local_width) - local_width))
        halves = [
            (part_rows(left, sent, True), triple[:cut]),
            (part_rows(left, sent, False), triple[cut:]),
            (part_rows(proj_left, sent, False), attended),
        ]
        first, value, proj = [product("dl,cl->dc", *pair).astype(bf16) for pair in halves]
        return [first, jnp.concatenate([jnp.pad(value, extra), jnp.pad(proj, extra)], axis=1)], sums

    cond_float = conditions[0].astype(f32)
    cond_act = silu(cond_float).astype(bf16)
    mod_local = product("sd,djc->jsc", cond_act, mod_weight) + mod_bias[:, None]
    modulation = tensor_join(mod_local, n_tensor)
    segs = modulation.shape[1]
    tables = jnp.concatenate(in_three(modulation) + [jnp.zeros_like(modulation)], axis=1).astype(bf16)
    slots = condition_segment[0][jnp.arange(4 * segs) % segs]
    real = jnp.arange(4 * segs) < 3 * segs
    picks = ((segment_ids[0][:, None] == slots[None]) & real[None]).astype(bf16)
    marks = jnp.concatenate([condition_segment[0], jnp.full((segs,), -1, jnp.int32)])[:, None]
    full, column = (length, model_width), shape((length, 1), f32)
    mine = (length, local_width)
    row = shape((1, model_width), f32)

    qkv_weight = qkv_weight.transpose((1, 2, 0))
    attn_in, mean_one, inverse_one, normed_mine, in_t = run(
        entry_kernel,
        [order, side],
        [(picks, "r"), (tables, "v"), (tokens, "r")],
        [(shape(full), "r"), (column, "r"), (column, "r"), (shape(mine, f32), "r")],
    )
    biases = jnp.stack([qv_bias[0], jnp.zeros_like(qv_bias[0]), qv_bias[1]])
    qkv = product("jcd,ld->jcl", qkv_weight, attn_in) + biases[:, :, None]
    qkv = qkv.astype(bf16).reshape((3, heads, HEAD_DIM, length))
    attended, stat = attention_forward(segment_ids, qkv)
    attended = attended.reshape((local_width, length))
    proj_part = product("cl,cd->ld", attended, proj_weight).astype(bf16)
    proj_part, proj_other = summands(proj_part, n_tensor)
    out_grad, proj_tied = tie(out_grad, proj_part)
    mlp_grad, down_bias_grad, grad_t = run(
        gate_kernel,
        [order],
        [(picks, "r"), (tables, "v"), (out_grad, "r")],
        [(shape(full), "r"), (row, "w")],
    )
    proj_other, mlp_grad = tie(proj_other, mlp_grad)
    middle_args = [
        (tables, "v"), (tokens, "r"), (proj_tied, "r"), (proj_other, "r"), (proj_bias[None], "v")
    ]
    mlp_in, mean_two, inverse_two, mlp_t = run(
        middle_kernel,
        [order],
        [(picks, "r")] + middle_args,
        [(shape(full), "r"), (column, "r"), (column, "r")],
    )
    hidden = product("ld,df->lf", mlp_in, up_weight) + up_bias
    active, slope = gelu_and_slope(hidden)
    active, slope = tie(active.astype(bf16), slope.astype(bf16))

    sends, _ = hidden_grads(True, grad_t, active)
    down_sum = Sum(sends, n_batch, in_kernel)
    (mlp_grad_then, active_then) = down_sum.send(mlp_grad, active)
    active_grad = product("ld,fd->lf", mlp_grad_then, down_weight)
    hidden_grad = (active_grad * slope.astype(f32)).astype(bf16)
    mlp_part = product("lf,df->ld", hidden_grad, up_weight).astype(bf16)
    mlp_part, mlp_other = summands(mlp_part, n_tensor)
    (hidden_then, mlp_tied) = tie(hidden_grad, mlp_part)
    sends, up_bias_grad = hidden_grads(True, mlp_t, hidden_then)
    up_sum = Sum(sends, n_batch, in_kernel)
    down_sum.keeps, _ = hidden_grads(False, grad_t, active_then)
    first, second, *down_sum.keeps = down_sum.take(*up_sum.sends, *down_sum.keeps)
    up_sum.sends = [first, second]
    (mlp_other, hidden_then) = down_sum.send(mlp_other, hidden_then)
    (mlp_other, hidden_then) = up_sum.send(mlp_other, hidden_then)
    attn_grad, proj_bias_grad, grad_mine, early_totals, attn_t = run(
        middle_grad_kernel,
        [order, side],
        [(picks, "r"), (marks, "v"), (segment_ids, "c")]
        + middle_args
        + [(mean_two, "r"), (inverse_two, "r"), (mlp_tied, "r"), (mlp_other, "r"), (out_grad, "r")],
        [
            (shape(full), "r"),
            (row, "w"),
            (shape(mine, f32), "r"),
            (shape((6 * segs, model_width), f32), "w"),
        ],
    )
    attended_grad = product("cd,ld->cl", proj_weight, attn_grad).astype(bf16)

    triple = attention_backward(
        segment_ids, qkv, stat, attended_grad.reshape((heads, HEAD_DIM, length))
    ).reshape((3 * local_width, length))
    up_sum.keeps, _ = hidden_grads(False, mlp_t, hidden_then)
    sends, (qk_bias_grad, value_bias_grad) = attention_grads(True, in_t, attn_t, triple, attended)
    qkv_sum = Sum(sends, n_batch, in_kernel)
    first, second, *up_sum.keeps = up_sum.take(*qkv_sum.sends, *up_sum.keeps)
    qkv_sum.sends = [first, second]
    (triple,) = down_sum.take(triple)
    (triple,) = up_sum.send(triple)
    (triple,) = qkv_sum.send(triple)
    (triple,) = down_sum.send(triple)
    attn_part = product(
        "jcl,jcd->ld", triple.reshape((3, local_width, length)), qkv_weight
    ).astype(bf16)
    kept, sent, sums = sweep(
        halves_kernel,
        length,
        [side],
        [
            (picks, "r"),
            (tables, "v"),
            (attn_part, "r"),
            (tokens, "r"),
            (mean_one, "r"),
            (inverse_one, "r"),
        ],
        [
            (shape(mine), "r"),
            (shape((length, padded(local_width + 4))), "r"),
            (shape((length, 2), f32), "r"),
        ],
        cost=0,
    )
    down_part = product("lf,fd->ld", after(active, kept), down_weight).astype(bf16)
    (kept, sent, down_part) = up_sum.take(kept, sent, down_part)
    (kept, sent) = down_sum.take(kept, sent)
    (kept, sent, triple) = up_sum.send(kept, sent, triple)
    (kept, sent, triple) = down_sum.send(kept, sent, triple)
    (mod_local, kept) = tie(mod_local, kept)
    tables_mine = jnp.concatenate(in_three(mod_local) + [jnp.zeros_like(mod_local)], axis=1).astype(bf16)
    if n_tensor == 2:
        other = exchange(sent)
    else:
        kept = lax.psum_scatter(attn_part, "tensor", scatter_dimension=1, tiled=True)
        other = jnp.zeros_like(sent)
        sums = lax.psum(sums, "tensor")
    qkv_sum.keeps, _ = attention_grads(False, in_t, attn_t, triple, attended)
    token_t, late_totals = sweep(
        functools.partial(token_grad_kernel, model_width),
        length,
        [],
        [
            (picks, "r"),
            (marks, "v"), (segment_ids, "c"),
            (tables_mine, "v"),
            (kept, "r"),
            (other, "r"),
            (sums, "r"),
            (normed_mine, "r"),
            (inverse_one, "r"),
            (grad_mine, "r"),
        ],
        [(shape((local_width, length), f32), "c"), (shape((4 * segs, local_width), f32), "w")],
        cost=0,
    )
    (late_totals, *qkv_sum.keeps) = qkv_sum.take(late_totals, *qkv_sum.keeps)
    (late_totals,) = up_sum.take(late_totals)
    (down_part, late_totals) = qkv_sum.send(down_part, late_totals)
    (down_part, late_totals) = up_sum.send(down_part, late_totals)
    (down_part,) = down_sum.take(down_part)
    down_part, down_other = summands(down_part, n_tensor)
    layer_out, gate_total = sweep(
        layer_kernel,
        length,
        [],
        [(picks, "r"), (marks, "v"), (segment_ids, "c")]
        + middle_args
        + [(down_part, "r"), (down_other, "r"), (down_bias[None], "v"), (out_grad, "r")],
        [(shape(full), "r"), (shape((2 * segs, model_width), f32), "w")],
        cost=0,
    )
    (gate_total,) = qkv_sum.take(gate_total)
    (gate_total,) = up_sum.take(gate_total)
    (gate_total,) = qkv_sum.send(gate_total)
    bias_rows = 2 * n_tensor + hidden_width // local_width + 2
    rows = (6 + n_tensor) * segs + 2 * bias_rows
    (packed,) = pl.pallas_call(
        pack_kernel,
        in_specs=[SMEM] + [VMEM] * 9,
        out_specs=[VMEM],
        out_shape=[shape((rows, local_width))],
        scratch_shapes=[pltpu.VMEM((-(-rows // 16) * 16, local_width), f32)],
        compiler_params=room(16),
        cost_estimate=FREE,
    )(
        side,
        early_totals,
        late_totals,
        gate_total,
        cond_act,
        proj_bias_grad,
        down_bias_grad,
        up_bias_grad,
        qk_bias_grad,
        value_bias_grad,
    )
    gathered = Gather(packed, n_batch, bits[:1:-1] + bits[1::-1])
    gathered.step()
    gathered.step()
    tgrad = packed[: 6 * segs].reshape((6, segs, local_width))
    down_sum.settle(gate_total)
    up_sum.settle(gate_total)
    cut = hidden_width // 2
    down = down_sum.result([(0, 0, cut), (1, 0, cut)])
    up = up_sum.result([(0, 0, cut), (1, 0, cut)])
    (*up, down_first, down_second) = qkv_sum.take(*up, *down)
    qkv_sum.send()
    gathered.step(*qkv_sum.sent)
    cond_then = after(tgrad, *qkv_sum.sent)
    qkv_sum.take()
    while gathered.order:
        gathered.step(*qkv_sum.got[-1])
    cond_part = product("jsc,djc->sd", cond_then, mod_weight)
    cond_part, cond_other = summands(cond_part.astype(bf16), n_tensor)
    cond_act_grad = cond_part.astype(f32) + cond_other.astype(f32)
    condition_grad = jax.vjp(silu, cond_float)[1](cond_act_grad)[0]

    held = gathered.held
    part = index * block // local_width
    cond_block = lax.dynamic_slice(
        held, (0, (6 + part) * segs, index * block % local_width), (n_batch, segs, block)
    )
    mod_sum, modbias_sum, bias_all = pl.pallas_call(
        functools.partial(finish_kernel, segs, (6 + n_tensor) * segs),
        in_specs=[VMEM] * 2,
        out_specs=[VMEM] * 3,
        out_shape=[
            shape((6, block, local_width), f32),
            shape((6, local_width), f32),
            shape((bias_rows, local_width), f32),
        ],
        scratch_shapes=[pltpu.VMEM((-(-rows // 8) * 8, local_width), f32)],
        compiler_params=room(24),
        cost_estimate=FREE,
    )(held, cond_block)
    qv_sum = bias_all[-2:]
    bias_all = bias_all[:-2].reshape(-1)
    projbias_sum = bias_all[:model_width]
    downbias_sum = bias_all[model_width : 2 * model_width]
    upbias_sum = bias_all[2 * model_width :]
    mod_sum = mod_sum.transpose((1, 0, 2))
    begin = padded(local_width)
    *last, proj_last = qkv_sum.result(
        [
            (0, 0, local_width),
            (0, local_width, 2 * local_width),
            (1, 0, local_width),
            (1, begin, begin + local_width),
        ]
    )
    last = jnp.stack(last, axis=1)
    up = jnp.concatenate(up, axis=1)
    down = jnp.concatenate([down_first, down_second], axis=1).T
    return (
        layer_out[None],
        token_t.T[None],
        condition_grad[None],
        last,
        qv_sum,
        proj_last.T,
        projbias_sum,
        up,
        upbias_sum,
        down,
        downbias_sum,
        mod_sum,
        modbias_sum,
    )


def solution(mesh):
    return jax.shard_map(
        functools.partial(on_device, mesh.shape["batch"]),
        mesh=mesh,
        in_specs=(
            P("batch", None, None),
            P("batch", None),
            P("batch", None, None),
            P("batch", None),
            P(None, None, "tensor"),
            P(None, "tensor"),
            P("tensor", None),
            P(),
            P(None, "tensor"),
            P("tensor"),
            P("tensor", None),
            P(),
            P(None, None, "tensor"),
            P(None, "tensor"),
            P("batch", None, None),
        ),
        out_specs=(
            P("batch", None, None),
            P("batch", None, "tensor"),
            P("batch", None, None),
            P("batch", None, "tensor"),
            P(None, "tensor"),
            P("tensor", "batch"),
            P(),
            P("batch", "tensor"),
            P("tensor"),
            P("tensor", "batch"),
            P(),
            P("batch", None, "tensor"),
            P(None, "tensor"),
        ),
        check_vma=False,
    )
```

```python
import functools

import jax
import jax.numpy as jnp
from jax import lax
from jax.experimental import pallas as pl
from jax.experimental.pallas import tpu as pltpu
from jax.sharding import PartitionSpec as P

EPS = 1e-06
HEAD_DIM = 72
SEGS = 8
MOST = 256
LOG2E = 1.4426950408889634
NEG = -1e30


def band(begin, width, length):
    low = max(0, (begin - MOST + 1) // 128 * 128)
    high = min(length, -(-(begin + width + MOST - 1) // 128) * 128)
    return low, high


def natural(array):
    return array.astype(jnp.float32).T.astype(jnp.bfloat16)


def marks(seg_row):
    slots = lax.broadcasted_iota(jnp.int32, (SEGS, seg_row.shape[-1]), 0)
    return (slots == seg_row[...]).astype(jnp.float32)


def fill(head, qkv, one_hot, q_aug, k_nat):
    query = jnp.concatenate([qkv[0, head].astype(jnp.float32), (1.0 - one_hot) * NEG], axis=0)
    q_aug[...] = query.astype(jnp.bfloat16)
    k_nat[...] = natural(jnp.concatenate([qkv[1, head].astype(jnp.float32), one_hot], axis=0))


def attention_forward_kernel(width, seg_row, qkv, out, stat, q_aug, k_nat):
    heads, length = qkv.shape[1], qkv.shape[3]
    factor = HEAD_DIM**-0.5 * LOG2E
    one_hot = marks(seg_row)

    def one(head, carry):
        fill(head, qkv, one_hot, q_aug, k_nat)
        for begin in range(0, length, width):
            low, high = band(begin, width, length)
            span = slice(begin, begin + width)
            scores = jnp.dot(
                k_nat[low:high, :], q_aug[:, span], preferred_element_type=jnp.float32
            )
            peak = jnp.max(scores, axis=0, keepdims=True) * factor
            shifted = jnp.exp2(scores * factor - peak)
            total = jnp.sum(shifted, axis=0, keepdims=True)
            got = jnp.dot(
                qkv[2, head, :, low:high],
                shifted.astype(jnp.bfloat16),
                preferred_element_type=jnp.float32,
            )
            out[head, :, span] = (got * (1.0 / total)).astype(jnp.bfloat16)
            stat[head, :, span] = peak + jnp.log2(total)
        return carry

    lax.fori_loop(0, heads, one, 0, unroll=2)


def attention_backward_kernel(
    width, seg_row, qkv, stat, grad, out, q_aug, k_nat, v_nat, q_nat, g_nat, p_all, s_all
):
    heads, length = qkv.shape[1], qkv.shape[3]
    scale = HEAD_DIM**-0.5
    factor = scale * LOG2E
    one_hot = marks(seg_row)

    def one(head, carry):
        fill(head, qkv, one_hot, q_aug, k_nat)
        v_nat[...] = natural(qkv[2, head])
        q_nat[...] = natural(qkv[0, head])
        g_nat[...] = natural(grad[head])
        for begin in range(0, length, width):
            low, high = band(begin, width, length)
            span = slice(begin, begin + width)
            scores = jnp.dot(
                k_nat[low:high, :], q_aug[:, span], preferred_element_type=jnp.float32
            )
            probs = jnp.exp2(scores * factor - stat[head, :, span])
            prob_grad = jnp.dot(
                v_nat[low:high, :], grad[head, :, span], preferred_element_type=jnp.float32
            )
            row = jnp.sum(prob_grad * probs, axis=0, keepdims=True)
            score_grad = (probs * (prob_grad - row)).astype(jnp.bfloat16)
            p_all[low:high, span] = probs.astype(jnp.bfloat16)
            s_all[low:high, span] = score_grad
            got = jnp.dot(
                qkv[1, head, :, low:high], score_grad, preferred_element_type=jnp.float32
            )
            out[0, head, :, span] = (got * scale).astype(jnp.bfloat16)
        for begin in range(0, length, width):
            span = slice(begin, begin + width)
            reach = [q for q in range(0, length, width) if band(q, width, length)[0] < begin + width and band(q, width, length)[1] > begin]
            low, high = reach[0], reach[-1] + width
            key_grad = jnp.dot(
                s_all[span, low:high], q_nat[low:high, :], preferred_element_type=jnp.float32
            )
            value_grad = jnp.dot(
                p_all[span, low:high], g_nat[low:high, :], preferred_element_type=jnp.float32
            )
            out[1, head, :, span] = (key_grad * scale).T.astype(jnp.bfloat16)
            out[2, head, :, span] = value_grad.T.astype(jnp.bfloat16)
        return carry

    if width < MOST:
        p_all[...] = jnp.zeros_like(p_all)
        s_all[...] = jnp.zeros_like(s_all)
    lax.fori_loop(0, heads, one, 0, unroll=2)


VMEM = pl.BlockSpec(memory_space=pltpu.VMEM)


CHUNK = 128


def dot(left, right):
    return jnp.dot(left, right, preferred_element_type=jnp.float32)


def dot_nt(left, right):
    return lax.dot_general(
        left, right, (((1,), (1,)), ((), ())), preferred_element_type=jnp.float32
    )


def wide(value):
    return value.astype(jnp.float32)


def turn(order, value, out, work):
    count = order.shape[0]
    rows = value.shape[1] // count
    work[...] = wide(value).T
    for at in range(0, count, 2):
        pair = [
            work[pl.ds(pl.multiple_of(order[at + i] * rows, 8), rows), :] for i in range(2)
        ]
        pair = jnp.concatenate(pair, axis=0).astype(jnp.bfloat16)
        out[at * rows : (at + 2) * rows, :] = pair


def own_part(side, value, width):
    part = value[:, :width]
    for at in range(1, value.shape[1] // width):
        part = jnp.where(side == at, value[:, at * width : (at + 1) * width], part)
    return part


def accumulate(total, value):
    @pl.when(pl.program_id(0) == 0)
    def _():
        total[...] = value

    @pl.when(pl.program_id(0) > 0)
    def _():
        total[...] += value


def segment_sums(slots, seg, *values):
    marks = (slots[...] == seg[...]).astype(jnp.bfloat16)
    marks = jnp.concatenate([marks, marks], axis=1)
    sums = []
    for value in values:
        high = value.astype(jnp.bfloat16)
        low = (value - wide(high)).astype(jnp.bfloat16)
        sums.append(dot(marks, jnp.concatenate([high, low], axis=0)))
    return jnp.concatenate(sums, axis=0)


def norm_parts(value):
    width = value.shape[1]
    mean = jnp.sum(value, axis=1, keepdims=True) / width
    center = value - mean
    spread = jnp.sum(center * center, axis=1, keepdims=True) / width
    return mean, center, lax.rsqrt(spread + EPS)


def entry_kernel(order, side, picks, tables, tokens, out, mean, inverse, normed_mine, *turned):
    pick = picks[...]
    middle, center, scale = norm_parts(wide(tokens[...]))
    mean[...] = middle
    inverse[...] = scale
    value = center * scale
    normed_mine[...] = own_part(side[0], value, normed_mine.shape[1])
    value = (value * (1.0 + dot(pick, tables[1])) + dot(pick, tables[0])).astype(jnp.bfloat16)
    out[...] = value
    if turned:
        turn(order, value, *turned)


def gate_kernel(order, picks, tables, grad, out, bias, *turned):
    value = (wide(grad[...]) * dot(picks[...], tables[5])).astype(jnp.bfloat16)
    out[...] = value
    accumulate(bias, jnp.sum(wide(value), axis=0, keepdims=True))
    if turned:
        turn(order, value, *turned)


def middle_of(pick, tables, tokens, part, other, bias):
    attn_out = wide(part[...]) + wide(other[...]) + bias[...]
    return attn_out, wide(tokens[...]) + dot(pick, tables[2]) * attn_out


def middle_kernel(order, picks, tables, tokens, part, other, bias, out, mean, inverse, *turned):
    pick = picks[...]
    value = middle_of(pick, tables, tokens, part, other, bias)[1]
    middle, center, scale = norm_parts(value)
    mean[...] = middle
    inverse[...] = scale
    value = center * scale * (1.0 + dot(pick, tables[4])) + dot(pick, tables[3])
    value = value.astype(jnp.bfloat16)
    out[...] = value
    if turned:
        turn(order, value, *turned)


def middle_grad_kernel(
    order, side, picks, marks, seg, tables, tokens, part, other, bias, mean, inverse, mlp, mlp_other, grad,
    out, bias_sum, grad_mine, totals, *turned
):
    pick = picks[...]
    width = grad.shape[1]
    attn_out, value = middle_of(pick, tables, tokens, part, other, bias)
    norm = (value - mean[...]) * inverse[...]
    in_grad = wide(mlp[...]) + wide(mlp_other[...])
    value = in_grad * (1.0 + dot(pick, tables[4]))
    plain = jnp.sum(value, axis=1, keepdims=True) / width
    cross = jnp.sum(value * norm, axis=1, keepdims=True) / width
    value = wide(grad[...]) + inverse[...] * (value - plain - norm * cross)
    grad_mine[...] = own_part(side[0], value, grad_mine.shape[1])
    accumulate(totals, segment_sums(marks, seg, value * attn_out, in_grad, in_grad * norm))
    value = (value * dot(pick, tables[2])).astype(jnp.bfloat16)
    out[...] = value
    accumulate(bias_sum, jnp.sum(wide(value), axis=0, keepdims=True))
    if turned:
        turn(order, value, *turned)


def halves_kernel(side, picks, tables, part, tokens, mean, inverse, kept, sent, sums):
    value = part[...]
    width = kept.shape[1]
    kept[...] = own_part(side[0], value, width)
    sent[:, :width] = own_part(1 - side[0], value, width)
    value = wide(value) * (1.0 + dot(picks[...], tables[1]))
    norm = (wide(tokens[...]) - mean[...]) * inverse[...]
    for at, term in enumerate((value, value * norm)):
        total = jnp.sum(term, axis=1, keepdims=True)
        high = total.astype(jnp.bfloat16)
        sums[:, at : at + 1] = total
        sent[:, width + 2 * at : width + 2 * at + 1] = high
        sent[:, width + 2 * at + 1 : width + 2 * at + 2] = (total - wide(high)).astype(jnp.bfloat16)


def token_grad_kernel(
    width, picks, marks, seg, tables, kept, other, sums, normed, inverse, grad, out_t, totals
):
    mine = kept.shape[1]
    value = wide(kept[...]) + wide(other[:, :mine])
    norm = normed[...]
    accumulate(totals, segment_sums(marks, seg, value, value * norm))
    value = value * (1.0 + dot(picks[...], tables[1]))
    for at, factor in enumerate((1.0, norm)):
        rest = wide(other[:, mine + 2 * at : mine + 2 * at + 1])
        rest = rest + wide(other[:, mine + 2 * at + 1 : mine + 2 * at + 2])
        value = value - factor * ((sums[:, at : at + 1] + rest) / width)
    out_t[...] = (grad[...] + inverse[...] * value).T


def layer_kernel(
    picks, marks, seg, tables, tokens, part, other, bias, down, down_other, down_bias, grad, out, totals
):
    pick = picks[...]
    mlp_out = wide(down[...]) + wide(down_other[...]) + down_bias[...]
    middle = middle_of(pick, tables, tokens, part, other, bias)[1]
    out[...] = (middle + dot(pick, tables[5]) * mlp_out).astype(jnp.bfloat16)
    accumulate(totals, segment_sums(marks, seg, wide(grad[...]) * mlp_out))


def row_parts(sent, first):
    if first:
        return (2, 3) if sent else (0, 1)
    return (1, 3) if sent else (0, 2)


def put_rows(left, right, out, parts, product):
    quarter = left.shape[0] // 4
    columns = slice(0, right.shape[0] if product is dot_nt else right.shape[1])
    if parts[1] == parts[0] + 1:
        rows = slice(parts[0] * quarter, (parts[1] + 1) * quarter)
        out[:, columns] = product(left[rows, :], right[...]).astype(jnp.bfloat16)
        return
    for at, part in enumerate(parts):
        rows = slice(part * quarter, (part + 1) * quarter)
        value = product(left[rows, :], right[...]).astype(jnp.bfloat16)
        out[at * quarter : (at + 1) * quarter, columns] = value


def mlp_grads_kernel(sent, summed, fetched, left, right, *refs):
    sources, (first, second), rest = refs[:fetched], refs[fetched : fetched + 2], refs[fetched + 2 :]
    step = pl.program_id(0)
    copies = []
    if fetched:
        copies = [
            pltpu.make_async_copy(source, target, rest[-1].at[at])
            for at, (source, target) in enumerate(zip(sources, rest[:fetched]))
        ]

    @pl.when(step == 0)
    def _():
        for copy in copies:
            copy.start()
        put_rows(left, right, first, row_parts(sent, True), dot)

    @pl.when(step == 1)
    def _():
        put_rows(left, right, second, row_parts(sent, False), dot)
        for copy in copies:
            copy.wait()

    if summed:
        rest[0][...] = jnp.sum(wide(right[...]), axis=0, keepdims=True)


def qkv_grads_kernel(sent, left, proj_left, both, value, attended, first, second, *sums):
    step = pl.program_id(0)

    def column_sums(array):
        ones = jnp.ones((8, array.shape[1]), jnp.bfloat16)
        return dot_nt(ones, array[...])

    @pl.when(step == 0)
    def _():
        put_rows(left, both, first, row_parts(sent, True), dot_nt)
        if sums:
            sums[0][...] = column_sums(both)
            sums[1][...] = column_sums(value)

    @pl.when(step == 1)
    def _():
        second[...] = jnp.zeros_like(second)
        put_rows(left, value, second, row_parts(sent, False), dot_nt)

    @pl.when(step == 2)
    def _():
        second[...] = jnp.zeros_like(second)
        put_rows(proj_left, attended, second, row_parts(sent, False), dot_nt)


SMEM = pl.BlockSpec(memory_space=pltpu.SMEM)
GRADS = 10
FREE = pl.CostEstimate(flops=1, bytes_accessed=1, transcendentals=0)


def micros(time):
    if time == 0:
        return FREE
    return pl.CostEstimate(flops=time * 10**9, bytes_accessed=time * 10**6, transcendentals=0)


def shape(dims, dtype=jnp.bfloat16):
    return jax.ShapeDtypeStruct(dims, dtype)


def room(mib):
    return pltpu.CompilerParams(vmem_limit_bytes=mib << 20)


def spec(dims, kind):
    if kind == "v":
        return VMEM
    if kind == "r":
        return pl.BlockSpec((CHUNK, dims[1]), lambda i: (i, 0))
    if kind == "c":
        return pl.BlockSpec((dims[0], CHUNK), lambda i: (0, i))
    return pl.BlockSpec(tuple(dims), lambda i: (0,) * len(dims))


def sweep(kernel, length, scalars, arrays, outs, work=(), mib=16, cost=200):
    return pl.pallas_call(
        kernel,
        grid=(length // CHUNK,),
        in_specs=[SMEM] * len(scalars) + [spec(a.shape, kind) for a, kind in arrays],
        out_specs=[spec(o.shape, kind) for o, kind in outs],
        out_shape=[o for o, _ in outs],
        scratch_shapes=[pltpu.VMEM(dims, jnp.float32) for dims in work],
        compiler_params=room(mib),
        cost_estimate=micros(cost),
    )(*scalars, *[a for a, _ in arrays])


def mlp_grads(sent, left, right, summed=False, fetch=()):
    width, length = left.shape
    hidden = right.shape[1]
    half = hidden // 2
    out = pl.BlockSpec((width // 2, half), lambda j: (0, 0))
    sums = [pl.BlockSpec((1, half), lambda j: (0, j))] if summed else []
    sums_shape = [shape((1, hidden), jnp.float32)] if summed else []
    return pl.pallas_call(
        functools.partial(mlp_grads_kernel, sent, summed, len(fetch)),
        grid=(2,),
        in_specs=[spec(left.shape, "w"), pl.BlockSpec((length, half), lambda j: (0, j))]
        + [pl.BlockSpec(memory_space=pl.ANY)] * len(fetch),
        out_specs=[out, out] + sums + [VMEM] * len(fetch),
        out_shape=[shape((width // 2, half))] * 2
        + sums_shape
        + [pltpu.VMEM(a.shape, a.dtype) for a in fetch],
        scratch_shapes=[pltpu.SemaphoreType.DMA((len(fetch),))] if fetch else [],
        compiler_params=room(24),
        cost_estimate=micros(GRADS),
    )(left, right, *fetch)


def sum_kernel(counts, splits, *refs):
    halves, at = [], 0
    for count in counts[:2]:
        total = wide(refs[at][...])
        for ref in refs[at + 1 : at + count]:
            total += wide(ref[...])
        halves.append(total)
        at += count
    outs = refs[at + counts[2] :]
    for half in range(2):
        begin = 0 if half == 0 else halves[0].shape[1]
        columns = slice(begin, begin + halves[half].shape[1])
        for ref in refs[at : at + counts[2]]:
            halves[half] += wide(ref[:, columns])
    if splits is None:
        for out, total in zip(outs, halves):
            out[...] = total.astype(out.dtype)
    elif splits == ():
        for total, begin in zip(halves, (0, halves[0].shape[1])):
            outs[0][:, begin : begin + total.shape[1]] = total.astype(outs[0].dtype)
    else:
        for out, (half, begin, end) in zip(outs, splits):
            out[...] = halves[half][:, begin:end]


def sum_rows(halves, joined, at, count, outs, splits=None):
    arrays = halves[0] + halves[1] + joined

    def rows(width):
        return pl.BlockSpec((count, width), lambda i: (at, 0))

    return pl.pallas_call(
        functools.partial(sum_kernel, (len(halves[0]), len(halves[1]), len(joined)), splits),
        grid=(1,),
        in_specs=[rows(a.shape[1]) for a in arrays],
        out_specs=[pl.BlockSpec(o.shape, lambda i: (0, 0)) for o in outs],
        out_shape=outs,
        compiler_params=room(16),
        cost_estimate=FREE,
    )(*arrays)


def pack_kernel(
    side, middle, late, gate, cond, proj_bias, down_bias, up_bias, qk_bias, value_bias, out, work
):
    width = out.shape[1]
    segs = cond.shape[0]
    own = [late[:segs, :], late[2 * segs : 3 * segs, :]]
    for source, at in ((middle, 0), (middle, 1), (middle, 2), (gate, 0)):
        own.append(own_part(side[0], source[2 * at * segs : (2 * at + 1) * segs, :], width))
    own += [wide(cond[:, at : at + width]) for at in range(0, cond.shape[1], width)]
    for at, value in enumerate(own):
        work[at * segs : (at + 1) * segs, :] = value
    rows = []
    for source in (proj_bias, down_bias, up_bias):
        rows += [source[0:1, at : at + width] for at in range(0, source.shape[1], width)]
    rows += [qk_bias[0:1, :width], value_bias[0:1, :]]
    first = len(own) * segs
    for at, value in enumerate(rows):
        high = wide(value.astype(jnp.bfloat16))
        work[first + at : first + at + 1, :] = high
        work[first + len(rows) + at : first + len(rows) + at + 1, :] = value - high
    out[...] = work[: out.shape[0], :].astype(jnp.bfloat16)


def finish_kernel(segs, first, held, cond, mod, modbias, bias, work):
    value = wide(held[...])
    devices, rows, width = value.shape
    left = wide(cond[...]).reshape((devices * segs, cond.shape[2])).T.astype(jnp.bfloat16)
    for at in range(mod.shape[0]):
        part = value[:, at * segs : (at + 1) * segs, :].reshape((devices * segs, width))
        mod[at] = dot(left, part.astype(jnp.bfloat16))
        modbias[at : at + 1, :] = jnp.sum(part, axis=0, keepdims=True)
    work[:rows, :] = jnp.sum(value, axis=0)
    count = bias.shape[0]
    bias[...] = work[first : first + count, :] + work[first + count : first + 2 * count, :]


def padded(width):
    return -(-width // 128) * 128


def qkv_grads(sent, left, proj_left, triple, attended):
    width, length = left.shape
    local = attended.shape[0]
    wide_block = padded(local)
    sums_spec = [pl.BlockSpec((8, 2 * local), lambda j: (0, 0)), pl.BlockSpec((8, local), lambda j: (0, 0))]
    sums_shape = [shape((8, 2 * local), jnp.float32), shape((8, local), jnp.float32)]
    return pl.pallas_call(
        functools.partial(qkv_grads_kernel, sent),
        grid=(3,),
        in_specs=[
            spec(left.shape, "w"),
            spec(left.shape, "w"),
            pl.BlockSpec((2 * local, length), lambda j: (0, 0)),
            pl.BlockSpec((local, length), lambda j: (2, 0)),
            spec(attended.shape, "w"),
        ],
        out_specs=[
            pl.BlockSpec((width // 2, 2 * local), lambda j: (0, 0)),
            pl.BlockSpec((width // 2, wide_block), lambda j: (0, jnp.maximum(j - 1, 0))),
        ]
        + sums_spec * sent,
        out_shape=[shape((width // 2, 2 * local)), shape((width // 2, 2 * wide_block))]
        + sums_shape * sent,
        compiler_params=room(32),
        cost_estimate=FREE,
    )(left, proj_left, triple, triple, attended)


def attention_forward(segments, qkv, width=256):
    heads, length = qkv.shape[1], qkv.shape[3]
    return pl.pallas_call(
        functools.partial(attention_forward_kernel, width),
        in_specs=[VMEM] * 2,
        out_specs=[VMEM] * 2,
        out_shape=[shape((heads, HEAD_DIM, length)), shape((heads, 1, length), jnp.float32)],
        scratch_shapes=[
            pltpu.VMEM((HEAD_DIM + SEGS, length), jnp.bfloat16),
            pltpu.VMEM((length, HEAD_DIM + SEGS), jnp.bfloat16),
        ],
        compiler_params=room(12),
        cost_estimate=micros(15),
    )(segments, qkv)


def attention_backward(segments, qkv, stat, grad, width=256):
    heads, length = qkv.shape[1], qkv.shape[3]
    return pl.pallas_call(
        functools.partial(attention_backward_kernel, width),
        in_specs=[VMEM] * 4,
        out_specs=VMEM,
        out_shape=shape(qkv.shape),
        scratch_shapes=[
            pltpu.VMEM((HEAD_DIM + SEGS, length), jnp.bfloat16),
            pltpu.VMEM((length, HEAD_DIM + SEGS), jnp.bfloat16),
        ]
        + [pltpu.VMEM((length, HEAD_DIM), jnp.bfloat16)] * 3
        + [pltpu.VMEM((length, length), jnp.bfloat16)] * 2,
        compiler_params=room(16),
        cost_estimate=micros(15),
    )(segments, qkv, stat, grad)


def silu(array):
    return array / (1.0 + jnp.exp(-array))


def product(spec, left, right):
    return jnp.einsum(spec, left, right, preferred_element_type=jnp.float32)


def exchange(array):
    return lax.ppermute(array, "tensor", [(0, 1), (1, 0)])


def summands(part, size):
    if size == 2:
        return part, exchange(part)
    return lax.psum(part, "tensor"), jnp.zeros_like(part)


def tensor_join(array, size):
    if size == 2:
        other = exchange(array)
        first = lax.axis_index("tensor") == 0
        return jnp.concatenate(
            [jnp.where(first, array, other), jnp.where(first, other, array)], axis=-1
        )
    return lax.all_gather(array, "tensor", axis=array.ndim - 1, tiled=True)


def partners(size, bit):
    return [(i, i ^ (1 << bit)) for i in range(size)]


def tie(*values):
    return lax.optimization_barrier(values)


def after(value, *others):
    return tie(value, *others)[0]


class Gather:
    def __init__(self, array, size, order):
        self.held, self.size, self.order = array[None], size, list(order)

    def step(self, *others):
        if self.order:
            bit = self.order.pop(0)
            self.held = after(self.held, *others)
            other = lax.ppermute(self.held, "batch", partners(self.size, bit))
            self.held = jnp.concatenate([self.held, other], axis=0)


class Sum:
    def __init__(self, sends, size, kernels):
        self.kernels = kernels
        self.sends, self.size, self.bits = sends, size, size.bit_length() - 1
        self.keeps, self.got = None, []

    def pieces(self, at, count, dtype, splits=None, outs=None):
        halves = [[self.keeps[h]] + [stage[h] for stage in self.got[:2]] for h in range(2)]
        joined = [new for (new,) in self.got[2:]]
        widths = [half[0].shape[1] for half in halves]
        if self.kernels:
            if outs is None:
                outs = [shape((count, width), dtype) for width in widths]
                if len(self.got) > 1:
                    outs, splits = [shape((count, sum(widths)), dtype)], ()
            return list(sum_rows(halves, joined, at, count, outs, splits))
        window = slice(at * count, (at + 1) * count)
        totals = [sum(a[window].astype(jnp.float32) for a in half) for half in halves]
        if len(self.got) < 2:
            return [total.astype(dtype) for total in totals]
        total = jnp.concatenate(totals, axis=1)
        total = sum((a[window].astype(jnp.float32) for a in joined), total)
        if outs is None:
            return [total.astype(dtype)]
        totals = [total[:, : widths[0]], total[:, widths[0] :]]
        return [totals[half][:, begin:end] for half, begin, end in splits]

    def send(self, *others):
        stage = len(self.got)
        sends, bits = self.sends, [stage]
        if stage > 0:
            left = self.keeps[0].shape[0] >> stage
            sends = self.pieces(1, left, jnp.bfloat16)
        if stage < 2:
            bits = [stage, 1 - stage]
        tied = tie(*sends, *others)
        self.sent = tied[: len(sends)]
        self.flying = [
            lax.ppermute(piece, "batch", partners(self.size, bit))
            for piece, bit in zip(tied, bits)
        ]
        return tied[len(sends) :]

    def take(self, *others):
        tied = tie(*self.flying, *others)
        self.got.append(tied[: len(self.flying)])
        return tied[len(self.flying) :]

    def settle(self, other):
        if len(self.got) == self.bits:
            self.keeps = list(tie(*self.keeps, other)[:2])

    def result(self, splits):
        while len(self.got) < self.bits:
            self.send()
            self.take()
        count = 2 * self.keeps[0].shape[0] // self.size
        outs = [shape((count, end - begin), jnp.float32) for _, begin, end in splits]
        return self.pieces(0, count, jnp.float32, splits, outs)


def gelu_and_slope(array):
    square = array * array
    bent = jnp.tanh(0.7978845608028654 * (array + 0.044715 * array * square))
    half = 0.5 * (1.0 + bent)
    inner = 0.7978845608028654 * (1.0 + 3.0 * 0.044715 * square)
    return array * half, half + 0.5 * array * (1.0 - bent * bent) * inner


def in_three(array):
    high = lax.reduce_precision(array, 8, 7)
    middle = lax.reduce_precision(array - high, 8, 7)
    return [high, middle, array - high - middle]


def on_device(
    n_batch,
    tokens,
    segment_ids,
    conditions,
    condition_segment,
    qkv_weight,
    qv_bias,
    proj_weight,
    proj_bias,
    up_weight,
    up_bias,
    down_weight,
    down_bias,
    mod_weight,
    mod_bias,
    out_grad,
):
    bf16, f32 = jnp.bfloat16, jnp.float32
    tokens, out_grad = tokens[0], out_grad[0]
    length, model_width = tokens.shape
    local_width = qkv_weight.shape[2]
    hidden_width = up_weight.shape[1]
    heads = local_width // HEAD_DIM
    n_tensor = model_width // local_width
    bits = list(range(n_batch.bit_length() - 1))
    block = model_width // n_batch
    in_kernel = block % 8 == 0
    index = lax.axis_index("batch")
    order = jnp.array(
        [sum((p >> bit & 1) << (bits[-1] - bit) for bit in bits) for p in range(n_batch)], jnp.int32
    )
    order = order ^ index
    side = lax.axis_index("tensor")[None]

    def run(kernel, scalars, arrays, outs):
        turned = shape((model_width, length))
        if in_kernel:
            chunk = (model_width, CHUNK)
            return sweep(kernel, length, scalars, arrays, outs + [(turned, "c")], [chunk])
        got = sweep(kernel, length, scalars, arrays, outs)
        return list(got) + [got[0].T.reshape((n_batch, block, length))[order].reshape(turned.shape)]

    def part_rows(left, sent, first):
        quarter = model_width // 4
        rows = [left[at * quarter : (at + 1) * quarter] for at in row_parts(sent, first)]
        return jnp.concatenate(rows)

    def hidden_grads(sent, left, right, summed=False, fetch=()):
        if in_kernel:
            first, second, *rest = mlp_grads(sent, left, right, summed, fetch)
            return [first, second], rest
        rest = [jnp.sum(right.astype(f32), axis=0)[None]] if summed else fetch
        cut = right.shape[1] // 2
        return [
            product("dl,lc->dc", part_rows(left, sent, True), right[:, :cut]).astype(bf16),
            product("dl,lc->dc", part_rows(left, sent, False), right[:, cut:]).astype(bf16),
        ], rest

    def attention_grads(sent, left, proj_left, triple, attended):
        if in_kernel:
            first, second, *sums = qkv_grads(sent, left, proj_left, triple, attended)
            return [first, second], sums
        sums = jnp.sum(triple.astype(f32), axis=1)[None]
        sums = (sums[:, : 2 * local_width], sums[:, 2 * local_width :])
        cut, extra = 2 * local_width, ((0, 0), (0, padded(local_width) - local_width))
        halves = [
            (part_rows(left, sent, True), triple[:cut]),
            (part_rows(left, sent, False), triple[cut:]),
            (part_rows(proj_left, sent, False), attended),
        ]
        first, value, proj = [product("dl,cl->dc", *pair).astype(bf16) for pair in halves]
        return [first, jnp.concatenate([jnp.pad(value, extra), jnp.pad(proj, extra)], axis=1)], sums

    cond_float = conditions[0].astype(f32)
    cond_act = silu(cond_float).astype(bf16)
    mod_local = product("sd,djc->jsc", cond_act, mod_weight) + mod_bias[:, None]
    modulation = tensor_join(mod_local, n_tensor)
    segs = modulation.shape[1]
    tables = jnp.concatenate(in_three(modulation) + [jnp.zeros_like(modulation)], axis=1).astype(bf16)
    slots = condition_segment[0][jnp.arange(4 * segs) % segs]
    real = jnp.arange(4 * segs) < 3 * segs
    picks = ((segment_ids[0][:, None] == slots[None]) & real[None]).astype(bf16)
    marks = jnp.concatenate([condition_segment[0], jnp.full((segs,), -1, jnp.int32)])[:, None]
    full, column = (length, model_width), shape((length, 1), f32)
    mine = (length, local_width)
    row = shape((1, model_width), f32)

    qkv_weight = qkv_weight.transpose((1, 2, 0))
    attn_in, mean_one, inverse_one, normed_mine, in_t = run(
        entry_kernel,
        [order, side],
        [(picks, "r"), (tables, "v"), (tokens, "r")],
        [(shape(full), "r"), (column, "r"), (column, "r"), (shape(mine, f32), "r")],
    )
    biases = jnp.stack([qv_bias[0], jnp.zeros_like(qv_bias[0]), qv_bias[1]])
    qkv = product("jcd,ld->jcl", qkv_weight, attn_in) + biases[:, :, None]
    qkv = qkv.astype(bf16).reshape((3, heads, HEAD_DIM, length))
    attended, stat = attention_forward(segment_ids, qkv)
    attended = attended.reshape((local_width, length))
    proj_part = product("cl,cd->ld", attended, proj_weight).astype(bf16)
    proj_part, proj_other = summands(proj_part, n_tensor)
    out_grad, proj_tied = tie(out_grad, proj_part)
    mlp_grad, down_bias_grad, grad_t = run(
        gate_kernel,
        [order],
        [(picks, "r"), (tables, "v"), (out_grad, "r")],
        [(shape(full), "r"), (row, "w")],
    )
    proj_other, mlp_grad = tie(proj_other, mlp_grad)
    middle_args = [
        (tables, "v"), (tokens, "r"), (proj_tied, "r"), (proj_other, "r"), (proj_bias[None], "v")
    ]
    mlp_in, mean_two, inverse_two, mlp_t = run(
        middle_kernel,
        [order],
        [(picks, "r")] + middle_args,
        [(shape(full), "r"), (column, "r"), (column, "r")],
    )
    hidden = product("ld,df->lf", mlp_in, up_weight) + up_bias
    active, slope = gelu_and_slope(hidden)
    active, slope = tie(active.astype(bf16), slope.astype(bf16))

    sends, (down_held, up_held) = hidden_grads(
        True, grad_t, active, fetch=(down_weight, up_weight)
    )
    down_sum = Sum(sends, n_batch, in_kernel)
    (mlp_grad_then, active_then) = down_sum.send(mlp_grad, active)
    active_grad = product("ld,fd->lf", mlp_grad_then, down_held)
    hidden_grad = (active_grad * slope.astype(f32)).astype(bf16)
    mlp_part = product("lf,df->ld", hidden_grad, up_held).astype(bf16)
    mlp_part, mlp_other = summands(mlp_part, n_tensor)
    (hidden_then, mlp_tied) = tie(hidden_grad, mlp_part)
    sends, (up_bias_grad,) = hidden_grads(True, mlp_t, hidden_then, summed=True)
    up_sum = Sum(sends, n_batch, in_kernel)
    down_sum.keeps, _ = hidden_grads(False, grad_t, active_then)
    first, second, *down_sum.keeps = down_sum.take(*up_sum.sends, *down_sum.keeps)
    up_sum.sends = [first, second]
    (mlp_other, hidden_then) = down_sum.send(mlp_other, hidden_then)
    (mlp_other, hidden_then) = up_sum.send(mlp_other, hidden_then)
    attn_grad, proj_bias_grad, grad_mine, early_totals, attn_t = run(
        middle_grad_kernel,
        [order, side],
        [(picks, "r"), (marks, "v"), (segment_ids, "c")]
        + middle_args
        + [(mean_two, "r"), (inverse_two, "r"), (mlp_tied, "r"), (mlp_other, "r"), (out_grad, "r")],
        [
            (shape(full), "r"),
            (row, "w"),
            (shape(mine, f32), "r"),
            (shape((6 * segs, model_width), f32), "w"),
        ],
    )
    attended_grad = product("cd,ld->cl", proj_weight, attn_grad).astype(bf16)

    triple = attention_backward(
        segment_ids, qkv, stat, attended_grad.reshape((heads, HEAD_DIM, length))
    ).reshape((3 * local_width, length))
    up_sum.keeps, _ = hidden_grads(False, mlp_t, hidden_then)
    sends, (qk_bias_grad, value_bias_grad) = attention_grads(True, in_t, attn_t, triple, attended)
    qkv_sum = Sum(sends, n_batch, in_kernel)
    first, second, *up_sum.keeps = up_sum.take(*qkv_sum.sends, *up_sum.keeps)
    qkv_sum.sends = [first, second]
    (triple,) = down_sum.take(triple)
    (triple,) = up_sum.send(triple)
    (triple,) = qkv_sum.send(triple)
    (triple,) = down_sum.send(triple)
    attn_part = product(
        "jcl,jcd->ld", triple.reshape((3, local_width, length)), qkv_weight
    ).astype(bf16)
    kept, sent, sums = sweep(
        halves_kernel,
        length,
        [side],
        [
            (picks, "r"),
            (tables, "v"),
            (attn_part, "r"),
            (tokens, "r"),
            (mean_one, "r"),
            (inverse_one, "r"),
        ],
        [
            (shape(mine), "r"),
            (shape((length, padded(local_width + 4))), "r"),
            (shape((length, 2), f32), "r"),
        ],
        cost=0,
    )
    down_part = product("lf,fd->ld", after(active, kept), down_weight).astype(bf16)
    (kept, sent, down_part) = up_sum.take(kept, sent, down_part)
    (kept, sent) = down_sum.take(kept, sent)
    (kept, sent, triple) = up_sum.send(kept, sent, triple)
    (kept, sent, triple) = down_sum.send(kept, sent, triple)
    (mod_local, kept) = tie(mod_local, kept)
    tables_mine = jnp.concatenate(in_three(mod_local) + [jnp.zeros_like(mod_local)], axis=1).astype(bf16)
    if n_tensor == 2:
        other = exchange(sent)
    else:
        kept = lax.psum_scatter(attn_part, "tensor", scatter_dimension=1, tiled=True)
        other = jnp.zeros_like(sent)
        sums = lax.psum(sums, "tensor")
    qkv_sum.keeps, _ = attention_grads(False, in_t, attn_t, triple, attended)
    token_t, late_totals = sweep(
        functools.partial(token_grad_kernel, model_width),
        length,
        [],
        [
            (picks, "r"),
            (marks, "v"), (segment_ids, "c"),
            (tables_mine, "v"),
            (kept, "r"),
            (other, "r"),
            (sums, "r"),
            (normed_mine, "r"),
            (inverse_one, "r"),
            (grad_mine, "r"),
        ],
        [(shape((local_width, length), f32), "c"), (shape((4 * segs, local_width), f32), "w")],
        cost=0,
    )
    (late_totals, *qkv_sum.keeps) = qkv_sum.take(late_totals, *qkv_sum.keeps)
    (late_totals,) = up_sum.take(late_totals)
    (down_part, late_totals) = qkv_sum.send(down_part, late_totals)
    (down_part, late_totals) = up_sum.send(down_part, late_totals)
    (down_part,) = down_sum.take(down_part)
    down_part, down_other = summands(down_part, n_tensor)
    layer_out, gate_total = sweep(
        layer_kernel,
        length,
        [],
        [(picks, "r"), (marks, "v"), (segment_ids, "c")]
        + middle_args
        + [(down_part, "r"), (down_other, "r"), (down_bias[None], "v"), (out_grad, "r")],
        [(shape(full), "r"), (shape((2 * segs, model_width), f32), "w")],
        cost=0,
    )
    (gate_total,) = qkv_sum.take(gate_total)
    (gate_total,) = up_sum.take(gate_total)
    (gate_total,) = qkv_sum.send(gate_total)
    bias_rows = 2 * n_tensor + hidden_width // local_width + 2
    rows = (6 + n_tensor) * segs + 2 * bias_rows
    (packed,) = pl.pallas_call(
        pack_kernel,
        in_specs=[SMEM] + [VMEM] * 9,
        out_specs=[VMEM],
        out_shape=[shape((rows, local_width))],
        scratch_shapes=[pltpu.VMEM((-(-rows // 16) * 16, local_width), f32)],
        compiler_params=room(16),
        cost_estimate=FREE,
    )(
        side,
        early_totals,
        late_totals,
        gate_total,
        cond_act,
        proj_bias_grad,
        down_bias_grad,
        up_bias_grad,
        qk_bias_grad,
        value_bias_grad,
    )
    gathered = Gather(packed, n_batch, bits[:1:-1] + bits[1::-1])
    gathered.step()
    gathered.step()
    tgrad = packed[: 6 * segs].reshape((6, segs, local_width))
    gathered.step()
    qkv_sum.take()
    qkv_sum.send()
    while gathered.order:
        gathered.step(*qkv_sum.sent)
    cond_then = after(tgrad, *qkv_sum.sent)
    down_sum.settle(qkv_sum.sent[0])
    up_sum.settle(qkv_sum.sent[0])
    cut = hidden_width // 2
    down = down_sum.result([(0, 0, cut), (1, 0, cut)])
    up = up_sum.result([(0, 0, cut), (1, 0, cut)])
    (*up, down_first, down_second) = qkv_sum.take(*up, *down)
    cond_part = product("jsc,djc->sd", cond_then, mod_weight)
    cond_part, cond_other = summands(cond_part.astype(bf16), n_tensor)
    cond_act_grad = cond_part.astype(f32) + cond_other.astype(f32)
    condition_grad = jax.vjp(silu, cond_float)[1](cond_act_grad)[0]

    held = gathered.held
    part = index * block // local_width
    cond_block = lax.dynamic_slice(
        held, (0, (6 + part) * segs, index * block % local_width), (n_batch, segs, block)
    )
    mod_sum, modbias_sum, bias_all = pl.pallas_call(
        functools.partial(finish_kernel, segs, (6 + n_tensor) * segs),
        in_specs=[VMEM] * 2,
        out_specs=[VMEM] * 3,
        out_shape=[
            shape((6, block, local_width), f32),
            shape((6, local_width), f32),
            shape((bias_rows, local_width), f32),
        ],
        scratch_shapes=[pltpu.VMEM((-(-rows // 8) * 8, local_width), f32)],
        compiler_params=room(24),
        cost_estimate=FREE,
    )(held, cond_block)
    qv_sum = bias_all[-2:]
    bias_all = bias_all[:-2].reshape(-1)
    projbias_sum = bias_all[:model_width]
    downbias_sum = bias_all[model_width : 2 * model_width]
    upbias_sum = bias_all[2 * model_width :]
    mod_sum = mod_sum.transpose((1, 0, 2))
    begin = padded(local_width)
    *last, proj_last = qkv_sum.result(
        [
            (0, 0, local_width),
            (0, local_width, 2 * local_width),
            (1, 0, local_width),
            (1, begin, begin + local_width),
        ]
    )
    last = jnp.stack(last, axis=1)
    up = jnp.concatenate(up, axis=1)
    down = jnp.concatenate([down_first, down_second], axis=1).T
    return (
        layer_out[None],
        token_t.T[None],
        condition_grad[None],
        last,
        qv_sum,
        proj_last.T,
        projbias_sum,
        up,
        upbias_sum,
        down,
        downbias_sum,
        mod_sum,
        modbias_sum,
    )


def solution(mesh):
    return jax.shard_map(
        functools.partial(on_device, mesh.shape["batch"]),
        mesh=mesh,
        in_specs=(
            P("batch", None, None),
            P("batch", None),
            P("batch", None, None),
            P("batch", None),
            P(None, None, "tensor"),
            P(None, "tensor"),
            P("tensor", None),
            P(),
            P(None, "tensor"),
            P("tensor"),
            P("tensor", None),
            P(),
            P(None, None, "tensor"),
            P(None, "tensor"),
            P("batch", None, None),
        ),
        out_specs=(
            P("batch", None, None),
            P("batch", None, "tensor"),
            P("batch", None, None),
            P("batch", None, "tensor"),
            P(None, "tensor"),
            P("tensor", "batch"),
            P(),
            P("batch", "tensor"),
            P("tensor"),
            P("tensor", "batch"),
            P(),
            P("batch", None, "tensor"),
            P(None, "tensor"),
        ),
        check_vma=False,
    )
```

```python
import functools

import jax
import jax.numpy as jnp
from jax import lax
from jax.experimental import pallas as pl
from jax.experimental.pallas import tpu as pltpu
from jax.sharding import PartitionSpec as P

EPS = 1e-06
HEAD_DIM = 72
SEGS = 8
MOST = 256
LOG2E = 1.4426950408889634
NEG = -1e30


def band(begin, width, length):
    low = max(0, (begin - MOST + 1) // 128 * 128)
    high = min(length, -(-(begin + width + MOST - 1) // 128) * 128)
    return low, high


def natural(array):
    return array.astype(jnp.float32).T.astype(jnp.bfloat16)


def marks(seg_row):
    slots = lax.broadcasted_iota(jnp.int32, (SEGS, seg_row.shape[-1]), 0)
    return (slots == seg_row[...]).astype(jnp.float32)


def fill(head, qkv, one_hot, q_aug, k_nat):
    query = jnp.concatenate([qkv[0, head].astype(jnp.float32), (1.0 - one_hot) * NEG], axis=0)
    q_aug[...] = query.astype(jnp.bfloat16)
    k_nat[...] = natural(jnp.concatenate([qkv[1, head].astype(jnp.float32), one_hot], axis=0))


def attention_forward_kernel(width, seg_row, qkv, out, stat, q_aug, k_nat):
    heads, length = qkv.shape[1], qkv.shape[3]
    factor = HEAD_DIM**-0.5 * LOG2E
    one_hot = marks(seg_row)

    def one(head, carry):
        fill(head, qkv, one_hot, q_aug, k_nat)
        for begin in range(0, length, width):
            low, high = band(begin, width, length)
            span = slice(begin, begin + width)
            scores = jnp.dot(
                k_nat[low:high, :], q_aug[:, span], preferred_element_type=jnp.float32
            )
            peak = jnp.max(scores, axis=0, keepdims=True) * factor
            shifted = jnp.exp2(scores * factor - peak)
            total = jnp.sum(shifted, axis=0, keepdims=True)
            got = jnp.dot(
                qkv[2, head, :, low:high],
                shifted.astype(jnp.bfloat16),
                preferred_element_type=jnp.float32,
            )
            out[head, :, span] = (got * (1.0 / total)).astype(jnp.bfloat16)
            stat[head, :, span] = peak + jnp.log2(total)
        return carry

    lax.fori_loop(0, heads, one, 0, unroll=2)


def attention_backward_kernel(
    width, seg_row, qkv, stat, grad, out, q_aug, k_nat, v_nat, q_nat, g_nat, p_all, s_all
):
    heads, length = qkv.shape[1], qkv.shape[3]
    scale = HEAD_DIM**-0.5
    factor = scale * LOG2E
    one_hot = marks(seg_row)

    def one(head, carry):
        fill(head, qkv, one_hot, q_aug, k_nat)
        v_nat[...] = natural(qkv[2, head])
        q_nat[...] = natural(qkv[0, head])
        g_nat[...] = natural(grad[head])
        for begin in range(0, length, width):
            low, high = band(begin, width, length)
            span = slice(begin, begin + width)
            scores = jnp.dot(
                k_nat[low:high, :], q_aug[:, span], preferred_element_type=jnp.float32
            )
            probs = jnp.exp2(scores * factor - stat[head, :, span])
            prob_grad = jnp.dot(
                v_nat[low:high, :], grad[head, :, span], preferred_element_type=jnp.float32
            )
            row = jnp.sum(prob_grad * probs, axis=0, keepdims=True)
            score_grad = (probs * (prob_grad - row)).astype(jnp.bfloat16)
            p_all[low:high, span] = probs.astype(jnp.bfloat16)
            s_all[low:high, span] = score_grad
            got = jnp.dot(
                qkv[1, head, :, low:high], score_grad, preferred_element_type=jnp.float32
            )
            out[0, head, :, span] = (got * scale).astype(jnp.bfloat16)
        for begin in range(0, length, width):
            span = slice(begin, begin + width)
            reach = [q for q in range(0, length, width) if band(q, width, length)[0] < begin + width and band(q, width, length)[1] > begin]
            low, high = reach[0], reach[-1] + width
            key_grad = jnp.dot(
                s_all[span, low:high], q_nat[low:high, :], preferred_element_type=jnp.float32
            )
            value_grad = jnp.dot(
                p_all[span, low:high], g_nat[low:high, :], preferred_element_type=jnp.float32
            )
            out[1, head, :, span] = (key_grad * scale).T.astype(jnp.bfloat16)
            out[2, head, :, span] = value_grad.T.astype(jnp.bfloat16)
        return carry

    if width < MOST:
        p_all[...] = jnp.zeros_like(p_all)
        s_all[...] = jnp.zeros_like(s_all)
    lax.fori_loop(0, heads, one, 0, unroll=2)


VMEM = pl.BlockSpec(memory_space=pltpu.VMEM)


CHUNK = 128


def dot(left, right):
    return jnp.dot(left, right, preferred_element_type=jnp.float32)


def dot_nt(left, right):
    return lax.dot_general(
        left, right, (((1,), (1,)), ((), ())), preferred_element_type=jnp.float32
    )


def wide(value):
    return value.astype(jnp.float32)


def turn(order, value, out, work):
    count = order.shape[0]
    rows = value.shape[1] // count
    work[...] = wide(value).T
    for at in range(0, count, 2):
        pair = [
            work[pl.ds(pl.multiple_of(order[at + i] * rows, 8), rows), :] for i in range(2)
        ]
        pair = jnp.concatenate(pair, axis=0).astype(jnp.bfloat16)
        out[at * rows : (at + 2) * rows, :] = pair


def own_part(side, value, width):
    part = value[:, :width]
    for at in range(1, value.shape[1] // width):
        part = jnp.where(side == at, value[:, at * width : (at + 1) * width], part)
    return part


def accumulate(total, value):
    @pl.when(pl.program_id(0) == 0)
    def _():
        total[...] = value

    @pl.when(pl.program_id(0) > 0)
    def _():
        total[...] += value


def segment_sums(slots, seg, *values):
    marks = (slots[...] == seg[...]).astype(jnp.bfloat16)
    marks = jnp.concatenate([marks, marks], axis=1)
    sums = []
    for value in values:
        high = value.astype(jnp.bfloat16)
        low = (value - wide(high)).astype(jnp.bfloat16)
        sums.append(dot(marks, jnp.concatenate([high, low], axis=0)))
    return jnp.concatenate(sums, axis=0)


def norm_parts(value):
    width = value.shape[1]
    mean = jnp.sum(value, axis=1, keepdims=True) / width
    center = value - mean
    spread = jnp.sum(center * center, axis=1, keepdims=True) / width
    return mean, center, lax.rsqrt(spread + EPS)


def entry_kernel(order, side, picks, tables, tokens, out, mean, inverse, normed_mine, *turned):
    pick = picks[...]
    middle, center, scale = norm_parts(wide(tokens[...]))
    mean[...] = middle
    inverse[...] = scale
    value = center * scale
    normed_mine[...] = own_part(side[0], value, normed_mine.shape[1])
    value = (value * (1.0 + dot(pick, tables[1])) + dot(pick, tables[0])).astype(jnp.bfloat16)
    out[...] = value
    if turned:
        turn(order, value, *turned)


def gate_kernel(order, picks, tables, grad, out, bias, *turned):
    value = (wide(grad[...]) * dot(picks[...], tables[5])).astype(jnp.bfloat16)
    out[...] = value
    accumulate(bias, jnp.sum(wide(value), axis=0, keepdims=True))
    if turned:
        turn(order, value, *turned)


def middle_of(pick, tables, tokens, part, other, bias):
    attn_out = wide(part[...]) + wide(other[...]) + bias[...]
    return attn_out, wide(tokens[...]) + dot(pick, tables[2]) * attn_out


def middle_kernel(order, picks, tables, tokens, part, other, bias, out, mean, inverse, *turned):
    pick = picks[...]
    value = middle_of(pick, tables, tokens, part, other, bias)[1]
    middle, center, scale = norm_parts(value)
    mean[...] = middle
    inverse[...] = scale
    value = center * scale * (1.0 + dot(pick, tables[4])) + dot(pick, tables[3])
    value = value.astype(jnp.bfloat16)
    out[...] = value
    if turned:
        turn(order, value, *turned)


def middle_grad_kernel(
    order, side, picks, marks, seg, tables, tokens, part, other, bias, mean, inverse, mlp, mlp_other, grad,
    out, bias_sum, grad_mine, totals, *turned
):
    pick = picks[...]
    width = grad.shape[1]
    attn_out, value = middle_of(pick, tables, tokens, part, other, bias)
    norm = (value - mean[...]) * inverse[...]
    in_grad = wide(mlp[...]) + wide(mlp_other[...])
    value = in_grad * (1.0 + dot(pick, tables[4]))
    plain = jnp.sum(value, axis=1, keepdims=True) / width
    cross = jnp.sum(value * norm, axis=1, keepdims=True) / width
    value = wide(grad[...]) + inverse[...] * (value - plain - norm * cross)
    grad_mine[...] = own_part(side[0], value, grad_mine.shape[1])
    accumulate(totals, segment_sums(marks, seg, value * attn_out, in_grad, in_grad * norm))
    value = (value * dot(pick, tables[2])).astype(jnp.bfloat16)
    out[...] = value
    accumulate(bias_sum, jnp.sum(wide(value), axis=0, keepdims=True))
    if turned:
        turn(order, value, *turned)


def halves_kernel(side, picks, tables, part, tokens, mean, inverse, kept, sent, sums):
    value = part[...]
    width = kept.shape[1]
    kept[...] = own_part(side[0], value, width)
    sent[:, :width] = own_part(1 - side[0], value, width)
    value = wide(value) * (1.0 + dot(picks[...], tables[1]))
    norm = (wide(tokens[...]) - mean[...]) * inverse[...]
    for at, term in enumerate((value, value * norm)):
        total = jnp.sum(term, axis=1, keepdims=True)
        high = total.astype(jnp.bfloat16)
        sums[:, at : at + 1] = total
        sent[:, width + 2 * at : width + 2 * at + 1] = high
        sent[:, width + 2 * at + 1 : width + 2 * at + 2] = (total - wide(high)).astype(jnp.bfloat16)


def token_grad_kernel(
    width, picks, marks, seg, tables, kept, other, sums, normed, inverse, grad, out_t, totals
):
    mine = kept.shape[1]
    value = wide(kept[...]) + wide(other[:, :mine])
    norm = normed[...]
    accumulate(totals, segment_sums(marks, seg, value, value * norm))
    value = value * (1.0 + dot(picks[...], tables[1]))
    for at, factor in enumerate((1.0, norm)):
        rest = wide(other[:, mine + 2 * at : mine + 2 * at + 1])
        rest = rest + wide(other[:, mine + 2 * at + 1 : mine + 2 * at + 2])
        value = value - factor * ((sums[:, at : at + 1] + rest) / width)
    out_t[...] = (grad[...] + inverse[...] * value).T


def layer_kernel(
    picks, marks, seg, tables, tokens, part, other, bias, down, down_other, down_bias, grad, out, totals
):
    pick = picks[...]
    mlp_out = wide(down[...]) + wide(down_other[...]) + down_bias[...]
    middle = middle_of(pick, tables, tokens, part, other, bias)[1]
    out[...] = (middle + dot(pick, tables[5]) * mlp_out).astype(jnp.bfloat16)
    accumulate(totals, segment_sums(marks, seg, wide(grad[...]) * mlp_out))


def row_parts(sent, first):
    if first:
        return (2, 3) if sent else (0, 1)
    return (1, 3) if sent else (0, 2)


def put_rows(left, right, out, parts, product):
    quarter = left.shape[0] // 4
    columns = slice(0, right.shape[0] if product is dot_nt else right.shape[1])
    if parts[1] == parts[0] + 1:
        rows = slice(parts[0] * quarter, (parts[1] + 1) * quarter)
        out[:, columns] = product(left[rows, :], right[...]).astype(jnp.bfloat16)
        return
    for at, part in enumerate(parts):
        rows = slice(part * quarter, (part + 1) * quarter)
        value = product(left[rows, :], right[...]).astype(jnp.bfloat16)
        out[at * quarter : (at + 1) * quarter, columns] = value


def mlp_grads_kernel(sent, summed, fetched, left, right, *refs):
    sources, (first, second), rest = refs[:fetched], refs[fetched : fetched + 2], refs[fetched + 2 :]
    step = pl.program_id(0)
    copies = []
    if fetched:
        copies = [
            pltpu.make_async_copy(source, target, rest[-1].at[at])
            for at, (source, target) in enumerate(zip(sources, rest[:fetched]))
        ]

    @pl.when(step == 0)
    def _():
        for copy in copies:
            copy.start()
        put_rows(left, right, first, row_parts(sent, True), dot)

    @pl.when(step == 1)
    def _():
        put_rows(left, right, second, row_parts(sent, False), dot)
        for copy in copies:
            copy.wait()

    if summed:
        rest[0][...] = jnp.sum(wide(right[...]), axis=0, keepdims=True)


def qkv_grads_kernel(sent, left, proj_left, both, value, attended, first, second, *sums):
    step = pl.program_id(0)

    def column_sums(array):
        ones = jnp.ones((8, array.shape[1]), jnp.bfloat16)
        return dot_nt(ones, array[...])

    @pl.when(step == 0)
    def _():
        put_rows(left, both, first, row_parts(sent, True), dot_nt)
        if sums:
            sums[0][...] = column_sums(both)
            sums[1][...] = column_sums(value)

    @pl.when(step == 1)
    def _():
        second[...] = jnp.zeros_like(second)
        put_rows(left, value, second, row_parts(sent, False), dot_nt)

    @pl.when(step == 2)
    def _():
        second[...] = jnp.zeros_like(second)
        put_rows(proj_left, attended, second, row_parts(sent, False), dot_nt)


SMEM = pl.BlockSpec(memory_space=pltpu.SMEM)
GRADS = 10
FREE = pl.CostEstimate(flops=1, bytes_accessed=1, transcendentals=0)


def micros(time):
    if time == 0:
        return FREE
    return pl.CostEstimate(flops=time * 10**9, bytes_accessed=time * 10**6, transcendentals=0)


def shape(dims, dtype=jnp.bfloat16):
    return jax.ShapeDtypeStruct(dims, dtype)


def room(mib):
    return pltpu.CompilerParams(vmem_limit_bytes=mib << 20)


def spec(dims, kind):
    if kind == "v":
        return VMEM
    if kind == "r":
        return pl.BlockSpec((CHUNK, dims[1]), lambda i: (i, 0))
    if kind == "c":
        return pl.BlockSpec((dims[0], CHUNK), lambda i: (0, i))
    return pl.BlockSpec(tuple(dims), lambda i: (0,) * len(dims))


def sweep(kernel, length, scalars, arrays, outs, work=(), mib=16, cost=200):
    return pl.pallas_call(
        kernel,
        grid=(length // CHUNK,),
        in_specs=[SMEM] * len(scalars) + [spec(a.shape, kind) for a, kind in arrays],
        out_specs=[spec(o.shape, kind) for o, kind in outs],
        out_shape=[o for o, _ in outs],
        scratch_shapes=[pltpu.VMEM(dims, jnp.float32) for dims in work],
        compiler_params=room(mib),
        cost_estimate=micros(cost),
    )(*scalars, *[a for a, _ in arrays])


def mlp_grads(sent, left, right, summed=False, fetch=()):
    width, length = left.shape
    hidden = right.shape[1]
    half = hidden // 2
    out = pl.BlockSpec((width // 2, half), lambda j: (0, 0))
    sums = [pl.BlockSpec((1, half), lambda j: (0, j))] if summed else []
    sums_shape = [shape((1, hidden), jnp.float32)] if summed else []
    return pl.pallas_call(
        functools.partial(mlp_grads_kernel, sent, summed, len(fetch)),
        grid=(2,),
        in_specs=[spec(left.shape, "w"), pl.BlockSpec((length, half), lambda j: (0, j))]
        + [pl.BlockSpec(memory_space=pl.ANY)] * len(fetch),
        out_specs=[out, out] + sums + [VMEM] * len(fetch),
        out_shape=[shape((width // 2, half))] * 2
        + sums_shape
        + [pltpu.VMEM(a.shape, a.dtype) for a in fetch],
        scratch_shapes=[pltpu.SemaphoreType.DMA((len(fetch),))] if fetch else [],
        compiler_params=room(24),
        cost_estimate=micros(GRADS),
    )(left, right, *fetch)


def sum_kernel(counts, splits, *refs):
    halves, at = [], 0
    for count in counts[:2]:
        total = wide(refs[at][...])
        for ref in refs[at + 1 : at + count]:
            total += wide(ref[...])
        halves.append(total)
        at += count
    outs = refs[at + counts[2] :]
    for half in range(2):
        begin = 0 if half == 0 else halves[0].shape[1]
        columns = slice(begin, begin + halves[half].shape[1])
        for ref in refs[at : at + counts[2]]:
            halves[half] += wide(ref[:, columns])
    if splits is None:
        for out, total in zip(outs, halves):
            out[...] = total.astype(out.dtype)
    elif splits == ():
        for total, begin in zip(halves, (0, halves[0].shape[1])):
            outs[0][:, begin : begin + total.shape[1]] = total.astype(outs[0].dtype)
    else:
        for out, (half, begin, end) in zip(outs, splits):
            out[...] = halves[half][:, begin:end]


def sum_rows(halves, joined, at, count, outs, splits=None):
    arrays = halves[0] + halves[1] + joined
    arrays = [pltpu.with_memory_space_constraint(a, pltpu.HBM) for a in arrays]

    def rows(width):
        return pl.BlockSpec((count, width), lambda i: (at, 0))

    return pl.pallas_call(
        functools.partial(sum_kernel, (len(halves[0]), len(halves[1]), len(joined)), splits),
        grid=(1,),
        in_specs=[rows(a.shape[1]) for a in arrays],
        out_specs=[pl.BlockSpec(o.shape, lambda i: (0, 0)) for o in outs],
        out_shape=outs,
        compiler_params=room(16),
        cost_estimate=FREE,
    )(*arrays)


def pack_kernel(
    side, middle, late, gate, cond, proj_bias, down_bias, up_bias, qk_bias, value_bias, out, work
):
    width = out.shape[1]
    segs = cond.shape[0]
    own = [late[:segs, :], late[2 * segs : 3 * segs, :]]
    for source, at in ((middle, 0), (middle, 1), (middle, 2), (gate, 0)):
        own.append(own_part(side[0], source[2 * at * segs : (2 * at + 1) * segs, :], width))
    own += [wide(cond[:, at : at + width]) for at in range(0, cond.shape[1], width)]
    for at, value in enumerate(own):
        work[at * segs : (at + 1) * segs, :] = value
    rows = []
    for source in (proj_bias, down_bias, up_bias):
        rows += [source[0:1, at : at + width] for at in range(0, source.shape[1], width)]
    rows += [qk_bias[0:1, :width], value_bias[0:1, :]]
    first = len(own) * segs
    for at, value in enumerate(rows):
        high = wide(value.astype(jnp.bfloat16))
        work[first + at : first + at + 1, :] = high
        work[first + len(rows) + at : first + len(rows) + at + 1, :] = value - high
    out[...] = work[: out.shape[0], :].astype(jnp.bfloat16)


def finish_kernel(segs, first, held, cond, mod, modbias, bias, work):
    value = wide(held[...])
    devices, rows, width = value.shape
    left = wide(cond[...]).reshape((devices * segs, cond.shape[2])).T.astype(jnp.bfloat16)
    for at in range(mod.shape[0]):
        part = value[:, at * segs : (at + 1) * segs, :].reshape((devices * segs, width))
        mod[at] = dot(left, part.astype(jnp.bfloat16))
        modbias[at : at + 1, :] = jnp.sum(part, axis=0, keepdims=True)
    work[:rows, :] = jnp.sum(value, axis=0)
    count = bias.shape[0]
    bias[...] = work[first : first + count, :] + work[first + count : first + 2 * count, :]


def padded(width):
    return -(-width // 128) * 128


def qkv_grads(sent, left, proj_left, triple, attended):
    width, length = left.shape
    local = attended.shape[0]
    wide_block = padded(local)
    sums_spec = [pl.BlockSpec((8, 2 * local), lambda j: (0, 0)), pl.BlockSpec((8, local), lambda j: (0, 0))]
    sums_shape = [shape((8, 2 * local), jnp.float32), shape((8, local), jnp.float32)]
    return pl.pallas_call(
        functools.partial(qkv_grads_kernel, sent),
        grid=(3,),
        in_specs=[
            spec(left.shape, "w"),
            spec(left.shape, "w"),
            pl.BlockSpec((2 * local, length), lambda j: (0, 0)),
            pl.BlockSpec((local, length), lambda j: (2, 0)),
            spec(attended.shape, "w"),
        ],
        out_specs=[
            pl.BlockSpec((width // 2, 2 * local), lambda j: (0, 0)),
            pl.BlockSpec((width // 2, wide_block), lambda j: (0, jnp.maximum(j - 1, 0))),
        ]
        + sums_spec * sent,
        out_shape=[shape((width // 2, 2 * local)), shape((width // 2, 2 * wide_block))]
        + sums_shape * sent,
        compiler_params=room(32),
        cost_estimate=FREE,
    )(left, proj_left, triple, triple, attended)


def attention_forward(segments, qkv, width=256):
    heads, length = qkv.shape[1], qkv.shape[3]
    return pl.pallas_call(
        functools.partial(attention_forward_kernel, width),
        in_specs=[VMEM] * 2,
        out_specs=[VMEM] * 2,
        out_shape=[shape((heads, HEAD_DIM, length)), shape((heads, 1, length), jnp.float32)],
        scratch_shapes=[
            pltpu.VMEM((HEAD_DIM + SEGS, length), jnp.bfloat16),
            pltpu.VMEM((length, HEAD_DIM + SEGS), jnp.bfloat16),
        ],
        compiler_params=room(12),
        cost_estimate=micros(15),
    )(segments, qkv)


def attention_backward(segments, qkv, stat, grad, width=256):
    heads, length = qkv.shape[1], qkv.shape[3]
    return pl.pallas_call(
        functools.partial(attention_backward_kernel, width),
        in_specs=[VMEM] * 4,
        out_specs=VMEM,
        out_shape=shape(qkv.shape),
        scratch_shapes=[
            pltpu.VMEM((HEAD_DIM + SEGS, length), jnp.bfloat16),
            pltpu.VMEM((length, HEAD_DIM + SEGS), jnp.bfloat16),
        ]
        + [pltpu.VMEM((length, HEAD_DIM), jnp.bfloat16)] * 3
        + [pltpu.VMEM((length, length), jnp.bfloat16)] * 2,
        compiler_params=room(16),
        cost_estimate=micros(15),
    )(segments, qkv, stat, grad)


def silu(array):
    return array / (1.0 + jnp.exp(-array))


def product(spec, left, right):
    return jnp.einsum(spec, left, right, preferred_element_type=jnp.float32)


def exchange(array):
    return lax.ppermute(array, "tensor", [(0, 1), (1, 0)])


def summands(part, size):
    if size == 2:
        return part, exchange(part)
    return lax.psum(part, "tensor"), jnp.zeros_like(part)


def tensor_join(array, size):
    if size == 2:
        other = exchange(array)
        first = lax.axis_index("tensor") == 0
        return jnp.concatenate(
            [jnp.where(first, array, other), jnp.where(first, other, array)], axis=-1
        )
    return lax.all_gather(array, "tensor", axis=array.ndim - 1, tiled=True)


def partners(size, bit):
    return [(i, i ^ (1 << bit)) for i in range(size)]


def tie(*values):
    return lax.optimization_barrier(values)


def after(value, *others):
    return tie(value, *others)[0]


class Gather:
    def __init__(self, array, size, order):
        self.held, self.size, self.order = array[None], size, list(order)

    def step(self, *others):
        if self.order:
            bit = self.order.pop(0)
            self.held = after(self.held, *others)
            other = lax.ppermute(self.held, "batch", partners(self.size, bit))
            self.held = jnp.concatenate([self.held, other], axis=0)


class Sum:
    def __init__(self, sends, size, kernels):
        self.kernels = kernels
        self.sends, self.size, self.bits = sends, size, size.bit_length() - 1
        self.keeps, self.got = None, []

    def pieces(self, at, count, dtype, splits=None, outs=None):
        halves = [[self.keeps[h]] + [stage[h] for stage in self.got[:2]] for h in range(2)]
        joined = [new for (new,) in self.got[2:]]
        widths = [half[0].shape[1] for half in halves]
        if self.kernels:
            if outs is None:
                outs = [shape((count, width), dtype) for width in widths]
                if len(self.got) > 1:
                    outs, splits = [shape((count, sum(widths)), dtype)], ()
            return list(sum_rows(halves, joined, at, count, outs, splits))
        window = slice(at * count, (at + 1) * count)
        totals = [sum(a[window].astype(jnp.float32) for a in half) for half in halves]
        if len(self.got) < 2:
            return [total.astype(dtype) for total in totals]
        total = jnp.concatenate(totals, axis=1)
        total = sum((a[window].astype(jnp.float32) for a in joined), total)
        if outs is None:
            return [total.astype(dtype)]
        totals = [total[:, : widths[0]], total[:, widths[0] :]]
        return [totals[half][:, begin:end] for half, begin, end in splits]

    def send(self, *others):
        stage = len(self.got)
        sends, bits = self.sends, [stage]
        if stage > 0:
            left = self.keeps[0].shape[0] >> stage
            sends = self.pieces(1, left, jnp.bfloat16)
        if stage < 2:
            bits = [stage, 1 - stage]
        tied = tie(*sends, *others)
        self.sent = tied[: len(sends)]
        self.flying = [
            lax.ppermute(piece, "batch", partners(self.size, bit))
            for piece, bit in zip(tied, bits)
        ]
        return tied[len(sends) :]

    def take(self, *others):
        tied = tie(*self.flying, *others)
        self.got.append(tied[: len(self.flying)])
        return tied[len(self.flying) :]

    def settle(self, other):
        if len(self.got) == self.bits:
            self.keeps = list(tie(*self.keeps, other)[:2])

    def result(self, splits):
        while len(self.got) < self.bits:
            self.send()
            self.take()
        count = 2 * self.keeps[0].shape[0] // self.size
        outs = [shape((count, end - begin), jnp.float32) for _, begin, end in splits]
        return self.pieces(0, count, jnp.float32, splits, outs)


def gelu_and_slope(array):
    square = array * array
    bent = jnp.tanh(0.7978845608028654 * (array + 0.044715 * array * square))
    half = 0.5 * (1.0 + bent)
    inner = 0.7978845608028654 * (1.0 + 3.0 * 0.044715 * square)
    return array * half, half + 0.5 * array * (1.0 - bent * bent) * inner


def in_three(array):
    high = lax.reduce_precision(array, 8, 7)
    middle = lax.reduce_precision(array - high, 8, 7)
    return [high, middle, array - high - middle]


def on_device(
    n_batch,
    tokens,
    segment_ids,
    conditions,
    condition_segment,
    qkv_weight,
    qv_bias,
    proj_weight,
    proj_bias,
    up_weight,
    up_bias,
    down_weight,
    down_bias,
    mod_weight,
    mod_bias,
    out_grad,
):
    bf16, f32 = jnp.bfloat16, jnp.float32
    tokens, out_grad = tokens[0], out_grad[0]
    length, model_width = tokens.shape
    local_width = qkv_weight.shape[2]
    hidden_width = up_weight.shape[1]
    heads = local_width // HEAD_DIM
    n_tensor = model_width // local_width
    bits = list(range(n_batch.bit_length() - 1))
    block = model_width // n_batch
    in_kernel = block % 8 == 0
    index = lax.axis_index("batch")
    order = jnp.array(
        [sum((p >> bit & 1) << (bits[-1] - bit) for bit in bits) for p in range(n_batch)], jnp.int32
    )
    order = order ^ index
    side = lax.axis_index("tensor")[None]

    def run(kernel, scalars, arrays, outs):
        turned = shape((model_width, length))
        if in_kernel:
            chunk = (model_width, CHUNK)
            return sweep(kernel, length, scalars, arrays, outs + [(turned, "c")], [chunk])
        got = sweep(kernel, length, scalars, arrays, outs)
        return list(got) + [got[0].T.reshape((n_batch, block, length))[order].reshape(turned.shape)]

    def part_rows(left, sent, first):
        quarter = model_width // 4
        rows = [left[at * quarter : (at + 1) * quarter] for at in row_parts(sent, first)]
        return jnp.concatenate(rows)

    def hidden_grads(sent, left, right, summed=False, fetch=()):
        if in_kernel:
            first, second, *rest = mlp_grads(sent, left, right, summed, fetch)
            return [first, second], rest
        rest = [jnp.sum(right.astype(f32), axis=0)[None]] if summed else fetch
        cut = right.shape[1] // 2
        return [
            product("dl,lc->dc", part_rows(left, sent, True), right[:, :cut]).astype(bf16),
            product("dl,lc->dc", part_rows(left, sent, False), right[:, cut:]).astype(bf16),
        ], rest

    def attention_grads(sent, left, proj_left, triple, attended):
        if in_kernel:
            first, second, *sums = qkv_grads(sent, left, proj_left, triple, attended)
            return [first, second], sums
        sums = jnp.sum(triple.astype(f32), axis=1)[None]
        sums = (sums[:, : 2 * local_width], sums[:, 2 * local_width :])
        cut, extra = 2 * local_width, ((0, 0), (0, padded(local_width) - local_width))
        halves = [
            (part_rows(left, sent, True), triple[:cut]),
            (part_rows(left, sent, False), triple[cut:]),
            (part_rows(proj_left, sent, False), attended),
        ]
        first, value, proj = [product("dl,cl->dc", *pair).astype(bf16) for pair in halves]
        return [first, jnp.concatenate([jnp.pad(value, extra), jnp.pad(proj, extra)], axis=1)], sums

    cond_float = conditions[0].astype(f32)
    cond_act = silu(cond_float).astype(bf16)
    mod_local = product("sd,djc->jsc", cond_act, mod_weight) + mod_bias[:, None]
    modulation = tensor_join(mod_local, n_tensor)
    segs = modulation.shape[1]
    tables = jnp.concatenate(in_three(modulation) + [jnp.zeros_like(modulation)], axis=1).astype(bf16)
    slots = condition_segment[0][jnp.arange(4 * segs) % segs]
    real = jnp.arange(4 * segs) < 3 * segs
    picks = ((segment_ids[0][:, None] == slots[None]) & real[None]).astype(bf16)
    marks = jnp.concatenate([condition_segment[0], jnp.full((segs,), -1, jnp.int32)])[:, None]
    full, column = (length, model_width), shape((length, 1), f32)
    mine = (length, local_width)
    row = shape((1, model_width), f32)

    qkv_weight = qkv_weight.transpose((1, 2, 0))
    attn_in, mean_one, inverse_one, normed_mine, in_t = run(
        entry_kernel,
        [order, side],
        [(picks, "r"), (tables, "v"), (tokens, "r")],
        [(shape(full), "r"), (column, "r"), (column, "r"), (shape(mine, f32), "r")],
    )
    biases = jnp.stack([qv_bias[0], jnp.zeros_like(qv_bias[0]), qv_bias[1]])
    qkv = product("jcd,ld->jcl", qkv_weight, attn_in) + biases[:, :, None]
    qkv = qkv.astype(bf16).reshape((3, heads, HEAD_DIM, length))
    attended, stat = attention_forward(segment_ids, qkv)
    attended = attended.reshape((local_width, length))
    proj_part = product("cl,cd->ld", attended, proj_weight).astype(bf16)
    proj_part, proj_other = summands(proj_part, n_tensor)
    out_grad, proj_tied = tie(out_grad, proj_part)
    mlp_grad, down_bias_grad, grad_t = run(
        gate_kernel,
        [order],
        [(picks, "r"), (tables, "v"), (out_grad, "r")],
        [(shape(full), "r"), (row, "w")],
    )
    proj_other, mlp_grad = tie(proj_other, mlp_grad)
    middle_args = [
        (tables, "v"), (tokens, "r"), (proj_tied, "r"), (proj_other, "r"), (proj_bias[None], "v")
    ]
    mlp_in, mean_two, inverse_two, mlp_t = run(
        middle_kernel,
        [order],
        [(picks, "r")] + middle_args,
        [(shape(full), "r"), (column, "r"), (column, "r")],
    )
    hidden = product("ld,df->lf", mlp_in, up_weight) + up_bias
    active, slope = gelu_and_slope(hidden)
    active, slope = tie(active.astype(bf16), slope.astype(bf16))

    sends, _ = hidden_grads(True, grad_t, active)
    down_sum = Sum(sends, n_batch, in_kernel)
    (mlp_grad_then, active_then) = down_sum.send(mlp_grad, active)
    active_grad = product("ld,fd->lf", mlp_grad_then, down_weight)
    hidden_grad = (active_grad * slope.astype(f32)).astype(bf16)
    mlp_part = product("lf,df->ld", hidden_grad, up_weight).astype(bf16)
    mlp_part, mlp_other = summands(mlp_part, n_tensor)
    (hidden_then, mlp_tied) = tie(hidden_grad, mlp_part)
    sends, (up_bias_grad,) = hidden_grads(True, mlp_t, hidden_then, summed=True)
    up_sum = Sum(sends, n_batch, in_kernel)
    down_sum.keeps, _ = hidden_grads(False, grad_t, active_then)
    first, second, *down_sum.keeps = down_sum.take(*up_sum.sends, *down_sum.keeps)
    up_sum.sends = [first, second]
    (mlp_other, hidden_then) = down_sum.send(mlp_other, hidden_then)
    (mlp_other, hidden_then) = up_sum.send(mlp_other, hidden_then)
    attn_grad, proj_bias_grad, grad_mine, early_totals, attn_t = run(
        middle_grad_kernel,
        [order, side],
        [(picks, "r"), (marks, "v"), (segment_ids, "c")]
        + middle_args
        + [(mean_two, "r"), (inverse_two, "r"), (mlp_tied, "r"), (mlp_other, "r"), (out_grad, "r")],
        [
            (shape(full), "r"),
            (row, "w"),
            (shape(mine, f32), "r"),
            (shape((6 * segs, model_width), f32), "w"),
        ],
    )
    attended_grad = product("cd,ld->cl", proj_weight, attn_grad).astype(bf16)

    triple = attention_backward(
        segment_ids, qkv, stat, attended_grad.reshape((heads, HEAD_DIM, length))
    ).reshape((3 * local_width, length))
    up_sum.keeps, _ = hidden_grads(False, mlp_t, hidden_then)
    sends, (qk_bias_grad, value_bias_grad) = attention_grads(True, in_t, attn_t, triple, attended)
    qkv_sum = Sum(sends, n_batch, in_kernel)
    first, second, *up_sum.keeps = up_sum.take(*qkv_sum.sends, *up_sum.keeps)
    qkv_sum.sends = [first, second]
    (triple,) = down_sum.take(triple)
    (triple,) = up_sum.send(triple)
    (triple,) = qkv_sum.send(triple)
    (triple,) = down_sum.send(triple)
    attn_part = product(
        "jcl,jcd->ld", triple.reshape((3, local_width, length)), qkv_weight
    ).astype(bf16)
    kept, sent, sums = sweep(
        halves_kernel,
        length,
        [side],
        [
            (picks, "r"),
            (tables, "v"),
            (attn_part, "r"),
            (tokens, "r"),
            (mean_one, "r"),
            (inverse_one, "r"),
        ],
        [
            (shape(mine), "r"),
            (shape((length, padded(local_width + 4))), "r"),
            (shape((length, 2), f32), "r"),
        ],
        cost=0,
    )
    down_part = product("lf,fd->ld", after(active, kept), down_weight).astype(bf16)
    (kept, sent, down_part) = up_sum.take(kept, sent, down_part)
    (kept, sent) = down_sum.take(kept, sent)
    (kept, sent, triple) = up_sum.send(kept, sent, triple)
    (kept, sent, triple) = down_sum.send(kept, sent, triple)
    (mod_local, kept) = tie(mod_local, kept)
    tables_mine = jnp.concatenate(in_three(mod_local) + [jnp.zeros_like(mod_local)], axis=1).astype(bf16)
    if n_tensor == 2:
        other = exchange(sent)
    else:
        kept = lax.psum_scatter(attn_part, "tensor", scatter_dimension=1, tiled=True)
        other = jnp.zeros_like(sent)
        sums = lax.psum(sums, "tensor")
    qkv_sum.keeps, _ = attention_grads(False, in_t, attn_t, triple, attended)
    token_t, late_totals = sweep(
        functools.partial(token_grad_kernel, model_width),
        length,
        [],
        [
            (picks, "r"),
            (marks, "v"), (segment_ids, "c"),
            (tables_mine, "v"),
            (kept, "r"),
            (other, "r"),
            (sums, "r"),
            (normed_mine, "r"),
            (inverse_one, "r"),
            (grad_mine, "r"),
        ],
        [(shape((local_width, length), f32), "c"), (shape((4 * segs, local_width), f32), "w")],
        cost=0,
    )
    (late_totals, *qkv_sum.keeps) = qkv_sum.take(late_totals, *qkv_sum.keeps)
    (late_totals,) = up_sum.take(late_totals)
    (down_part, late_totals) = qkv_sum.send(down_part, late_totals)
    (down_part, late_totals) = up_sum.send(down_part, late_totals)
    (down_part,) = down_sum.take(down_part)
    down_part, down_other = summands(down_part, n_tensor)
    layer_out, gate_total = sweep(
        layer_kernel,
        length,
        [],
        [(picks, "r"), (marks, "v"), (segment_ids, "c")]
        + middle_args
        + [(down_part, "r"), (down_other, "r"), (down_bias[None], "v"), (out_grad, "r")],
        [(shape(full), "r"), (shape((2 * segs, model_width), f32), "w")],
        cost=0,
    )
    (gate_total,) = qkv_sum.take(gate_total)
    (gate_total,) = up_sum.take(gate_total)
    (gate_total,) = qkv_sum.send(gate_total)
    bias_rows = 2 * n_tensor + hidden_width // local_width + 2
    rows = (6 + n_tensor) * segs + 2 * bias_rows
    (packed,) = pl.pallas_call(
        pack_kernel,
        in_specs=[SMEM] + [VMEM] * 9,
        out_specs=[VMEM],
        out_shape=[shape((rows, local_width))],
        scratch_shapes=[pltpu.VMEM((-(-rows // 16) * 16, local_width), f32)],
        compiler_params=room(16),
        cost_estimate=FREE,
    )(
        side,
        early_totals,
        late_totals,
        gate_total,
        cond_act,
        proj_bias_grad,
        down_bias_grad,
        up_bias_grad,
        qk_bias_grad,
        value_bias_grad,
    )
    gathered = Gather(packed, n_batch, bits[:1:-1] + bits[1::-1])
    gathered.step()
    gathered.step()
    tgrad = packed[: 6 * segs].reshape((6, segs, local_width))
    gathered.step()
    qkv_sum.take()
    qkv_sum.send()
    while gathered.order:
        gathered.step()
    cond_then = after(tgrad, *qkv_sum.sent)
    down_sum.settle(qkv_sum.sent[0])
    up_sum.settle(qkv_sum.sent[0])
    cut = hidden_width // 2
    down = down_sum.result([(0, 0, cut), (1, 0, cut)])
    up = up_sum.result([(0, 0, cut), (1, 0, cut)])
    (*up, down_first, down_second) = qkv_sum.take(*up, *down)
    cond_part = product("jsc,djc->sd", cond_then, mod_weight)
    cond_part, cond_other = summands(cond_part.astype(bf16), n_tensor)
    cond_act_grad = cond_part.astype(f32) + cond_other.astype(f32)
    condition_grad = jax.vjp(silu, cond_float)[1](cond_act_grad)[0]

    held = gathered.held
    part = index * block // local_width
    cond_block = lax.dynamic_slice(
        held, (0, (6 + part) * segs, index * block % local_width), (n_batch, segs, block)
    )
    mod_sum, modbias_sum, bias_all = pl.pallas_call(
        functools.partial(finish_kernel, segs, (6 + n_tensor) * segs),
        in_specs=[VMEM] * 2,
        out_specs=[VMEM] * 3,
        out_shape=[
            shape((6, block, local_width), f32),
            shape((6, local_width), f32),
            shape((bias_rows, local_width), f32),
        ],
        scratch_shapes=[pltpu.VMEM((-(-rows // 8) * 8, local_width), f32)],
        compiler_params=room(24),
        cost_estimate=FREE,
    )(held, cond_block)
    qv_sum = bias_all[-2:]
    bias_all = bias_all[:-2].reshape(-1)
    projbias_sum = bias_all[:model_width]
    downbias_sum = bias_all[model_width : 2 * model_width]
    upbias_sum = bias_all[2 * model_width :]
    mod_sum = mod_sum.transpose((1, 0, 2))
    begin = padded(local_width)
    *last, proj_last = qkv_sum.result(
        [
            (0, 0, local_width),
            (0, local_width, 2 * local_width),
            (1, 0, local_width),
            (1, begin, begin + local_width),
        ]
    )
    last = jnp.stack(last, axis=1)
    up = jnp.concatenate(up, axis=1)
    down = jnp.concatenate([down_first, down_second], axis=1).T
    return (
        layer_out[None],
        token_t.T[None],
        condition_grad[None],
        last,
        qv_sum,
        proj_last.T,
        projbias_sum,
        up,
        upbias_sum,
        down,
        downbias_sum,
        mod_sum,
        modbias_sum,
    )


def solution(mesh):
    return jax.shard_map(
        functools.partial(on_device, mesh.shape["batch"]),
        mesh=mesh,
        in_specs=(
            P("batch", None, None),
            P("batch", None),
            P("batch", None, None),
            P("batch", None),
            P(None, None, "tensor"),
            P(None, "tensor"),
            P("tensor", None),
            P(),
            P(None, "tensor"),
            P("tensor"),
            P("tensor", None),
            P(),
            P(None, None, "tensor"),
            P(None, "tensor"),
            P("batch", None, None),
        ),
        out_specs=(
            P("batch", None, None),
            P("batch", None, "tensor"),
            P("batch", None, None),
            P("batch", None, "tensor"),
            P(None, "tensor"),
            P("tensor", "batch"),
            P(),
            P("batch", "tensor"),
            P("tensor"),
            P("tensor", "batch"),
            P(),
            P("batch", None, "tensor"),
            P(None, "tensor"),
        ),
        check_vma=False,
    )
```

```python
import functools

import jax
import jax.numpy as jnp
from jax import lax
from jax.experimental import pallas as pl
from jax.experimental.pallas import tpu as pltpu
from jax.sharding import PartitionSpec as P

EPS = 1e-06
HEAD_DIM = 72
SEGS = 8
MOST = 256
LOG2E = 1.4426950408889634
NEG = -1e30


def band(begin, width, length):
    low = max(0, (begin - MOST + 1) // 128 * 128)
    high = min(length, -(-(begin + width + MOST - 1) // 128) * 128)
    return low, high


def natural(array):
    return array.astype(jnp.float32).T.astype(jnp.bfloat16)


def marks(seg_row):
    slots = lax.broadcasted_iota(jnp.int32, (SEGS, seg_row.shape[-1]), 0)
    return (slots == seg_row[...]).astype(jnp.float32)


def fill(head, qkv, one_hot, q_aug, k_nat):
    query = jnp.concatenate([qkv[0, head].astype(jnp.float32), (1.0 - one_hot) * NEG], axis=0)
    q_aug[...] = query.astype(jnp.bfloat16)
    k_nat[...] = natural(jnp.concatenate([qkv[1, head].astype(jnp.float32), one_hot], axis=0))


def attention_forward_kernel(width, seg_row, qkv, out, stat, q_aug, k_nat):
    heads, length = qkv.shape[1], qkv.shape[3]
    factor = HEAD_DIM**-0.5 * LOG2E
    one_hot = marks(seg_row)

    def one(head, carry):
        fill(head, qkv, one_hot, q_aug, k_nat)
        for begin in range(0, length, width):
            low, high = band(begin, width, length)
            span = slice(begin, begin + width)
            scores = jnp.dot(
                k_nat[low:high, :], q_aug[:, span], preferred_element_type=jnp.float32
            )
            peak = jnp.max(scores, axis=0, keepdims=True) * factor
            shifted = jnp.exp2(scores * factor - peak)
            total = jnp.sum(shifted, axis=0, keepdims=True)
            got = jnp.dot(
                qkv[2, head, :, low:high],
                shifted.astype(jnp.bfloat16),
                preferred_element_type=jnp.float32,
            )
            out[head, :, span] = (got * (1.0 / total)).astype(jnp.bfloat16)
            stat[head, :, span] = peak + jnp.log2(total)
        return carry

    lax.fori_loop(0, heads, one, 0, unroll=2)


def attention_backward_kernel(
    width, seg_row, qkv, stat, grad, out, q_aug, k_nat, v_nat, q_nat, g_nat, p_all, s_all
):
    heads, length = qkv.shape[1], qkv.shape[3]
    scale = HEAD_DIM**-0.5
    factor = scale * LOG2E
    one_hot = marks(seg_row)

    def one(head, carry):
        fill(head, qkv, one_hot, q_aug, k_nat)
        v_nat[...] = natural(qkv[2, head])
        q_nat[...] = natural(qkv[0, head])
        g_nat[...] = natural(grad[head])
        for begin in range(0, length, width):
            low, high = band(begin, width, length)
            span = slice(begin, begin + width)
            scores = jnp.dot(
                k_nat[low:high, :], q_aug[:, span], preferred_element_type=jnp.float32
            )
            probs = jnp.exp2(scores * factor - stat[head, :, span])
            prob_grad = jnp.dot(
                v_nat[low:high, :], grad[head, :, span], preferred_element_type=jnp.float32
            )
            row = jnp.sum(prob_grad * probs, axis=0, keepdims=True)
            score_grad = (probs * (prob_grad - row)).astype(jnp.bfloat16)
            p_all[low:high, span] = probs.astype(jnp.bfloat16)
            s_all[low:high, span] = score_grad
            got = jnp.dot(
                qkv[1, head, :, low:high], score_grad, preferred_element_type=jnp.float32
            )
            out[0, head, :, span] = (got * scale).astype(jnp.bfloat16)
        for begin in range(0, length, width):
            span = slice(begin, begin + width)
            reach = [q for q in range(0, length, width) if band(q, width, length)[0] < begin + width and band(q, width, length)[1] > begin]
            low, high = reach[0], reach[-1] + width
            key_grad = jnp.dot(
                s_all[span, low:high], q_nat[low:high, :], preferred_element_type=jnp.float32
            )
            value_grad = jnp.dot(
                p_all[span, low:high], g_nat[low:high, :], preferred_element_type=jnp.float32
            )
            out[1, head, :, span] = (key_grad * scale).T.astype(jnp.bfloat16)
            out[2, head, :, span] = value_grad.T.astype(jnp.bfloat16)
        return carry

    if width < MOST:
        p_all[...] = jnp.zeros_like(p_all)
        s_all[...] = jnp.zeros_like(s_all)
    lax.fori_loop(0, heads, one, 0, unroll=2)


VMEM = pl.BlockSpec(memory_space=pltpu.VMEM)


CHUNK = 128


def dot(left, right):
    return jnp.dot(left, right, preferred_element_type=jnp.float32)


def dot_nt(left, right):
    return lax.dot_general(
        left, right, (((1,), (1,)), ((), ())), preferred_element_type=jnp.float32
    )


def wide(value):
    return value.astype(jnp.float32)


def turn(order, value, out, work):
    count = order.shape[0]
    rows = value.shape[1] // count
    work[...] = wide(value).T
    for at in range(0, count, 2):
        pair = [
            work[pl.ds(pl.multiple_of(order[at + i] * rows, 8), rows), :] for i in range(2)
        ]
        pair = jnp.concatenate(pair, axis=0).astype(jnp.bfloat16)
        out[at * rows : (at + 2) * rows, :] = pair


def own_part(side, value, width):
    part = value[:, :width]
    for at in range(1, value.shape[1] // width):
        part = jnp.where(side == at, value[:, at * width : (at + 1) * width], part)
    return part


def accumulate(total, value):
    @pl.when(pl.program_id(0) == 0)
    def _():
        total[...] = value

    @pl.when(pl.program_id(0) > 0)
    def _():
        total[...] += value


def segment_sums(slots, seg, *values):
    marks = (slots[...] == seg[...]).astype(jnp.bfloat16)
    marks = jnp.concatenate([marks, marks], axis=1)
    sums = []
    for value in values:
        high = value.astype(jnp.bfloat16)
        low = (value - wide(high)).astype(jnp.bfloat16)
        sums.append(dot(marks, jnp.concatenate([high, low], axis=0)))
    return jnp.concatenate(sums, axis=0)


def norm_parts(value):
    width = value.shape[1]
    mean = jnp.sum(value, axis=1, keepdims=True) / width
    center = value - mean
    spread = jnp.sum(center * center, axis=1, keepdims=True) / width
    return mean, center, lax.rsqrt(spread + EPS)


def entry_kernel(
    order, side, slots, seg, tables, bias, tokens,
    out, mean, inverse, normed_mine, picks, biases, *turned
):
    segs = slots.shape[0] // 2
    column = jnp.concatenate([slots[:segs, :]] * 3 + [slots[segs:, :]], axis=0)
    pick = (column == seg[...]).astype(jnp.float32).T.astype(jnp.bfloat16)
    picks[...] = pick
    biases[0:1, :] = bias[0:1, :]
    biases[1:2, :] = jnp.zeros_like(biases[1:2, :])
    biases[2:3, :] = bias[1:2, :]
    middle, center, scale = norm_parts(wide(tokens[...]))
    mean[...] = middle
    inverse[...] = scale
    value = center * scale
    normed_mine[...] = own_part(side[0], value, normed_mine.shape[1])
    value = (value * (1.0 + dot(pick, tables[1])) + dot(pick, tables[0])).astype(jnp.bfloat16)
    out[...] = value
    if turned:
        turn(order, value, *turned)


def gate_kernel(order, picks, tables, grad, out, bias, *turned):
    value = (wide(grad[...]) * dot(picks[...], tables[5])).astype(jnp.bfloat16)
    out[...] = value
    accumulate(bias, jnp.sum(wide(value), axis=0, keepdims=True))
    if turned:
        turn(order, value, *turned)


def middle_of(pick, tables, tokens, part, other, bias):
    attn_out = wide(part[...]) + wide(other[...]) + bias[...]
    return attn_out, wide(tokens[...]) + dot(pick, tables[2]) * attn_out


def middle_kernel(order, picks, tables, tokens, part, other, bias, out, mean, inverse, *turned):
    pick = picks[...]
    value = middle_of(pick, tables, tokens, part, other, bias)[1]
    middle, center, scale = norm_parts(value)
    mean[...] = middle
    inverse[...] = scale
    value = center * scale * (1.0 + dot(pick, tables[4])) + dot(pick, tables[3])
    value = value.astype(jnp.bfloat16)
    out[...] = value
    if turned:
        turn(order, value, *turned)


def middle_grad_kernel(
    order, side, picks, marks, seg, tables, tokens, part, other, bias, mean, inverse, mlp, mlp_other, grad,
    out, bias_sum, grad_mine, totals, *turned
):
    pick = picks[...]
    width = grad.shape[1]
    attn_out, value = middle_of(pick, tables, tokens, part, other, bias)
    norm = (value - mean[...]) * inverse[...]
    in_grad = wide(mlp[...]) + wide(mlp_other[...])
    value = in_grad * (1.0 + dot(pick, tables[4]))
    plain = jnp.sum(value, axis=1, keepdims=True) / width
    cross = jnp.sum(value * norm, axis=1, keepdims=True) / width
    value = wide(grad[...]) + inverse[...] * (value - plain - norm * cross)
    grad_mine[...] = own_part(side[0], value, grad_mine.shape[1])
    accumulate(totals, segment_sums(marks, seg, value * attn_out, in_grad, in_grad * norm))
    value = (value * dot(pick, tables[2])).astype(jnp.bfloat16)
    out[...] = value
    accumulate(bias_sum, jnp.sum(wide(value), axis=0, keepdims=True))
    if turned:
        turn(order, value, *turned)


def halves_kernel(side, picks, tables, part, tokens, mean, inverse, kept, sent, sums):
    value = part[...]
    width = kept.shape[1]
    kept[...] = own_part(side[0], value, width)
    sent[:, :width] = own_part(1 - side[0], value, width)
    value = wide(value) * (1.0 + dot(picks[...], tables[1]))
    norm = (wide(tokens[...]) - mean[...]) * inverse[...]
    for at, term in enumerate((value, value * norm)):
        total = jnp.sum(term, axis=1, keepdims=True)
        high = total.astype(jnp.bfloat16)
        sums[:, at : at + 1] = total
        sent[:, width + 2 * at : width + 2 * at + 1] = high
        sent[:, width + 2 * at + 1 : width + 2 * at + 2] = (total - wide(high)).astype(jnp.bfloat16)


def token_grad_kernel(
    width, picks, marks, seg, tables, kept, other, sums, normed, inverse, grad, out_t, totals
):
    mine = kept.shape[1]
    value = wide(kept[...]) + wide(other[:, :mine])
    norm = normed[...]
    accumulate(totals, segment_sums(marks, seg, value, value * norm))
    value = value * (1.0 + dot(picks[...], tables[1]))
    for at, factor in enumerate((1.0, norm)):
        rest = wide(other[:, mine + 2 * at : mine + 2 * at + 1])
        rest = rest + wide(other[:, mine + 2 * at + 1 : mine + 2 * at + 2])
        value = value - factor * ((sums[:, at : at + 1] + rest) / width)
    out_t[...] = (grad[...] + inverse[...] * value).T


def layer_kernel(
    picks, marks, seg, tables, tokens, part, other, bias, down, down_other, down_bias, grad, out, totals
):
    pick = picks[...]
    mlp_out = wide(down[...]) + wide(down_other[...]) + down_bias[...]
    middle = middle_of(pick, tables, tokens, part, other, bias)[1]
    out[...] = (middle + dot(pick, tables[5]) * mlp_out).astype(jnp.bfloat16)
    accumulate(totals, segment_sums(marks, seg, wide(grad[...]) * mlp_out))


def row_parts(sent, first):
    if first:
        return (2, 3) if sent else (0, 1)
    return (1, 3) if sent else (0, 2)


def put_rows(left, right, out, parts, product):
    quarter = left.shape[0] // 4
    columns = slice(0, right.shape[0] if product is dot_nt else right.shape[1])
    if parts[1] == parts[0] + 1:
        rows = slice(parts[0] * quarter, (parts[1] + 1) * quarter)
        out[:, columns] = product(left[rows, :], right[...]).astype(jnp.bfloat16)
        return
    for at, part in enumerate(parts):
        rows = slice(part * quarter, (part + 1) * quarter)
        value = product(left[rows, :], right[...]).astype(jnp.bfloat16)
        out[at * quarter : (at + 1) * quarter, columns] = value


def mlp_grads_kernel(sent, summed, fetched, left, right, *refs):
    sources, (first, second), rest = refs[:fetched], refs[fetched : fetched + 2], refs[fetched + 2 :]
    step = pl.program_id(0)
    copies = []
    if fetched:
        copies = [
            pltpu.make_async_copy(source, target, rest[-1].at[at])
            for at, (source, target) in enumerate(zip(sources, rest[:fetched]))
        ]

    @pl.when(step == 0)
    def _():
        for copy in copies:
            copy.start()
        put_rows(left, right, first, row_parts(sent, True), dot)

    @pl.when(step == 1)
    def _():
        put_rows(left, right, second, row_parts(sent, False), dot)
        for copy in copies:
            copy.wait()

    if summed:
        rest[0][...] = jnp.sum(wide(right[...]), axis=0, keepdims=True)


def qkv_grads_kernel(sent, left, proj_left, both, value, attended, first, second, *sums):
    step = pl.program_id(0)

    def column_sums(array):
        ones = jnp.ones((8, array.shape[1]), jnp.bfloat16)
        return dot_nt(ones, array[...])

    @pl.when(step == 0)
    def _():
        put_rows(left, both, first, row_parts(sent, True), dot_nt)
        if sums:
            sums[0][...] = column_sums(both)
            sums[1][...] = column_sums(value)

    @pl.when(step == 1)
    def _():
        second[...] = jnp.zeros_like(second)
        put_rows(left, value, second, row_parts(sent, False), dot_nt)

    @pl.when(step == 2)
    def _():
        second[...] = jnp.zeros_like(second)
        put_rows(proj_left, attended, second, row_parts(sent, False), dot_nt)


SMEM = pl.BlockSpec(memory_space=pltpu.SMEM)
GRADS = 10
FREE = pl.CostEstimate(flops=1, bytes_accessed=1, transcendentals=0)


def micros(time):
    if time == 0:
        return FREE
    return pl.CostEstimate(flops=time * 10**9, bytes_accessed=time * 10**6, transcendentals=0)


def shape(dims, dtype=jnp.bfloat16):
    return jax.ShapeDtypeStruct(dims, dtype)


def room(mib):
    return pltpu.CompilerParams(vmem_limit_bytes=mib << 20)


def spec(dims, kind):
    if kind == "v":
        return VMEM
    if kind == "r":
        return pl.BlockSpec((CHUNK, dims[1]), lambda i: (i, 0))
    if kind == "c":
        return pl.BlockSpec((dims[0], CHUNK), lambda i: (0, i))
    return pl.BlockSpec(tuple(dims), lambda i: (0,) * len(dims))


def sweep(kernel, length, scalars, arrays, outs, work=(), mib=16, cost=200):
    return pl.pallas_call(
        kernel,
        grid=(length // CHUNK,),
        in_specs=[SMEM] * len(scalars) + [spec(a.shape, kind) for a, kind in arrays],
        out_specs=[spec(o.shape, kind) for o, kind in outs],
        out_shape=[o for o, _ in outs],
        scratch_shapes=[pltpu.VMEM(dims, jnp.float32) for dims in work],
        compiler_params=room(mib),
        cost_estimate=micros(cost),
    )(*scalars, *[a for a, _ in arrays])


def mlp_grads(sent, left, right, summed=False, fetch=()):
    width, length = left.shape
    hidden = right.shape[1]
    half = hidden // 2
    out = pl.BlockSpec((width // 2, half), lambda j: (0, 0))
    sums = [pl.BlockSpec((1, half), lambda j: (0, j))] if summed else []
    sums_shape = [shape((1, hidden), jnp.float32)] if summed else []
    return pl.pallas_call(
        functools.partial(mlp_grads_kernel, sent, summed, len(fetch)),
        grid=(2,),
        in_specs=[spec(left.shape, "w"), pl.BlockSpec((length, half), lambda j: (0, j))]
        + [pl.BlockSpec(memory_space=pl.ANY)] * len(fetch),
        out_specs=[out, out] + sums + [VMEM] * len(fetch),
        out_shape=[shape((width // 2, half))] * 2
        + sums_shape
        + [pltpu.VMEM(a.shape, a.dtype) for a in fetch],
        scratch_shapes=[pltpu.SemaphoreType.DMA((len(fetch),))] if fetch else [],
        compiler_params=room(24),
        cost_estimate=micros(GRADS),
    )(left, right, *fetch)


def sum_kernel(counts, splits, *refs):
    halves, at = [], 0
    for count in counts[:2]:
        total = wide(refs[at][...])
        for ref in refs[at + 1 : at + count]:
            total += wide(ref[...])
        halves.append(total)
        at += count
    outs = refs[at + counts[2] :]
    for half in range(2):
        begin = 0 if half == 0 else halves[0].shape[1]
        columns = slice(begin, begin + halves[half].shape[1])
        for ref in refs[at : at + counts[2]]:
            halves[half] += wide(ref[:, columns])
    if splits is None:
        for out, total in zip(outs, halves):
            out[...] = total.astype(out.dtype)
    elif splits == ():
        for total, begin in zip(halves, (0, halves[0].shape[1])):
            outs[0][:, begin : begin + total.shape[1]] = total.astype(outs[0].dtype)
    else:
        for out, (half, begin, end) in zip(outs, splits):
            out[...] = halves[half][:, begin:end]


def sum_rows(halves, joined, at, count, outs, splits=None):
    arrays = halves[0] + halves[1] + joined
    arrays = [pltpu.with_memory_space_constraint(a, pltpu.HBM) for a in arrays]

    def rows(width):
        return pl.BlockSpec((count, width), lambda i: (at, 0))

    return pl.pallas_call(
        functools.partial(sum_kernel, (len(halves[0]), len(halves[1]), len(joined)), splits),
        grid=(1,),
        in_specs=[rows(a.shape[1]) for a in arrays],
        out_specs=[pl.BlockSpec(o.shape, lambda i: (0, 0)) for o in outs],
        out_shape=outs,
        compiler_params=room(16),
        cost_estimate=FREE,
    )(*arrays)


def pack_kernel(
    side, middle, late, gate, cond, proj_bias, down_bias, up_bias, qk_bias, value_bias, out, work
):
    width = out.shape[1]
    segs = cond.shape[0]
    own = [late[:segs, :], late[2 * segs : 3 * segs, :]]
    for source, at in ((middle, 0), (middle, 1), (middle, 2), (gate, 0)):
        own.append(own_part(side[0], source[2 * at * segs : (2 * at + 1) * segs, :], width))
    own += [wide(cond[:, at : at + width]) for at in range(0, cond.shape[1], width)]
    for at, value in enumerate(own):
        work[at * segs : (at + 1) * segs, :] = value
    rows = []
    for source in (proj_bias, down_bias, up_bias):
        rows += [source[0:1, at : at + width] for at in range(0, source.shape[1], width)]
    rows += [qk_bias[0:1, :width], value_bias[0:1, :]]
    first = len(own) * segs
    for at, value in enumerate(rows):
        high = wide(value.astype(jnp.bfloat16))
        work[first + at : first + at + 1, :] = high
        work[first + len(rows) + at : first + len(rows) + at + 1, :] = value - high
    out[...] = work[: out.shape[0], :].astype(jnp.bfloat16)


def finish_kernel(segs, first, held, cond, mod, modbias, bias, work):
    value = wide(held[...])
    devices, rows, width = value.shape
    left = wide(cond[...]).reshape((devices * segs, cond.shape[2])).T.astype(jnp.bfloat16)
    for at in range(mod.shape[0]):
        part = value[:, at * segs : (at + 1) * segs, :].reshape((devices * segs, width))
        mod[at] = dot(left, part.astype(jnp.bfloat16))
        modbias[at : at + 1, :] = jnp.sum(part, axis=0, keepdims=True)
    work[:rows, :] = jnp.sum(value, axis=0)
    count = bias.shape[0]
    bias[...] = work[first : first + count, :] + work[first + count : first + 2 * count, :]


def padded(width):
    return -(-width // 128) * 128


def qkv_grads(sent, left, proj_left, triple, attended):
    width, length = left.shape
    local = attended.shape[0]
    wide_block = padded(local)
    sums_spec = [pl.BlockSpec((8, 2 * local), lambda j: (0, 0)), pl.BlockSpec((8, local), lambda j: (0, 0))]
    sums_shape = [shape((8, 2 * local), jnp.float32), shape((8, local), jnp.float32)]
    return pl.pallas_call(
        functools.partial(qkv_grads_kernel, sent),
        grid=(3,),
        in_specs=[
            spec(left.shape, "w"),
            spec(left.shape, "w"),
            pl.BlockSpec((2 * local, length), lambda j: (0, 0)),
            pl.BlockSpec((local, length), lambda j: (2, 0)),
            spec(attended.shape, "w"),
        ],
        out_specs=[
            pl.BlockSpec((width // 2, 2 * local), lambda j: (0, 0)),
            pl.BlockSpec((width // 2, wide_block), lambda j: (0, jnp.maximum(j - 1, 0))),
        ]
        + sums_spec * sent,
        out_shape=[shape((width // 2, 2 * local)), shape((width // 2, 2 * wide_block))]
        + sums_shape * sent,
        compiler_params=room(32),
        cost_estimate=FREE,
    )(left, proj_left, triple, triple, attended)


def attention_forward(segments, qkv, width=256):
    heads, length = qkv.shape[1], qkv.shape[3]
    return pl.pallas_call(
        functools.partial(attention_forward_kernel, width),
        in_specs=[VMEM] * 2,
        out_specs=[VMEM] * 2,
        out_shape=[shape((heads, HEAD_DIM, length)), shape((heads, 1, length), jnp.float32)],
        scratch_shapes=[
            pltpu.VMEM((HEAD_DIM + SEGS, length), jnp.bfloat16),
            pltpu.VMEM((length, HEAD_DIM + SEGS), jnp.bfloat16),
        ],
        compiler_params=room(12),
        cost_estimate=micros(15),
    )(segments, qkv)


def attention_backward(segments, qkv, stat, grad, width=256):
    heads, length = qkv.shape[1], qkv.shape[3]
    return pl.pallas_call(
        functools.partial(attention_backward_kernel, width),
        in_specs=[VMEM] * 4,
        out_specs=VMEM,
        out_shape=shape(qkv.shape),
        scratch_shapes=[
            pltpu.VMEM((HEAD_DIM + SEGS, length), jnp.bfloat16),
            pltpu.VMEM((length, HEAD_DIM + SEGS), jnp.bfloat16),
        ]
        + [pltpu.VMEM((length, HEAD_DIM), jnp.bfloat16)] * 3
        + [pltpu.VMEM((length, length), jnp.bfloat16)] * 2,
        compiler_params=room(16),
        cost_estimate=micros(15),
    )(segments, qkv, stat, grad)


def silu(array):
    return array / (1.0 + jnp.exp(-array))


def product(spec, left, right):
    return jnp.einsum(spec, left, right, preferred_element_type=jnp.float32)


def exchange(array):
    return lax.ppermute(array, "tensor", [(0, 1), (1, 0)])


def summands(part, size):
    if size == 2:
        return part, exchange(part)
    return lax.psum(part, "tensor"), jnp.zeros_like(part)


def tensor_join(array, size):
    if size == 2:
        other = exchange(array)
        first = lax.axis_index("tensor") == 0
        return jnp.concatenate(
            [jnp.where(first, array, other), jnp.where(first, other, array)], axis=-1
        )
    return lax.all_gather(array, "tensor", axis=array.ndim - 1, tiled=True)


def partners(size, bit):
    return [(i, i ^ (1 << bit)) for i in range(size)]


def tie(*values):
    return lax.optimization_barrier(values)


def after(value, *others):
    return tie(value, *others)[0]


class Gather:
    def __init__(self, array, size, order):
        self.held, self.size, self.order = array[None], size, list(order)

    def step(self, *others):
        if self.order:
            bit = self.order.pop(0)
            self.held = after(self.held, *others)
            other = lax.ppermute(self.held, "batch", partners(self.size, bit))
            self.held = jnp.concatenate([self.held, other], axis=0)


class Sum:
    def __init__(self, sends, size, kernels):
        self.kernels = kernels
        self.sends, self.size, self.bits = sends, size, size.bit_length() - 1
        self.keeps, self.got = None, []

    def pieces(self, at, count, dtype, splits=None, outs=None):
        halves = [[self.keeps[h]] + [stage[h] for stage in self.got[:2]] for h in range(2)]
        joined = [new for (new,) in self.got[2:]]
        widths = [half[0].shape[1] for half in halves]
        if self.kernels:
            if outs is None:
                outs = [shape((count, width), dtype) for width in widths]
                if len(self.got) > 1:
                    outs, splits = [shape((count, sum(widths)), dtype)], ()
            return list(sum_rows(halves, joined, at, count, outs, splits))
        window = slice(at * count, (at + 1) * count)
        totals = [sum(a[window].astype(jnp.float32) for a in half) for half in halves]
        if len(self.got) < 2:
            return [total.astype(dtype) for total in totals]
        total = jnp.concatenate(totals, axis=1)
        total = sum((a[window].astype(jnp.float32) for a in joined), total)
        if outs is None:
            return [total.astype(dtype)]
        totals = [total[:, : widths[0]], total[:, widths[0] :]]
        return [totals[half][:, begin:end] for half, begin, end in splits]

    def send(self, *others):
        stage = len(self.got)
        sends, bits = self.sends, [stage]
        if stage > 0:
            left = self.keeps[0].shape[0] >> stage
            sends = self.pieces(1, left, jnp.bfloat16)
        if stage < 2:
            bits = [stage, 1 - stage]
        tied = tie(*sends, *others)
        self.sent = tied[: len(sends)]
        self.flying = [
            lax.ppermute(piece, "batch", partners(self.size, bit))
            for piece, bit in zip(tied, bits)
        ]
        return tied[len(sends) :]

    def take(self, *others):
        tied = tie(*self.flying, *others)
        self.got.append(tied[: len(self.flying)])
        return tied[len(self.flying) :]

    def settle(self, other):
        if len(self.got) == self.bits:
            self.keeps = list(tie(*self.keeps, other)[:2])

    def result(self, splits):
        while len(self.got) < self.bits:
            self.send()
            self.take()
        count = 2 * self.keeps[0].shape[0] // self.size
        outs = [shape((count, end - begin), jnp.float32) for _, begin, end in splits]
        return self.pieces(0, count, jnp.float32, splits, outs)


def gelu_and_slope(array):
    square = array * array
    bent = jnp.tanh(0.7978845608028654 * (array + 0.044715 * array * square))
    half = 0.5 * (1.0 + bent)
    inner = 0.7978845608028654 * (1.0 + 3.0 * 0.044715 * square)
    return array * half, half + 0.5 * array * (1.0 - bent * bent) * inner


def in_three(array):
    high = lax.reduce_precision(array, 8, 7)
    middle = lax.reduce_precision(array - high, 8, 7)
    return [high, middle, array - high - middle]


def on_device(
    n_batch,
    tokens,
    segment_ids,
    conditions,
    condition_segment,
    qkv_weight,
    qv_bias,
    proj_weight,
    proj_bias,
    up_weight,
    up_bias,
    down_weight,
    down_bias,
    mod_weight,
    mod_bias,
    out_grad,
):
    bf16, f32 = jnp.bfloat16, jnp.float32
    tokens, out_grad = tokens[0], out_grad[0]
    length, model_width = tokens.shape
    local_width = qkv_weight.shape[2]
    hidden_width = up_weight.shape[1]
    heads = local_width // HEAD_DIM
    n_tensor = model_width // local_width
    bits = list(range(n_batch.bit_length() - 1))
    block = model_width // n_batch
    in_kernel = block % 8 == 0
    index = lax.axis_index("batch")
    order = jnp.array(
        [sum((p >> bit & 1) << (bits[-1] - bit) for bit in bits) for p in range(n_batch)], jnp.int32
    )
    order = order ^ index
    side = lax.axis_index("tensor")[None]

    def run(kernel, scalars, arrays, outs):
        turned = shape((model_width, length))
        if in_kernel:
            chunk = (model_width, CHUNK)
            return sweep(kernel, length, scalars, arrays, outs + [(turned, "c")], [chunk])
        got = sweep(kernel, length, scalars, arrays, outs)
        return list(got) + [got[0].T.reshape((n_batch, block, length))[order].reshape(turned.shape)]

    def part_rows(left, sent, first):
        quarter = model_width // 4
        rows = [left[at * quarter : (at + 1) * quarter] for at in row_parts(sent, first)]
        return jnp.concatenate(rows)

    def hidden_grads(sent, left, right, summed=False, fetch=()):
        if in_kernel:
            first, second, *rest = mlp_grads(sent, left, right, summed, fetch)
            return [first, second], rest
        rest = [jnp.sum(right.astype(f32), axis=0)[None]] if summed else fetch
        cut = right.shape[1] // 2
        return [
            product("dl,lc->dc", part_rows(left, sent, True), right[:, :cut]).astype(bf16),
            product("dl,lc->dc", part_rows(left, sent, False), right[:, cut:]).astype(bf16),
        ], rest

    def attention_grads(sent, left, proj_left, triple, attended):
        if in_kernel:
            first, second, *sums = qkv_grads(sent, left, proj_left, triple, attended)
            return [first, second], sums
        sums = jnp.sum(triple.astype(f32), axis=1)[None]
        sums = (sums[:, : 2 * local_width], sums[:, 2 * local_width :])
        cut, extra = 2 * local_width, ((0, 0), (0, padded(local_width) - local_width))
        halves = [
            (part_rows(left, sent, True), triple[:cut]),
            (part_rows(left, sent, False), triple[cut:]),
            (part_rows(proj_left, sent, False), attended),
        ]
        first, value, proj = [product("dl,cl->dc", *pair).astype(bf16) for pair in halves]
        return [first, jnp.concatenate([jnp.pad(value, extra), jnp.pad(proj, extra)], axis=1)], sums

    cond_float = conditions[0].astype(f32)
    cond_act = silu(cond_float).astype(bf16)
    mod_local = product("sd,djc->jsc", cond_act, mod_weight) + mod_bias[:, None]
    modulation = tensor_join(mod_local, n_tensor)
    segs = modulation.shape[1]
    tables = jnp.concatenate(in_three(modulation) + [jnp.zeros_like(modulation)], axis=1).astype(bf16)
    marks = jnp.concatenate([condition_segment[0], jnp.full((segs,), -1, jnp.int32)])[:, None]
    full, column = (length, model_width), shape((length, 1), f32)
    mine = (length, local_width)
    row = shape((1, model_width), f32)

    qkv_weight = qkv_weight.transpose((1, 2, 0))
    attn_in, mean_one, inverse_one, normed_mine, picks, biases, in_t = run(
        entry_kernel,
        [order, side],
        [(marks, "v"), (segment_ids, "c"), (tables, "v"), (qv_bias, "v"), (tokens, "r")],
        [
            (shape(full), "r"),
            (column, "r"),
            (column, "r"),
            (shape(mine, f32), "r"),
            (shape((length, 4 * segs)), "r"),
            (shape((3, local_width), f32), "w"),
        ],
    )
    qkv = product("jcd,ld->jcl", qkv_weight, attn_in) + biases[:, :, None]
    qkv = qkv.astype(bf16).reshape((3, heads, HEAD_DIM, length))
    attended, stat = attention_forward(segment_ids, qkv)
    attended = attended.reshape((local_width, length))
    proj_part = product("cl,cd->ld", attended, proj_weight).astype(bf16)
    proj_part, proj_other = summands(proj_part, n_tensor)
    out_grad, proj_tied = tie(out_grad, proj_part)
    mlp_grad, down_bias_grad, grad_t = run(
        gate_kernel,
        [order],
        [(picks, "r"), (tables, "v"), (out_grad, "r")],
        [(shape(full), "r"), (row, "w")],
    )
    proj_other, mlp_grad = tie(proj_other, mlp_grad)
    middle_args = [
        (tables, "v"), (tokens, "r"), (proj_tied, "r"), (proj_other, "r"), (proj_bias[None], "v")
    ]
    mlp_in, mean_two, inverse_two, mlp_t = run(
        middle_kernel,
        [order],
        [(picks, "r")] + middle_args,
        [(shape(full), "r"), (column, "r"), (column, "r")],
    )
    hidden = product("ld,df->lf", mlp_in, up_weight) + up_bias
    active, slope = gelu_and_slope(hidden)
    active, slope = tie(active.astype(bf16), slope.astype(bf16))

    sends, _ = hidden_grads(True, grad_t, active)
    down_sum = Sum(sends, n_batch, in_kernel)
    (mlp_grad_then, active_then) = down_sum.send(mlp_grad, active)
    active_grad = product("ld,fd->lf", mlp_grad_then, down_weight)
    hidden_grad = (active_grad * slope.astype(f32)).astype(bf16)
    mlp_part = product("lf,df->ld", hidden_grad, up_weight).astype(bf16)
    mlp_part, mlp_other = summands(mlp_part, n_tensor)
    (hidden_then, mlp_tied) = tie(hidden_grad, mlp_part)
    sends, (up_bias_grad,) = hidden_grads(True, mlp_t, hidden_then, summed=True)
    up_sum = Sum(sends, n_batch, in_kernel)
    down_sum.keeps, _ = hidden_grads(False, grad_t, active_then)
    first, second, *down_sum.keeps = down_sum.take(*up_sum.sends, *down_sum.keeps)
    up_sum.sends = [first, second]
    (mlp_other, hidden_then) = down_sum.send(mlp_other, hidden_then)
    (mlp_other, hidden_then) = up_sum.send(mlp_other, hidden_then)
    attn_grad, proj_bias_grad, grad_mine, early_totals, attn_t = run(
        middle_grad_kernel,
        [order, side],
        [(picks, "r"), (marks, "v"), (segment_ids, "c")]
        + middle_args
        + [(mean_two, "r"), (inverse_two, "r"), (mlp_tied, "r"), (mlp_other, "r"), (out_grad, "r")],
        [
            (shape(full), "r"),
            (row, "w"),
            (shape(mine, f32), "r"),
            (shape((6 * segs, model_width), f32), "w"),
        ],
    )
    attended_grad = product("cd,ld->cl", proj_weight, attn_grad).astype(bf16)

    triple = attention_backward(
        segment_ids, qkv, stat, attended_grad.reshape((heads, HEAD_DIM, length))
    ).reshape((3 * local_width, length))
    up_sum.keeps, _ = hidden_grads(False, mlp_t, hidden_then)
    sends, (qk_bias_grad, value_bias_grad) = attention_grads(True, in_t, attn_t, triple, attended)
    qkv_sum = Sum(sends, n_batch, in_kernel)
    first, second, *up_sum.keeps = up_sum.take(*qkv_sum.sends, *up_sum.keeps)
    qkv_sum.sends = [first, second]
    (triple,) = down_sum.take(triple)
    (triple,) = up_sum.send(triple)
    (triple,) = qkv_sum.send(triple)
    (triple,) = down_sum.send(triple)
    attn_part = product(
        "jcl,jcd->ld", triple.reshape((3, local_width, length)), qkv_weight
    ).astype(bf16)
    kept, sent, sums = sweep(
        halves_kernel,
        length,
        [side],
        [
            (picks, "r"),
            (tables, "v"),
            (attn_part, "r"),
            (tokens, "r"),
            (mean_one, "r"),
            (inverse_one, "r"),
        ],
        [
            (shape(mine), "r"),
            (shape((length, padded(local_width + 4))), "r"),
            (shape((length, 2), f32), "r"),
        ],
        cost=0,
    )
    down_part = product("lf,fd->ld", after(active, kept), down_weight).astype(bf16)
    (kept, sent, down_part) = up_sum.take(kept, sent, down_part)
    (kept, sent) = down_sum.take(kept, sent)
    (kept, sent, triple) = up_sum.send(kept, sent, triple)
    (kept, sent, triple) = down_sum.send(kept, sent, triple)
    (mod_local, kept) = tie(mod_local, kept)
    tables_mine = jnp.concatenate(in_three(mod_local) + [jnp.zeros_like(mod_local)], axis=1).astype(bf16)
    if n_tensor == 2:
        other = exchange(sent)
    else:
        kept = lax.psum_scatter(attn_part, "tensor", scatter_dimension=1, tiled=True)
        other = jnp.zeros_like(sent)
        sums = lax.psum(sums, "tensor")
    qkv_sum.keeps, _ = attention_grads(False, in_t, attn_t, triple, attended)
    token_t, late_totals = sweep(
        functools.partial(token_grad_kernel, model_width),
        length,
        [],
        [
            (picks, "r"),
            (marks, "v"), (segment_ids, "c"),
            (tables_mine, "v"),
            (kept, "r"),
            (other, "r"),
            (sums, "r"),
            (normed_mine, "r"),
            (inverse_one, "r"),
            (grad_mine, "r"),
        ],
        [(shape((local_width, length), f32), "c"), (shape((4 * segs, local_width), f32), "w")],
        cost=0,
    )
    (late_totals, *qkv_sum.keeps) = qkv_sum.take(late_totals, *qkv_sum.keeps)
    (late_totals,) = up_sum.take(late_totals)
    (down_part, late_totals) = qkv_sum.send(down_part, late_totals)
    (down_part, late_totals) = up_sum.send(down_part, late_totals)
    (down_part,) = down_sum.take(down_part)
    down_part, down_other = summands(down_part, n_tensor)
    layer_out, gate_total = sweep(
        layer_kernel,
        length,
        [],
        [(picks, "r"), (marks, "v"), (segment_ids, "c")]
        + middle_args
        + [(down_part, "r"), (down_other, "r"), (down_bias[None], "v"), (out_grad, "r")],
        [(shape(full), "r"), (shape((2 * segs, model_width), f32), "w")],
        cost=0,
    )
    bias_rows = 2 * n_tensor + hidden_width // local_width + 2
    rows = (6 + n_tensor) * segs + 2 * bias_rows
    (packed,) = pl.pallas_call(
        pack_kernel,
        in_specs=[SMEM] + [VMEM] * 9,
        out_specs=[VMEM],
        out_shape=[shape((rows, local_width))],
        scratch_shapes=[pltpu.VMEM((-(-rows // 16) * 16, local_width), f32)],
        compiler_params=room(16),
        cost_estimate=FREE,
    )(
        side,
        early_totals,
        late_totals,
        gate_total,
        cond_act,
        proj_bias_grad,
        down_bias_grad,
        up_bias_grad,
        qk_bias_grad,
        value_bias_grad,
    )
    gathered = Gather(packed, n_batch, bits[:1:-1] + bits[1::-1])
    gathered.step()
    (packed, gathered.held) = qkv_sum.take(packed, gathered.held)
    (packed,) = up_sum.take(packed)
    (packed,) = qkv_sum.send(packed)
    gathered.step()
    tgrad = packed[: 6 * segs].reshape((6, segs, local_width))
    gathered.step()
    qkv_sum.take()
    qkv_sum.send()
    while gathered.order:
        gathered.step()
    cond_then = after(tgrad, *qkv_sum.sent)
    down_sum.settle(qkv_sum.sent[0])
    up_sum.settle(qkv_sum.sent[0])
    cut = hidden_width // 2
    down = down_sum.result([(0, 0, cut), (1, 0, cut)])
    up = up_sum.result([(0, 0, cut), (1, 0, cut)])
    (*up, down_first, down_second) = qkv_sum.take(*up, *down)
    cond_part = product("jsc,djc->sd", cond_then, mod_weight)
    cond_part, cond_other = summands(cond_part.astype(bf16), n_tensor)
    cond_act_grad = cond_part.astype(f32) + cond_other.astype(f32)
    condition_grad = jax.vjp(silu, cond_float)[1](cond_act_grad)[0]

    held = gathered.held
    part = index * block // local_width
    cond_block = lax.dynamic_slice(
        held, (0, (6 + part) * segs, index * block % local_width), (n_batch, segs, block)
    )
    mod_sum, modbias_sum, bias_all = pl.pallas_call(
        functools.partial(finish_kernel, segs, (6 + n_tensor) * segs),
        in_specs=[VMEM] * 2,
        out_specs=[VMEM] * 3,
        out_shape=[
            shape((6, block, local_width), f32),
            shape((6, local_width), f32),
            shape((bias_rows, local_width), f32),
        ],
        scratch_shapes=[pltpu.VMEM((-(-rows // 8) * 8, local_width), f32)],
        compiler_params=room(24),
        cost_estimate=FREE,
    )(held, cond_block)
    qv_sum = bias_all[-2:]
    bias_all = bias_all[:-2].reshape(-1)
    projbias_sum = bias_all[:model_width]
    downbias_sum = bias_all[model_width : 2 * model_width]
    upbias_sum = bias_all[2 * model_width :]
    mod_sum = mod_sum.transpose((1, 0, 2))
    begin = padded(local_width)
    *last, proj_last = qkv_sum.result(
        [
            (0, 0, local_width),
            (0, local_width, 2 * local_width),
            (1, 0, local_width),
            (1, begin, begin + local_width),
        ]
    )
    last = jnp.stack(last, axis=1)
    up = jnp.concatenate(up, axis=1)
    down = jnp.concatenate([down_first, down_second], axis=1).T
    return (
        layer_out[None],
        token_t.T[None],
        condition_grad[None],
        last,
        qv_sum,
        proj_last.T,
        projbias_sum,
        up,
        upbias_sum,
        down,
        downbias_sum,
        mod_sum,
        modbias_sum,
    )


def solution(mesh):
    return jax.shard_map(
        functools.partial(on_device, mesh.shape["batch"]),
        mesh=mesh,
        in_specs=(
            P("batch", None, None),
            P("batch", None),
            P("batch", None, None),
            P("batch", None),
            P(None, None, "tensor"),
            P(None, "tensor"),
            P("tensor", None),
            P(),
            P(None, "tensor"),
            P("tensor"),
            P("tensor", None),
            P(),
            P(None, None, "tensor"),
            P(None, "tensor"),
            P("batch", None, None),
        ),
        out_specs=(
            P("batch", None, None),
            P("batch", None, "tensor"),
            P("batch", None, None),
            P("batch", None, "tensor"),
            P(None, "tensor"),
            P("tensor", "batch"),
            P(),
            P("batch", "tensor"),
            P("tensor"),
            P("tensor", "batch"),
            P(),
            P("batch", None, "tensor"),
            P(None, "tensor"),
        ),
        check_vma=False,
    )
```

```python
import functools

import jax
import jax.numpy as jnp
from jax import lax
from jax.experimental import pallas as pl
from jax.experimental.pallas import tpu as pltpu
from jax.sharding import PartitionSpec as P

EPS = 1e-06
HEAD_DIM = 72
SEGS = 8
MOST = 256
LOG2E = 1.4426950408889634
NEG = -1e30


def band(begin, width, length):
    low = max(0, (begin - MOST + 1) // 128 * 128)
    high = min(length, -(-(begin + width + MOST - 1) // 128) * 128)
    return low, high


def natural(array):
    return array.astype(jnp.float32).T.astype(jnp.bfloat16)


def marks(seg_row):
    slots = lax.broadcasted_iota(jnp.int32, (SEGS, seg_row.shape[-1]), 0)
    return (slots == seg_row[...]).astype(jnp.float32)


def fill(head, qkv, one_hot, q_aug, k_nat):
    query = jnp.concatenate([qkv[0, head].astype(jnp.float32), (1.0 - one_hot) * NEG], axis=0)
    q_aug[...] = query.astype(jnp.bfloat16)
    k_nat[...] = natural(jnp.concatenate([qkv[1, head].astype(jnp.float32), one_hot], axis=0))


def attention_forward_kernel(width, seg_row, qkv, out, stat, q_aug, k_nat):
    heads, length = qkv.shape[1], qkv.shape[3]
    factor = HEAD_DIM**-0.5 * LOG2E
    one_hot = marks(seg_row)

    def one(head, carry):
        fill(head, qkv, one_hot, q_aug, k_nat)
        for begin in range(0, length, width):
            low, high = band(begin, width, length)
            span = slice(begin, begin + width)
            scores = jnp.dot(
                k_nat[low:high, :], q_aug[:, span], preferred_element_type=jnp.float32
            )
            peak = jnp.max(scores, axis=0, keepdims=True) * factor
            shifted = jnp.exp2(scores * factor - peak)
            total = jnp.sum(shifted, axis=0, keepdims=True)
            got = jnp.dot(
                qkv[2, head, :, low:high],
                shifted.astype(jnp.bfloat16),
                preferred_element_type=jnp.float32,
            )
            out[head, :, span] = (got * (1.0 / total)).astype(jnp.bfloat16)
            stat[head, :, span] = peak + jnp.log2(total)
        return carry

    lax.fori_loop(0, heads, one, 0, unroll=2)


def attention_backward_kernel(
    width, seg_row, qkv, stat, grad, out, q_aug, k_nat, v_nat, q_nat, g_nat, p_all, s_all
):
    heads, length = qkv.shape[1], qkv.shape[3]
    scale = HEAD_DIM**-0.5
    factor = scale * LOG2E
    one_hot = marks(seg_row)

    def one(head, carry):
        fill(head, qkv, one_hot, q_aug, k_nat)
        v_nat[...] = natural(qkv[2, head])
        q_nat[...] = natural(qkv[0, head])
        g_nat[...] = natural(grad[head])
        for begin in range(0, length, width):
            low, high = band(begin, width, length)
            span = slice(begin, begin + width)
            scores = jnp.dot(
                k_nat[low:high, :], q_aug[:, span], preferred_element_type=jnp.float32
            )
            probs = jnp.exp2(scores * factor - stat[head, :, span])
            prob_grad = jnp.dot(
                v_nat[low:high, :], grad[head, :, span], preferred_element_type=jnp.float32
            )
            row = jnp.sum(prob_grad * probs, axis=0, keepdims=True)
            score_grad = (probs * (prob_grad - row)).astype(jnp.bfloat16)
            p_all[low:high, span] = probs.astype(jnp.bfloat16)
            s_all[low:high, span] = score_grad
            got = jnp.dot(
                qkv[1, head, :, low:high], score_grad, preferred_element_type=jnp.float32
            )
            out[0, head, :, span] = (got * scale).astype(jnp.bfloat16)
        for begin in range(0, length, width):
            span = slice(begin, begin + width)
            reach = [q for q in range(0, length, width) if band(q, width, length)[0] < begin + width and band(q, width, length)[1] > begin]
            low, high = reach[0], reach[-1] + width
            key_grad = jnp.dot(
                s_all[span, low:high], q_nat[low:high, :], preferred_element_type=jnp.float32
            )
            value_grad = jnp.dot(
                p_all[span, low:high], g_nat[low:high, :], preferred_element_type=jnp.float32
            )
            out[1, head, :, span] = (key_grad * scale).T.astype(jnp.bfloat16)
            out[2, head, :, span] = value_grad.T.astype(jnp.bfloat16)
        return carry

    if width < MOST:
        p_all[...] = jnp.zeros_like(p_all)
        s_all[...] = jnp.zeros_like(s_all)
    lax.fori_loop(0, heads, one, 0, unroll=2)


VMEM = pl.BlockSpec(memory_space=pltpu.VMEM)


CHUNK = 128


def dot(left, right):
    return jnp.dot(left, right, preferred_element_type=jnp.float32)


def dot_nt(left, right):
    return lax.dot_general(
        left, right, (((1,), (1,)), ((), ())), preferred_element_type=jnp.float32
    )


def wide(value):
    return value.astype(jnp.float32)


def turn(order, value, out, work):
    count = order.shape[0]
    rows = value.shape[1] // count
    work[...] = wide(value).T
    for at in range(0, count, 2):
        pair = [
            work[pl.ds(pl.multiple_of(order[at + i] * rows, 8), rows), :] for i in range(2)
        ]
        pair = jnp.concatenate(pair, axis=0).astype(jnp.bfloat16)
        out[at * rows : (at + 2) * rows, :] = pair


def own_part(side, value, width):
    part = value[:, :width]
    for at in range(1, value.shape[1] // width):
        part = jnp.where(side == at, value[:, at * width : (at + 1) * width], part)
    return part


def accumulate(total, value):
    @pl.when(pl.program_id(0) == 0)
    def _():
        total[...] = value

    @pl.when(pl.program_id(0) > 0)
    def _():
        total[...] += value


def segment_sums(slots, seg, *values):
    marks = (slots[...] == seg[...]).astype(jnp.bfloat16)
    marks = jnp.concatenate([marks, marks], axis=1)
    sums = []
    for value in values:
        high = value.astype(jnp.bfloat16)
        low = (value - wide(high)).astype(jnp.bfloat16)
        sums.append(dot(marks, jnp.concatenate([high, low], axis=0)))
    return jnp.concatenate(sums, axis=0)


def norm_parts(value):
    width = value.shape[1]
    mean = jnp.sum(value, axis=1, keepdims=True) / width
    center = value - mean
    spread = jnp.sum(center * center, axis=1, keepdims=True) / width
    return mean, center, lax.rsqrt(spread + EPS)


def entry_kernel(
    order, side, slots, seg, tables, bias, tokens,
    out, mean, inverse, normed_mine, picks, biases, *turned
):
    segs = slots.shape[0] // 2
    column = jnp.concatenate([slots[:segs, :]] * 3 + [slots[segs:, :]], axis=0)
    pick = (column == seg[...]).astype(jnp.float32).T.astype(jnp.bfloat16)
    picks[...] = pick
    biases[0:1, :] = bias[0:1, :]
    biases[1:2, :] = jnp.zeros_like(biases[1:2, :])
    biases[2:3, :] = bias[1:2, :]
    middle, center, scale = norm_parts(wide(tokens[...]))
    mean[...] = middle
    inverse[...] = scale
    value = center * scale
    normed_mine[...] = own_part(side[0], value, normed_mine.shape[1])
    value = (value * (1.0 + dot(pick, tables[1])) + dot(pick, tables[0])).astype(jnp.bfloat16)
    out[...] = value
    if turned:
        turn(order, value, *turned)


def gate_kernel(order, picks, tables, grad, out, bias, *turned):
    value = (wide(grad[...]) * dot(picks[...], tables[5])).astype(jnp.bfloat16)
    out[...] = value
    accumulate(bias, jnp.sum(wide(value), axis=0, keepdims=True))
    if turned:
        turn(order, value, *turned)


def middle_of(pick, tables, tokens, part, other, bias):
    attn_out = wide(part[...]) + wide(other[...]) + bias[...]
    return attn_out, wide(tokens[...]) + dot(pick, tables[2]) * attn_out


def middle_kernel(order, picks, tables, tokens, part, other, bias, out, mean, inverse, *turned):
    pick = picks[...]
    value = middle_of(pick, tables, tokens, part, other, bias)[1]
    middle, center, scale = norm_parts(value)
    mean[...] = middle
    inverse[...] = scale
    value = center * scale * (1.0 + dot(pick, tables[4])) + dot(pick, tables[3])
    value = value.astype(jnp.bfloat16)
    out[...] = value
    if turned:
        turn(order, value, *turned)


def middle_grad_kernel(
    order, side, picks, marks, seg, tables, tokens, part, other, bias, mean, inverse, mlp, mlp_other, grad,
    out, bias_sum, grad_mine, totals, *turned
):
    pick = picks[...]
    width = grad.shape[1]
    attn_out, value = middle_of(pick, tables, tokens, part, other, bias)
    norm = (value - mean[...]) * inverse[...]
    in_grad = wide(mlp[...]) + wide(mlp_other[...])
    value = in_grad * (1.0 + dot(pick, tables[4]))
    plain = jnp.sum(value, axis=1, keepdims=True) / width
    cross = jnp.sum(value * norm, axis=1, keepdims=True) / width
    value = wide(grad[...]) + inverse[...] * (value - plain - norm * cross)
    grad_mine[...] = own_part(side[0], value, grad_mine.shape[1])
    accumulate(totals, segment_sums(marks, seg, value * attn_out, in_grad, in_grad * norm))
    value = (value * dot(pick, tables[2])).astype(jnp.bfloat16)
    out[...] = value
    accumulate(bias_sum, jnp.sum(wide(value), axis=0, keepdims=True))
    if turned:
        turn(order, value, *turned)


def halves_kernel(side, picks, tables, part, tokens, mean, inverse, kept, sent, sums):
    value = part[...]
    width = kept.shape[1]
    kept[...] = own_part(side[0], value, width)
    sent[:, :width] = own_part(1 - side[0], value, width)
    value = wide(value) * (1.0 + dot(picks[...], tables[1]))
    norm = (wide(tokens[...]) - mean[...]) * inverse[...]
    for at, term in enumerate((value, value * norm)):
        total = jnp.sum(term, axis=1, keepdims=True)
        high = total.astype(jnp.bfloat16)
        sums[:, at : at + 1] = total
        sent[:, width + 2 * at : width + 2 * at + 1] = high
        sent[:, width + 2 * at + 1 : width + 2 * at + 2] = (total - wide(high)).astype(jnp.bfloat16)


def token_grad_kernel(
    width, picks, marks, seg, tables, kept, other, sums, normed, inverse, grad, out_t, totals
):
    mine = kept.shape[1]
    value = wide(kept[...]) + wide(other[:, :mine])
    norm = normed[...]
    accumulate(totals, segment_sums(marks, seg, value, value * norm))
    value = value * (1.0 + dot(picks[...], tables[1]))
    for at, factor in enumerate((1.0, norm)):
        rest = wide(other[:, mine + 2 * at : mine + 2 * at + 1])
        rest = rest + wide(other[:, mine + 2 * at + 1 : mine + 2 * at + 2])
        value = value - factor * ((sums[:, at : at + 1] + rest) / width)
    out_t[...] = (grad[...] + inverse[...] * value).T


def layer_kernel(
    picks, marks, seg, tables, tokens, part, other, bias, down, down_other, down_bias, grad, out, totals
):
    pick = picks[...]
    mlp_out = wide(down[...]) + wide(down_other[...]) + down_bias[...]
    middle = middle_of(pick, tables, tokens, part, other, bias)[1]
    out[...] = (middle + dot(pick, tables[5]) * mlp_out).astype(jnp.bfloat16)
    accumulate(totals, segment_sums(marks, seg, wide(grad[...]) * mlp_out))


def row_parts(sent, first):
    if first:
        return (2, 3) if sent else (0, 1)
    return (1, 3) if sent else (0, 2)


def put_rows(left, right, out, parts, product):
    quarter = left.shape[0] // 4
    columns = slice(0, right.shape[0] if product is dot_nt else right.shape[1])
    if parts[1] == parts[0] + 1:
        rows = slice(parts[0] * quarter, (parts[1] + 1) * quarter)
        out[:, columns] = product(left[rows, :], right[...]).astype(jnp.bfloat16)
        return
    for at, part in enumerate(parts):
        rows = slice(part * quarter, (part + 1) * quarter)
        value = product(left[rows, :], right[...]).astype(jnp.bfloat16)
        out[at * quarter : (at + 1) * quarter, columns] = value


def mlp_grads_kernel(sent, summed, fetched, left, right, *refs):
    sources, (first, second), rest = refs[:fetched], refs[fetched : fetched + 2], refs[fetched + 2 :]
    step = pl.program_id(0)
    copies = []
    if fetched:
        copies = [
            pltpu.make_async_copy(source, target, rest[-1].at[at])
            for at, (source, target) in enumerate(zip(sources, rest[:fetched]))
        ]

    @pl.when(step == 0)
    def _():
        for copy in copies:
            copy.start()
        put_rows(left, right, first, row_parts(sent, True), dot)

    @pl.when(step == 1)
    def _():
        put_rows(left, right, second, row_parts(sent, False), dot)
        for copy in copies:
            copy.wait()

    if summed:
        rest[0][...] = jnp.sum(wide(right[...]), axis=0, keepdims=True)


def qkv_grads_kernel(sent, left, proj_left, both, value, attended, first, second, *sums):
    step = pl.program_id(0)

    def column_sums(array):
        ones = jnp.ones((8, array.shape[1]), jnp.bfloat16)
        return dot_nt(ones, array[...])

    @pl.when(step == 0)
    def _():
        put_rows(left, both, first, row_parts(sent, True), dot_nt)
        if sums:
            sums[0][...] = column_sums(both)
            sums[1][...] = column_sums(value)

    @pl.when(step == 1)
    def _():
        second[...] = jnp.zeros_like(second)
        put_rows(left, value, second, row_parts(sent, False), dot_nt)

    @pl.when(step == 2)
    def _():
        second[...] = jnp.zeros_like(second)
        put_rows(proj_left, attended, second, row_parts(sent, False), dot_nt)


SMEM = pl.BlockSpec(memory_space=pltpu.SMEM)
GRADS = 10
FREE = pl.CostEstimate(flops=1, bytes_accessed=1, transcendentals=0)


def micros(time):
    if time == 0:
        return FREE
    return pl.CostEstimate(flops=time * 10**9, bytes_accessed=time * 10**6, transcendentals=0)


def shape(dims, dtype=jnp.bfloat16):
    return jax.ShapeDtypeStruct(dims, dtype)


def room(mib):
    return pltpu.CompilerParams(vmem_limit_bytes=mib << 20)


def spec(dims, kind):
    if kind == "v":
        return VMEM
    if kind == "r":
        return pl.BlockSpec((CHUNK, dims[1]), lambda i: (i, 0))
    if kind == "c":
        return pl.BlockSpec((dims[0], CHUNK), lambda i: (0, i))
    return pl.BlockSpec(tuple(dims), lambda i: (0,) * len(dims))


def sweep(kernel, length, scalars, arrays, outs, work=(), mib=16, cost=200):
    return pl.pallas_call(
        kernel,
        grid=(length // CHUNK,),
        in_specs=[SMEM] * len(scalars) + [spec(a.shape, kind) for a, kind in arrays],
        out_specs=[spec(o.shape, kind) for o, kind in outs],
        out_shape=[o for o, _ in outs],
        scratch_shapes=[pltpu.VMEM(dims, jnp.float32) for dims in work],
        compiler_params=room(mib),
        cost_estimate=micros(cost),
    )(*scalars, *[a for a, _ in arrays])


def mlp_grads(sent, left, right, summed=False, fetch=()):
    width, length = left.shape
    hidden = right.shape[1]
    half = hidden // 2
    out = pl.BlockSpec((width // 2, half), lambda j: (0, 0))
    sums = [pl.BlockSpec((1, half), lambda j: (0, j))] if summed else []
    sums_shape = [shape((1, hidden), jnp.float32)] if summed else []
    return pl.pallas_call(
        functools.partial(mlp_grads_kernel, sent, summed, len(fetch)),
        grid=(2,),
        in_specs=[spec(left.shape, "w"), pl.BlockSpec((length, half), lambda j: (0, j))]
        + [pl.BlockSpec(memory_space=pl.ANY)] * len(fetch),
        out_specs=[out, out] + sums + [VMEM] * len(fetch),
        out_shape=[shape((width // 2, half))] * 2
        + sums_shape
        + [pltpu.VMEM(a.shape, a.dtype) for a in fetch],
        scratch_shapes=[pltpu.SemaphoreType.DMA((len(fetch),))] if fetch else [],
        compiler_params=room(24),
        cost_estimate=micros(GRADS),
    )(left, right, *fetch)


def sum_kernel(counts, splits, *refs):
    halves, at = [], 0
    for count in counts[:2]:
        total = wide(refs[at][...])
        for ref in refs[at + 1 : at + count]:
            total += wide(ref[...])
        halves.append(total)
        at += count
    outs = refs[at + counts[2] :]
    for half in range(2):
        begin = 0 if half == 0 else halves[0].shape[1]
        columns = slice(begin, begin + halves[half].shape[1])
        for ref in refs[at : at + counts[2]]:
            halves[half] += wide(ref[:, columns])
    if splits is None:
        for out, total in zip(outs, halves):
            out[...] = total.astype(out.dtype)
    elif splits == ():
        for total, begin in zip(halves, (0, halves[0].shape[1])):
            outs[0][:, begin : begin + total.shape[1]] = total.astype(outs[0].dtype)
    else:
        for out, (half, begin, end) in zip(outs, splits):
            out[...] = halves[half][:, begin:end]


def sum_rows(halves, joined, at, count, outs, splits=None):
    arrays = halves[0] + halves[1] + joined
    arrays = [pltpu.with_memory_space_constraint(a, pltpu.HBM) for a in arrays]

    def rows(width):
        return pl.BlockSpec((count, width), lambda i: (at, 0))

    return pl.pallas_call(
        functools.partial(sum_kernel, (len(halves[0]), len(halves[1]), len(joined)), splits),
        grid=(1,),
        in_specs=[rows(a.shape[1]) for a in arrays],
        out_specs=[pl.BlockSpec(o.shape, lambda i: (0, 0)) for o in outs],
        out_shape=outs,
        compiler_params=room(16),
        cost_estimate=FREE,
    )(*arrays)


def pack_kernel(
    side, middle, late, gate, cond, proj_bias, down_bias, up_bias, qk_bias, value_bias, out, work
):
    width = out.shape[1]
    segs = cond.shape[0]
    own = [late[:segs, :], late[2 * segs : 3 * segs, :]]
    for source, at in ((middle, 0), (middle, 1), (middle, 2), (gate, 0)):
        own.append(own_part(side[0], source[2 * at * segs : (2 * at + 1) * segs, :], width))
    own += [wide(cond[:, at : at + width]) for at in range(0, cond.shape[1], width)]
    for at, value in enumerate(own):
        work[at * segs : (at + 1) * segs, :] = value
    rows = []
    for source in (proj_bias, down_bias, up_bias):
        rows += [source[0:1, at : at + width] for at in range(0, source.shape[1], width)]
    rows += [qk_bias[0:1, :width], value_bias[0:1, :]]
    first = len(own) * segs
    for at, value in enumerate(rows):
        high = wide(value.astype(jnp.bfloat16))
        work[first + at : first + at + 1, :] = high
        work[first + len(rows) + at : first + len(rows) + at + 1, :] = value - high
    out[...] = work[: out.shape[0], :].astype(jnp.bfloat16)


def finish_kernel(segs, first, held, cond, mod, modbias, bias, work):
    value = wide(held[...])
    devices, rows, width = value.shape
    left = wide(cond[...]).reshape((devices * segs, cond.shape[2])).T.astype(jnp.bfloat16)
    for at in range(mod.shape[0]):
        part = value[:, at * segs : (at + 1) * segs, :].reshape((devices * segs, width))
        mod[at] = dot(left, part.astype(jnp.bfloat16))
        modbias[at : at + 1, :] = jnp.sum(part, axis=0, keepdims=True)
    work[:rows, :] = jnp.sum(value, axis=0)
    count = bias.shape[0]
    bias[...] = work[first : first + count, :] + work[first + count : first + 2 * count, :]


def padded(width):
    return -(-width // 128) * 128


def qkv_grads(sent, left, proj_left, triple, attended):
    width, length = left.shape
    local = attended.shape[0]
    wide_block = padded(local)
    sums_spec = [pl.BlockSpec((8, 2 * local), lambda j: (0, 0)), pl.BlockSpec((8, local), lambda j: (0, 0))]
    sums_shape = [shape((8, 2 * local), jnp.float32), shape((8, local), jnp.float32)]
    return pl.pallas_call(
        functools.partial(qkv_grads_kernel, sent),
        grid=(3,),
        in_specs=[
            spec(left.shape, "w"),
            spec(left.shape, "w"),
            pl.BlockSpec((2 * local, length), lambda j: (0, 0)),
            pl.BlockSpec((local, length), lambda j: (2, 0)),
            spec(attended.shape, "w"),
        ],
        out_specs=[
            pl.BlockSpec((width // 2, 2 * local), lambda j: (0, 0)),
            pl.BlockSpec((width // 2, wide_block), lambda j: (0, jnp.maximum(j - 1, 0))),
        ]
        + sums_spec * sent,
        out_shape=[shape((width // 2, 2 * local)), shape((width // 2, 2 * wide_block))]
        + sums_shape * sent,
        compiler_params=room(32),
        cost_estimate=FREE,
    )(left, proj_left, triple, triple, attended)


def attention_forward(segments, qkv, width=256):
    heads, length = qkv.shape[1], qkv.shape[3]
    return pl.pallas_call(
        functools.partial(attention_forward_kernel, width),
        in_specs=[VMEM] * 2,
        out_specs=[VMEM] * 2,
        out_shape=[shape((heads, HEAD_DIM, length)), shape((heads, 1, length), jnp.float32)],
        scratch_shapes=[
            pltpu.VMEM((HEAD_DIM + SEGS, length), jnp.bfloat16),
            pltpu.VMEM((length, HEAD_DIM + SEGS), jnp.bfloat16),
        ],
        compiler_params=room(12),
        cost_estimate=micros(15),
    )(segments, qkv)


def attention_backward(segments, qkv, stat, grad, width=256):
    heads, length = qkv.shape[1], qkv.shape[3]
    return pl.pallas_call(
        functools.partial(attention_backward_kernel, width),
        in_specs=[VMEM] * 4,
        out_specs=VMEM,
        out_shape=shape(qkv.shape),
        scratch_shapes=[
            pltpu.VMEM((HEAD_DIM + SEGS, length), jnp.bfloat16),
            pltpu.VMEM((length, HEAD_DIM + SEGS), jnp.bfloat16),
        ]
        + [pltpu.VMEM((length, HEAD_DIM), jnp.bfloat16)] * 3
        + [pltpu.VMEM((length, length), jnp.bfloat16)] * 2,
        compiler_params=room(16),
        cost_estimate=micros(15),
    )(segments, qkv, stat, grad)


def silu(array):
    return array / (1.0 + jnp.exp(-array))


def product(spec, left, right):
    return jnp.einsum(spec, left, right, preferred_element_type=jnp.float32)


def exchange(array):
    return lax.ppermute(array, "tensor", [(0, 1), (1, 0)])


def summands(part, size):
    if size == 2:
        return part, exchange(part)
    return lax.psum(part, "tensor"), jnp.zeros_like(part)


def tensor_join(array, size):
    if size == 2:
        other = exchange(array)
        first = lax.axis_index("tensor") == 0
        return jnp.concatenate(
            [jnp.where(first, array, other), jnp.where(first, other, array)], axis=-1
        )
    return lax.all_gather(array, "tensor", axis=array.ndim - 1, tiled=True)


def partners(size, bit):
    return [(i, i ^ (1 << bit)) for i in range(size)]


def tie(*values):
    return lax.optimization_barrier(values)


def after(value, *others):
    return tie(value, *others)[0]


class Gather:
    def __init__(self, array, size, order):
        self.held, self.size, self.order = array[None], size, list(order)

    def step(self, *others):
        if self.order:
            bit = self.order.pop(0)
            self.held = after(self.held, *others)
            other = lax.ppermute(self.held, "batch", partners(self.size, bit))
            self.held = jnp.concatenate([self.held, other], axis=0)


class Sum:
    def __init__(self, sends, size, kernels):
        self.kernels = kernels
        self.sends, self.size, self.bits = sends, size, size.bit_length() - 1
        self.keeps, self.got = None, []

    def pieces(self, at, count, dtype, splits=None, outs=None):
        halves = [[self.keeps[h]] + [stage[h] for stage in self.got[:2]] for h in range(2)]
        joined = [new for (new,) in self.got[2:]]
        widths = [half[0].shape[1] for half in halves]
        if self.kernels:
            if outs is None:
                outs = [shape((count, width), dtype) for width in widths]
                if len(self.got) > 1:
                    outs, splits = [shape((count, sum(widths)), dtype)], ()
            return list(sum_rows(halves, joined, at, count, outs, splits))
        window = slice(at * count, (at + 1) * count)
        totals = [sum(a[window].astype(jnp.float32) for a in half) for half in halves]
        if len(self.got) < 2:
            return [total.astype(dtype) for total in totals]
        total = jnp.concatenate(totals, axis=1)
        total = sum((a[window].astype(jnp.float32) for a in joined), total)
        if outs is None:
            return [total.astype(dtype)]
        totals = [total[:, : widths[0]], total[:, widths[0] :]]
        return [totals[half][:, begin:end] for half, begin, end in splits]

    def send(self, *others):
        stage = len(self.got)
        sends, bits = self.sends, [stage]
        if stage > 0:
            left = self.keeps[0].shape[0] >> stage
            sends = self.pieces(1, left, jnp.bfloat16)
        if stage < 2:
            bits = [stage, 1 - stage]
        tied = tie(*sends, *others)
        self.sent = tied[: len(sends)]
        self.flying = [
            lax.ppermute(piece, "batch", partners(self.size, bit))
            for piece, bit in zip(tied, bits)
        ]
        return tied[len(sends) :]

    def take(self, *others):
        tied = tie(*self.flying, *others)
        self.got.append(tied[: len(self.flying)])
        return tied[len(self.flying) :]

    def settle(self, other):
        if len(self.got) == self.bits:
            self.keeps = list(tie(*self.keeps, other)[:2])

    def result(self, splits):
        while len(self.got) < self.bits:
            self.send()
            self.take()
        count = 2 * self.keeps[0].shape[0] // self.size
        outs = [shape((count, end - begin), jnp.float32) for _, begin, end in splits]
        return self.pieces(0, count, jnp.float32, splits, outs)


def gelu_and_slope(array):
    square = array * array
    bent = jnp.tanh(0.7978845608028654 * (array + 0.044715 * array * square))
    half = 0.5 * (1.0 + bent)
    inner = 0.7978845608028654 * (1.0 + 3.0 * 0.044715 * square)
    return array * half, half + 0.5 * array * (1.0 - bent * bent) * inner


def in_three(array):
    high = lax.reduce_precision(array, 8, 7)
    middle = lax.reduce_precision(array - high, 8, 7)
    return [high, middle, array - high - middle]


def on_device(
    n_batch,
    tokens,
    segment_ids,
    conditions,
    condition_segment,
    qkv_weight,
    qv_bias,
    proj_weight,
    proj_bias,
    up_weight,
    up_bias,
    down_weight,
    down_bias,
    mod_weight,
    mod_bias,
    out_grad,
):
    bf16, f32 = jnp.bfloat16, jnp.float32
    tokens, out_grad = tokens[0], out_grad[0]
    length, model_width = tokens.shape
    local_width = qkv_weight.shape[2]
    hidden_width = up_weight.shape[1]
    heads = local_width // HEAD_DIM
    n_tensor = model_width // local_width
    bits = list(range(n_batch.bit_length() - 1))
    block = model_width // n_batch
    in_kernel = block % 8 == 0
    index = lax.axis_index("batch")
    order = jnp.array(
        [sum((p >> bit & 1) << (bits[-1] - bit) for bit in bits) for p in range(n_batch)], jnp.int32
    )
    order = order ^ index
    side = lax.axis_index("tensor")[None]

    def run(kernel, scalars, arrays, outs):
        turned = shape((model_width, length))
        if in_kernel:
            chunk = (model_width, CHUNK)
            return sweep(kernel, length, scalars, arrays, outs + [(turned, "c")], [chunk])
        got = sweep(kernel, length, scalars, arrays, outs)
        return list(got) + [got[0].T.reshape((n_batch, block, length))[order].reshape(turned.shape)]

    def part_rows(left, sent, first):
        quarter = model_width // 4
        rows = [left[at * quarter : (at + 1) * quarter] for at in row_parts(sent, first)]
        return jnp.concatenate(rows)

    def hidden_grads(sent, left, right, summed=False, fetch=()):
        if in_kernel:
            first, second, *rest = mlp_grads(sent, left, right, summed, fetch)
            return [first, second], rest
        rest = [jnp.sum(right.astype(f32), axis=0)[None]] if summed else fetch
        cut = right.shape[1] // 2
        return [
            product("dl,lc->dc", part_rows(left, sent, True), right[:, :cut]).astype(bf16),
            product("dl,lc->dc", part_rows(left, sent, False), right[:, cut:]).astype(bf16),
        ], rest

    def attention_grads(sent, left, proj_left, triple, attended):
        if in_kernel:
            first, second, *sums = qkv_grads(sent, left, proj_left, triple, attended)
            return [first, second], sums
        sums = jnp.sum(triple.astype(f32), axis=1)[None]
        sums = (sums[:, : 2 * local_width], sums[:, 2 * local_width :])
        cut, extra = 2 * local_width, ((0, 0), (0, padded(local_width) - local_width))
        halves = [
            (part_rows(left, sent, True), triple[:cut]),
            (part_rows(left, sent, False), triple[cut:]),
            (part_rows(proj_left, sent, False), attended),
        ]
        first, value, proj = [product("dl,cl->dc", *pair).astype(bf16) for pair in halves]
        return [first, jnp.concatenate([jnp.pad(value, extra), jnp.pad(proj, extra)], axis=1)], sums

    cond_float = conditions[0].astype(f32)
    cond_act = silu(cond_float).astype(bf16)
    mod_local = product("sd,djc->jsc", cond_act, mod_weight) + mod_bias[:, None]
    modulation = tensor_join(mod_local, n_tensor)
    segs = modulation.shape[1]
    tables = jnp.concatenate(in_three(modulation) + [jnp.zeros_like(modulation)], axis=1).astype(bf16)
    marks = jnp.concatenate([condition_segment[0], jnp.full((segs,), -1, jnp.int32)])[:, None]
    full, column = (length, model_width), shape((length, 1), f32)
    mine = (length, local_width)
    row = shape((1, model_width), f32)

    qkv_weight = qkv_weight.transpose((1, 2, 0))
    attn_in, mean_one, inverse_one, normed_mine, picks, biases, in_t = run(
        entry_kernel,
        [order, side],
        [(marks, "v"), (segment_ids, "c"), (tables, "v"), (qv_bias, "v"), (tokens, "r")],
        [
            (shape(full), "r"),
            (column, "r"),
            (column, "r"),
            (shape(mine, f32), "r"),
            (shape((length, 4 * segs)), "r"),
            (shape((3, local_width), f32), "w"),
        ],
    )
    qkv = product("jcd,ld->jcl", qkv_weight, attn_in) + biases[:, :, None]
    qkv = qkv.astype(bf16).reshape((3, heads, HEAD_DIM, length))
    attended, stat = attention_forward(segment_ids, qkv)
    attended = attended.reshape((local_width, length))
    proj_part = product("cl,cd->ld", attended, proj_weight).astype(bf16)
    proj_part, proj_other = summands(proj_part, n_tensor)
    out_grad, proj_tied = tie(out_grad, proj_part)
    mlp_grad, down_bias_grad, grad_t = run(
        gate_kernel,
        [order],
        [(picks, "r"), (tables, "v"), (out_grad, "r")],
        [(shape(full), "r"), (row, "w")],
    )
    proj_other, mlp_grad = tie(proj_other, mlp_grad)
    middle_args = [
        (tables, "v"), (tokens, "r"), (proj_tied, "r"), (proj_other, "r"), (proj_bias[None], "v")
    ]
    mlp_in, mean_two, inverse_two, mlp_t = run(
        middle_kernel,
        [order],
        [(picks, "r")] + middle_args,
        [(shape(full), "r"), (column, "r"), (column, "r")],
    )
    hidden = product("ld,df->lf", mlp_in, up_weight) + up_bias
    active, slope = gelu_and_slope(hidden)
    active, slope = tie(active.astype(bf16), slope.astype(bf16))

    sends, _ = hidden_grads(True, grad_t, active)
    down_sum = Sum(sends, n_batch, in_kernel)
    (mlp_grad_then, active_then) = down_sum.send(mlp_grad, active)
    active_grad = product("ld,fd->lf", mlp_grad_then, down_weight)
    hidden_grad = (active_grad * slope.astype(f32)).astype(bf16)
    mlp_part = product("lf,df->ld", hidden_grad, up_weight).astype(bf16)
    mlp_part, mlp_other = summands(mlp_part, n_tensor)
    (hidden_then, mlp_tied) = tie(hidden_grad, mlp_part)
    sends, (up_bias_grad,) = hidden_grads(True, mlp_t, hidden_then, summed=True)
    up_sum = Sum(sends, n_batch, in_kernel)
    down_sum.keeps, _ = hidden_grads(False, grad_t, active_then)
    first, second, *down_sum.keeps = down_sum.take(*up_sum.sends, *down_sum.keeps)
    up_sum.sends = [first, second]
    (mlp_other, hidden_then) = down_sum.send(mlp_other, hidden_then)
    (mlp_other, hidden_then) = up_sum.send(mlp_other, hidden_then)
    attn_grad, proj_bias_grad, grad_mine, early_totals, attn_t = run(
        middle_grad_kernel,
        [order, side],
        [(picks, "r"), (marks, "v"), (segment_ids, "c")]
        + middle_args
        + [(mean_two, "r"), (inverse_two, "r"), (mlp_tied, "r"), (mlp_other, "r"), (out_grad, "r")],
        [
            (shape(full), "r"),
            (row, "w"),
            (shape(mine, f32), "r"),
            (shape((6 * segs, model_width), f32), "w"),
        ],
    )
    attended_grad = product("cd,ld->cl", proj_weight, attn_grad).astype(bf16)

    triple = attention_backward(
        segment_ids, qkv, stat, attended_grad.reshape((heads, HEAD_DIM, length))
    ).reshape((3 * local_width, length))
    up_sum.keeps, _ = hidden_grads(False, mlp_t, hidden_then)
    sends, (qk_bias_grad, value_bias_grad) = attention_grads(True, in_t, attn_t, triple, attended)
    qkv_sum = Sum(sends, n_batch, in_kernel)
    first, second, *up_sum.keeps = up_sum.take(*qkv_sum.sends, *up_sum.keeps)
    qkv_sum.sends = [first, second]
    (triple,) = down_sum.take(triple)
    (triple,) = up_sum.send(triple)
    (triple,) = qkv_sum.send(triple)
    (triple,) = down_sum.send(triple)
    attn_part = product(
        "jcl,jcd->ld", triple.reshape((3, local_width, length)), qkv_weight
    ).astype(bf16)
    kept, sent, sums = sweep(
        halves_kernel,
        length,
        [side],
        [
            (picks, "r"),
            (tables, "v"),
            (attn_part, "r"),
            (tokens, "r"),
            (mean_one, "r"),
            (inverse_one, "r"),
        ],
        [
            (shape(mine), "r"),
            (shape((length, padded(local_width + 4))), "r"),
            (shape((length, 2), f32), "r"),
        ],
        cost=0,
    )
    down_part = product("lf,fd->ld", after(active, kept), down_weight).astype(bf16)
    (kept, sent, down_part) = up_sum.take(kept, sent, down_part)
    (kept, sent) = down_sum.take(kept, sent)
    (kept, sent, triple) = up_sum.send(kept, sent, triple)
    (kept, sent, triple) = down_sum.send(kept, sent, triple)
    (mod_local, kept) = tie(mod_local, kept)
    tables_mine = jnp.concatenate(in_three(mod_local) + [jnp.zeros_like(mod_local)], axis=1).astype(bf16)
    if n_tensor == 2:
        other = exchange(sent)
    else:
        kept = lax.psum_scatter(attn_part, "tensor", scatter_dimension=1, tiled=True)
        other = jnp.zeros_like(sent)
        sums = lax.psum(sums, "tensor")
    qkv_sum.keeps, _ = attention_grads(False, in_t, attn_t, triple, attended)
    token_t, late_totals = sweep(
        functools.partial(token_grad_kernel, model_width),
        length,
        [],
        [
            (picks, "r"),
            (marks, "v"), (segment_ids, "c"),
            (tables_mine, "v"),
            (kept, "r"),
            (other, "r"),
            (sums, "r"),
            (normed_mine, "r"),
            (inverse_one, "r"),
            (grad_mine, "r"),
        ],
        [(shape((local_width, length), f32), "c"), (shape((4 * segs, local_width), f32), "w")],
        cost=0,
    )
    (late_totals, *qkv_sum.keeps) = qkv_sum.take(late_totals, *qkv_sum.keeps)
    (late_totals,) = up_sum.take(late_totals)
    (down_part, late_totals) = qkv_sum.send(down_part, late_totals)
    (down_part, late_totals) = up_sum.send(down_part, late_totals)
    (down_part,) = down_sum.take(down_part)
    down_part, down_other = summands(down_part, n_tensor)
    layer_out, gate_total = sweep(
        layer_kernel,
        length,
        [],
        [(picks, "r"), (marks, "v"), (segment_ids, "c")]
        + middle_args
        + [(down_part, "r"), (down_other, "r"), (down_bias[None], "v"), (out_grad, "r")],
        [(shape(full), "r"), (shape((2 * segs, model_width), f32), "w")],
        cost=0,
    )
    (gate_total,) = up_sum.take(gate_total)
    bias_rows = 2 * n_tensor + hidden_width // local_width + 2
    rows = (6 + n_tensor) * segs + 2 * bias_rows
    (packed,) = pl.pallas_call(
        pack_kernel,
        in_specs=[SMEM] + [VMEM] * 9,
        out_specs=[VMEM],
        out_shape=[shape((rows, local_width))],
        scratch_shapes=[pltpu.VMEM((-(-rows // 16) * 16, local_width), f32)],
        compiler_params=room(16),
        cost_estimate=FREE,
    )(
        side,
        early_totals,
        late_totals,
        gate_total,
        cond_act,
        proj_bias_grad,
        down_bias_grad,
        up_bias_grad,
        qk_bias_grad,
        value_bias_grad,
    )
    gathered = Gather(packed, n_batch, bits[:1:-1] + bits[1::-1])
    gathered.step()
    (packed, gathered.held) = qkv_sum.take(packed, gathered.held)
    (packed,) = qkv_sum.send(packed)
    gathered.step()
    tgrad = packed[: 6 * segs].reshape((6, segs, local_width))
    gathered.step()
    (gathered.held,) = qkv_sum.take(gathered.held)
    qkv_sum.send()
    while gathered.order:
        gathered.step()
    down_sum.settle(qkv_sum.sent[0])
    up_sum.settle(qkv_sum.sent[0])
    cut = hidden_width // 2
    down = down_sum.result([(0, 0, cut), (1, 0, cut)])
    up = up_sum.result([(0, 0, cut), (1, 0, cut)])
    (*up, down_first, down_second) = qkv_sum.take(*up, *down)
    cond_then = after(tgrad, *qkv_sum.got[-1])
    cond_part = product("jsc,djc->sd", cond_then, mod_weight)
    cond_part, cond_other = summands(cond_part.astype(bf16), n_tensor)
    cond_act_grad = cond_part.astype(f32) + cond_other.astype(f32)
    condition_grad = jax.vjp(silu, cond_float)[1](cond_act_grad)[0]

    held = gathered.held
    part = index * block // local_width
    cond_block = lax.dynamic_slice(
        held, (0, (6 + part) * segs, index * block % local_width), (n_batch, segs, block)
    )
    mod_sum, modbias_sum, bias_all = pl.pallas_call(
        functools.partial(finish_kernel, segs, (6 + n_tensor) * segs),
        in_specs=[VMEM] * 2,
        out_specs=[VMEM] * 3,
        out_shape=[
            shape((6, block, local_width), f32),
            shape((6, local_width), f32),
            shape((bias_rows, local_width), f32),
        ],
        scratch_shapes=[pltpu.VMEM((-(-rows // 8) * 8, local_width), f32)],
        compiler_params=room(24),
        cost_estimate=FREE,
    )(held, cond_block)
    qv_sum = bias_all[-2:]
    bias_all = bias_all[:-2].reshape(-1)
    projbias_sum = bias_all[:model_width]
    downbias_sum = bias_all[model_width : 2 * model_width]
    upbias_sum = bias_all[2 * model_width :]
    mod_sum = mod_sum.transpose((1, 0, 2))
    begin = padded(local_width)
    *last, proj_last = qkv_sum.result(
        [
            (0, 0, local_width),
            (0, local_width, 2 * local_width),
            (1, 0, local_width),
            (1, begin, begin + local_width),
        ]
    )
    last = jnp.stack(last, axis=1)
    up = jnp.concatenate(up, axis=1)
    down = jnp.concatenate([down_first, down_second], axis=1).T
    return (
        layer_out[None],
        token_t.T[None],
        condition_grad[None],
        last,
        qv_sum,
        proj_last.T,
        projbias_sum,
        up,
        upbias_sum,
        down,
        downbias_sum,
        mod_sum,
        modbias_sum,
    )


def solution(mesh):
    return jax.shard_map(
        functools.partial(on_device, mesh.shape["batch"]),
        mesh=mesh,
        in_specs=(
            P("batch", None, None),
            P("batch", None),
            P("batch", None, None),
            P("batch", None),
            P(None, None, "tensor"),
            P(None, "tensor"),
            P("tensor", None),
            P(),
            P(None, "tensor"),
            P("tensor"),
            P("tensor", None),
            P(),
            P(None, None, "tensor"),
            P(None, "tensor"),
            P("batch", None, None),
        ),
        out_specs=(
            P("batch", None, None),
            P("batch", None, "tensor"),
            P("batch", None, None),
            P("batch", None, "tensor"),
            P(None, "tensor"),
            P("tensor", "batch"),
            P(),
            P("batch", "tensor"),
            P("tensor"),
            P("tensor", "batch"),
            P(),
            P("batch", None, "tensor"),
            P(None, "tensor"),
        ),
        check_vma=False,
    )
```

```python
import functools

import jax
import jax.numpy as jnp
from jax import lax
from jax.experimental import pallas as pl
from jax.experimental.pallas import tpu as pltpu
from jax.sharding import PartitionSpec as P

EPS = 1e-06
HEAD_DIM = 72
SEGS = 8
MOST = 256
LOG2E = 1.4426950408889634
NEG = -1e30


def band(begin, width, length):
    low = max(0, (begin - MOST + 1) // 128 * 128)
    high = min(length, -(-(begin + width + MOST - 1) // 128) * 128)
    return low, high


def natural(array):
    return array.astype(jnp.float32).T.astype(jnp.bfloat16)


def marks(seg_row):
    slots = lax.broadcasted_iota(jnp.int32, (SEGS, seg_row.shape[-1]), 0)
    return (slots == seg_row[...]).astype(jnp.float32)


def fill(head, qkv, one_hot, q_aug, k_nat):
    query = jnp.concatenate([qkv[0, head].astype(jnp.float32), (1.0 - one_hot) * NEG], axis=0)
    q_aug[...] = query.astype(jnp.bfloat16)
    k_nat[...] = natural(jnp.concatenate([qkv[1, head].astype(jnp.float32), one_hot], axis=0))


def attention_forward_kernel(width, seg_row, qkv, out, stat, q_aug, k_nat):
    heads, length = qkv.shape[1], qkv.shape[3]
    factor = HEAD_DIM**-0.5 * LOG2E
    one_hot = marks(seg_row)

    def one(head, carry):
        fill(head, qkv, one_hot, q_aug, k_nat)
        for begin in range(0, length, width):
            low, high = band(begin, width, length)
            span = slice(begin, begin + width)
            scores = jnp.dot(
                k_nat[low:high, :], q_aug[:, span], preferred_element_type=jnp.float32
            )
            peak = jnp.max(scores, axis=0, keepdims=True) * factor
            shifted = jnp.exp2(scores * factor - peak)
            total = jnp.sum(shifted, axis=0, keepdims=True)
            got = jnp.dot(
                qkv[2, head, :, low:high],
                shifted.astype(jnp.bfloat16),
                preferred_element_type=jnp.float32,
            )
            out[head, :, span] = (got * (1.0 / total)).astype(jnp.bfloat16)
            stat[head, :, span] = peak + jnp.log2(total)
        return carry

    lax.fori_loop(0, heads, one, 0, unroll=2)


def attention_backward_kernel(
    width, seg_row, qkv, stat, grad, out, q_aug, k_nat, v_nat, q_nat, g_nat, p_all, s_all
):
    heads, length = qkv.shape[1], qkv.shape[3]
    scale = HEAD_DIM**-0.5
    factor = scale * LOG2E
    one_hot = marks(seg_row)

    def one(head, carry):
        fill(head, qkv, one_hot, q_aug, k_nat)
        v_nat[...] = natural(qkv[2, head])
        q_nat[...] = natural(qkv[0, head])
        g_nat[...] = natural(grad[head])
        for begin in range(0, length, width):
            low, high = band(begin, width, length)
            span = slice(begin, begin + width)
            scores = jnp.dot(
                k_nat[low:high, :], q_aug[:, span], preferred_element_type=jnp.float32
            )
            probs = jnp.exp2(scores * factor - stat[head, :, span])
            prob_grad = jnp.dot(
                v_nat[low:high, :], grad[head, :, span], preferred_element_type=jnp.float32
            )
            row = jnp.sum(prob_grad * probs, axis=0, keepdims=True)
            score_grad = (probs * (prob_grad - row)).astype(jnp.bfloat16)
            p_all[low:high, span] = probs.astype(jnp.bfloat16)
            s_all[low:high, span] = score_grad
            got = jnp.dot(
                qkv[1, head, :, low:high], score_grad, preferred_element_type=jnp.float32
            )
            out[0, head, :, span] = (got * scale).astype(jnp.bfloat16)
        for begin in range(0, length, width):
            span = slice(begin, begin + width)
            reach = [q for q in range(0, length, width) if band(q, width, length)[0] < begin + width and band(q, width, length)[1] > begin]
            low, high = reach[0], reach[-1] + width
            key_grad = jnp.dot(
                s_all[span, low:high], q_nat[low:high, :], preferred_element_type=jnp.float32
            )
            value_grad = jnp.dot(
                p_all[span, low:high], g_nat[low:high, :], preferred_element_type=jnp.float32
            )
            out[1, head, :, span] = (key_grad * scale).T.astype(jnp.bfloat16)
            out[2, head, :, span] = value_grad.T.astype(jnp.bfloat16)
        return carry

    if width < MOST:
        p_all[...] = jnp.zeros_like(p_all)
        s_all[...] = jnp.zeros_like(s_all)
    lax.fori_loop(0, heads, one, 0, unroll=2)


VMEM = pl.BlockSpec(memory_space=pltpu.VMEM)


CHUNK = 128


def dot(left, right):
    return jnp.dot(left, right, preferred_element_type=jnp.float32)


def dot_nt(left, right):
    return lax.dot_general(
        left, right, (((1,), (1,)), ((), ())), preferred_element_type=jnp.float32
    )


def wide(value):
    return value.astype(jnp.float32)


def turn(order, value, out, work):
    count = order.shape[0]
    rows = value.shape[1] // count
    work[...] = wide(value).T
    for at in range(0, count, 2):
        pair = [
            work[pl.ds(pl.multiple_of(order[at + i] * rows, 8), rows), :] for i in range(2)
        ]
        pair = jnp.concatenate(pair, axis=0).astype(jnp.bfloat16)
        out[at * rows : (at + 2) * rows, :] = pair


def own_part(side, value, width):
    part = value[:, :width]
    for at in range(1, value.shape[1] // width):
        part = jnp.where(side == at, value[:, at * width : (at + 1) * width], part)
    return part


def accumulate(total, value):
    @pl.when(pl.program_id(0) == 0)
    def _():
        total[...] = value

    @pl.when(pl.program_id(0) > 0)
    def _():
        total[...] += value


def segment_sums(slots, seg, *values):
    marks = (slots[...] == seg[...]).astype(jnp.bfloat16)
    marks = jnp.concatenate([marks, marks], axis=1)
    sums = []
    for value in values:
        high = value.astype(jnp.bfloat16)
        low = (value - wide(high)).astype(jnp.bfloat16)
        sums.append(dot(marks, jnp.concatenate([high, low], axis=0)))
    return jnp.concatenate(sums, axis=0)


def norm_parts(value):
    width = value.shape[1]
    mean = jnp.sum(value, axis=1, keepdims=True) / width
    center = value - mean
    spread = jnp.sum(center * center, axis=1, keepdims=True) / width
    return mean, center, lax.rsqrt(spread + EPS)


def entry_kernel(
    order, side, slots, seg, tables, bias, tokens,
    out, mean, inverse, normed_mine, picks, biases, *turned
):
    segs = slots.shape[0] // 2
    column = jnp.concatenate([slots[:segs, :]] * 3 + [slots[segs:, :]], axis=0)
    pick = (column == seg[...]).astype(jnp.float32).T.astype(jnp.bfloat16)
    picks[...] = pick
    biases[0:1, :] = bias[0:1, :]
    biases[1:2, :] = jnp.zeros_like(biases[1:2, :])
    biases[2:3, :] = bias[1:2, :]
    middle, center, scale = norm_parts(wide(tokens[...]))
    mean[...] = middle
    inverse[...] = scale
    value = center * scale
    normed_mine[...] = own_part(side[0], value, normed_mine.shape[1])
    value = (value * (1.0 + dot(pick, tables[1])) + dot(pick, tables[0])).astype(jnp.bfloat16)
    out[...] = value
    if turned:
        turn(order, value, *turned)


def gate_kernel(order, picks, tables, grad, out, bias, *turned):
    value = (wide(grad[...]) * dot(picks[...], tables[5])).astype(jnp.bfloat16)
    out[...] = value
    accumulate(bias, jnp.sum(wide(value), axis=0, keepdims=True))
    if turned:
        turn(order, value, *turned)


def middle_of(pick, tables, tokens, part, other, bias):
    attn_out = wide(part[...]) + wide(other[...]) + bias[...]
    return attn_out, wide(tokens[...]) + dot(pick, tables[2]) * attn_out


def middle_kernel(order, picks, tables, tokens, part, other, bias, out, mean, inverse, *turned):
    pick = picks[...]
    value = middle_of(pick, tables, tokens, part, other, bias)[1]
    middle, center, scale = norm_parts(value)
    mean[...] = middle
    inverse[...] = scale
    value = center * scale * (1.0 + dot(pick, tables[4])) + dot(pick, tables[3])
    value = value.astype(jnp.bfloat16)
    out[...] = value
    if turned:
        turn(order, value, *turned)


def middle_grad_kernel(
    order, side, picks, marks, seg, tables, tokens, part, other, bias, mean, inverse, mlp, mlp_other, grad,
    out, bias_sum, grad_mine, totals, *turned
):
    pick = picks[...]
    width = grad.shape[1]
    attn_out, value = middle_of(pick, tables, tokens, part, other, bias)
    norm = (value - mean[...]) * inverse[...]
    in_grad = wide(mlp[...]) + wide(mlp_other[...])
    value = in_grad * (1.0 + dot(pick, tables[4]))
    plain = jnp.sum(value, axis=1, keepdims=True) / width
    cross = jnp.sum(value * norm, axis=1, keepdims=True) / width
    value = wide(grad[...]) + inverse[...] * (value - plain - norm * cross)
    grad_mine[...] = own_part(side[0], value, grad_mine.shape[1])
    accumulate(totals, segment_sums(marks, seg, value * attn_out, in_grad, in_grad * norm))
    value = (value * dot(pick, tables[2])).astype(jnp.bfloat16)
    out[...] = value
    accumulate(bias_sum, jnp.sum(wide(value), axis=0, keepdims=True))
    if turned:
        turn(order, value, *turned)


def halves_kernel(side, picks, tables, part, tokens, mean, inverse, kept, sent, sums):
    value = part[...]
    width = kept.shape[1]
    kept[...] = own_part(side[0], value, width)
    sent[:, :width] = own_part(1 - side[0], value, width)
    value = wide(value) * (1.0 + dot(picks[...], tables[1]))
    norm = (wide(tokens[...]) - mean[...]) * inverse[...]
    for at, term in enumerate((value, value * norm)):
        total = jnp.sum(term, axis=1, keepdims=True)
        high = total.astype(jnp.bfloat16)
        sums[:, at : at + 1] = total
        sent[:, width + 2 * at : width + 2 * at + 1] = high
        sent[:, width + 2 * at + 1 : width + 2 * at + 2] = (total - wide(high)).astype(jnp.bfloat16)


def token_grad_kernel(
    width, picks, marks, seg, tables, kept, other, sums, normed, inverse, grad, out_t, totals
):
    mine = kept.shape[1]
    value = wide(kept[...]) + wide(other[:, :mine])
    norm = normed[...]
    accumulate(totals, segment_sums(marks, seg, value, value * norm))
    value = value * (1.0 + dot(picks[...], tables[1]))
    for at, factor in enumerate((1.0, norm)):
        rest = wide(other[:, mine + 2 * at : mine + 2 * at + 1])
        rest = rest + wide(other[:, mine + 2 * at + 1 : mine + 2 * at + 2])
        value = value - factor * ((sums[:, at : at + 1] + rest) / width)
    out_t[...] = (grad[...] + inverse[...] * value).T


def layer_kernel(
    picks, marks, seg, tables, tokens, part, other, bias, down, down_other, down_bias, grad, out, totals
):
    pick = picks[...]
    mlp_out = wide(down[...]) + wide(down_other[...]) + down_bias[...]
    middle = middle_of(pick, tables, tokens, part, other, bias)[1]
    out[...] = (middle + dot(pick, tables[5]) * mlp_out).astype(jnp.bfloat16)
    accumulate(totals, segment_sums(marks, seg, wide(grad[...]) * mlp_out))


def row_parts(sent, first):
    if first:
        return (2, 3) if sent else (0, 1)
    return (1, 3) if sent else (0, 2)


def put_rows(left, right, out, parts, product, begin=0):
    quarter = left.shape[0] // 4
    columns = slice(begin, begin + (right.shape[0] if product is dot_nt else right.shape[1]))
    if parts[1] == parts[0] + 1:
        rows = slice(parts[0] * quarter, (parts[1] + 1) * quarter)
        out[:, columns] = product(left[rows, :], right[...]).astype(jnp.bfloat16)
        return
    for at, part in enumerate(parts):
        rows = slice(part * quarter, (part + 1) * quarter)
        value = product(left[rows, :], right[...]).astype(jnp.bfloat16)
        out[at * quarter : (at + 1) * quarter, columns] = value


def mlp_grads_kernel(sent, summed, fetched, left, right, *refs):
    sources, (first, second), rest = refs[:fetched], refs[fetched : fetched + 2], refs[fetched + 2 :]
    step = pl.program_id(0)
    copies = []
    if fetched:
        copies = [
            pltpu.make_async_copy(source, target, rest[-1].at[at])
            for at, (source, target) in enumerate(zip(sources, rest[:fetched]))
        ]

    @pl.when(step == 0)
    def _():
        for copy in copies:
            copy.start()
        put_rows(left, right, first, row_parts(sent, True), dot)

    @pl.when(step == 1)
    def _():
        put_rows(left, right, second, row_parts(sent, False), dot)
        for copy in copies:
            copy.wait()

    if summed:
        rest[0][...] = jnp.sum(wide(right[...]), axis=0, keepdims=True)


def qkv_grads_kernel(sent, left, proj_left, both, value, attended, first, second, *sums):
    step = pl.program_id(0)

    def column_sums(array):
        ones = jnp.ones((8, array.shape[1]), jnp.bfloat16)
        return dot_nt(ones, array[...])

    @pl.when(step == 0)
    def _():
        put_rows(left, both, first, row_parts(sent, True), dot_nt)
        if sums:
            sums[0][...] = column_sums(both)
            sums[1][...] = column_sums(value)

    @pl.when(step == 1)
    def _():
        second[...] = jnp.zeros_like(second)
        put_rows(left, value, second, row_parts(sent, False), dot_nt)

    @pl.when(step == 2)
    def _():
        begin = second.shape[1] - attended.shape[0]
        put_rows(proj_left, attended, second, row_parts(sent, False), dot_nt, begin)


SMEM = pl.BlockSpec(memory_space=pltpu.SMEM)
GRADS = 10
FREE = pl.CostEstimate(flops=1, bytes_accessed=1, transcendentals=0)


def micros(time):
    if time == 0:
        return FREE
    return pl.CostEstimate(flops=time * 10**9, bytes_accessed=time * 10**6, transcendentals=0)


def shape(dims, dtype=jnp.bfloat16):
    return jax.ShapeDtypeStruct(dims, dtype)


def room(mib):
    return pltpu.CompilerParams(vmem_limit_bytes=mib << 20)


def spec(dims, kind):
    if kind == "v":
        return VMEM
    if kind == "r":
        return pl.BlockSpec((CHUNK, dims[1]), lambda i: (i, 0))
    if kind == "c":
        return pl.BlockSpec((dims[0], CHUNK), lambda i: (0, i))
    return pl.BlockSpec(tuple(dims), lambda i: (0,) * len(dims))


def sweep(kernel, length, scalars, arrays, outs, work=(), mib=16, cost=200):
    return pl.pallas_call(
        kernel,
        grid=(length // CHUNK,),
        in_specs=[SMEM] * len(scalars) + [spec(a.shape, kind) for a, kind in arrays],
        out_specs=[spec(o.shape, kind) for o, kind in outs],
        out_shape=[o for o, _ in outs],
        scratch_shapes=[pltpu.VMEM(dims, jnp.float32) for dims in work],
        compiler_params=room(mib),
        cost_estimate=micros(cost),
    )(*scalars, *[a for a, _ in arrays])


def mlp_grads(sent, left, right, summed=False, fetch=()):
    width, length = left.shape
    hidden = right.shape[1]
    half = hidden // 2
    out = pl.BlockSpec((width // 2, half), lambda j: (0, 0))
    sums = [pl.BlockSpec((1, half), lambda j: (0, j))] if summed else []
    sums_shape = [shape((1, hidden), jnp.float32)] if summed else []
    return pl.pallas_call(
        functools.partial(mlp_grads_kernel, sent, summed, len(fetch)),
        grid=(2,),
        in_specs=[spec(left.shape, "w"), pl.BlockSpec((length, half), lambda j: (0, j))]
        + [pl.BlockSpec(memory_space=pl.ANY)] * len(fetch),
        out_specs=[out, out] + sums + [VMEM] * len(fetch),
        out_shape=[shape((width // 2, half))] * 2
        + sums_shape
        + [pltpu.VMEM(a.shape, a.dtype) for a in fetch],
        scratch_shapes=[pltpu.SemaphoreType.DMA((len(fetch),))] if fetch else [],
        compiler_params=room(24),
        cost_estimate=micros(GRADS),
    )(left, right, *fetch)


def sum_kernel(counts, splits, *refs):
    halves, at = [], 0
    for count in counts[:2]:
        total = wide(refs[at][...])
        for ref in refs[at + 1 : at + count]:
            total += wide(ref[...])
        halves.append(total)
        at += count
    outs = refs[at + counts[2] :]
    for half in range(2):
        begin = 0 if half == 0 else halves[0].shape[1]
        columns = slice(begin, begin + halves[half].shape[1])
        for ref in refs[at : at + counts[2]]:
            halves[half] += wide(ref[:, columns])
    if splits is None:
        for out, total in zip(outs, halves):
            out[...] = total.astype(out.dtype)
    elif splits == ():
        for total, begin in zip(halves, (0, halves[0].shape[1])):
            outs[0][:, begin : begin + total.shape[1]] = total.astype(outs[0].dtype)
    else:
        for at, (half, begin, end) in enumerate(splits):
            if at < 3:
                outs[0][at] = halves[half][:, begin:end]
            else:
                outs[1][...] = halves[half][:, begin:end]


def sum_rows(halves, joined, at, count, outs, splits=None):
    arrays = halves[0] + halves[1] + joined
    arrays = [pltpu.with_memory_space_constraint(a, pltpu.HBM) for a in arrays]

    def rows(width):
        return pl.BlockSpec((count, width), lambda i: (at, 0))

    return pl.pallas_call(
        functools.partial(sum_kernel, (len(halves[0]), len(halves[1]), len(joined)), splits),
        grid=(1,),
        in_specs=[rows(a.shape[1]) for a in arrays],
        out_specs=[pl.BlockSpec(o.shape, lambda i, n=len(o.shape): (0,) * n) for o in outs],
        out_shape=outs,
        compiler_params=room(16),
        cost_estimate=FREE,
    )(*arrays)


def pack_kernel(
    side, middle, late, gate, cond, proj_bias, down_bias, up_bias, qk_bias, value_bias, out, work
):
    width = out.shape[1]
    segs = cond.shape[0]
    own = [late[:segs, :], late[2 * segs : 3 * segs, :]]
    for source, at in ((middle, 0), (middle, 1), (middle, 2), (gate, 0)):
        own.append(own_part(side[0], source[2 * at * segs : (2 * at + 1) * segs, :], width))
    own += [wide(cond[:, at : at + width]) for at in range(0, cond.shape[1], width)]
    for at, value in enumerate(own):
        work[at * segs : (at + 1) * segs, :] = value
    rows = []
    for source in (proj_bias, down_bias, up_bias):
        rows += [source[0:1, at : at + width] for at in range(0, source.shape[1], width)]
    rows += [qk_bias[0:1, :width], value_bias[0:1, :]]
    first = len(own) * segs
    for at, value in enumerate(rows):
        high = wide(value.astype(jnp.bfloat16))
        work[first + at : first + at + 1, :] = high
        work[first + len(rows) + at : first + len(rows) + at + 1, :] = value - high
    out[...] = work[: out.shape[0], :].astype(jnp.bfloat16)


def finish_kernel(segs, first, held, other, cond, other_cond, mod, modbias, bias, work):
    value = jnp.concatenate([wide(held[...]), wide(other[...])], axis=0)
    left = jnp.concatenate([wide(cond[...]), wide(other_cond[...])], axis=0)
    devices, rows, width = value.shape
    left = left.reshape((devices * segs, left.shape[2])).T.astype(jnp.bfloat16)
    for at in range(mod.shape[0]):
        part = value[:, at * segs : (at + 1) * segs, :].reshape((devices * segs, width))
        mod[at] = dot(left, part.astype(jnp.bfloat16))
        modbias[at : at + 1, :] = jnp.sum(part, axis=0, keepdims=True)
    work[:rows, :] = jnp.sum(value, axis=0)
    count = bias.shape[0]
    bias[...] = work[first : first + count, :] + work[first + count : first + 2 * count, :]


def padded(width):
    return -(-width // 128) * 128


def qkv_grads(sent, left, proj_left, triple, attended):
    width, length = left.shape
    local = attended.shape[0]
    wide_block = padded(local)
    sums_spec = [pl.BlockSpec((8, 2 * local), lambda j: (0, 0)), pl.BlockSpec((8, local), lambda j: (0, 0))]
    sums_shape = [shape((8, 2 * local), jnp.float32), shape((8, local), jnp.float32)]
    return pl.pallas_call(
        functools.partial(qkv_grads_kernel, sent),
        grid=(3,),
        in_specs=[
            spec(left.shape, "w"),
            spec(left.shape, "w"),
            pl.BlockSpec((2 * local, length), lambda j: (0, 0)),
            pl.BlockSpec((local, length), lambda j: (2, 0)),
            spec(attended.shape, "w"),
        ],
        out_specs=[
            pl.BlockSpec((width // 2, 2 * local), lambda j: (0, 0)),
            pl.BlockSpec((width // 2, wide_block + local), lambda j: (0, 0)),
        ]
        + sums_spec * sent,
        out_shape=[shape((width // 2, 2 * local)), shape((width // 2, wide_block + local))]
        + sums_shape * sent,
        compiler_params=room(32),
        cost_estimate=FREE,
    )(left, proj_left, triple, triple, attended)


def attention_forward(segments, qkv, width=256):
    heads, length = qkv.shape[1], qkv.shape[3]
    return pl.pallas_call(
        functools.partial(attention_forward_kernel, width),
        in_specs=[VMEM] * 2,
        out_specs=[VMEM] * 2,
        out_shape=[shape((heads, HEAD_DIM, length)), shape((heads, 1, length), jnp.float32)],
        scratch_shapes=[
            pltpu.VMEM((HEAD_DIM + SEGS, length), jnp.bfloat16),
            pltpu.VMEM((length, HEAD_DIM + SEGS), jnp.bfloat16),
        ],
        compiler_params=room(12),
        cost_estimate=micros(15),
    )(segments, qkv)


def attention_backward(segments, qkv, stat, grad, width=256):
    heads, length = qkv.shape[1], qkv.shape[3]
    return pl.pallas_call(
        functools.partial(attention_backward_kernel, width),
        in_specs=[VMEM] * 4,
        out_specs=VMEM,
        out_shape=shape(qkv.shape),
        scratch_shapes=[
            pltpu.VMEM((HEAD_DIM + SEGS, length), jnp.bfloat16),
            pltpu.VMEM((length, HEAD_DIM + SEGS), jnp.bfloat16),
        ]
        + [pltpu.VMEM((length, HEAD_DIM), jnp.bfloat16)] * 3
        + [pltpu.VMEM((length, length), jnp.bfloat16)] * 2,
        compiler_params=room(16),
        cost_estimate=micros(15),
    )(segments, qkv, stat, grad)


def silu(array):
    return array / (1.0 + jnp.exp(-array))


def product(spec, left, right):
    return jnp.einsum(spec, left, right, preferred_element_type=jnp.float32)


def exchange(array):
    return lax.ppermute(array, "tensor", [(0, 1), (1, 0)])


def summands(part, size):
    if size == 2:
        return part, exchange(part)
    return lax.psum(part, "tensor"), jnp.zeros_like(part)


def tensor_join(array, size):
    if size == 2:
        other = exchange(array)
        first = lax.axis_index("tensor") == 0
        return jnp.concatenate(
            [jnp.where(first, array, other), jnp.where(first, other, array)], axis=-1
        )
    return lax.all_gather(array, "tensor", axis=array.ndim - 1, tiled=True)


def partners(size, bit):
    return [(i, i ^ (1 << bit)) for i in range(size)]


def tie(*values):
    return lax.optimization_barrier(values)


def after(value, *others):
    return tie(value, *others)[0]


class Gather:
    def __init__(self, array, size, order):
        self.held, self.size, self.order = array[None], size, list(order)

    def last(self):
        bit = self.order.pop(0)
        return self.held, lax.ppermute(self.held, "batch", partners(self.size, bit))

    def step(self, *others):
        if self.order:
            bit = self.order.pop(0)
            self.held = after(self.held, *others)
            other = lax.ppermute(self.held, "batch", partners(self.size, bit))
            self.held = jnp.concatenate([self.held, other], axis=0)


class Sum:
    def __init__(self, sends, size, kernels):
        self.kernels = kernels
        self.sends, self.size, self.bits = sends, size, size.bit_length() - 1
        self.keeps, self.got = None, []

    def pieces(self, at, count, dtype, splits=None, outs=None):
        halves = [[self.keeps[h]] + [stage[h] for stage in self.got[:2]] for h in range(2)]
        joined = [new for (new,) in self.got[2:]]
        widths = [half[0].shape[1] for half in halves]
        if self.kernels:
            if outs is None:
                outs = [shape((count, width), dtype) for width in widths]
                if len(self.got) > 1:
                    outs, splits = [shape((count, sum(widths)), dtype)], ()
            return list(sum_rows(halves, joined, at, count, outs, splits))
        window = slice(at * count, (at + 1) * count)
        totals = [sum(a[window].astype(jnp.float32) for a in half) for half in halves]
        if len(self.got) < 2:
            return [total.astype(dtype) for total in totals]
        total = jnp.concatenate(totals, axis=1)
        total = sum((a[window].astype(jnp.float32) for a in joined), total)
        if outs is None:
            return [total.astype(dtype)]
        if splits == ():
            return [total.astype(dtype)]
        totals = [total[:, : widths[0]], total[:, widths[0] :]]
        parts = [totals[half][:, begin:end] for half, begin, end in splits]
        return [jnp.stack(parts[:3]), parts[3]]

    def send(self, *others):
        stage = len(self.got)
        sends, bits = self.sends, [stage]
        if stage > 0:
            left = self.keeps[0].shape[0] >> stage
            sends = self.pieces(1, left, jnp.bfloat16)
        if stage < 2:
            bits = [stage, 1 - stage]
        tied = tie(*sends, *others)
        self.sent = tied[: len(sends)]
        self.flying = [
            lax.ppermute(piece, "batch", partners(self.size, bit))
            for piece, bit in zip(tied, bits)
        ]
        return tied[len(sends) :]

    def take(self, *others):
        tied = tie(*self.flying, *others)
        self.got.append(tied[: len(self.flying)])
        return tied[len(self.flying) :]

    def settle(self, other):
        if len(self.got) == self.bits:
            self.keeps = list(tie(*self.keeps, other)[:2])

    def result(self, splits=()):
        while len(self.got) < self.bits:
            self.send()
            self.take()
        count = 2 * self.keeps[0].shape[0] // self.size
        if splits:
            width = splits[0][2] - splits[0][1]
            outs = [shape((3, count, width), jnp.float32), shape((count, width), jnp.float32)]
        else:
            outs = [shape((count, sum(keep.shape[1] for keep in self.keeps)), jnp.float32)]
        return self.pieces(0, count, jnp.float32, splits, outs)


def gelu_and_slope(array):
    square = array * array
    bent = jnp.tanh(0.7978845608028654 * (array + 0.044715 * array * square))
    half = 0.5 * (1.0 + bent)
    inner = 0.7978845608028654 * (1.0 + 3.0 * 0.044715 * square)
    return array * half, half + 0.5 * array * (1.0 - bent * bent) * inner


def in_three(array):
    high = lax.reduce_precision(array, 8, 7)
    middle = lax.reduce_precision(array - high, 8, 7)
    return [high, middle, array - high - middle]


def on_device(
    n_batch,
    tokens,
    segment_ids,
    conditions,
    condition_segment,
    qkv_weight,
    qv_bias,
    proj_weight,
    proj_bias,
    up_weight,
    up_bias,
    down_weight,
    down_bias,
    mod_weight,
    mod_bias,
    out_grad,
):
    bf16, f32 = jnp.bfloat16, jnp.float32
    tokens, out_grad = tokens[0], out_grad[0]
    length, model_width = tokens.shape
    local_width = qkv_weight.shape[2]
    hidden_width = up_weight.shape[1]
    heads = local_width // HEAD_DIM
    n_tensor = model_width // local_width
    bits = list(range(n_batch.bit_length() - 1))
    block = model_width // n_batch
    in_kernel = block % 8 == 0
    index = lax.axis_index("batch")
    order = jnp.array(
        [sum((p >> bit & 1) << (bits[-1] - bit) for bit in bits) for p in range(n_batch)], jnp.int32
    )
    order = order ^ index
    side = lax.axis_index("tensor")[None]

    def run(kernel, scalars, arrays, outs):
        turned = shape((model_width, length))
        if in_kernel:
            chunk = (model_width, CHUNK)
            return sweep(kernel, length, scalars, arrays, outs + [(turned, "c")], [chunk])
        got = sweep(kernel, length, scalars, arrays, outs)
        return list(got) + [got[0].T.reshape((n_batch, block, length))[order].reshape(turned.shape)]

    def part_rows(left, sent, first):
        quarter = model_width // 4
        rows = [left[at * quarter : (at + 1) * quarter] for at in row_parts(sent, first)]
        return jnp.concatenate(rows)

    def hidden_grads(sent, left, right, summed=False, fetch=()):
        if in_kernel:
            first, second, *rest = mlp_grads(sent, left, right, summed, fetch)
            return [first, second], rest
        rest = [jnp.sum(right.astype(f32), axis=0)[None]] if summed else fetch
        cut = right.shape[1] // 2
        return [
            product("dl,lc->dc", part_rows(left, sent, True), right[:, :cut]).astype(bf16),
            product("dl,lc->dc", part_rows(left, sent, False), right[:, cut:]).astype(bf16),
        ], rest

    def attention_grads(sent, left, proj_left, triple, attended):
        if in_kernel:
            first, second, *sums = qkv_grads(sent, left, proj_left, triple, attended)
            return [first, second], sums
        sums = jnp.sum(triple.astype(f32), axis=1)[None]
        sums = (sums[:, : 2 * local_width], sums[:, 2 * local_width :])
        cut, extra = 2 * local_width, ((0, 0), (0, padded(local_width) - local_width))
        halves = [
            (part_rows(left, sent, True), triple[:cut]),
            (part_rows(left, sent, False), triple[cut:]),
            (part_rows(proj_left, sent, False), attended),
        ]
        first, value, proj = [product("dl,cl->dc", *pair).astype(bf16) for pair in halves]
        return [first, jnp.concatenate([jnp.pad(value, extra), proj], axis=1)], sums

    cond_float = conditions[0].astype(f32)
    cond_act = silu(cond_float).astype(bf16)
    mod_local = product("sd,djc->jsc", cond_act, mod_weight) + mod_bias[:, None]
    modulation = tensor_join(mod_local, n_tensor)
    segs = modulation.shape[1]
    tables = jnp.concatenate(in_three(modulation) + [jnp.zeros_like(modulation)], axis=1).astype(bf16)
    marks = jnp.concatenate([condition_segment[0], jnp.full((segs,), -1, jnp.int32)])[:, None]
    full, column = (length, model_width), shape((length, 1), f32)
    mine = (length, local_width)
    row = shape((1, model_width), f32)

    qkv_weight = qkv_weight.transpose((1, 2, 0))
    attn_in, mean_one, inverse_one, normed_mine, picks, biases, in_t = run(
        entry_kernel,
        [order, side],
        [(marks, "v"), (segment_ids, "c"), (tables, "v"), (qv_bias, "v"), (tokens, "r")],
        [
            (shape(full), "r"),
            (column, "r"),
            (column, "r"),
            (shape(mine, f32), "r"),
            (shape((length, 4 * segs)), "r"),
            (shape((3, local_width), f32), "w"),
        ],
    )
    qkv = product("jcd,ld->jcl", qkv_weight, attn_in) + biases[:, :, None]
    qkv = qkv.astype(bf16).reshape((3, heads, HEAD_DIM, length))
    attended, stat = attention_forward(segment_ids, qkv)
    attended = attended.reshape((local_width, length))
    proj_part = product("cl,cd->ld", attended, proj_weight).astype(bf16)
    proj_part, proj_other = summands(proj_part, n_tensor)
    out_grad, proj_tied = tie(out_grad, proj_part)
    mlp_grad, down_bias_grad, grad_t = run(
        gate_kernel,
        [order],
        [(picks, "r"), (tables, "v"), (out_grad, "r")],
        [(shape(full), "r"), (row, "w")],
    )
    proj_other, mlp_grad = tie(proj_other, mlp_grad)
    middle_args = [
        (tables, "v"), (tokens, "r"), (proj_tied, "r"), (proj_other, "r"), (proj_bias[None], "v")
    ]
    mlp_in, mean_two, inverse_two, mlp_t = run(
        middle_kernel,
        [order],
        [(picks, "r")] + middle_args,
        [(shape(full), "r"), (column, "r"), (column, "r")],
    )
    hidden = product("ld,df->lf", mlp_in, up_weight) + up_bias
    active, slope = gelu_and_slope(hidden)
    active, slope = tie(active.astype(bf16), slope.astype(bf16))

    sends, _ = hidden_grads(True, grad_t, active)
    down_sum = Sum(sends, n_batch, in_kernel)
    (mlp_grad_then, active_then) = down_sum.send(mlp_grad, active)
    active_grad = product("ld,fd->lf", mlp_grad_then, down_weight)
    hidden_grad = (active_grad * slope.astype(f32)).astype(bf16)
    mlp_part = product("lf,df->ld", hidden_grad, up_weight).astype(bf16)
    mlp_part, mlp_other = summands(mlp_part, n_tensor)
    (hidden_then, mlp_tied) = tie(hidden_grad, mlp_part)
    sends, (up_bias_grad,) = hidden_grads(True, mlp_t, hidden_then, summed=True)
    up_sum = Sum(sends, n_batch, in_kernel)
    down_sum.keeps, _ = hidden_grads(False, grad_t, active_then)
    first, second, *down_sum.keeps = down_sum.take(*up_sum.sends, *down_sum.keeps)
    up_sum.sends = [first, second]
    (mlp_other, hidden_then) = down_sum.send(mlp_other, hidden_then)
    (mlp_other, hidden_then) = up_sum.send(mlp_other, hidden_then)
    attn_grad, proj_bias_grad, grad_mine, early_totals, attn_t = run(
        middle_grad_kernel,
        [order, side],
        [(picks, "r"), (marks, "v"), (segment_ids, "c")]
        + middle_args
        + [(mean_two, "r"), (inverse_two, "r"), (mlp_tied, "r"), (mlp_other, "r"), (out_grad, "r")],
        [
            (shape(full), "r"),
            (row, "w"),
            (shape(mine, f32), "r"),
            (shape((6 * segs, model_width), f32), "w"),
        ],
    )
    attended_grad = product("cd,ld->cl", proj_weight, attn_grad).astype(bf16)

    triple = attention_backward(
        segment_ids, qkv, stat, attended_grad.reshape((heads, HEAD_DIM, length))
    ).reshape((3 * local_width, length))
    up_sum.keeps, _ = hidden_grads(False, mlp_t, hidden_then)
    sends, (qk_bias_grad, value_bias_grad) = attention_grads(True, in_t, attn_t, triple, attended)
    qkv_sum = Sum(sends, n_batch, in_kernel)
    first, second, *up_sum.keeps = up_sum.take(*qkv_sum.sends, *up_sum.keeps)
    qkv_sum.sends = [first, second]
    (triple,) = down_sum.take(triple)
    (triple,) = up_sum.send(triple)
    (triple,) = qkv_sum.send(triple)
    (triple,) = down_sum.send(triple)
    attn_part = product(
        "jcl,jcd->ld", triple.reshape((3, local_width, length)), qkv_weight
    ).astype(bf16)
    kept, sent, sums = sweep(
        halves_kernel,
        length,
        [side],
        [
            (picks, "r"),
            (tables, "v"),
            (attn_part, "r"),
            (tokens, "r"),
            (mean_one, "r"),
            (inverse_one, "r"),
        ],
        [
            (shape(mine), "r"),
            (shape((length, padded(local_width + 4))), "r"),
            (shape((length, 2), f32), "r"),
        ],
        cost=0,
    )
    down_part = product("lf,fd->ld", after(active, kept), down_weight).astype(bf16)
    (kept, sent, down_part) = up_sum.take(kept, sent, down_part)
    (kept, sent) = down_sum.take(kept, sent)
    (kept, sent, triple) = up_sum.send(kept, sent, triple)
    (kept, sent, triple) = down_sum.send(kept, sent, triple)
    (mod_local, kept) = tie(mod_local, kept)
    tables_mine = jnp.concatenate(in_three(mod_local) + [jnp.zeros_like(mod_local)], axis=1).astype(bf16)
    if n_tensor == 2:
        other = exchange(sent)
    else:
        kept = lax.psum_scatter(attn_part, "tensor", scatter_dimension=1, tiled=True)
        other = jnp.zeros_like(sent)
        sums = lax.psum(sums, "tensor")
    qkv_sum.keeps, _ = attention_grads(False, in_t, attn_t, triple, attended)
    token_t, late_totals = sweep(
        functools.partial(token_grad_kernel, model_width),
        length,
        [],
        [
            (picks, "r"),
            (marks, "v"), (segment_ids, "c"),
            (tables_mine, "v"),
            (kept, "r"),
            (other, "r"),
            (sums, "r"),
            (normed_mine, "r"),
            (inverse_one, "r"),
            (grad_mine, "r"),
        ],
        [(shape((local_width, length), f32), "c"), (shape((4 * segs, local_width), f32), "w")],
        cost=0,
    )
    (late_totals, *qkv_sum.keeps) = qkv_sum.take(late_totals, *qkv_sum.keeps)
    (late_totals,) = up_sum.take(late_totals)
    (down_part, late_totals) = qkv_sum.send(down_part, late_totals)
    (down_part, late_totals) = up_sum.send(down_part, late_totals)
    (down_part,) = down_sum.take(down_part)
    down_part, down_other = summands(down_part, n_tensor)
    layer_out, gate_total = sweep(
        layer_kernel,
        length,
        [],
        [(picks, "r"), (marks, "v"), (segment_ids, "c")]
        + middle_args
        + [(down_part, "r"), (down_other, "r"), (down_bias[None], "v"), (out_grad, "r")],
        [(shape(full), "r"), (shape((2 * segs, model_width), f32), "w")],
        cost=0,
    )
    bias_rows = 2 * n_tensor + hidden_width // local_width + 2
    rows = (6 + n_tensor) * segs + 2 * bias_rows
    (packed,) = pl.pallas_call(
        pack_kernel,
        in_specs=[SMEM] + [VMEM] * 9,
        out_specs=[VMEM],
        out_shape=[shape((rows, local_width))],
        scratch_shapes=[pltpu.VMEM((-(-rows // 16) * 16, local_width), f32)],
        compiler_params=room(16),
        cost_estimate=FREE,
    )(
        side,
        early_totals,
        late_totals,
        gate_total,
        cond_act,
        proj_bias_grad,
        down_bias_grad,
        up_bias_grad,
        qk_bias_grad,
        value_bias_grad,
    )
    gathered = Gather(packed, n_batch, bits[:1:-1] + bits[1::-1])
    gathered.step()
    (packed, gathered.held) = qkv_sum.take(packed, gathered.held)
    (packed,) = up_sum.take(packed)
    (packed,) = qkv_sum.send(packed)
    gathered.step()
    tgrad = packed[: 6 * segs].reshape((6, segs, local_width))
    gathered.step()
    (gathered.held,) = qkv_sum.take(gathered.held)
    qkv_sum.send()
    while len(gathered.order) > 1:
        gathered.step()
    halves = gathered.last()
    down_sum.settle(qkv_sum.sent[0])
    up_sum.settle(qkv_sum.sent[0])
    (down,), (up,) = down_sum.result(), up_sum.result()
    cond_then = after(tgrad, up)
    (up, down) = qkv_sum.take(up, down)
    cond_part = product("jsc,djc->sd", cond_then, mod_weight)
    cond_part, cond_other = summands(cond_part.astype(bf16), n_tensor)
    cond_act_grad = cond_part.astype(f32) + cond_other.astype(f32)
    condition_grad = jax.vjp(silu, cond_float)[1](cond_act_grad)[0]

    part = index * block // local_width
    cond_blocks = [
        lax.dynamic_slice(
            half,
            (0, (6 + part) * segs, index * block % local_width),
            (half.shape[0], segs, block),
        )
        for half in halves
    ]
    mod_sum, modbias_sum, bias_all = pl.pallas_call(
        functools.partial(finish_kernel, segs, (6 + n_tensor) * segs),
        in_specs=[VMEM] * 4,
        out_specs=[VMEM] * 3,
        out_shape=[
            shape((6, block, local_width), f32),
            shape((6, local_width), f32),
            shape((bias_rows, local_width), f32),
        ],
        scratch_shapes=[pltpu.VMEM((-(-rows // 8) * 8, local_width), f32)],
        compiler_params=room(24),
        cost_estimate=FREE,
    )(*halves, *cond_blocks)
    qv_sum = bias_all[-2:]
    bias_all = bias_all[:-2].reshape(-1)
    projbias_sum = bias_all[:model_width]
    downbias_sum = bias_all[model_width : 2 * model_width]
    upbias_sum = bias_all[2 * model_width :]
    mod_sum = mod_sum.transpose((1, 0, 2))
    begin = padded(local_width)
    last, proj_last = qkv_sum.result(
        [
            (0, 0, local_width),
            (0, local_width, 2 * local_width),
            (1, 0, local_width),
            (1, begin, begin + local_width),
        ]
    )
    last = last.transpose((1, 0, 2))
    return (
        layer_out[None],
        token_t.T[None],
        condition_grad[None],
        last,
        qv_sum,
        proj_last.T,
        projbias_sum,
        up,
        upbias_sum,
        down.T,
        downbias_sum,
        mod_sum,
        modbias_sum,
    )


def solution(mesh):
    return jax.shard_map(
        functools.partial(on_device, mesh.shape["batch"]),
        mesh=mesh,
        in_specs=(
            P("batch", None, None),
            P("batch", None),
            P("batch", None, None),
            P("batch", None),
            P(None, None, "tensor"),
            P(None, "tensor"),
            P("tensor", None),
            P(),
            P(None, "tensor"),
            P("tensor"),
            P("tensor", None),
            P(),
            P(None, None, "tensor"),
            P(None, "tensor"),
            P("batch", None, None),
        ),
        out_specs=(
            P("batch", None, None),
            P("batch", None, "tensor"),
            P("batch", None, None),
            P("batch", None, "tensor"),
            P(None, "tensor"),
            P("tensor", "batch"),
            P(),
            P("batch", "tensor"),
            P("tensor"),
            P("tensor", "batch"),
            P(),
            P("batch", None, "tensor"),
            P(None, "tensor"),
        ),
        check_vma=False,
    )
```

```python
import functools

import jax
import jax.numpy as jnp
from jax import lax
from jax.experimental import pallas as pl
from jax.experimental.pallas import tpu as pltpu
from jax.sharding import PartitionSpec as P

EPS = 1e-06
HEAD_DIM = 72
SEGS = 8
MOST = 256
LOG2E = 1.4426950408889634
NEG = -1e30


def band(begin, width, length):
    low = max(0, (begin - MOST + 1) // 128 * 128)
    high = min(length, -(-(begin + width + MOST - 1) // 128) * 128)
    return low, high


def natural(array):
    return array.astype(jnp.float32).T.astype(jnp.bfloat16)


def marks(seg_row):
    slots = lax.broadcasted_iota(jnp.int32, (SEGS, seg_row.shape[-1]), 0)
    return (slots == seg_row[...]).astype(jnp.float32)


def fill(head, qkv, one_hot, q_aug, k_nat):
    query = jnp.concatenate([qkv[0, head].astype(jnp.float32), (1.0 - one_hot) * NEG], axis=0)
    q_aug[...] = query.astype(jnp.bfloat16)
    k_nat[...] = natural(jnp.concatenate([qkv[1, head].astype(jnp.float32), one_hot], axis=0))


def attention_forward_kernel(width, seg_row, qkv, out, stat, q_aug, k_nat):
    heads, length = qkv.shape[1], qkv.shape[3]
    factor = HEAD_DIM**-0.5 * LOG2E
    one_hot = marks(seg_row)

    def one(head, carry):
        fill(head, qkv, one_hot, q_aug, k_nat)
        for begin in range(0, length, width):
            low, high = band(begin, width, length)
            span = slice(begin, begin + width)
            scores = jnp.dot(
                k_nat[low:high, :], q_aug[:, span], preferred_element_type=jnp.float32
            )
            peak = jnp.max(scores, axis=0, keepdims=True) * factor
            shifted = jnp.exp2(scores * factor - peak)
            total = jnp.sum(shifted, axis=0, keepdims=True)
            got = jnp.dot(
                qkv[2, head, :, low:high],
                shifted.astype(jnp.bfloat16),
                preferred_element_type=jnp.float32,
            )
            out[head, :, span] = (got * (1.0 / total)).astype(jnp.bfloat16)
            stat[head, :, span] = peak + jnp.log2(total)
        return carry

    lax.fori_loop(0, heads, one, 0, unroll=2)


def attention_backward_kernel(
    width, seg_row, qkv, stat, grad, out, q_aug, k_nat, v_nat, q_nat, g_nat, p_all, s_all
):
    heads, length = qkv.shape[1], qkv.shape[3]
    scale = HEAD_DIM**-0.5
    factor = scale * LOG2E
    one_hot = marks(seg_row)

    def one(head, carry):
        fill(head, qkv, one_hot, q_aug, k_nat)
        v_nat[...] = natural(qkv[2, head])
        q_nat[...] = natural(qkv[0, head])
        g_nat[...] = natural(grad[head])
        for begin in range(0, length, width):
            low, high = band(begin, width, length)
            span = slice(begin, begin + width)
            scores = jnp.dot(
                k_nat[low:high, :], q_aug[:, span], preferred_element_type=jnp.float32
            )
            probs = jnp.exp2(scores * factor - stat[head, :, span])
            prob_grad = jnp.dot(
                v_nat[low:high, :], grad[head, :, span], preferred_element_type=jnp.float32
            )
            row = jnp.sum(prob_grad * probs, axis=0, keepdims=True)
            score_grad = (probs * (prob_grad - row)).astype(jnp.bfloat16)
            p_all[low:high, span] = probs.astype(jnp.bfloat16)
            s_all[low:high, span] = score_grad
            got = jnp.dot(
                qkv[1, head, :, low:high], score_grad, preferred_element_type=jnp.float32
            )
            out[0, head, :, span] = (got * scale).astype(jnp.bfloat16)
        for begin in range(0, length, width):
            span = slice(begin, begin + width)
            reach = [q for q in range(0, length, width) if band(q, width, length)[0] < begin + width and band(q, width, length)[1] > begin]
            low, high = reach[0], reach[-1] + width
            key_grad = jnp.dot(
                s_all[span, low:high], q_nat[low:high, :], preferred_element_type=jnp.float32
            )
            value_grad = jnp.dot(
                p_all[span, low:high], g_nat[low:high, :], preferred_element_type=jnp.float32
            )
            out[1, head, :, span] = (key_grad * scale).T.astype(jnp.bfloat16)
            out[2, head, :, span] = value_grad.T.astype(jnp.bfloat16)
        return carry

    if width < MOST:
        p_all[...] = jnp.zeros_like(p_all)
        s_all[...] = jnp.zeros_like(s_all)
    lax.fori_loop(0, heads, one, 0, unroll=2)


VMEM = pl.BlockSpec(memory_space=pltpu.VMEM)


CHUNK = 128


def dot(left, right):
    return jnp.dot(left, right, preferred_element_type=jnp.float32)


def dot_nt(left, right):
    return lax.dot_general(
        left, right, (((1,), (1,)), ((), ())), preferred_element_type=jnp.float32
    )


def wide(value):
    return value.astype(jnp.float32)


def turn(order, value, out, work):
    count = order.shape[0]
    rows = value.shape[1] // count
    work[...] = wide(value).T
    for at in range(0, count, 2):
        pair = [
            work[pl.ds(pl.multiple_of(order[at + i] * rows, 8), rows), :] for i in range(2)
        ]
        pair = jnp.concatenate(pair, axis=0).astype(jnp.bfloat16)
        out[at * rows : (at + 2) * rows, :] = pair


def own_part(side, value, width):
    part = value[:, :width]
    for at in range(1, value.shape[1] // width):
        part = jnp.where(side == at, value[:, at * width : (at + 1) * width], part)
    return part


def accumulate(total, value):
    @pl.when(pl.program_id(0) == 0)
    def _():
        total[...] = value

    @pl.when(pl.program_id(0) > 0)
    def _():
        total[...] += value


def segment_sums(slots, seg, *values):
    marks = (slots[...] == seg[...]).astype(jnp.bfloat16)
    marks = jnp.concatenate([marks, marks], axis=1)
    sums = []
    for value in values:
        high = value.astype(jnp.bfloat16)
        low = (value - wide(high)).astype(jnp.bfloat16)
        sums.append(dot(marks, jnp.concatenate([high, low], axis=0)))
    return jnp.concatenate(sums, axis=0)


def norm_parts(value):
    width = value.shape[1]
    mean = jnp.sum(value, axis=1, keepdims=True) / width
    center = value - mean
    spread = jnp.sum(center * center, axis=1, keepdims=True) / width
    return mean, center, lax.rsqrt(spread + EPS)


def entry_kernel(
    order, side, slots, seg, tables, bias, tokens,
    out, mean, inverse, normed_mine, picks, biases, *turned
):
    segs = slots.shape[0] // 2
    column = jnp.concatenate([slots[:segs, :]] * 3 + [slots[segs:, :]], axis=0)
    pick = (column == seg[...]).astype(jnp.float32).T.astype(jnp.bfloat16)
    picks[...] = pick
    biases[0:1, :] = bias[0:1, :]
    biases[1:2, :] = jnp.zeros_like(biases[1:2, :])
    biases[2:3, :] = bias[1:2, :]
    middle, center, scale = norm_parts(wide(tokens[...]))
    mean[...] = middle
    inverse[...] = scale
    value = center * scale
    normed_mine[...] = own_part(side[0], value, normed_mine.shape[1])
    value = (value * (1.0 + dot(pick, tables[1])) + dot(pick, tables[0])).astype(jnp.bfloat16)
    out[...] = value
    if turned:
        turn(order, value, *turned)


def gate_kernel(order, picks, tables, grad, out, bias, *turned):
    value = (wide(grad[...]) * dot(picks[...], tables[5])).astype(jnp.bfloat16)
    out[...] = value
    accumulate(bias, jnp.sum(wide(value), axis=0, keepdims=True))
    if turned:
        turn(order, value, *turned)


def middle_of(pick, tables, tokens, part, other, bias):
    attn_out = wide(part[...]) + wide(other[...]) + bias[...]
    return attn_out, wide(tokens[...]) + dot(pick, tables[2]) * attn_out


def middle_kernel(order, picks, tables, tokens, part, other, bias, out, mean, inverse, *turned):
    pick = picks[...]
    value = middle_of(pick, tables, tokens, part, other, bias)[1]
    middle, center, scale = norm_parts(value)
    mean[...] = middle
    inverse[...] = scale
    value = center * scale * (1.0 + dot(pick, tables[4])) + dot(pick, tables[3])
    value = value.astype(jnp.bfloat16)
    out[...] = value
    if turned:
        turn(order, value, *turned)


def middle_grad_kernel(
    order, side, picks, marks, seg, tables, tokens, part, other, bias, mean, inverse, mlp, mlp_other, grad,
    out, bias_sum, grad_mine, totals, *turned
):
    pick = picks[...]
    width = grad.shape[1]
    attn_out, value = middle_of(pick, tables, tokens, part, other, bias)
    norm = (value - mean[...]) * inverse[...]
    in_grad = wide(mlp[...]) + wide(mlp_other[...])
    value = in_grad * (1.0 + dot(pick, tables[4]))
    plain = jnp.sum(value, axis=1, keepdims=True) / width
    cross = jnp.sum(value * norm, axis=1, keepdims=True) / width
    value = wide(grad[...]) + inverse[...] * (value - plain - norm * cross)
    grad_mine[...] = own_part(side[0], value, grad_mine.shape[1])
    accumulate(totals, segment_sums(marks, seg, value * attn_out, in_grad, in_grad * norm))
    value = (value * dot(pick, tables[2])).astype(jnp.bfloat16)
    out[...] = value
    accumulate(bias_sum, jnp.sum(wide(value), axis=0, keepdims=True))
    if turned:
        turn(order, value, *turned)


def halves_kernel(side, picks, tables, part, tokens, mean, inverse, kept, sent, sums):
    value = part[...]
    width = kept.shape[1]
    kept[...] = own_part(side[0], value, width)
    sent[:, :width] = own_part(1 - side[0], value, width)
    value = wide(value) * (1.0 + dot(picks[...], tables[1]))
    norm = (wide(tokens[...]) - mean[...]) * inverse[...]
    for at, term in enumerate((value, value * norm)):
        total = jnp.sum(term, axis=1, keepdims=True)
        high = total.astype(jnp.bfloat16)
        sums[:, at : at + 1] = total
        sent[:, width + 2 * at : width + 2 * at + 1] = high
        sent[:, width + 2 * at + 1 : width + 2 * at + 2] = (total - wide(high)).astype(jnp.bfloat16)


def token_grad_kernel(
    width, picks, marks, seg, tables, kept, other, sums, normed, inverse, grad, out_t, totals
):
    mine = kept.shape[1]
    value = wide(kept[...]) + wide(other[:, :mine])
    norm = normed[...]
    accumulate(totals, segment_sums(marks, seg, value, value * norm))
    value = value * (1.0 + dot(picks[...], tables[1]))
    for at, factor in enumerate((1.0, norm)):
        rest = wide(other[:, mine + 2 * at : mine + 2 * at + 1])
        rest = rest + wide(other[:, mine + 2 * at + 1 : mine + 2 * at + 2])
        value = value - factor * ((sums[:, at : at + 1] + rest) / width)
    out_t[...] = (grad[...] + inverse[...] * value).T


def layer_kernel(
    picks, marks, seg, tables, tokens, part, other, bias, down, down_other, down_bias, grad, out, totals
):
    pick = picks[...]
    mlp_out = wide(down[...]) + wide(down_other[...]) + down_bias[...]
    middle = middle_of(pick, tables, tokens, part, other, bias)[1]
    out[...] = (middle + dot(pick, tables[5]) * mlp_out).astype(jnp.bfloat16)
    accumulate(totals, segment_sums(marks, seg, wide(grad[...]) * mlp_out))


def row_parts(sent, first):
    if first:
        return (2, 3) if sent else (0, 1)
    return (1, 3) if sent else (0, 2)


def put_rows(left, right, out, parts, product, begin=0):
    quarter = left.shape[0] // 4
    columns = slice(begin, begin + (right.shape[0] if product is dot_nt else right.shape[1]))
    if parts[1] == parts[0] + 1:
        rows = slice(parts[0] * quarter, (parts[1] + 1) * quarter)
        out[:, columns] = product(left[rows, :], right[...]).astype(jnp.bfloat16)
        return
    for at, part in enumerate(parts):
        rows = slice(part * quarter, (part + 1) * quarter)
        value = product(left[rows, :], right[...]).astype(jnp.bfloat16)
        out[at * quarter : (at + 1) * quarter, columns] = value


def mlp_grads_kernel(sent, summed, fetched, left, right, *refs):
    sources, (first, second), rest = refs[:fetched], refs[fetched : fetched + 2], refs[fetched + 2 :]
    step = pl.program_id(0)
    copies = []
    if fetched:
        copies = [
            pltpu.make_async_copy(source, target, rest[-1].at[at])
            for at, (source, target) in enumerate(zip(sources, rest[:fetched]))
        ]

    @pl.when(step == 0)
    def _():
        for copy in copies:
            copy.start()
        put_rows(left, right, first, row_parts(sent, True), dot)

    @pl.when(step == 1)
    def _():
        put_rows(left, right, second, row_parts(sent, False), dot)
        for copy in copies:
            copy.wait()

    if summed:
        rest[0][...] = jnp.sum(wide(right[...]), axis=0, keepdims=True)


def qkv_grads_kernel(sent, left, proj_left, both, value, attended, first, second, *sums):
    step = pl.program_id(0)

    def column_sums(array):
        ones = jnp.ones((8, array.shape[1]), jnp.bfloat16)
        return dot_nt(ones, array[...])

    @pl.when(step == 0)
    def _():
        put_rows(left, both, first, row_parts(sent, True), dot_nt)
        if sums:
            sums[0][...] = column_sums(both)
            sums[1][...] = column_sums(value)

    @pl.when(step == 1)
    def _():
        second[...] = jnp.zeros_like(second)
        put_rows(left, value, second, row_parts(sent, False), dot_nt)

    @pl.when(step == 2)
    def _():
        begin = second.shape[1] - attended.shape[0]
        put_rows(proj_left, attended, second, row_parts(sent, False), dot_nt, begin)


SMEM = pl.BlockSpec(memory_space=pltpu.SMEM)
GRADS = 10
FREE = pl.CostEstimate(flops=1, bytes_accessed=1, transcendentals=0)


def micros(time):
    if time == 0:
        return FREE
    return pl.CostEstimate(flops=time * 10**9, bytes_accessed=time * 10**6, transcendentals=0)


def shape(dims, dtype=jnp.bfloat16):
    return jax.ShapeDtypeStruct(dims, dtype)


def room(mib):
    return pltpu.CompilerParams(vmem_limit_bytes=mib << 20)


def spec(dims, kind):
    if kind == "v":
        return VMEM
    if kind == "r":
        return pl.BlockSpec((CHUNK, dims[1]), lambda i: (i, 0))
    if kind == "c":
        return pl.BlockSpec((dims[0], CHUNK), lambda i: (0, i))
    return pl.BlockSpec(tuple(dims), lambda i: (0,) * len(dims))


def sweep(kernel, length, scalars, arrays, outs, work=(), mib=16, cost=200):
    return pl.pallas_call(
        kernel,
        grid=(length // CHUNK,),
        in_specs=[SMEM] * len(scalars) + [spec(a.shape, kind) for a, kind in arrays],
        out_specs=[spec(o.shape, kind) for o, kind in outs],
        out_shape=[o for o, _ in outs],
        scratch_shapes=[pltpu.VMEM(dims, jnp.float32) for dims in work],
        compiler_params=room(mib),
        cost_estimate=micros(cost),
    )(*scalars, *[a for a, _ in arrays])


def mlp_grads(sent, left, right, summed=False, fetch=()):
    width, length = left.shape
    hidden = right.shape[1]
    half = hidden // 2
    out = pl.BlockSpec((width // 2, half), lambda j: (0, 0))
    sums = [pl.BlockSpec((1, half), lambda j: (0, j))] if summed else []
    sums_shape = [shape((1, hidden), jnp.float32)] if summed else []
    return pl.pallas_call(
        functools.partial(mlp_grads_kernel, sent, summed, len(fetch)),
        grid=(2,),
        in_specs=[spec(left.shape, "w"), pl.BlockSpec((length, half), lambda j: (0, j))]
        + [pl.BlockSpec(memory_space=pl.ANY)] * len(fetch),
        out_specs=[out, out] + sums + [VMEM] * len(fetch),
        out_shape=[shape((width // 2, half))] * 2
        + sums_shape
        + [pltpu.VMEM(a.shape, a.dtype) for a in fetch],
        scratch_shapes=[pltpu.SemaphoreType.DMA((len(fetch),))] if fetch else [],
        compiler_params=room(24),
        cost_estimate=micros(GRADS),
    )(left, right, *fetch)


def sum_kernel(counts, splits, *refs):
    halves, at = [], 0
    for count in counts[:2]:
        total = wide(refs[at][...])
        for ref in refs[at + 1 : at + count]:
            total += wide(ref[...])
        halves.append(total)
        at += count
    outs = refs[at + counts[2] :]
    for half in range(2):
        begin = 0 if half == 0 else halves[0].shape[1]
        columns = slice(begin, begin + halves[half].shape[1])
        for ref in refs[at : at + counts[2]]:
            halves[half] += wide(ref[:, columns])
    if splits is None:
        for out, total in zip(outs, halves):
            out[...] = total.astype(out.dtype)
    elif splits == ():
        for total, begin in zip(halves, (0, halves[0].shape[1])):
            outs[0][:, begin : begin + total.shape[1]] = total.astype(outs[0].dtype)
    else:
        for at, (half, begin, end) in enumerate(splits):
            if at < 3:
                outs[0][at] = halves[half][:, begin:end]
            else:
                outs[1][...] = halves[half][:, begin:end]


def sum_rows(halves, joined, at, count, outs, splits=None):
    arrays = halves[0] + halves[1] + joined
    arrays = [pltpu.with_memory_space_constraint(a, pltpu.HBM) for a in arrays]

    def rows(width):
        return pl.BlockSpec((count, width), lambda i: (at, 0))

    return pl.pallas_call(
        functools.partial(sum_kernel, (len(halves[0]), len(halves[1]), len(joined)), splits),
        grid=(1,),
        in_specs=[rows(a.shape[1]) for a in arrays],
        out_specs=[pl.BlockSpec(o.shape, lambda i, n=len(o.shape): (0,) * n) for o in outs],
        out_shape=outs,
        compiler_params=room(16),
        cost_estimate=FREE,
    )(*arrays)


def pack_kernel(
    side, middle, late, gate, cond, proj_bias, down_bias, up_bias, qk_bias, value_bias, out, work
):
    width = out.shape[1]
    segs = cond.shape[0]
    own = [late[:segs, :], late[2 * segs : 3 * segs, :]]
    for source, at in ((middle, 0), (middle, 1), (middle, 2), (gate, 0)):
        own.append(own_part(side[0], source[2 * at * segs : (2 * at + 1) * segs, :], width))
    own += [wide(cond[:, at : at + width]) for at in range(0, cond.shape[1], width)]
    for at, value in enumerate(own):
        work[at * segs : (at + 1) * segs, :] = value
    rows = []
    for source in (proj_bias, down_bias, up_bias):
        rows += [source[0:1, at : at + width] for at in range(0, source.shape[1], width)]
    rows += [qk_bias[0:1, :width], value_bias[0:1, :]]
    first = len(own) * segs
    for at, value in enumerate(rows):
        work[first + at : first + at + 1, :] = value
    out[...] = work[: out.shape[0], :].astype(jnp.bfloat16)


def finish_kernel(segs, first, held, other, cond, other_cond, mod, modbias, bias, work):
    value = jnp.concatenate([wide(held[...]), wide(other[...])], axis=0)
    left = jnp.concatenate([wide(cond[...]), wide(other_cond[...])], axis=0)
    devices, rows, width = value.shape
    left = left.reshape((devices * segs, left.shape[2])).T.astype(jnp.bfloat16)
    for at in range(mod.shape[0]):
        part = value[:, at * segs : (at + 1) * segs, :].reshape((devices * segs, width))
        mod[at] = dot(left, part.astype(jnp.bfloat16))
        modbias[at : at + 1, :] = jnp.sum(part, axis=0, keepdims=True)
    work[:rows, :] = jnp.sum(value, axis=0)
    count = bias.shape[0]
    bias[...] = work[first : first + count, :]


def padded(width):
    return -(-width // 128) * 128


def qkv_grads(sent, left, proj_left, triple, attended):
    width, length = left.shape
    local = attended.shape[0]
    wide_block = padded(local)
    sums_spec = [pl.BlockSpec((8, 2 * local), lambda j: (0, 0)), pl.BlockSpec((8, local), lambda j: (0, 0))]
    sums_shape = [shape((8, 2 * local), jnp.float32), shape((8, local), jnp.float32)]
    return pl.pallas_call(
        functools.partial(qkv_grads_kernel, sent),
        grid=(3,),
        in_specs=[
            spec(left.shape, "w"),
            spec(left.shape, "w"),
            pl.BlockSpec((2 * local, length), lambda j: (0, 0)),
            pl.BlockSpec((local, length), lambda j: (2, 0)),
            spec(attended.shape, "w"),
        ],
        out_specs=[
            pl.BlockSpec((width // 2, 2 * local), lambda j: (0, 0)),
            pl.BlockSpec((width // 2, wide_block + local), lambda j: (0, 0)),
        ]
        + sums_spec * sent,
        out_shape=[shape((width // 2, 2 * local)), shape((width // 2, wide_block + local))]
        + sums_shape * sent,
        compiler_params=room(32),
        cost_estimate=FREE,
    )(left, proj_left, triple, triple, attended)


def attention_forward(segments, qkv, width=256):
    heads, length = qkv.shape[1], qkv.shape[3]
    return pl.pallas_call(
        functools.partial(attention_forward_kernel, width),
        in_specs=[VMEM] * 2,
        out_specs=[VMEM] * 2,
        out_shape=[shape((heads, HEAD_DIM, length)), shape((heads, 1, length), jnp.float32)],
        scratch_shapes=[
            pltpu.VMEM((HEAD_DIM + SEGS, length), jnp.bfloat16),
            pltpu.VMEM((length, HEAD_DIM + SEGS), jnp.bfloat16),
        ],
        compiler_params=room(12),
        cost_estimate=micros(15),
    )(segments, qkv)


def attention_backward(segments, qkv, stat, grad, width=256):
    heads, length = qkv.shape[1], qkv.shape[3]
    return pl.pallas_call(
        functools.partial(attention_backward_kernel, width),
        in_specs=[VMEM] * 4,
        out_specs=VMEM,
        out_shape=shape(qkv.shape),
        scratch_shapes=[
            pltpu.VMEM((HEAD_DIM + SEGS, length), jnp.bfloat16),
            pltpu.VMEM((length, HEAD_DIM + SEGS), jnp.bfloat16),
        ]
        + [pltpu.VMEM((length, HEAD_DIM), jnp.bfloat16)] * 3
        + [pltpu.VMEM((length, length), jnp.bfloat16)] * 2,
        compiler_params=room(16),
        cost_estimate=micros(15),
    )(segments, qkv, stat, grad)


def silu(array):
    return array / (1.0 + jnp.exp(-array))


def product(spec, left, right):
    return jnp.einsum(spec, left, right, preferred_element_type=jnp.float32)


def exchange(array):
    return lax.ppermute(array, "tensor", [(0, 1), (1, 0)])


def summands(part, size):
    if size == 2:
        return part, exchange(part)
    return lax.psum(part, "tensor"), jnp.zeros_like(part)


def tensor_join(array, size):
    if size == 2:
        other = exchange(array)
        first = lax.axis_index("tensor") == 0
        return jnp.concatenate(
            [jnp.where(first, array, other), jnp.where(first, other, array)], axis=-1
        )
    return lax.all_gather(array, "tensor", axis=array.ndim - 1, tiled=True)


def partners(size, bit):
    return [(i, i ^ (1 << bit)) for i in range(size)]


def tie(*values):
    return lax.optimization_barrier(values)


def after(value, *others):
    return tie(value, *others)[0]


class Gather:
    def __init__(self, array, size, order):
        self.held, self.size, self.order = array[None], size, list(order)

    def last(self):
        bit = self.order.pop(0)
        return self.held, lax.ppermute(self.held, "batch", partners(self.size, bit))

    def step(self, *others):
        if self.order:
            bit = self.order.pop(0)
            self.held = after(self.held, *others)
            other = lax.ppermute(self.held, "batch", partners(self.size, bit))
            self.held = jnp.concatenate([self.held, other], axis=0)


class Sum:
    def __init__(self, sends, size, kernels):
        self.kernels = kernels
        self.sends, self.size, self.bits = sends, size, size.bit_length() - 1
        self.keeps, self.got = None, []

    def pieces(self, at, count, dtype, splits=None, outs=None):
        halves = [[self.keeps[h]] + [stage[h] for stage in self.got[:2]] for h in range(2)]
        joined = [new for (new,) in self.got[2:]]
        widths = [half[0].shape[1] for half in halves]
        if self.kernels:
            if outs is None:
                outs = [shape((count, width), dtype) for width in widths]
                if len(self.got) > 1:
                    outs, splits = [shape((count, sum(widths)), dtype)], ()
            return list(sum_rows(halves, joined, at, count, outs, splits))
        window = slice(at * count, (at + 1) * count)
        totals = [sum(a[window].astype(jnp.float32) for a in half) for half in halves]
        if len(self.got) < 2:
            return [total.astype(dtype) for total in totals]
        total = jnp.concatenate(totals, axis=1)
        total = sum((a[window].astype(jnp.float32) for a in joined), total)
        if outs is None:
            return [total.astype(dtype)]
        if splits == ():
            return [total.astype(dtype)]
        totals = [total[:, : widths[0]], total[:, widths[0] :]]
        parts = [totals[half][:, begin:end] for half, begin, end in splits]
        return [jnp.stack(parts[:3]), parts[3]]

    def send(self, *others):
        stage = len(self.got)
        sends, bits = self.sends, [stage]
        if stage > 0:
            left = self.keeps[0].shape[0] >> stage
            sends = self.pieces(1, left, jnp.bfloat16)
        if stage < 2:
            bits = [stage, 1 - stage]
        tied = tie(*sends, *others)
        self.sent = tied[: len(sends)]
        self.flying = [
            lax.ppermute(piece, "batch", partners(self.size, bit))
            for piece, bit in zip(tied, bits)
        ]
        return tied[len(sends) :]

    def take(self, *others):
        tied = tie(*self.flying, *others)
        self.got.append(tied[: len(self.flying)])
        return tied[len(self.flying) :]

    def settle(self, other):
        if len(self.got) == self.bits:
            self.keeps = list(tie(*self.keeps, other)[:2])

    def result(self, splits=()):
        while len(self.got) < self.bits:
            self.send()
            self.take()
        count = 2 * self.keeps[0].shape[0] // self.size
        if splits:
            width = splits[0][2] - splits[0][1]
            outs = [shape((3, count, width), jnp.float32), shape((count, width), jnp.float32)]
        else:
            outs = [shape((count, sum(keep.shape[1] for keep in self.keeps)), jnp.float32)]
        return self.pieces(0, count, jnp.float32, splits, outs)


def gelu_and_slope(array):
    square = array * array
    bent = jnp.tanh(0.7978845608028654 * (array + 0.044715 * array * square))
    half = 0.5 * (1.0 + bent)
    inner = 0.7978845608028654 * (1.0 + 3.0 * 0.044715 * square)
    return array * half, half + 0.5 * array * (1.0 - bent * bent) * inner


def in_three(array):
    high = lax.reduce_precision(array, 8, 7)
    middle = lax.reduce_precision(array - high, 8, 7)
    return [high, middle, array - high - middle]


def on_device(
    n_batch,
    tokens,
    segment_ids,
    conditions,
    condition_segment,
    qkv_weight,
    qv_bias,
    proj_weight,
    proj_bias,
    up_weight,
    up_bias,
    down_weight,
    down_bias,
    mod_weight,
    mod_bias,
    out_grad,
):
    bf16, f32 = jnp.bfloat16, jnp.float32
    tokens, out_grad = tokens[0], out_grad[0]
    length, model_width = tokens.shape
    local_width = qkv_weight.shape[2]
    hidden_width = up_weight.shape[1]
    heads = local_width // HEAD_DIM
    n_tensor = model_width // local_width
    bits = list(range(n_batch.bit_length() - 1))
    block = model_width // n_batch
    in_kernel = block % 8 == 0
    index = lax.axis_index("batch")
    order = jnp.array(
        [sum((p >> bit & 1) << (bits[-1] - bit) for bit in bits) for p in range(n_batch)], jnp.int32
    )
    order = order ^ index
    side = lax.axis_index("tensor")[None]

    def run(kernel, scalars, arrays, outs):
        turned = shape((model_width, length))
        if in_kernel:
            chunk = (model_width, CHUNK)
            return sweep(kernel, length, scalars, arrays, outs + [(turned, "c")], [chunk])
        got = sweep(kernel, length, scalars, arrays, outs)
        return list(got) + [got[0].T.reshape((n_batch, block, length))[order].reshape(turned.shape)]

    def part_rows(left, sent, first):
        quarter = model_width // 4
        rows = [left[at * quarter : (at + 1) * quarter] for at in row_parts(sent, first)]
        return jnp.concatenate(rows)

    def hidden_grads(sent, left, right, summed=False, fetch=()):
        if in_kernel:
            first, second, *rest = mlp_grads(sent, left, right, summed, fetch)
            return [first, second], rest
        rest = [jnp.sum(right.astype(f32), axis=0)[None]] if summed else fetch
        cut = right.shape[1] // 2
        return [
            product("dl,lc->dc", part_rows(left, sent, True), right[:, :cut]).astype(bf16),
            product("dl,lc->dc", part_rows(left, sent, False), right[:, cut:]).astype(bf16),
        ], rest

    def attention_grads(sent, left, proj_left, triple, attended):
        if in_kernel:
            first, second, *sums = qkv_grads(sent, left, proj_left, triple, attended)
            return [first, second], sums
        sums = jnp.sum(triple.astype(f32), axis=1)[None]
        sums = (sums[:, : 2 * local_width], sums[:, 2 * local_width :])
        cut, extra = 2 * local_width, ((0, 0), (0, padded(local_width) - local_width))
        halves = [
            (part_rows(left, sent, True), triple[:cut]),
            (part_rows(left, sent, False), triple[cut:]),
            (part_rows(proj_left, sent, False), attended),
        ]
        first, value, proj = [product("dl,cl->dc", *pair).astype(bf16) for pair in halves]
        return [first, jnp.concatenate([jnp.pad(value, extra), proj], axis=1)], sums

    cond_float = conditions[0].astype(f32)
    cond_act = silu(cond_float).astype(bf16)
    mod_local = product("sd,djc->jsc", cond_act, mod_weight) + mod_bias[:, None]
    modulation = tensor_join(mod_local, n_tensor)
    segs = modulation.shape[1]
    tables = jnp.concatenate(in_three(modulation) + [jnp.zeros_like(modulation)], axis=1).astype(bf16)
    marks = jnp.concatenate([condition_segment[0], jnp.full((segs,), -1, jnp.int32)])[:, None]
    full, column = (length, model_width), shape((length, 1), f32)
    mine = (length, local_width)
    row = shape((1, model_width), f32)

    qkv_weight = qkv_weight.transpose((1, 2, 0))
    attn_in, mean_one, inverse_one, normed_mine, picks, biases, in_t = run(
        entry_kernel,
        [order, side],
        [(marks, "v"), (segment_ids, "c"), (tables, "v"), (qv_bias, "v"), (tokens, "r")],
        [
            (shape(full), "r"),
            (column, "r"),
            (column, "r"),
            (shape(mine, f32), "r"),
            (shape((length, 4 * segs)), "r"),
            (shape((3, local_width), f32), "w"),
        ],
    )
    qkv = product("jcd,ld->jcl", qkv_weight, attn_in) + biases[:, :, None]
    qkv = qkv.astype(bf16).reshape((3, heads, HEAD_DIM, length))
    attended, stat = attention_forward(segment_ids, qkv)
    attended = attended.reshape((local_width, length))
    proj_part = product("cl,cd->ld", attended, proj_weight).astype(bf16)
    proj_part, proj_other = summands(proj_part, n_tensor)
    out_grad, proj_tied = tie(out_grad, proj_part)
    mlp_grad, down_bias_grad, grad_t = run(
        gate_kernel,
        [order],
        [(picks, "r"), (tables, "v"), (out_grad, "r")],
        [(shape(full), "r"), (row, "w")],
    )
    proj_other, mlp_grad = tie(proj_other, mlp_grad)
    middle_args = [
        (tables, "v"), (tokens, "r"), (proj_tied, "r"), (proj_other, "r"), (proj_bias[None], "v")
    ]
    mlp_in, mean_two, inverse_two, mlp_t = run(
        middle_kernel,
        [order],
        [(picks, "r")] + middle_args,
        [(shape(full), "r"), (column, "r"), (column, "r")],
    )
    hidden = product("ld,df->lf", mlp_in, up_weight) + up_bias
    active, slope = gelu_and_slope(hidden)
    active, slope = tie(active.astype(bf16), slope.astype(bf16))

    sends, _ = hidden_grads(True, grad_t, active)
    down_sum = Sum(sends, n_batch, in_kernel)
    (mlp_grad_then, active_then) = down_sum.send(mlp_grad, active)
    active_grad = product("ld,fd->lf", mlp_grad_then, down_weight)
    hidden_grad = (active_grad * slope.astype(f32)).astype(bf16)
    mlp_part = product("lf,df->ld", hidden_grad, up_weight).astype(bf16)
    mlp_part, mlp_other = summands(mlp_part, n_tensor)
    (hidden_then, mlp_tied) = tie(hidden_grad, mlp_part)
    sends, (up_bias_grad,) = hidden_grads(True, mlp_t, hidden_then, summed=True)
    up_sum = Sum(sends, n_batch, in_kernel)
    down_sum.keeps, _ = hidden_grads(False, grad_t, active_then)
    first, second, *down_sum.keeps = down_sum.take(*up_sum.sends, *down_sum.keeps)
    up_sum.sends = [first, second]
    (mlp_other, hidden_then) = down_sum.send(mlp_other, hidden_then)
    (mlp_other, hidden_then) = up_sum.send(mlp_other, hidden_then)
    attn_grad, proj_bias_grad, grad_mine, early_totals, attn_t = run(
        middle_grad_kernel,
        [order, side],
        [(picks, "r"), (marks, "v"), (segment_ids, "c")]
        + middle_args
        + [(mean_two, "r"), (inverse_two, "r"), (mlp_tied, "r"), (mlp_other, "r"), (out_grad, "r")],
        [
            (shape(full), "r"),
            (row, "w"),
            (shape(mine, f32), "r"),
            (shape((6 * segs, model_width), f32), "w"),
        ],
    )
    attended_grad = product("cd,ld->cl", proj_weight, attn_grad).astype(bf16)

    triple = attention_backward(
        segment_ids, qkv, stat, attended_grad.reshape((heads, HEAD_DIM, length))
    ).reshape((3 * local_width, length))
    up_sum.keeps, _ = hidden_grads(False, mlp_t, hidden_then)
    sends, (qk_bias_grad, value_bias_grad) = attention_grads(True, in_t, attn_t, triple, attended)
    qkv_sum = Sum(sends, n_batch, in_kernel)
    first, second, *up_sum.keeps = up_sum.take(*qkv_sum.sends, *up_sum.keeps)
    qkv_sum.sends = [first, second]
    (triple,) = down_sum.take(triple)
    (triple,) = up_sum.send(triple)
    (triple,) = qkv_sum.send(triple)
    (triple,) = down_sum.send(triple)
    attn_part = product(
        "jcl,jcd->ld", triple.reshape((3, local_width, length)), qkv_weight
    ).astype(bf16)
    kept, sent, sums = sweep(
        halves_kernel,
        length,
        [side],
        [
            (picks, "r"),
            (tables, "v"),
            (attn_part, "r"),
            (tokens, "r"),
            (mean_one, "r"),
            (inverse_one, "r"),
        ],
        [
            (shape(mine), "r"),
            (shape((length, padded(local_width + 4))), "r"),
            (shape((length, 2), f32), "r"),
        ],
        cost=0,
    )
    down_part = product("lf,fd->ld", after(active, kept), down_weight).astype(bf16)
    (kept, sent, down_part) = up_sum.take(kept, sent, down_part)
    (kept, sent) = down_sum.take(kept, sent)
    (kept, sent, triple) = up_sum.send(kept, sent, triple)
    (kept, sent, triple) = down_sum.send(kept, sent, triple)
    (mod_local, kept) = tie(mod_local, kept)
    tables_mine = jnp.concatenate(in_three(mod_local) + [jnp.zeros_like(mod_local)], axis=1).astype(bf16)
    if n_tensor == 2:
        other = exchange(sent)
    else:
        kept = lax.psum_scatter(attn_part, "tensor", scatter_dimension=1, tiled=True)
        other = jnp.zeros_like(sent)
        sums = lax.psum(sums, "tensor")
    qkv_sum.keeps, _ = attention_grads(False, in_t, attn_t, triple, attended)
    token_t, late_totals = sweep(
        functools.partial(token_grad_kernel, model_width),
        length,
        [],
        [
            (picks, "r"),
            (marks, "v"), (segment_ids, "c"),
            (tables_mine, "v"),
            (kept, "r"),
            (other, "r"),
            (sums, "r"),
            (normed_mine, "r"),
            (inverse_one, "r"),
            (grad_mine, "r"),
        ],
        [(shape((local_width, length), f32), "c"), (shape((4 * segs, local_width), f32), "w")],
        cost=0,
    )
    (late_totals, *qkv_sum.keeps) = qkv_sum.take(late_totals, *qkv_sum.keeps)
    (late_totals,) = up_sum.take(late_totals)
    (down_part, late_totals) = qkv_sum.send(down_part, late_totals)
    (down_part, late_totals) = up_sum.send(down_part, late_totals)
    (down_part,) = down_sum.take(down_part)
    down_part, down_other = summands(down_part, n_tensor)
    layer_out, gate_total = sweep(
        layer_kernel,
        length,
        [],
        [(picks, "r"), (marks, "v"), (segment_ids, "c")]
        + middle_args
        + [(down_part, "r"), (down_other, "r"), (down_bias[None], "v"), (out_grad, "r")],
        [(shape(full), "r"), (shape((2 * segs, model_width), f32), "w")],
        cost=0,
    )
    (gate_total,) = up_sum.take(gate_total)
    bias_rows = 2 * n_tensor + hidden_width // local_width + 2
    rows = (6 + n_tensor) * segs + bias_rows
    (packed,) = pl.pallas_call(
        pack_kernel,
        in_specs=[SMEM] + [VMEM] * 9,
        out_specs=[VMEM],
        out_shape=[shape((rows, local_width))],
        scratch_shapes=[pltpu.VMEM((-(-rows // 16) * 16, local_width), f32)],
        compiler_params=room(16),
        cost_estimate=FREE,
    )(
        side,
        early_totals,
        late_totals,
        gate_total,
        cond_act,
        proj_bias_grad,
        down_bias_grad,
        up_bias_grad,
        qk_bias_grad,
        value_bias_grad,
    )
    gathered = Gather(packed, n_batch, bits[:1:-1] + bits[1::-1])
    gathered.step()
    (packed, gathered.held) = qkv_sum.take(packed, gathered.held)
    (packed,) = qkv_sum.send(packed)
    gathered.step()
    tgrad = packed[: 6 * segs].reshape((6, segs, local_width))
    gathered.step()
    (gathered.held,) = qkv_sum.take(gathered.held)
    qkv_sum.send()
    while len(gathered.order) > 1:
        gathered.step()
    halves = gathered.last()
    down_sum.settle(qkv_sum.sent[0])
    up_sum.settle(qkv_sum.sent[0])
    (down,), (up,) = down_sum.result(), up_sum.result()
    (up, down) = qkv_sum.take(up, down)
    cond_then = after(tgrad, *qkv_sum.got[-1])
    cond_part = product("jsc,djc->sd", cond_then, mod_weight)
    cond_part, cond_other = summands(cond_part.astype(bf16), n_tensor)
    cond_act_grad = cond_part.astype(f32) + cond_other.astype(f32)
    condition_grad = jax.vjp(silu, cond_float)[1](cond_act_grad)[0]

    part = index * block // local_width
    cond_blocks = [
        lax.dynamic_slice(
            half,
            (0, (6 + part) * segs, index * block % local_width),
            (half.shape[0], segs, block),
        )
        for half in halves
    ]
    mod_sum, modbias_sum, bias_all = pl.pallas_call(
        functools.partial(finish_kernel, segs, (6 + n_tensor) * segs),
        in_specs=[VMEM] * 4,
        out_specs=[VMEM] * 3,
        out_shape=[
            shape((6, block, local_width), f32),
            shape((6, local_width), f32),
            shape((bias_rows, local_width), f32),
        ],
        scratch_shapes=[pltpu.VMEM((-(-rows // 8) * 8, local_width), f32)],
        compiler_params=room(24),
        cost_estimate=FREE,
    )(*halves, *cond_blocks)
    qv_sum = bias_all[-2:]
    bias_all = bias_all[:-2].reshape(-1)
    projbias_sum = bias_all[:model_width]
    downbias_sum = bias_all[model_width : 2 * model_width]
    upbias_sum = bias_all[2 * model_width :]
    mod_sum = mod_sum.transpose((1, 0, 2))
    begin = padded(local_width)
    last, proj_last = qkv_sum.result(
        [
            (0, 0, local_width),
            (0, local_width, 2 * local_width),
            (1, 0, local_width),
            (1, begin, begin + local_width),
        ]
    )
    last = last.transpose((1, 0, 2))
    return (
        layer_out[None],
        token_t.T[None],
        condition_grad[None],
        last,
        qv_sum,
        proj_last.T,
        projbias_sum,
        up,
        upbias_sum,
        down.T,
        downbias_sum,
        mod_sum,
        modbias_sum,
    )


def solution(mesh):
    return jax.shard_map(
        functools.partial(on_device, mesh.shape["batch"]),
        mesh=mesh,
        in_specs=(
            P("batch", None, None),
            P("batch", None),
            P("batch", None, None),
            P("batch", None),
            P(None, None, "tensor"),
            P(None, "tensor"),
            P("tensor", None),
            P(),
            P(None, "tensor"),
            P("tensor"),
            P("tensor", None),
            P(),
            P(None, None, "tensor"),
            P(None, "tensor"),
            P("batch", None, None),
        ),
        out_specs=(
            P("batch", None, None),
            P("batch", None, "tensor"),
            P("batch", None, None),
            P("batch", None, "tensor"),
            P(None, "tensor"),
            P("tensor", "batch"),
            P(),
            P("batch", "tensor"),
            P("tensor"),
            P("tensor", "batch"),
            P(),
            P("batch", None, "tensor"),
            P(None, "tensor"),
        ),
        check_vma=False,
    )
```

```python
import functools

import jax
import jax.numpy as jnp
from jax import lax
from jax.experimental import pallas as pl
from jax.experimental.pallas import tpu as pltpu
from jax.sharding import PartitionSpec as P

EPS = 1e-06
HEAD_DIM = 72
SEGS = 8
MOST = 256
LOG2E = 1.4426950408889634
NEG = -1e30


def band(begin, width, length):
    low = max(0, (begin - MOST + 1) // 128 * 128)
    high = min(length, -(-(begin + width + MOST - 1) // 128) * 128)
    return low, high


def natural(array):
    return array.astype(jnp.float32).T.astype(jnp.bfloat16)


def marks(seg_row):
    slots = lax.broadcasted_iota(jnp.int32, (SEGS, seg_row.shape[-1]), 0)
    return (slots == seg_row[...]).astype(jnp.float32)


def fill(head, qkv, one_hot, q_aug, k_nat):
    query = jnp.concatenate([qkv[0, head].astype(jnp.float32), (1.0 - one_hot) * NEG], axis=0)
    q_aug[...] = query.astype(jnp.bfloat16)
    k_nat[...] = natural(jnp.concatenate([qkv[1, head].astype(jnp.float32), one_hot], axis=0))


def attention_forward_kernel(width, seg_row, qkv, out, stat, q_aug, k_nat):
    heads, length = qkv.shape[1], qkv.shape[3]
    factor = HEAD_DIM**-0.5 * LOG2E
    one_hot = marks(seg_row)

    def one(head, carry):
        fill(head, qkv, one_hot, q_aug, k_nat)
        for begin in range(0, length, width):
            low, high = band(begin, width, length)
            span = slice(begin, begin + width)
            scores = jnp.dot(
                k_nat[low:high, :], q_aug[:, span], preferred_element_type=jnp.float32
            )
            peak = jnp.max(scores, axis=0, keepdims=True) * factor
            shifted = jnp.exp2(scores * factor - peak)
            total = jnp.sum(shifted, axis=0, keepdims=True)
            got = jnp.dot(
                qkv[2, head, :, low:high],
                shifted.astype(jnp.bfloat16),
                preferred_element_type=jnp.float32,
            )
            out[head, :, span] = (got * (1.0 / total)).astype(jnp.bfloat16)
            stat[head, :, span] = peak + jnp.log2(total)
        return carry

    lax.fori_loop(0, heads, one, 0, unroll=2)


def attention_backward_kernel(
    width, seg_row, qkv, stat, grad, out, q_aug, k_nat, v_nat, q_nat, g_nat, p_all, s_all
):
    heads, length = qkv.shape[1], qkv.shape[3]
    scale = HEAD_DIM**-0.5
    factor = scale * LOG2E
    one_hot = marks(seg_row)

    def one(head, carry):
        fill(head, qkv, one_hot, q_aug, k_nat)
        v_nat[...] = natural(qkv[2, head])
        q_nat[...] = natural(qkv[0, head])
        g_nat[...] = natural(grad[head])
        for begin in range(0, length, width):
            low, high = band(begin, width, length)
            span = slice(begin, begin + width)
            scores = jnp.dot(
                k_nat[low:high, :], q_aug[:, span], preferred_element_type=jnp.float32
            )
            probs = jnp.exp2(scores * factor - stat[head, :, span])
            prob_grad = jnp.dot(
                v_nat[low:high, :], grad[head, :, span], preferred_element_type=jnp.float32
            )
            row = jnp.sum(prob_grad * probs, axis=0, keepdims=True)
            score_grad = (probs * (prob_grad - row)).astype(jnp.bfloat16)
            p_all[low:high, span] = probs.astype(jnp.bfloat16)
            s_all[low:high, span] = score_grad
            got = jnp.dot(
                qkv[1, head, :, low:high], score_grad, preferred_element_type=jnp.float32
            )
            out[0, head, :, span] = (got * scale).astype(jnp.bfloat16)
        for begin in range(0, length, width):
            span = slice(begin, begin + width)
            reach = [q for q in range(0, length, width) if band(q, width, length)[0] < begin + width and band(q, width, length)[1] > begin]
            low, high = reach[0], reach[-1] + width
            key_grad = jnp.dot(
                s_all[span, low:high], q_nat[low:high, :], preferred_element_type=jnp.float32
            )
            value_grad = jnp.dot(
                p_all[span, low:high], g_nat[low:high, :], preferred_element_type=jnp.float32
            )
            out[1, head, :, span] = (key_grad * scale).T.astype(jnp.bfloat16)
            out[2, head, :, span] = value_grad.T.astype(jnp.bfloat16)
        return carry

    if width < MOST:
        p_all[...] = jnp.zeros_like(p_all)
        s_all[...] = jnp.zeros_like(s_all)
    lax.fori_loop(0, heads, one, 0, unroll=2)


VMEM = pl.BlockSpec(memory_space=pltpu.VMEM)


CHUNK = 128


def dot(left, right):
    return jnp.dot(left, right, preferred_element_type=jnp.float32)


def dot_nt(left, right):
    return lax.dot_general(
        left, right, (((1,), (1,)), ((), ())), preferred_element_type=jnp.float32
    )


def wide(value):
    return value.astype(jnp.float32)


def turn(order, value, out, work):
    count = order.shape[0]
    rows = value.shape[1] // count
    work[...] = wide(value).T
    for at in range(0, count, 2):
        pair = [
            work[pl.ds(pl.multiple_of(order[at + i] * rows, 8), rows), :] for i in range(2)
        ]
        pair = jnp.concatenate(pair, axis=0).astype(jnp.bfloat16)
        out[at * rows : (at + 2) * rows, :] = pair


def own_part(side, value, width):
    part = value[:, :width]
    for at in range(1, value.shape[1] // width):
        part = jnp.where(side == at, value[:, at * width : (at + 1) * width], part)
    return part


def accumulate(total, value):
    @pl.when(pl.program_id(0) == 0)
    def _():
        total[...] = value

    @pl.when(pl.program_id(0) > 0)
    def _():
        total[...] += value


def segment_sums(slots, seg, *values):
    marks = (slots[...] == seg[...]).astype(jnp.bfloat16)
    marks = jnp.concatenate([marks, marks], axis=1)
    sums = []
    for value in values:
        high = value.astype(jnp.bfloat16)
        low = (value - wide(high)).astype(jnp.bfloat16)
        sums.append(dot(marks, jnp.concatenate([high, low], axis=0)))
    return jnp.concatenate(sums, axis=0)


def norm_parts(value):
    width = value.shape[1]
    mean = jnp.sum(value, axis=1, keepdims=True) / width
    center = value - mean
    spread = jnp.sum(center * center, axis=1, keepdims=True) / width
    return mean, center, lax.rsqrt(spread + EPS)


def entry_kernel(
    order, side, slots, seg, tables, bias, tokens,
    out, mean, inverse, normed_mine, picks, biases, *turned
):
    segs = slots.shape[0] // 2
    column = jnp.concatenate([slots[:segs, :]] * 3 + [slots[segs:, :]], axis=0)
    pick = (column == seg[...]).astype(jnp.float32).T.astype(jnp.bfloat16)
    picks[...] = pick
    biases[0:1, :] = bias[0:1, :]
    biases[1:2, :] = jnp.zeros_like(biases[1:2, :])
    biases[2:3, :] = bias[1:2, :]
    middle, center, scale = norm_parts(wide(tokens[...]))
    mean[...] = middle
    inverse[...] = scale
    value = center * scale
    normed_mine[...] = own_part(side[0], value, normed_mine.shape[1])
    value = (value * (1.0 + dot(pick, tables[1])) + dot(pick, tables[0])).astype(jnp.bfloat16)
    out[...] = value
    if turned:
        turn(order, value, *turned)


def gate_kernel(order, picks, tables, grad, out, bias, *turned):
    value = (wide(grad[...]) * dot(picks[...], tables[5])).astype(jnp.bfloat16)
    out[...] = value
    accumulate(bias, jnp.sum(wide(value), axis=0, keepdims=True))
    if turned:
        turn(order, value, *turned)


def middle_of(pick, tables, tokens, part, other, bias):
    attn_out = wide(part[...]) + wide(other[...]) + bias[...]
    return attn_out, wide(tokens[...]) + dot(pick, tables[2]) * attn_out


def middle_kernel(order, picks, tables, tokens, part, other, bias, out, mean, inverse, *turned):
    pick = picks[...]
    value = middle_of(pick, tables, tokens, part, other, bias)[1]
    middle, center, scale = norm_parts(value)
    mean[...] = middle
    inverse[...] = scale
    value = center * scale * (1.0 + dot(pick, tables[4])) + dot(pick, tables[3])
    value = value.astype(jnp.bfloat16)
    out[...] = value
    if turned:
        turn(order, value, *turned)


def middle_grad_kernel(
    order, side, picks, marks, seg, tables, tokens, part, other, bias, mean, inverse, mlp, mlp_other, grad,
    out, bias_sum, grad_mine, totals, *turned
):
    pick = picks[...]
    width = grad.shape[1]
    attn_out, value = middle_of(pick, tables, tokens, part, other, bias)
    norm = (value - mean[...]) * inverse[...]
    in_grad = wide(mlp[...]) + wide(mlp_other[...])
    value = in_grad * (1.0 + dot(pick, tables[4]))
    plain = jnp.sum(value, axis=1, keepdims=True) / width
    cross = jnp.sum(value * norm, axis=1, keepdims=True) / width
    value = wide(grad[...]) + inverse[...] * (value - plain - norm * cross)
    grad_mine[...] = own_part(side[0], value, grad_mine.shape[1])
    accumulate(totals, segment_sums(marks, seg, value * attn_out, in_grad, in_grad * norm))
    value = (value * dot(pick, tables[2])).astype(jnp.bfloat16)
    out[...] = value
    accumulate(bias_sum, jnp.sum(wide(value), axis=0, keepdims=True))
    if turned:
        turn(order, value, *turned)


def halves_kernel(side, picks, tables, part, tokens, mean, inverse, kept, sent, sums):
    value = part[...]
    width = kept.shape[1]
    kept[...] = own_part(side[0], value, width)
    sent[:, :width] = own_part(1 - side[0], value, width)
    value = wide(value) * (1.0 + dot(picks[...], tables[1]))
    norm = (wide(tokens[...]) - mean[...]) * inverse[...]
    for at, term in enumerate((value, value * norm)):
        total = jnp.sum(term, axis=1, keepdims=True)
        high = total.astype(jnp.bfloat16)
        sums[:, at : at + 1] = total
        sent[:, width + 2 * at : width + 2 * at + 1] = high
        sent[:, width + 2 * at + 1 : width + 2 * at + 2] = (total - wide(high)).astype(jnp.bfloat16)


def token_grad_kernel(
    width, picks, marks, seg, tables, kept, other, sums, normed, inverse, grad, out_t, totals
):
    mine = kept.shape[1]
    value = wide(kept[...]) + wide(other[:, :mine])
    norm = normed[...]
    accumulate(totals, segment_sums(marks, seg, value, value * norm))
    value = value * (1.0 + dot(picks[...], tables[1]))
    for at, factor in enumerate((1.0, norm)):
        rest = wide(other[:, mine + 2 * at : mine + 2 * at + 1])
        rest = rest + wide(other[:, mine + 2 * at + 1 : mine + 2 * at + 2])
        value = value - factor * ((sums[:, at : at + 1] + rest) / width)
    out_t[...] = (grad[...] + inverse[...] * value).T


def layer_kernel(
    picks, marks, seg, tables, tokens, part, other, bias, down, down_other, down_bias, grad, out, totals
):
    pick = picks[...]
    mlp_out = wide(down[...]) + wide(down_other[...]) + down_bias[...]
    middle = middle_of(pick, tables, tokens, part, other, bias)[1]
    out[...] = (middle + dot(pick, tables[5]) * mlp_out).astype(jnp.bfloat16)
    accumulate(totals, segment_sums(marks, seg, wide(grad[...]) * mlp_out))


def row_parts(sent, first):
    if first:
        return (2, 3) if sent else (0, 1)
    return (1, 3) if sent else (0, 2)


def put_rows(left, right, out, parts, product, begin=0):
    quarter = left.shape[0] // 4
    columns = slice(begin, begin + (right.shape[0] if product is dot_nt else right.shape[1]))
    if parts[1] == parts[0] + 1:
        rows = slice(parts[0] * quarter, (parts[1] + 1) * quarter)
        out[:, columns] = product(left[rows, :], right[...]).astype(jnp.bfloat16)
        return
    for at, part in enumerate(parts):
        rows = slice(part * quarter, (part + 1) * quarter)
        value = product(left[rows, :], right[...]).astype(jnp.bfloat16)
        out[at * quarter : (at + 1) * quarter, columns] = value


def mlp_grads_kernel(sent, summed, fetched, left, right, *refs):
    sources, (first, second), rest = refs[:fetched], refs[fetched : fetched + 2], refs[fetched + 2 :]
    step = pl.program_id(0)
    copies = []
    if fetched:
        copies = [
            pltpu.make_async_copy(source, target, rest[-1].at[at])
            for at, (source, target) in enumerate(zip(sources, rest[:fetched]))
        ]

    @pl.when(step == 0)
    def _():
        for copy in copies:
            copy.start()
        put_rows(left, right, first, row_parts(sent, True), dot)

    @pl.when(step == 1)
    def _():
        put_rows(left, right, second, row_parts(sent, False), dot)
        for copy in copies:
            copy.wait()

    if summed:
        rest[0][...] = jnp.sum(wide(right[...]), axis=0, keepdims=True)


def qkv_grads_kernel(sent, left, proj_left, both, value, attended, first, second, *sums):
    step = pl.program_id(0)

    def column_sums(array):
        ones = jnp.ones((8, array.shape[1]), jnp.bfloat16)
        return dot_nt(ones, array[...])

    @pl.when(step == 0)
    def _():
        put_rows(left, both, first, row_parts(sent, True), dot_nt)
        if sums:
            sums[0][...] = column_sums(both)
            sums[1][...] = column_sums(value)

    @pl.when(step == 1)
    def _():
        second[...] = jnp.zeros_like(second)
        put_rows(left, value, second, row_parts(sent, False), dot_nt)

    @pl.when(step == 2)
    def _():
        begin = second.shape[1] - attended.shape[0]
        put_rows(proj_left, attended, second, row_parts(sent, False), dot_nt, begin)


SMEM = pl.BlockSpec(memory_space=pltpu.SMEM)
GRADS = 10
FREE = pl.CostEstimate(flops=1, bytes_accessed=1, transcendentals=0)


def micros(time):
    if time == 0:
        return FREE
    return pl.CostEstimate(flops=time * 10**9, bytes_accessed=time * 10**6, transcendentals=0)


def shape(dims, dtype=jnp.bfloat16):
    return jax.ShapeDtypeStruct(dims, dtype)


def room(mib):
    return pltpu.CompilerParams(vmem_limit_bytes=mib << 20)


def spec(dims, kind):
    if kind == "v":
        return VMEM
    if kind == "r":
        return pl.BlockSpec((CHUNK, dims[1]), lambda i: (i, 0))
    if kind == "c":
        return pl.BlockSpec((dims[0], CHUNK), lambda i: (0, i))
    return pl.BlockSpec(tuple(dims), lambda i: (0,) * len(dims))


def sweep(kernel, length, scalars, arrays, outs, work=(), mib=16, cost=200):
    return pl.pallas_call(
        kernel,
        grid=(length // CHUNK,),
        in_specs=[SMEM] * len(scalars) + [spec(a.shape, kind) for a, kind in arrays],
        out_specs=[spec(o.shape, kind) for o, kind in outs],
        out_shape=[o for o, _ in outs],
        scratch_shapes=[pltpu.VMEM(dims, jnp.float32) for dims in work],
        compiler_params=room(mib),
        cost_estimate=micros(cost),
    )(*scalars, *[a for a, _ in arrays])


def mlp_grads(sent, left, right, summed=False, fetch=()):
    width, length = left.shape
    hidden = right.shape[1]
    half = hidden // 2
    out = pl.BlockSpec((width // 2, half), lambda j: (0, 0))
    sums = [pl.BlockSpec((1, half), lambda j: (0, j))] if summed else []
    sums_shape = [shape((1, hidden), jnp.float32)] if summed else []
    return pl.pallas_call(
        functools.partial(mlp_grads_kernel, sent, summed, len(fetch)),
        grid=(2,),
        in_specs=[spec(left.shape, "w"), pl.BlockSpec((length, half), lambda j: (0, j))]
        + [pl.BlockSpec(memory_space=pl.ANY)] * len(fetch),
        out_specs=[out, out] + sums + [VMEM] * len(fetch),
        out_shape=[shape((width // 2, half))] * 2
        + sums_shape
        + [pltpu.VMEM(a.shape, a.dtype) for a in fetch],
        scratch_shapes=[pltpu.SemaphoreType.DMA((len(fetch),))] if fetch else [],
        compiler_params=room(24),
        cost_estimate=micros(GRADS),
    )(left, right, *fetch)


def sum_kernel(counts, splits, *refs):
    halves, at = [], 0
    for count in counts[:2]:
        total = wide(refs[at][...])
        for ref in refs[at + 1 : at + count]:
            total += wide(ref[...])
        halves.append(total)
        at += count
    outs = refs[at + counts[2] :]
    for half in range(2):
        begin = 0 if half == 0 else halves[0].shape[1]
        columns = slice(begin, begin + halves[half].shape[1])
        for ref in refs[at : at + counts[2]]:
            halves[half] += wide(ref[:, columns])
    if splits is None:
        for out, total in zip(outs, halves):
            out[...] = total.astype(out.dtype)
    elif splits == ():
        for total, begin in zip(halves, (0, halves[0].shape[1])):
            outs[0][:, begin : begin + total.shape[1]] = total.astype(outs[0].dtype)
    else:
        for at, (half, begin, end) in enumerate(splits):
            if at < 3:
                outs[0][at] = halves[half][:, begin:end]
            else:
                outs[1][...] = halves[half][:, begin:end]


def sum_rows(halves, joined, at, count, outs, splits=None):
    arrays = halves[0] + halves[1] + joined
    arrays = [pltpu.with_memory_space_constraint(a, pltpu.HBM) for a in arrays]

    def rows(width):
        return pl.BlockSpec((count, width), lambda i: (at, 0))

    return pl.pallas_call(
        functools.partial(sum_kernel, (len(halves[0]), len(halves[1]), len(joined)), splits),
        grid=(1,),
        in_specs=[rows(a.shape[1]) for a in arrays],
        out_specs=[pl.BlockSpec(o.shape, lambda i, n=len(o.shape): (0,) * n) for o in outs],
        out_shape=outs,
        compiler_params=room(16),
        cost_estimate=FREE,
    )(*arrays)


def pack_kernel(
    side, middle, late, gate, cond, proj_bias, down_bias, up_bias, qk_bias, value_bias, out, work
):
    width = out.shape[1]
    segs = cond.shape[0]
    own = [late[:segs, :], late[2 * segs : 3 * segs, :]]
    for source, at in ((middle, 0), (middle, 1), (middle, 2), (gate, 0)):
        own.append(own_part(side[0], source[2 * at * segs : (2 * at + 1) * segs, :], width))
    own += [wide(cond[:, at : at + width]) for at in range(0, cond.shape[1], width)]
    for at, value in enumerate(own):
        work[at * segs : (at + 1) * segs, :] = value
    rows = []
    for source in (proj_bias, down_bias, up_bias):
        rows += [source[0:1, at : at + width] for at in range(0, source.shape[1], width)]
    rows += [qk_bias[0:1, :width], value_bias[0:1, :]]
    first = len(own) * segs
    for at, value in enumerate(rows):
        work[first + at : first + at + 1, :] = value
    out[...] = work[: out.shape[0], :].astype(jnp.bfloat16)


def finish_kernel(segs, first, held, other, cond, other_cond, mod, modbias, bias, work):
    value = jnp.concatenate([wide(held[...]), wide(other[...])], axis=0)
    left = jnp.concatenate([wide(cond[...]), wide(other_cond[...])], axis=0)
    devices, rows, width = value.shape
    left = left.reshape((devices * segs, left.shape[2])).T.astype(jnp.bfloat16)
    for at in range(mod.shape[0]):
        part = value[:, at * segs : (at + 1) * segs, :].reshape((devices * segs, width))
        mod[at] = dot(left, part.astype(jnp.bfloat16))
        modbias[at : at + 1, :] = jnp.sum(part, axis=0, keepdims=True)
    work[:rows, :] = jnp.sum(value, axis=0)
    count = bias.shape[0]
    bias[...] = work[first : first + count, :]


def padded(width):
    return -(-width // 128) * 128


def qkv_grads(sent, left, proj_left, triple, attended):
    width, length = left.shape
    local = attended.shape[0]
    wide_block = padded(local)
    sums_spec = [pl.BlockSpec((8, 2 * local), lambda j: (0, 0)), pl.BlockSpec((8, local), lambda j: (0, 0))]
    sums_shape = [shape((8, 2 * local), jnp.float32), shape((8, local), jnp.float32)]
    return pl.pallas_call(
        functools.partial(qkv_grads_kernel, sent),
        grid=(3,),
        in_specs=[
            spec(left.shape, "w"),
            spec(left.shape, "w"),
            pl.BlockSpec((2 * local, length), lambda j: (0, 0)),
            pl.BlockSpec((local, length), lambda j: (2, 0)),
            spec(attended.shape, "w"),
        ],
        out_specs=[
            pl.BlockSpec((width // 2, 2 * local), lambda j: (0, 0)),
            pl.BlockSpec((width // 2, wide_block + local), lambda j: (0, 0)),
        ]
        + sums_spec * sent,
        out_shape=[shape((width // 2, 2 * local)), shape((width // 2, wide_block + local))]
        + sums_shape * sent,
        compiler_params=room(32),
        cost_estimate=FREE,
    )(left, proj_left, triple, triple, attended)


def attention_forward(segments, qkv, width=256):
    heads, length = qkv.shape[1], qkv.shape[3]
    return pl.pallas_call(
        functools.partial(attention_forward_kernel, width),
        in_specs=[VMEM] * 2,
        out_specs=[VMEM] * 2,
        out_shape=[shape((heads, HEAD_DIM, length)), shape((heads, 1, length), jnp.float32)],
        scratch_shapes=[
            pltpu.VMEM((HEAD_DIM + SEGS, length), jnp.bfloat16),
            pltpu.VMEM((length, HEAD_DIM + SEGS), jnp.bfloat16),
        ],
        compiler_params=room(12),
        cost_estimate=micros(15),
    )(segments, qkv)


def attention_backward(segments, qkv, stat, grad, width=256):
    heads, length = qkv.shape[1], qkv.shape[3]
    return pl.pallas_call(
        functools.partial(attention_backward_kernel, width),
        in_specs=[VMEM] * 4,
        out_specs=VMEM,
        out_shape=shape(qkv.shape),
        scratch_shapes=[
            pltpu.VMEM((HEAD_DIM + SEGS, length), jnp.bfloat16),
            pltpu.VMEM((length, HEAD_DIM + SEGS), jnp.bfloat16),
        ]
        + [pltpu.VMEM((length, HEAD_DIM), jnp.bfloat16)] * 3
        + [pltpu.VMEM((length, length), jnp.bfloat16)] * 2,
        compiler_params=room(16),
        cost_estimate=micros(15),
    )(segments, qkv, stat, grad)


def silu(array):
    return array / (1.0 + jnp.exp(-array))


def product(spec, left, right):
    return jnp.einsum(spec, left, right, preferred_element_type=jnp.float32)


def exchange(array):
    return lax.ppermute(array, "tensor", [(0, 1), (1, 0)])


def summands(part, size):
    if size == 2:
        return part, exchange(part)
    return lax.psum(part, "tensor"), jnp.zeros_like(part)


def tensor_join(array, size):
    if size == 2:
        other = exchange(array)
        first = lax.axis_index("tensor") == 0
        return jnp.concatenate(
            [jnp.where(first, array, other), jnp.where(first, other, array)], axis=-1
        )
    return lax.all_gather(array, "tensor", axis=array.ndim - 1, tiled=True)


def partners(size, bit):
    return [(i, i ^ (1 << bit)) for i in range(size)]


def tie(*values):
    return lax.optimization_barrier(values)


def after(value, *others):
    return tie(value, *others)[0]


class Gather:
    def __init__(self, array, size, order):
        self.held, self.size, self.order = array[None], size, list(order)

    def last(self):
        bit = self.order.pop(0)
        return self.held, lax.ppermute(self.held, "batch", partners(self.size, bit))

    def step(self, *others):
        if self.order:
            bit = self.order.pop(0)
            self.held = after(self.held, *others)
            other = lax.ppermute(self.held, "batch", partners(self.size, bit))
            self.held = jnp.concatenate([self.held, other], axis=0)


class Sum:
    def __init__(self, sends, size, kernels):
        self.kernels = kernels
        self.sends, self.size, self.bits = sends, size, size.bit_length() - 1
        self.keeps, self.got = None, []

    def pieces(self, at, count, dtype, splits=None, outs=None):
        halves = [[self.keeps[h]] + [stage[h] for stage in self.got[:2]] for h in range(2)]
        joined = [new for (new,) in self.got[2:]]
        widths = [half[0].shape[1] for half in halves]
        if self.kernels:
            if outs is None:
                outs = [shape((count, width), dtype) for width in widths]
                if len(self.got) > 1:
                    outs, splits = [shape((count, sum(widths)), dtype)], ()
            return list(sum_rows(halves, joined, at, count, outs, splits))
        window = slice(at * count, (at + 1) * count)
        totals = [sum(a[window].astype(jnp.float32) for a in half) for half in halves]
        if len(self.got) < 2:
            return [total.astype(dtype) for total in totals]
        total = jnp.concatenate(totals, axis=1)
        total = sum((a[window].astype(jnp.float32) for a in joined), total)
        if outs is None:
            return [total.astype(dtype)]
        if splits == ():
            return [total.astype(dtype)]
        totals = [total[:, : widths[0]], total[:, widths[0] :]]
        parts = [totals[half][:, begin:end] for half, begin, end in splits]
        return [jnp.stack(parts[:3]), parts[3]]

    def send(self, *others):
        stage = len(self.got)
        sends, bits = self.sends, [stage]
        if stage > 0:
            left = self.keeps[0].shape[0] >> stage
            sends = self.pieces(1, left, jnp.bfloat16)
        if stage < 2:
            bits = [stage, 1 - stage]
        tied = tie(*sends, *others)
        self.sent = tied[: len(sends)]
        self.flying = [
            lax.ppermute(piece, "batch", partners(self.size, bit))
            for piece, bit in zip(tied, bits)
        ]
        return tied[len(sends) :]

    def take(self, *others):
        tied = tie(*self.flying, *others)
        self.got.append(tied[: len(self.flying)])
        return tied[len(self.flying) :]

    def settle(self, other):
        if len(self.got) == self.bits:
            self.keeps = list(tie(*self.keeps, other)[:2])

    def result(self, splits=()):
        while len(self.got) < self.bits:
            self.send()
            self.take()
        count = 2 * self.keeps[0].shape[0] // self.size
        if splits:
            width = splits[0][2] - splits[0][1]
            outs = [shape((3, count, width), jnp.float32), shape((count, width), jnp.float32)]
        else:
            outs = [shape((count, sum(keep.shape[1] for keep in self.keeps)), jnp.float32)]
        return self.pieces(0, count, jnp.float32, splits, outs)


def gelu_and_slope(array):
    square = array * array
    bent = jnp.tanh(0.7978845608028654 * (array + 0.044715 * array * square))
    half = 0.5 * (1.0 + bent)
    inner = 0.7978845608028654 * (1.0 + 3.0 * 0.044715 * square)
    return array * half, half + 0.5 * array * (1.0 - bent * bent) * inner


def in_three(array):
    high = lax.reduce_precision(array, 8, 7)
    middle = lax.reduce_precision(array - high, 8, 7)
    return [high, middle, array - high - middle]


def on_device(
    n_batch,
    tokens,
    segment_ids,
    conditions,
    condition_segment,
    qkv_weight,
    qv_bias,
    proj_weight,
    proj_bias,
    up_weight,
    up_bias,
    down_weight,
    down_bias,
    mod_weight,
    mod_bias,
    out_grad,
):
    bf16, f32 = jnp.bfloat16, jnp.float32
    tokens, out_grad = tokens[0], out_grad[0]
    length, model_width = tokens.shape
    local_width = qkv_weight.shape[2]
    hidden_width = up_weight.shape[1]
    heads = local_width // HEAD_DIM
    n_tensor = model_width // local_width
    bits = list(range(n_batch.bit_length() - 1))
    block = model_width // n_batch
    in_kernel = block % 8 == 0
    index = lax.axis_index("batch")
    order = jnp.array(
        [sum((p >> bit & 1) << (bits[-1] - bit) for bit in bits) for p in range(n_batch)], jnp.int32
    )
    order = order ^ index
    side = lax.axis_index("tensor")[None]

    def run(kernel, scalars, arrays, outs):
        turned = shape((model_width, length))
        if in_kernel:
            chunk = (model_width, CHUNK)
            return sweep(kernel, length, scalars, arrays, outs + [(turned, "c")], [chunk])
        got = sweep(kernel, length, scalars, arrays, outs)
        return list(got) + [got[0].T.reshape((n_batch, block, length))[order].reshape(turned.shape)]

    def part_rows(left, sent, first):
        quarter = model_width // 4
        rows = [left[at * quarter : (at + 1) * quarter] for at in row_parts(sent, first)]
        return jnp.concatenate(rows)

    def hidden_grads(sent, left, right, summed=False, fetch=()):
        if in_kernel:
            first, second, *rest = mlp_grads(sent, left, right, summed, fetch)
            return [first, second], rest
        rest = [jnp.sum(right.astype(f32), axis=0)[None]] if summed else fetch
        cut = right.shape[1] // 2
        return [
            product("dl,lc->dc", part_rows(left, sent, True), right[:, :cut]).astype(bf16),
            product("dl,lc->dc", part_rows(left, sent, False), right[:, cut:]).astype(bf16),
        ], rest

    def attention_grads(sent, left, proj_left, triple, attended):
        if in_kernel:
            first, second, *sums = qkv_grads(sent, left, proj_left, triple, attended)
            return [first, second], sums
        sums = jnp.sum(triple.astype(f32), axis=1)[None]
        sums = (sums[:, : 2 * local_width], sums[:, 2 * local_width :])
        cut, extra = 2 * local_width, ((0, 0), (0, padded(local_width) - local_width))
        halves = [
            (part_rows(left, sent, True), triple[:cut]),
            (part_rows(left, sent, False), triple[cut:]),
            (part_rows(proj_left, sent, False), attended),
        ]
        first, value, proj = [product("dl,cl->dc", *pair).astype(bf16) for pair in halves]
        return [first, jnp.concatenate([jnp.pad(value, extra), proj], axis=1)], sums

    cond_float = conditions[0].astype(f32)
    cond_act = silu(cond_float).astype(bf16)
    mod_local = product("sd,djc->jsc", cond_act, mod_weight) + mod_bias[:, None]
    modulation = tensor_join(mod_local, n_tensor)
    segs = modulation.shape[1]
    tables = jnp.concatenate(in_three(modulation) + [jnp.zeros_like(modulation)], axis=1).astype(bf16)
    marks = jnp.concatenate([condition_segment[0], jnp.full((segs,), -1, jnp.int32)])[:, None]
    full, column = (length, model_width), shape((length, 1), f32)
    mine = (length, local_width)
    row = shape((1, model_width), f32)

    qkv_weight = qkv_weight.transpose((1, 2, 0))
    attn_in, mean_one, inverse_one, normed_mine, picks, biases, in_t = run(
        entry_kernel,
        [order, side],
        [(marks, "v"), (segment_ids, "c"), (tables, "v"), (qv_bias, "v"), (tokens, "r")],
        [
            (shape(full), "r"),
            (column, "r"),
            (column, "r"),
            (shape(mine, f32), "r"),
            (shape((length, 4 * segs)), "r"),
            (shape((3, local_width), f32), "w"),
        ],
    )
    qkv = product("jcd,ld->jcl", qkv_weight, attn_in) + biases[:, :, None]
    qkv = qkv.astype(bf16).reshape((3, heads, HEAD_DIM, length))
    attended, stat = attention_forward(segment_ids, qkv)
    attended = attended.reshape((local_width, length))
    proj_part = product("cl,cd->ld", attended, proj_weight).astype(bf16)
    proj_part, proj_other = summands(proj_part, n_tensor)
    out_grad, proj_tied = tie(out_grad, proj_part)
    mlp_grad, down_bias_grad, grad_t = run(
        gate_kernel,
        [order],
        [(picks, "r"), (tables, "v"), (out_grad, "r")],
        [(shape(full), "r"), (row, "w")],
    )
    proj_other, mlp_grad = tie(proj_other, mlp_grad)
    middle_args = [
        (tables, "v"), (tokens, "r"), (proj_tied, "r"), (proj_other, "r"), (proj_bias[None], "v")
    ]
    mlp_in, mean_two, inverse_two, mlp_t = run(
        middle_kernel,
        [order],
        [(picks, "r")] + middle_args,
        [(shape(full), "r"), (column, "r"), (column, "r")],
    )
    hidden = product("ld,df->lf", mlp_in, up_weight) + up_bias
    active, slope = gelu_and_slope(hidden)
    active, slope = tie(active.astype(bf16), slope.astype(bf16))

    sends, _ = hidden_grads(True, grad_t, active)
    down_sum = Sum(sends, n_batch, in_kernel)
    (mlp_grad_then, active_then) = down_sum.send(mlp_grad, active)
    active_grad = product("ld,fd->lf", mlp_grad_then, down_weight)
    hidden_grad = (active_grad * slope.astype(f32)).astype(bf16)
    mlp_part = product("lf,df->ld", hidden_grad, up_weight).astype(bf16)
    mlp_part, mlp_other = summands(mlp_part, n_tensor)
    (hidden_then, mlp_tied) = tie(hidden_grad, mlp_part)
    sends, (up_bias_grad,) = hidden_grads(True, mlp_t, hidden_then, summed=True)
    up_sum = Sum(sends, n_batch, in_kernel)
    down_sum.keeps, _ = hidden_grads(False, grad_t, active_then)
    first, second, *down_sum.keeps = down_sum.take(*up_sum.sends, *down_sum.keeps)
    up_sum.sends = [first, second]
    (mlp_other, hidden_then) = down_sum.send(mlp_other, hidden_then)
    (mlp_other, hidden_then) = up_sum.send(mlp_other, hidden_then)
    attn_grad, proj_bias_grad, grad_mine, early_totals, attn_t = run(
        middle_grad_kernel,
        [order, side],
        [(picks, "r"), (marks, "v"), (segment_ids, "c")]
        + middle_args
        + [(mean_two, "r"), (inverse_two, "r"), (mlp_tied, "r"), (mlp_other, "r"), (out_grad, "r")],
        [
            (shape(full), "r"),
            (row, "w"),
            (shape(mine, f32), "r"),
            (shape((6 * segs, model_width), f32), "w"),
        ],
    )
    attended_grad = product("cd,ld->cl", proj_weight, attn_grad).astype(bf16)

    triple = attention_backward(
        segment_ids, qkv, stat, attended_grad.reshape((heads, HEAD_DIM, length))
    ).reshape((3 * local_width, length))
    up_sum.keeps, _ = hidden_grads(False, mlp_t, hidden_then)
    sends, (qk_bias_grad, value_bias_grad) = attention_grads(True, in_t, attn_t, triple, attended)
    qkv_sum = Sum(sends, n_batch, in_kernel)
    first, second, *up_sum.keeps = up_sum.take(*qkv_sum.sends, *up_sum.keeps)
    qkv_sum.sends = [first, second]
    (triple,) = down_sum.take(triple)
    (triple,) = up_sum.send(triple)
    (triple,) = qkv_sum.send(triple)
    (triple,) = down_sum.send(triple)
    attn_part = product(
        "jcl,jcd->ld", triple.reshape((3, local_width, length)), qkv_weight
    ).astype(bf16)
    kept, sent, sums = sweep(
        halves_kernel,
        length,
        [side],
        [
            (picks, "r"),
            (tables, "v"),
            (attn_part, "r"),
            (tokens, "r"),
            (mean_one, "r"),
            (inverse_one, "r"),
        ],
        [
            (shape(mine), "r"),
            (shape((length, padded(local_width + 4))), "r"),
            (shape((length, 2), f32), "r"),
        ],
        cost=0,
    )
    down_part = product("lf,fd->ld", after(active, kept), down_weight).astype(bf16)
    (kept, sent, down_part) = up_sum.take(kept, sent, down_part)
    (kept, sent) = down_sum.take(kept, sent)
    (kept, sent, triple) = up_sum.send(kept, sent, triple)
    (kept, sent, triple) = down_sum.send(kept, sent, triple)
    (mod_local, kept) = tie(mod_local, kept)
    tables_mine = jnp.concatenate(in_three(mod_local) + [jnp.zeros_like(mod_local)], axis=1).astype(bf16)
    if n_tensor == 2:
        other = exchange(sent)
    else:
        kept = lax.psum_scatter(attn_part, "tensor", scatter_dimension=1, tiled=True)
        other = jnp.zeros_like(sent)
        sums = lax.psum(sums, "tensor")
    qkv_sum.keeps, _ = attention_grads(False, in_t, attn_t, triple, attended)
    token_t, late_totals = sweep(
        functools.partial(token_grad_kernel, model_width),
        length,
        [],
        [
            (picks, "r"),
            (marks, "v"), (segment_ids, "c"),
            (tables_mine, "v"),
            (kept, "r"),
            (other, "r"),
            (sums, "r"),
            (normed_mine, "r"),
            (inverse_one, "r"),
            (grad_mine, "r"),
        ],
        [(shape((local_width, length), f32), "c"), (shape((4 * segs, local_width), f32), "w")],
        cost=0,
    )
    (late_totals, *qkv_sum.keeps) = qkv_sum.take(late_totals, *qkv_sum.keeps)
    (late_totals,) = up_sum.take(late_totals)
    (down_part, late_totals) = qkv_sum.send(down_part, late_totals)
    (down_part, late_totals) = up_sum.send(down_part, late_totals)
    (down_part,) = down_sum.take(down_part)
    down_part, down_other = summands(down_part, n_tensor)
    layer_out, gate_total = sweep(
        layer_kernel,
        length,
        [],
        [(picks, "r"), (marks, "v"), (segment_ids, "c")]
        + middle_args
        + [(down_part, "r"), (down_other, "r"), (down_bias[None], "v"), (out_grad, "r")],
        [(shape(full), "r"), (shape((2 * segs, model_width), f32), "w")],
        cost=0,
    )
    (gate_total,) = up_sum.take(gate_total)
    bias_rows = 2 * n_tensor + hidden_width // local_width + 2
    rows = (6 + n_tensor) * segs + bias_rows
    (packed,) = pl.pallas_call(
        pack_kernel,
        in_specs=[SMEM] + [VMEM] * 9,
        out_specs=[VMEM],
        out_shape=[shape((rows, local_width))],
        scratch_shapes=[pltpu.VMEM((-(-rows // 16) * 16, local_width), f32)],
        compiler_params=room(16),
        cost_estimate=FREE,
    )(
        side,
        early_totals,
        late_totals,
        gate_total,
        cond_act,
        proj_bias_grad,
        down_bias_grad,
        up_bias_grad,
        qk_bias_grad,
        value_bias_grad,
    )
    gathered = Gather(packed, n_batch, bits[:1:-1] + bits[1::-1])
    gathered.step()
    (packed, gathered.held) = qkv_sum.take(packed, gathered.held)
    (packed,) = qkv_sum.send(packed)
    gathered.step()
    tgrad = packed[: 6 * segs].reshape((6, segs, local_width))
    gathered.step()
    (gathered.held,) = qkv_sum.take(gathered.held)
    qkv_sum.send()
    while len(gathered.order) > 1:
        gathered.step()
    halves = gathered.last()
    down_sum.settle(qkv_sum.sent[0])
    up_sum.settle(qkv_sum.sent[0])
    (down,), (up,) = down_sum.result(), up_sum.result()
    (up, down) = qkv_sum.take(up, down)
    cond_then = after(tgrad, *qkv_sum.sent)
    cond_part = product("jsc,djc->sd", cond_then, mod_weight)
    cond_part, cond_other = summands(cond_part.astype(bf16), n_tensor)
    cond_act_grad = cond_part.astype(f32) + cond_other.astype(f32)
    condition_grad = jax.vjp(silu, cond_float)[1](cond_act_grad)[0]

    part = index * block // local_width
    cond_blocks = [
        lax.dynamic_slice(
            half,
            (0, (6 + part) * segs, index * block % local_width),
            (half.shape[0], segs, block),
        )
        for half in halves
    ]
    mod_sum, modbias_sum, bias_all = pl.pallas_call(
        functools.partial(finish_kernel, segs, (6 + n_tensor) * segs),
        in_specs=[VMEM] * 4,
        out_specs=[VMEM] * 3,
        out_shape=[
            shape((6, block, local_width), f32),
            shape((6, local_width), f32),
            shape((bias_rows, local_width), f32),
        ],
        scratch_shapes=[pltpu.VMEM((-(-rows // 8) * 8, local_width), f32)],
        compiler_params=room(24),
        cost_estimate=FREE,
    )(*halves, *cond_blocks)
    qv_sum = bias_all[-2:]
    bias_all = bias_all[:-2].reshape(-1)
    projbias_sum = bias_all[:model_width]
    downbias_sum = bias_all[model_width : 2 * model_width]
    upbias_sum = bias_all[2 * model_width :]
    mod_sum = mod_sum.transpose((1, 0, 2))
    begin = padded(local_width)
    last, proj_last = qkv_sum.result(
        [
            (0, 0, local_width),
            (0, local_width, 2 * local_width),
            (1, 0, local_width),
            (1, begin, begin + local_width),
        ]
    )
    last = last.transpose((1, 0, 2))
    return (
        layer_out[None],
        token_t.T[None],
        condition_grad[None],
        last,
        qv_sum,
        proj_last.T,
        projbias_sum,
        up,
        upbias_sum,
        down.T,
        downbias_sum,
        mod_sum,
        modbias_sum,
    )


def solution(mesh):
    return jax.shard_map(
        functools.partial(on_device, mesh.shape["batch"]),
        mesh=mesh,
        in_specs=(
            P("batch", None, None),
            P("batch", None),
            P("batch", None, None),
            P("batch", None),
            P(None, None, "tensor"),
            P(None, "tensor"),
            P("tensor", None),
            P(),
            P(None, "tensor"),
            P("tensor"),
            P("tensor", None),
            P(),
            P(None, None, "tensor"),
            P(None, "tensor"),
            P("batch", None, None),
        ),
        out_specs=(
            P("batch", None, None),
            P("batch", None, "tensor"),
            P("batch", None, None),
            P("batch", None, "tensor"),
            P(None, "tensor"),
            P("tensor", "batch"),
            P(),
            P("batch", "tensor"),
            P("tensor"),
            P("tensor", "batch"),
            P(),
            P("batch", None, "tensor"),
            P(None, "tensor"),
        ),
        check_vma=False,
    )
```

```python
import functools

import jax
import jax.numpy as jnp
from jax import lax
from jax.experimental import pallas as pl
from jax.experimental.pallas import tpu as pltpu
from jax.sharding import PartitionSpec as P

EPS = 1e-06
HEAD_DIM = 72
SEGS = 8
MOST = 256
LOG2E = 1.4426950408889634
NEG = -1e30


def band(begin, width, length):
    low = max(0, (begin - MOST + 1) // 128 * 128)
    high = min(length, -(-(begin + width + MOST - 1) // 128) * 128)
    return low, high


def natural(array):
    return array.astype(jnp.float32).T.astype(jnp.bfloat16)


def marks(seg_row):
    slots = lax.broadcasted_iota(jnp.int32, (SEGS, seg_row.shape[-1]), 0)
    return (slots == seg_row[...]).astype(jnp.float32)


def fill(head, qkv, one_hot, q_aug, k_nat):
    query = jnp.concatenate([qkv[0, head].astype(jnp.float32), (1.0 - one_hot) * NEG], axis=0)
    q_aug[...] = query.astype(jnp.bfloat16)
    k_nat[...] = natural(jnp.concatenate([qkv[1, head].astype(jnp.float32), one_hot], axis=0))


def attention_forward_kernel(width, seg_row, qkv, out, stat, q_aug, k_nat):
    heads, length = qkv.shape[1], qkv.shape[3]
    factor = HEAD_DIM**-0.5 * LOG2E
    one_hot = marks(seg_row)

    def one(head, carry):
        fill(head, qkv, one_hot, q_aug, k_nat)
        for begin in range(0, length, width):
            low, high = band(begin, width, length)
            span = slice(begin, begin + width)
            scores = jnp.dot(
                k_nat[low:high, :], q_aug[:, span], preferred_element_type=jnp.float32
            )
            peak = jnp.max(scores, axis=0, keepdims=True) * factor
            shifted = jnp.exp2(scores * factor - peak)
            total = jnp.sum(shifted, axis=0, keepdims=True)
            got = jnp.dot(
                qkv[2, head, :, low:high],
                shifted.astype(jnp.bfloat16),
                preferred_element_type=jnp.float32,
            )
            out[head, :, span] = (got * (1.0 / total)).astype(jnp.bfloat16)
            stat[head, :, span] = peak + jnp.log2(total)
        return carry

    lax.fori_loop(0, heads, one, 0, unroll=2)


def attention_backward_kernel(
    width, seg_row, qkv, stat, grad, out, q_aug, k_nat, v_nat, q_nat, g_nat, p_all, s_all
):
    heads, length = qkv.shape[1], qkv.shape[3]
    scale = HEAD_DIM**-0.5
    factor = scale * LOG2E
    one_hot = marks(seg_row)

    def one(head, carry):
        fill(head, qkv, one_hot, q_aug, k_nat)
        v_nat[...] = natural(qkv[2, head])
        q_nat[...] = natural(qkv[0, head])
        g_nat[...] = natural(grad[head])
        for begin in range(0, length, width):
            low, high = band(begin, width, length)
            span = slice(begin, begin + width)
            scores = jnp.dot(
                k_nat[low:high, :], q_aug[:, span], preferred_element_type=jnp.float32
            )
            probs = jnp.exp2(scores * factor - stat[head, :, span])
            prob_grad = jnp.dot(
                v_nat[low:high, :], grad[head, :, span], preferred_element_type=jnp.float32
            )
            row = jnp.sum(prob_grad * probs, axis=0, keepdims=True)
            score_grad = (probs * (prob_grad - row)).astype(jnp.bfloat16)
            p_all[low:high, span] = probs.astype(jnp.bfloat16)
            s_all[low:high, span] = score_grad
            got = jnp.dot(
                qkv[1, head, :, low:high], score_grad, preferred_element_type=jnp.float32
            )
            out[0, head, :, span] = (got * scale).astype(jnp.bfloat16)
        for begin in range(0, length, width):
            span = slice(begin, begin + width)
            reach = [q for q in range(0, length, width) if band(q, width, length)[0] < begin + width and band(q, width, length)[1] > begin]
            low, high = reach[0], reach[-1] + width
            key_grad = jnp.dot(
                s_all[span, low:high], q_nat[low:high, :], preferred_element_type=jnp.float32
            )
            value_grad = jnp.dot(
                p_all[span, low:high], g_nat[low:high, :], preferred_element_type=jnp.float32
            )
            out[1, head, :, span] = (key_grad * scale).T.astype(jnp.bfloat16)
            out[2, head, :, span] = value_grad.T.astype(jnp.bfloat16)
        return carry

    if width < MOST:
        p_all[...] = jnp.zeros_like(p_all)
        s_all[...] = jnp.zeros_like(s_all)
    lax.fori_loop(0, heads, one, 0, unroll=2)


VMEM = pl.BlockSpec(memory_space=pltpu.VMEM)


CHUNK = 256


def dot(left, right):
    return jnp.dot(left, right, preferred_element_type=jnp.float32)


def dot_nt(left, right):
    return lax.dot_general(
        left, right, (((1,), (1,)), ((), ())), preferred_element_type=jnp.float32
    )


def wide(value):
    return value.astype(jnp.float32)


def turn(order, value, out, work):
    count = order.shape[0]
    rows = value.shape[1] // count
    work[...] = wide(value).T
    for at in range(0, count, 2):
        pair = [
            work[pl.ds(pl.multiple_of(order[at + i] * rows, 8), rows), :] for i in range(2)
        ]
        pair = jnp.concatenate(pair, axis=0).astype(jnp.bfloat16)
        out[at * rows : (at + 2) * rows, :] = pair


def own_part(side, value, width):
    part = value[:, :width]
    for at in range(1, value.shape[1] // width):
        part = jnp.where(side == at, value[:, at * width : (at + 1) * width], part)
    return part


def accumulate(total, value):
    @pl.when(pl.program_id(0) == 0)
    def _():
        total[...] = value

    @pl.when(pl.program_id(0) > 0)
    def _():
        total[...] += value


def segment_sums(slots, seg, *values):
    marks = (slots[...] == seg[...]).astype(jnp.bfloat16)
    marks = jnp.concatenate([marks, marks], axis=1)
    sums = []
    for value in values:
        high = value.astype(jnp.bfloat16)
        low = (value - wide(high)).astype(jnp.bfloat16)
        sums.append(dot(marks, jnp.concatenate([high, low], axis=0)))
    return jnp.concatenate(sums, axis=0)


def norm_parts(value):
    width = value.shape[1]
    mean = jnp.sum(value, axis=1, keepdims=True) / width
    center = value - mean
    spread = jnp.sum(center * center, axis=1, keepdims=True) / width
    return mean, center, lax.rsqrt(spread + EPS)


def entry_kernel(
    order, side, slots, seg, tables, bias, tokens,
    out, mean, inverse, normed_mine, picks, biases, *turned
):
    segs = slots.shape[0] // 2
    column = jnp.concatenate([slots[:segs, :]] * 3 + [slots[segs:, :]], axis=0)
    pick = (column == seg[...]).astype(jnp.float32).T.astype(jnp.bfloat16)
    picks[...] = pick
    biases[0:1, :] = bias[0:1, :]
    biases[1:2, :] = jnp.zeros_like(biases[1:2, :])
    biases[2:3, :] = bias[1:2, :]
    middle, center, scale = norm_parts(wide(tokens[...]))
    mean[...] = middle
    inverse[...] = scale
    value = center * scale
    normed_mine[...] = own_part(side[0], value, normed_mine.shape[1])
    value = (value * (1.0 + dot(pick, tables[1])) + dot(pick, tables[0])).astype(jnp.bfloat16)
    out[...] = value
    if turned:
        turn(order, value, *turned)


def gate_kernel(order, picks, tables, grad, out, bias, *turned):
    value = (wide(grad[...]) * dot(picks[...], tables[5])).astype(jnp.bfloat16)
    out[...] = value
    accumulate(bias, jnp.sum(wide(value), axis=0, keepdims=True))
    if turned:
        turn(order, value, *turned)


def middle_of(pick, tables, tokens, part, other, bias):
    attn_out = wide(part[...]) + wide(other[...]) + bias[...]
    return attn_out, wide(tokens[...]) + dot(pick, tables[2]) * attn_out


def middle_kernel(order, picks, tables, tokens, part, other, bias, out, mean, inverse, *turned):
    pick = picks[...]
    value = middle_of(pick, tables, tokens, part, other, bias)[1]
    middle, center, scale = norm_parts(value)
    mean[...] = middle
    inverse[...] = scale
    value = center * scale * (1.0 + dot(pick, tables[4])) + dot(pick, tables[3])
    value = value.astype(jnp.bfloat16)
    out[...] = value
    if turned:
        turn(order, value, *turned)


def middle_grad_kernel(
    order, side, picks, marks, seg, tables, tokens, part, other, bias, mean, inverse, mlp, mlp_other, grad,
    out, bias_sum, grad_mine, totals, *turned
):
    pick = picks[...]
    width = grad.shape[1]
    attn_out, value = middle_of(pick, tables, tokens, part, other, bias)
    norm = (value - mean[...]) * inverse[...]
    in_grad = wide(mlp[...]) + wide(mlp_other[...])
    value = in_grad * (1.0 + dot(pick, tables[4]))
    plain = jnp.sum(value, axis=1, keepdims=True) / width
    cross = jnp.sum(value * norm, axis=1, keepdims=True) / width
    value = wide(grad[...]) + inverse[...] * (value - plain - norm * cross)
    grad_mine[...] = own_part(side[0], value, grad_mine.shape[1])
    accumulate(totals, segment_sums(marks, seg, value * attn_out, in_grad, in_grad * norm))
    value = (value * dot(pick, tables[2])).astype(jnp.bfloat16)
    out[...] = value
    accumulate(bias_sum, jnp.sum(wide(value), axis=0, keepdims=True))
    if turned:
        turn(order, value, *turned)


def halves_kernel(side, picks, tables, part, tokens, mean, inverse, kept, sent, sums):
    value = part[...]
    width = kept.shape[1]
    kept[...] = own_part(side[0], value, width)
    sent[:, :width] = own_part(1 - side[0], value, width)
    value = wide(value) * (1.0 + dot(picks[...], tables[1]))
    norm = (wide(tokens[...]) - mean[...]) * inverse[...]
    for at, term in enumerate((value, value * norm)):
        total = jnp.sum(term, axis=1, keepdims=True)
        high = total.astype(jnp.bfloat16)
        sums[:, at : at + 1] = total
        sent[:, width + 2 * at : width + 2 * at + 1] = high
        sent[:, width + 2 * at + 1 : width + 2 * at + 2] = (total - wide(high)).astype(jnp.bfloat16)


def token_grad_kernel(
    width, picks, marks, seg, tables, kept, other, sums, normed, inverse, grad, out_t, totals
):
    mine = kept.shape[1]
    value = wide(kept[...]) + wide(other[:, :mine])
    norm = normed[...]
    accumulate(totals, segment_sums(marks, seg, value, value * norm))
    value = value * (1.0 + dot(picks[...], tables[1]))
    for at, factor in enumerate((1.0, norm)):
        rest = wide(other[:, mine + 2 * at : mine + 2 * at + 1])
        rest = rest + wide(other[:, mine + 2 * at + 1 : mine + 2 * at + 2])
        value = value - factor * ((sums[:, at : at + 1] + rest) / width)
    out_t[...] = (grad[...] + inverse[...] * value).T


def layer_kernel(
    picks, marks, seg, tables, tokens, part, other, bias, down, down_other, down_bias, grad, out, totals
):
    pick = picks[...]
    mlp_out = wide(down[...]) + wide(down_other[...]) + down_bias[...]
    middle = middle_of(pick, tables, tokens, part, other, bias)[1]
    out[...] = (middle + dot(pick, tables[5]) * mlp_out).astype(jnp.bfloat16)
    accumulate(totals, segment_sums(marks, seg, wide(grad[...]) * mlp_out))


def row_parts(sent, first):
    if first:
        return (2, 3) if sent else (0, 1)
    return (1, 3) if sent else (0, 2)


def put_rows(left, right, out, parts, product, begin=0):
    quarter = left.shape[0] // 4
    columns = slice(begin, begin + (right.shape[0] if product is dot_nt else right.shape[1]))
    if parts[1] == parts[0] + 1:
        rows = slice(parts[0] * quarter, (parts[1] + 1) * quarter)
        out[:, columns] = product(left[rows, :], right[...]).astype(jnp.bfloat16)
        return
    for at, part in enumerate(parts):
        rows = slice(part * quarter, (part + 1) * quarter)
        value = product(left[rows, :], right[...]).astype(jnp.bfloat16)
        out[at * quarter : (at + 1) * quarter, columns] = value


def mlp_grads_kernel(sent, summed, fetched, left, right, *refs):
    sources, (first, second), rest = refs[:fetched], refs[fetched : fetched + 2], refs[fetched + 2 :]
    step = pl.program_id(0)
    copies = []
    if fetched:
        copies = [
            pltpu.make_async_copy(source, target, rest[-1].at[at])
            for at, (source, target) in enumerate(zip(sources, rest[:fetched]))
        ]

    @pl.when(step == 0)
    def _():
        for copy in copies:
            copy.start()
        put_rows(left, right, first, row_parts(sent, True), dot)

    @pl.when(step == 1)
    def _():
        put_rows(left, right, second, row_parts(sent, False), dot)
        for copy in copies:
            copy.wait()

    if summed:
        rest[0][...] = jnp.sum(wide(right[...]), axis=0, keepdims=True)


def qkv_grads_kernel(sent, left, proj_left, both, value, attended, first, second, *sums):
    step = pl.program_id(0)

    def column_sums(array):
        ones = jnp.ones((8, array.shape[1]), jnp.bfloat16)
        return dot_nt(ones, array[...])

    @pl.when(step == 0)
    def _():
        put_rows(left, both, first, row_parts(sent, True), dot_nt)
        if sums:
            sums[0][...] = column_sums(both)
            sums[1][...] = column_sums(value)

    @pl.when(step == 1)
    def _():
        second[...] = jnp.zeros_like(second)
        put_rows(left, value, second, row_parts(sent, False), dot_nt)

    @pl.when(step == 2)
    def _():
        begin = second.shape[1] - attended.shape[0]
        put_rows(proj_left, attended, second, row_parts(sent, False), dot_nt, begin)


SMEM = pl.BlockSpec(memory_space=pltpu.SMEM)
GRADS = 10
FREE = pl.CostEstimate(flops=1, bytes_accessed=1, transcendentals=0)


def micros(time):
    if time == 0:
        return FREE
    return pl.CostEstimate(flops=time * 10**9, bytes_accessed=time * 10**6, transcendentals=0)


def shape(dims, dtype=jnp.bfloat16):
    return jax.ShapeDtypeStruct(dims, dtype)


def room(mib):
    return pltpu.CompilerParams(vmem_limit_bytes=mib << 20)


def spec(dims, kind):
    if kind == "v":
        return VMEM
    if kind == "r":
        return pl.BlockSpec((CHUNK, dims[1]), lambda i: (i, 0))
    if kind == "c":
        return pl.BlockSpec((dims[0], CHUNK), lambda i: (0, i))
    return pl.BlockSpec(tuple(dims), lambda i: (0,) * len(dims))


def sweep(kernel, length, scalars, arrays, outs, work=(), mib=32, cost=200):
    return pl.pallas_call(
        kernel,
        grid=(length // CHUNK,),
        in_specs=[SMEM] * len(scalars) + [spec(a.shape, kind) for a, kind in arrays],
        out_specs=[spec(o.shape, kind) for o, kind in outs],
        out_shape=[o for o, _ in outs],
        scratch_shapes=[pltpu.VMEM(dims, jnp.float32) for dims in work],
        compiler_params=room(mib),
        cost_estimate=micros(cost),
    )(*scalars, *[a for a, _ in arrays])


def mlp_grads(sent, left, right, summed=False, fetch=()):
    width, length = left.shape
    hidden = right.shape[1]
    half = hidden // 2
    out = pl.BlockSpec((width // 2, half), lambda j: (0, 0))
    sums = [pl.BlockSpec((1, half), lambda j: (0, j))] if summed else []
    sums_shape = [shape((1, hidden), jnp.float32)] if summed else []
    return pl.pallas_call(
        functools.partial(mlp_grads_kernel, sent, summed, len(fetch)),
        grid=(2,),
        in_specs=[spec(left.shape, "w"), pl.BlockSpec((length, half), lambda j: (0, j))]
        + [pl.BlockSpec(memory_space=pl.ANY)] * len(fetch),
        out_specs=[out, out] + sums + [VMEM] * len(fetch),
        out_shape=[shape((width // 2, half))] * 2
        + sums_shape
        + [pltpu.VMEM(a.shape, a.dtype) for a in fetch],
        scratch_shapes=[pltpu.SemaphoreType.DMA((len(fetch),))] if fetch else [],
        compiler_params=room(24),
        cost_estimate=micros(GRADS),
    )(left, right, *fetch)


def sum_kernel(counts, splits, *refs):
    halves, at = [], 0
    for count in counts[:2]:
        total = wide(refs[at][...])
        for ref in refs[at + 1 : at + count]:
            total += wide(ref[...])
        halves.append(total)
        at += count
    outs = refs[at + counts[2] :]
    for half in range(2):
        begin = 0 if half == 0 else halves[0].shape[1]
        columns = slice(begin, begin + halves[half].shape[1])
        for ref in refs[at : at + counts[2]]:
            halves[half] += wide(ref[:, columns])
    if splits is None:
        for out, total in zip(outs, halves):
            out[...] = total.astype(out.dtype)
    elif splits == ():
        for total, begin in zip(halves, (0, halves[0].shape[1])):
            outs[0][:, begin : begin + total.shape[1]] = total.astype(outs[0].dtype)
    else:
        for at, (half, begin, end) in enumerate(splits):
            if at < 3:
                outs[0][at] = halves[half][:, begin:end]
            else:
                outs[1][...] = halves[half][:, begin:end]


def sum_rows(halves, joined, at, count, outs, splits=None):
    arrays = halves[0] + halves[1] + joined
    arrays = [pltpu.with_memory_space_constraint(a, pltpu.HBM) for a in arrays]

    def rows(width):
        return pl.BlockSpec((count, width), lambda i: (at, 0))

    return pl.pallas_call(
        functools.partial(sum_kernel, (len(halves[0]), len(halves[1]), len(joined)), splits),
        grid=(1,),
        in_specs=[rows(a.shape[1]) for a in arrays],
        out_specs=[pl.BlockSpec(o.shape, lambda i, n=len(o.shape): (0,) * n) for o in outs],
        out_shape=outs,
        compiler_params=room(16),
        cost_estimate=FREE,
    )(*arrays)


def pack_kernel(
    side, middle, late, gate, cond, proj_bias, down_bias, up_bias, qk_bias, value_bias, out, work
):
    width = out.shape[1]
    segs = cond.shape[0]
    own = [late[:segs, :], late[2 * segs : 3 * segs, :]]
    for source, at in ((middle, 0), (middle, 1), (middle, 2), (gate, 0)):
        own.append(own_part(side[0], source[2 * at * segs : (2 * at + 1) * segs, :], width))
    own += [wide(cond[:, at : at + width]) for at in range(0, cond.shape[1], width)]
    for at, value in enumerate(own):
        work[at * segs : (at + 1) * segs, :] = value
    rows = []
    for source in (proj_bias, down_bias, up_bias):
        rows += [source[0:1, at : at + width] for at in range(0, source.shape[1], width)]
    rows += [qk_bias[0:1, :width], value_bias[0:1, :]]
    first = len(own) * segs
    for at, value in enumerate(rows):
        work[first + at : first + at + 1, :] = value
    out[...] = work[: out.shape[0], :].astype(jnp.bfloat16)


def finish_kernel(segs, first, held, other, cond, other_cond, mod, modbias, bias, work):
    value = jnp.concatenate([wide(held[...]), wide(other[...])], axis=0)
    left = jnp.concatenate([wide(cond[...]), wide(other_cond[...])], axis=0)
    devices, rows, width = value.shape
    left = left.reshape((devices * segs, left.shape[2])).T.astype(jnp.bfloat16)
    for at in range(mod.shape[0]):
        part = value[:, at * segs : (at + 1) * segs, :].reshape((devices * segs, width))
        mod[at] = dot(left, part.astype(jnp.bfloat16))
        modbias[at : at + 1, :] = jnp.sum(part, axis=0, keepdims=True)
    work[:rows, :] = jnp.sum(value, axis=0)
    count = bias.shape[0]
    bias[...] = work[first : first + count, :]


def padded(width):
    return -(-width // 128) * 128


def qkv_grads(sent, left, proj_left, triple, attended):
    width, length = left.shape
    local = attended.shape[0]
    wide_block = padded(local)
    sums_spec = [pl.BlockSpec((8, 2 * local), lambda j: (0, 0)), pl.BlockSpec((8, local), lambda j: (0, 0))]
    sums_shape = [shape((8, 2 * local), jnp.float32), shape((8, local), jnp.float32)]
    return pl.pallas_call(
        functools.partial(qkv_grads_kernel, sent),
        grid=(3,),
        in_specs=[
            spec(left.shape, "w"),
            spec(left.shape, "w"),
            pl.BlockSpec((2 * local, length), lambda j: (0, 0)),
            pl.BlockSpec((local, length), lambda j: (2, 0)),
            spec(attended.shape, "w"),
        ],
        out_specs=[
            pl.BlockSpec((width // 2, 2 * local), lambda j: (0, 0)),
            pl.BlockSpec((width // 2, wide_block + local), lambda j: (0, 0)),
        ]
        + sums_spec * sent,
        out_shape=[shape((width // 2, 2 * local)), shape((width // 2, wide_block + local))]
        + sums_shape * sent,
        compiler_params=room(32),
        cost_estimate=FREE,
    )(left, proj_left, triple, triple, attended)


def attention_forward(segments, qkv, width=256):
    heads, length = qkv.shape[1], qkv.shape[3]
    return pl.pallas_call(
        functools.partial(attention_forward_kernel, width),
        in_specs=[VMEM] * 2,
        out_specs=[VMEM] * 2,
        out_shape=[shape((heads, HEAD_DIM, length)), shape((heads, 1, length), jnp.float32)],
        scratch_shapes=[
            pltpu.VMEM((HEAD_DIM + SEGS, length), jnp.bfloat16),
            pltpu.VMEM((length, HEAD_DIM + SEGS), jnp.bfloat16),
        ],
        compiler_params=room(12),
        cost_estimate=micros(15),
    )(segments, qkv)


def attention_backward(segments, qkv, stat, grad, width=256):
    heads, length = qkv.shape[1], qkv.shape[3]
    return pl.pallas_call(
        functools.partial(attention_backward_kernel, width),
        in_specs=[VMEM] * 4,
        out_specs=VMEM,
        out_shape=shape(qkv.shape),
        scratch_shapes=[
            pltpu.VMEM((HEAD_DIM + SEGS, length), jnp.bfloat16),
            pltpu.VMEM((length, HEAD_DIM + SEGS), jnp.bfloat16),
        ]
        + [pltpu.VMEM((length, HEAD_DIM), jnp.bfloat16)] * 3
        + [pltpu.VMEM((length, length), jnp.bfloat16)] * 2,
        compiler_params=room(16),
        cost_estimate=micros(15),
    )(segments, qkv, stat, grad)


def silu(array):
    return array / (1.0 + jnp.exp(-array))


def product(spec, left, right):
    return jnp.einsum(spec, left, right, preferred_element_type=jnp.float32)


def exchange(array):
    return lax.ppermute(array, "tensor", [(0, 1), (1, 0)])


def summands(part, size):
    if size == 2:
        return part, exchange(part)
    return lax.psum(part, "tensor"), jnp.zeros_like(part)


def tensor_join(array, size):
    if size == 2:
        other = exchange(array)
        first = lax.axis_index("tensor") == 0
        return jnp.concatenate(
            [jnp.where(first, array, other), jnp.where(first, other, array)], axis=-1
        )
    return lax.all_gather(array, "tensor", axis=array.ndim - 1, tiled=True)


def partners(size, bit):
    return [(i, i ^ (1 << bit)) for i in range(size)]


def tie(*values):
    return lax.optimization_barrier(values)


def after(value, *others):
    return tie(value, *others)[0]


class Gather:
    def __init__(self, array, size, order):
        self.held, self.size, self.order = array[None], size, list(order)

    def last(self):
        bit = self.order.pop(0)
        return self.held, lax.ppermute(self.held, "batch", partners(self.size, bit))

    def step(self, *others):
        if self.order:
            bit = self.order.pop(0)
            self.held = after(self.held, *others)
            other = lax.ppermute(self.held, "batch", partners(self.size, bit))
            self.held = jnp.concatenate([self.held, other], axis=0)


class Sum:
    def __init__(self, sends, size, kernels):
        self.kernels = kernels
        self.sends, self.size, self.bits = sends, size, size.bit_length() - 1
        self.keeps, self.got = None, []

    def pieces(self, at, count, dtype, splits=None, outs=None):
        halves = [[self.keeps[h]] + [stage[h] for stage in self.got[:2]] for h in range(2)]
        joined = [new for (new,) in self.got[2:]]
        widths = [half[0].shape[1] for half in halves]
        if self.kernels:
            if outs is None:
                outs = [shape((count, width), dtype) for width in widths]
                if len(self.got) > 1:
                    outs, splits = [shape((count, sum(widths)), dtype)], ()
            return list(sum_rows(halves, joined, at, count, outs, splits))
        window = slice(at * count, (at + 1) * count)
        totals = [sum(a[window].astype(jnp.float32) for a in half) for half in halves]
        if len(self.got) < 2:
            return [total.astype(dtype) for total in totals]
        total = jnp.concatenate(totals, axis=1)
        total = sum((a[window].astype(jnp.float32) for a in joined), total)
        if outs is None:
            return [total.astype(dtype)]
        if splits == ():
            return [total.astype(dtype)]
        totals = [total[:, : widths[0]], total[:, widths[0] :]]
        parts = [totals[half][:, begin:end] for half, begin, end in splits]
        return [jnp.stack(parts[:3]), parts[3]]

    def send(self, *others):
        stage = len(self.got)
        sends, bits = self.sends, [stage]
        if stage > 0:
            left = self.keeps[0].shape[0] >> stage
            sends = self.pieces(1, left, jnp.bfloat16)
        if stage < 2:
            bits = [stage, 1 - stage]
        tied = tie(*sends, *others)
        self.sent = tied[: len(sends)]
        self.flying = [
            lax.ppermute(piece, "batch", partners(self.size, bit))
            for piece, bit in zip(tied, bits)
        ]
        return tied[len(sends) :]

    def take(self, *others):
        tied = tie(*self.flying, *others)
        self.got.append(tied[: len(self.flying)])
        return tied[len(self.flying) :]

    def settle(self, other):
        if len(self.got) == self.bits:
            self.keeps = list(tie(*self.keeps, other)[:2])

    def result(self, splits=()):
        while len(self.got) < self.bits:
            self.send()
            self.take()
        count = 2 * self.keeps[0].shape[0] // self.size
        if splits:
            width = splits[0][2] - splits[0][1]
            outs = [shape((3, count, width), jnp.float32), shape((count, width), jnp.float32)]
        else:
            outs = [shape((count, sum(keep.shape[1] for keep in self.keeps)), jnp.float32)]
        return self.pieces(0, count, jnp.float32, splits, outs)


def gelu_and_slope(array):
    square = array * array
    bent = jnp.tanh(0.7978845608028654 * (array + 0.044715 * array * square))
    half = 0.5 * (1.0 + bent)
    inner = 0.7978845608028654 * (1.0 + 3.0 * 0.044715 * square)
    return array * half, half + 0.5 * array * (1.0 - bent * bent) * inner


def in_three(array):
    high = lax.reduce_precision(array, 8, 7)
    middle = lax.reduce_precision(array - high, 8, 7)
    return [high, middle, array - high - middle]


def on_device(
    n_batch,
    tokens,
    segment_ids,
    conditions,
    condition_segment,
    qkv_weight,
    qv_bias,
    proj_weight,
    proj_bias,
    up_weight,
    up_bias,
    down_weight,
    down_bias,
    mod_weight,
    mod_bias,
    out_grad,
):
    bf16, f32 = jnp.bfloat16, jnp.float32
    tokens, out_grad = tokens[0], out_grad[0]
    length, model_width = tokens.shape
    local_width = qkv_weight.shape[2]
    hidden_width = up_weight.shape[1]
    heads = local_width // HEAD_DIM
    n_tensor = model_width // local_width
    bits = list(range(n_batch.bit_length() - 1))
    block = model_width // n_batch
    in_kernel = block % 8 == 0
    index = lax.axis_index("batch")
    order = jnp.array(
        [sum((p >> bit & 1) << (bits[-1] - bit) for bit in bits) for p in range(n_batch)], jnp.int32
    )
    order = order ^ index
    side = lax.axis_index("tensor")[None]

    def run(kernel, scalars, arrays, outs):
        turned = shape((model_width, length))
        if in_kernel:
            chunk = (model_width, CHUNK)
            return sweep(kernel, length, scalars, arrays, outs + [(turned, "c")], [chunk])
        got = sweep(kernel, length, scalars, arrays, outs)
        return list(got) + [got[0].T.reshape((n_batch, block, length))[order].reshape(turned.shape)]

    def part_rows(left, sent, first):
        quarter = model_width // 4
        rows = [left[at * quarter : (at + 1) * quarter] for at in row_parts(sent, first)]
        return jnp.concatenate(rows)

    def hidden_grads(sent, left, right, summed=False, fetch=()):
        if in_kernel:
            first, second, *rest = mlp_grads(sent, left, right, summed, fetch)
            return [first, second], rest
        rest = [jnp.sum(right.astype(f32), axis=0)[None]] if summed else fetch
        cut = right.shape[1] // 2
        return [
            product("dl,lc->dc", part_rows(left, sent, True), right[:, :cut]).astype(bf16),
            product("dl,lc->dc", part_rows(left, sent, False), right[:, cut:]).astype(bf16),
        ], rest

    def attention_grads(sent, left, proj_left, triple, attended):
        if in_kernel:
            first, second, *sums = qkv_grads(sent, left, proj_left, triple, attended)
            return [first, second], sums
        sums = jnp.sum(triple.astype(f32), axis=1)[None]
        sums = (sums[:, : 2 * local_width], sums[:, 2 * local_width :])
        cut, extra = 2 * local_width, ((0, 0), (0, padded(local_width) - local_width))
        halves = [
            (part_rows(left, sent, True), triple[:cut]),
            (part_rows(left, sent, False), triple[cut:]),
            (part_rows(proj_left, sent, False), attended),
        ]
        first, value, proj = [product("dl,cl->dc", *pair).astype(bf16) for pair in halves]
        return [first, jnp.concatenate([jnp.pad(value, extra), proj], axis=1)], sums

    cond_float = conditions[0].astype(f32)
    cond_act = silu(cond_float).astype(bf16)
    mod_local = product("sd,djc->jsc", cond_act, mod_weight) + mod_bias[:, None]
    modulation = tensor_join(mod_local, n_tensor)
    segs = modulation.shape[1]
    tables = jnp.concatenate(in_three(modulation) + [jnp.zeros_like(modulation)], axis=1).astype(bf16)
    marks = jnp.concatenate([condition_segment[0], jnp.full((segs,), -1, jnp.int32)])[:, None]
    full, column = (length, model_width), shape((length, 1), f32)
    mine = (length, local_width)
    row = shape((1, model_width), f32)

    qkv_weight = qkv_weight.transpose((1, 2, 0))
    attn_in, mean_one, inverse_one, normed_mine, picks, biases, in_t = run(
        entry_kernel,
        [order, side],
        [(marks, "v"), (segment_ids, "c"), (tables, "v"), (qv_bias, "v"), (tokens, "r")],
        [
            (shape(full), "r"),
            (column, "r"),
            (column, "r"),
            (shape(mine, f32), "r"),
            (shape((length, 4 * segs)), "r"),
            (shape((3, local_width), f32), "w"),
        ],
    )
    qkv = product("jcd,ld->jcl", qkv_weight, attn_in) + biases[:, :, None]
    qkv = qkv.astype(bf16).reshape((3, heads, HEAD_DIM, length))
    attended, stat = attention_forward(segment_ids, qkv)
    attended = attended.reshape((local_width, length))
    proj_part = product("cl,cd->ld", attended, proj_weight).astype(bf16)
    proj_part, proj_other = summands(proj_part, n_tensor)
    out_grad, proj_tied = tie(out_grad, proj_part)
    mlp_grad, down_bias_grad, grad_t = run(
        gate_kernel,
        [order],
        [(picks, "r"), (tables, "v"), (out_grad, "r")],
        [(shape(full), "r"), (row, "w")],
    )
    proj_other, mlp_grad = tie(proj_other, mlp_grad)
    middle_args = [
        (tables, "v"), (tokens, "r"), (proj_tied, "r"), (proj_other, "r"), (proj_bias[None], "v")
    ]
    mlp_in, mean_two, inverse_two, mlp_t = run(
        middle_kernel,
        [order],
        [(picks, "r")] + middle_args,
        [(shape(full), "r"), (column, "r"), (column, "r")],
    )
    hidden = product("ld,df->lf", mlp_in, up_weight) + up_bias
    active, slope = gelu_and_slope(hidden)
    active, slope = tie(active.astype(bf16), slope.astype(bf16))

    sends, _ = hidden_grads(True, grad_t, active)
    down_sum = Sum(sends, n_batch, in_kernel)
    (mlp_grad_then, active_then) = down_sum.send(mlp_grad, active)
    active_grad = product("ld,fd->lf", mlp_grad_then, down_weight)
    hidden_grad = (active_grad * slope.astype(f32)).astype(bf16)
    mlp_part = product("lf,df->ld", hidden_grad, up_weight).astype(bf16)
    mlp_part, mlp_other = summands(mlp_part, n_tensor)
    (hidden_then, mlp_tied) = tie(hidden_grad, mlp_part)
    sends, (up_bias_grad,) = hidden_grads(True, mlp_t, hidden_then, summed=True)
    up_sum = Sum(sends, n_batch, in_kernel)
    down_sum.keeps, _ = hidden_grads(False, grad_t, active_then)
    first, second, *down_sum.keeps = down_sum.take(*up_sum.sends, *down_sum.keeps)
    up_sum.sends = [first, second]
    (mlp_other, hidden_then) = down_sum.send(mlp_other, hidden_then)
    (mlp_other, hidden_then) = up_sum.send(mlp_other, hidden_then)
    attn_grad, proj_bias_grad, grad_mine, early_totals, attn_t = run(
        middle_grad_kernel,
        [order, side],
        [(picks, "r"), (marks, "v"), (segment_ids, "c")]
        + middle_args
        + [(mean_two, "r"), (inverse_two, "r"), (mlp_tied, "r"), (mlp_other, "r"), (out_grad, "r")],
        [
            (shape(full), "r"),
            (row, "w"),
            (shape(mine, f32), "r"),
            (shape((6 * segs, model_width), f32), "w"),
        ],
    )
    attended_grad = product("cd,ld->cl", proj_weight, attn_grad).astype(bf16)

    triple = attention_backward(
        segment_ids, qkv, stat, attended_grad.reshape((heads, HEAD_DIM, length))
    ).reshape((3 * local_width, length))
    up_sum.keeps, _ = hidden_grads(False, mlp_t, hidden_then)
    sends, (qk_bias_grad, value_bias_grad) = attention_grads(True, in_t, attn_t, triple, attended)
    qkv_sum = Sum(sends, n_batch, in_kernel)
    first, second, *up_sum.keeps = up_sum.take(*qkv_sum.sends, *up_sum.keeps)
    qkv_sum.sends = [first, second]
    (triple,) = down_sum.take(triple)
    (triple,) = up_sum.send(triple)
    (triple,) = qkv_sum.send(triple)
    (triple,) = down_sum.send(triple)
    attn_part = product(
        "jcl,jcd->ld", triple.reshape((3, local_width, length)), qkv_weight
    ).astype(bf16)
    kept, sent, sums = sweep(
        halves_kernel,
        length,
        [side],
        [
            (picks, "r"),
            (tables, "v"),
            (attn_part, "r"),
            (tokens, "r"),
            (mean_one, "r"),
            (inverse_one, "r"),
        ],
        [
            (shape(mine), "r"),
            (shape((length, padded(local_width + 4))), "r"),
            (shape((length, 2), f32), "r"),
        ],
        cost=0,
    )
    down_part = product("lf,fd->ld", after(active, kept), down_weight).astype(bf16)
    (kept, sent, down_part) = up_sum.take(kept, sent, down_part)
    (kept, sent) = down_sum.take(kept, sent)
    (kept, sent, triple) = up_sum.send(kept, sent, triple)
    (kept, sent, triple) = down_sum.send(kept, sent, triple)
    (mod_local, kept) = tie(mod_local, kept)
    tables_mine = jnp.concatenate(in_three(mod_local) + [jnp.zeros_like(mod_local)], axis=1).astype(bf16)
    if n_tensor == 2:
        other = exchange(sent)
    else:
        kept = lax.psum_scatter(attn_part, "tensor", scatter_dimension=1, tiled=True)
        other = jnp.zeros_like(sent)
        sums = lax.psum(sums, "tensor")
    qkv_sum.keeps, _ = attention_grads(False, in_t, attn_t, triple, attended)
    token_t, late_totals = sweep(
        functools.partial(token_grad_kernel, model_width),
        length,
        [],
        [
            (picks, "r"),
            (marks, "v"), (segment_ids, "c"),
            (tables_mine, "v"),
            (kept, "r"),
            (other, "r"),
            (sums, "r"),
            (normed_mine, "r"),
            (inverse_one, "r"),
            (grad_mine, "r"),
        ],
        [(shape((local_width, length), f32), "c"), (shape((4 * segs, local_width), f32), "w")],
        cost=0,
    )
    (late_totals, *qkv_sum.keeps) = qkv_sum.take(late_totals, *qkv_sum.keeps)
    (late_totals,) = up_sum.take(late_totals)
    (down_part, late_totals) = qkv_sum.send(down_part, late_totals)
    (down_part, late_totals) = up_sum.send(down_part, late_totals)
    (down_part,) = down_sum.take(down_part)
    down_part, down_other = summands(down_part, n_tensor)
    layer_out, gate_total = sweep(
        layer_kernel,
        length,
        [],
        [(picks, "r"), (marks, "v"), (segment_ids, "c")]
        + middle_args
        + [(down_part, "r"), (down_other, "r"), (down_bias[None], "v"), (out_grad, "r")],
        [(shape(full), "r"), (shape((2 * segs, model_width), f32), "w")],
        cost=0,
    )
    (gate_total,) = up_sum.take(gate_total)
    bias_rows = 2 * n_tensor + hidden_width // local_width + 2
    rows = (6 + n_tensor) * segs + bias_rows
    (packed,) = pl.pallas_call(
        pack_kernel,
        in_specs=[SMEM] + [VMEM] * 9,
        out_specs=[VMEM],
        out_shape=[shape((rows, local_width))],
        scratch_shapes=[pltpu.VMEM((-(-rows // 16) * 16, local_width), f32)],
        compiler_params=room(16),
        cost_estimate=FREE,
    )(
        side,
        early_totals,
        late_totals,
        gate_total,
        cond_act,
        proj_bias_grad,
        down_bias_grad,
        up_bias_grad,
        qk_bias_grad,
        value_bias_grad,
    )
    gathered = Gather(packed, n_batch, bits[:1:-1] + bits[1::-1])
    gathered.step()
    (packed, gathered.held) = qkv_sum.take(packed, gathered.held)
    (packed,) = qkv_sum.send(packed)
    gathered.step()
    tgrad = packed[: 6 * segs].reshape((6, segs, local_width))
    gathered.step()
    (gathered.held,) = qkv_sum.take(gathered.held)
    qkv_sum.send()
    while len(gathered.order) > 1:
        gathered.step()
    halves = gathered.last()
    down_sum.settle(qkv_sum.sent[0])
    up_sum.settle(qkv_sum.sent[0])
    (down,), (up,) = down_sum.result(), up_sum.result()
    (up, down) = qkv_sum.take(up, down)
    cond_then = after(tgrad, *qkv_sum.sent)
    cond_part = product("jsc,djc->sd", cond_then, mod_weight)
    cond_part, cond_other = summands(cond_part.astype(bf16), n_tensor)
    cond_act_grad = cond_part.astype(f32) + cond_other.astype(f32)
    condition_grad = jax.vjp(silu, cond_float)[1](cond_act_grad)[0]

    part = index * block // local_width
    cond_blocks = [
        lax.dynamic_slice(
            half,
            (0, (6 + part) * segs, index * block % local_width),
            (half.shape[0], segs, block),
        )
        for half in halves
    ]
    mod_sum, modbias_sum, bias_all = pl.pallas_call(
        functools.partial(finish_kernel, segs, (6 + n_tensor) * segs),
        in_specs=[VMEM] * 4,
        out_specs=[VMEM] * 3,
        out_shape=[
            shape((6, block, local_width), f32),
            shape((6, local_width), f32),
            shape((bias_rows, local_width), f32),
        ],
        scratch_shapes=[pltpu.VMEM((-(-rows // 8) * 8, local_width), f32)],
        compiler_params=room(24),
        cost_estimate=FREE,
    )(*halves, *cond_blocks)
    qv_sum = bias_all[-2:]
    bias_all = bias_all[:-2].reshape(-1)
    projbias_sum = bias_all[:model_width]
    downbias_sum = bias_all[model_width : 2 * model_width]
    upbias_sum = bias_all[2 * model_width :]
    mod_sum = mod_sum.transpose((1, 0, 2))
    begin = padded(local_width)
    last, proj_last = qkv_sum.result(
        [
            (0, 0, local_width),
            (0, local_width, 2 * local_width),
            (1, 0, local_width),
            (1, begin, begin + local_width),
        ]
    )
    last = last.transpose((1, 0, 2))
    return (
        layer_out[None],
        token_t.T[None],
        condition_grad[None],
        last,
        qv_sum,
        proj_last.T,
        projbias_sum,
        up,
        upbias_sum,
        down.T,
        downbias_sum,
        mod_sum,
        modbias_sum,
    )


def solution(mesh):
    return jax.shard_map(
        functools.partial(on_device, mesh.shape["batch"]),
        mesh=mesh,
        in_specs=(
            P("batch", None, None),
            P("batch", None),
            P("batch", None, None),
            P("batch", None),
            P(None, None, "tensor"),
            P(None, "tensor"),
            P("tensor", None),
            P(),
            P(None, "tensor"),
            P("tensor"),
            P("tensor", None),
            P(),
            P(None, None, "tensor"),
            P(None, "tensor"),
            P("batch", None, None),
        ),
        out_specs=(
            P("batch", None, None),
            P("batch", None, "tensor"),
            P("batch", None, None),
            P("batch", None, "tensor"),
            P(None, "tensor"),
            P("tensor", "batch"),
            P(),
            P("batch", "tensor"),
            P("tensor"),
            P("tensor", "batch"),
            P(),
            P("batch", None, "tensor"),
            P(None, "tensor"),
        ),
        check_vma=False,
    )
```

```python
import functools

import jax
import jax.numpy as jnp
from jax import lax
from jax.experimental import pallas as pl
from jax.experimental.pallas import tpu as pltpu
from jax.sharding import PartitionSpec as P

EPS = 1e-06
HEAD_DIM = 72
SEGS = 8
MOST = 256
LOG2E = 1.4426950408889634
NEG = -1e30


def band(begin, width, length):
    low = max(0, (begin - MOST + 1) // 128 * 128)
    high = min(length, -(-(begin + width + MOST - 1) // 128) * 128)
    return low, high


def natural(array):
    return array.astype(jnp.float32).T.astype(jnp.bfloat16)


def marks(seg_row):
    slots = lax.broadcasted_iota(jnp.int32, (SEGS, seg_row.shape[-1]), 0)
    return (slots == seg_row[...]).astype(jnp.float32)


def fill(head, qkv, one_hot, q_aug, k_nat):
    query = jnp.concatenate([qkv[0, head].astype(jnp.float32), (1.0 - one_hot) * NEG], axis=0)
    q_aug[...] = query.astype(jnp.bfloat16)
    k_nat[...] = natural(jnp.concatenate([qkv[1, head].astype(jnp.float32), one_hot], axis=0))


def attention_forward_kernel(width, seg_row, qkv, out, stat, q_aug, k_nat):
    heads, length = qkv.shape[1], qkv.shape[3]
    factor = HEAD_DIM**-0.5 * LOG2E
    one_hot = marks(seg_row)

    def one(head, carry):
        fill(head, qkv, one_hot, q_aug, k_nat)
        for begin in range(0, length, width):
            low, high = band(begin, width, length)
            span = slice(begin, begin + width)
            scores = jnp.dot(
                k_nat[low:high, :], q_aug[:, span], preferred_element_type=jnp.float32
            )
            peak = jnp.max(scores, axis=0, keepdims=True) * factor
            shifted = jnp.exp2(scores * factor - peak)
            total = jnp.sum(shifted, axis=0, keepdims=True)
            got = jnp.dot(
                qkv[2, head, :, low:high],
                shifted.astype(jnp.bfloat16),
                preferred_element_type=jnp.float32,
            )
            out[head, :, span] = (got * (1.0 / total)).astype(jnp.bfloat16)
            stat[head, :, span] = peak + jnp.log2(total)
        return carry

    lax.fori_loop(0, heads, one, 0, unroll=2)


def attention_backward_kernel(
    width, seg_row, qkv, stat, grad, out, q_aug, k_nat, v_nat, q_nat, g_nat, p_all, s_all
):
    heads, length = qkv.shape[1], qkv.shape[3]
    scale = HEAD_DIM**-0.5
    factor = scale * LOG2E
    one_hot = marks(seg_row)

    def one(head, carry):
        fill(head, qkv, one_hot, q_aug, k_nat)
        v_nat[...] = natural(qkv[2, head])
        q_nat[...] = natural(qkv[0, head])
        g_nat[...] = natural(grad[head])
        for begin in range(0, length, width):
            low, high = band(begin, width, length)
            span = slice(begin, begin + width)
            scores = jnp.dot(
                k_nat[low:high, :], q_aug[:, span], preferred_element_type=jnp.float32
            )
            probs = jnp.exp2(scores * factor - stat[head, :, span])
            prob_grad = jnp.dot(
                v_nat[low:high, :], grad[head, :, span], preferred_element_type=jnp.float32
            )
            row = jnp.sum(prob_grad * probs, axis=0, keepdims=True)
            score_grad = (probs * (prob_grad - row)).astype(jnp.bfloat16)
            p_all[low:high, span] = probs.astype(jnp.bfloat16)
            s_all[low:high, span] = score_grad
            got = jnp.dot(
                qkv[1, head, :, low:high], score_grad, preferred_element_type=jnp.float32
            )
            out[0, head, :, span] = (got * scale).astype(jnp.bfloat16)
        for begin in range(0, length, width):
            span = slice(begin, begin + width)
            reach = [q for q in range(0, length, width) if band(q, width, length)[0] < begin + width and band(q, width, length)[1] > begin]
            low, high = reach[0], reach[-1] + width
            key_grad = jnp.dot(
                s_all[span, low:high], q_nat[low:high, :], preferred_element_type=jnp.float32
            )
            value_grad = jnp.dot(
                p_all[span, low:high], g_nat[low:high, :], preferred_element_type=jnp.float32
            )
            out[1, head, :, span] = (key_grad * scale).T.astype(jnp.bfloat16)
            out[2, head, :, span] = value_grad.T.astype(jnp.bfloat16)
        return carry

    if width < MOST:
        p_all[...] = jnp.zeros_like(p_all)
        s_all[...] = jnp.zeros_like(s_all)
    lax.fori_loop(0, heads, one, 0, unroll=2)


VMEM = pl.BlockSpec(memory_space=pltpu.VMEM)


CHUNK = 384


def dot(left, right):
    return jnp.dot(left, right, preferred_element_type=jnp.float32)


def dot_nt(left, right):
    return lax.dot_general(
        left, right, (((1,), (1,)), ((), ())), preferred_element_type=jnp.float32
    )


def wide(value):
    return value.astype(jnp.float32)


def turn(order, value, out, work):
    count = order.shape[0]
    rows = value.shape[1] // count
    work[...] = wide(value).T
    for at in range(0, count, 2):
        pair = [
            work[pl.ds(pl.multiple_of(order[at + i] * rows, 8), rows), :] for i in range(2)
        ]
        pair = jnp.concatenate(pair, axis=0).astype(jnp.bfloat16)
        out[at * rows : (at + 2) * rows, :] = pair


def own_part(side, value, width):
    part = value[:, :width]
    for at in range(1, value.shape[1] // width):
        part = jnp.where(side == at, value[:, at * width : (at + 1) * width], part)
    return part


def accumulate(total, value):
    @pl.when(pl.program_id(0) == 0)
    def _():
        total[...] = value

    @pl.when(pl.program_id(0) > 0)
    def _():
        total[...] += value


def segment_sums(slots, seg, *values):
    marks = (slots[...] == seg[...]).astype(jnp.bfloat16)
    marks = jnp.concatenate([marks, marks], axis=1)
    sums = []
    for value in values:
        high = value.astype(jnp.bfloat16)
        low = (value - wide(high)).astype(jnp.bfloat16)
        sums.append(dot(marks, jnp.concatenate([high, low], axis=0)))
    return jnp.concatenate(sums, axis=0)


def norm_parts(value):
    width = value.shape[1]
    mean = jnp.sum(value, axis=1, keepdims=True) / width
    center = value - mean
    spread = jnp.sum(center * center, axis=1, keepdims=True) / width
    return mean, center, lax.rsqrt(spread + EPS)


def entry_kernel(
    order, side, slots, seg, tables, bias, tokens,
    out, mean, inverse, normed_mine, picks, biases, *turned
):
    segs = slots.shape[0] // 2
    column = jnp.concatenate([slots[:segs, :]] * 3 + [slots[segs:, :]], axis=0)
    pick = (column == seg[...]).astype(jnp.float32).T.astype(jnp.bfloat16)
    picks[...] = pick
    biases[0:1, :] = bias[0:1, :]
    biases[1:2, :] = jnp.zeros_like(biases[1:2, :])
    biases[2:3, :] = bias[1:2, :]
    middle, center, scale = norm_parts(wide(tokens[...]))
    mean[...] = middle
    inverse[...] = scale
    value = center * scale
    normed_mine[...] = own_part(side[0], value, normed_mine.shape[1])
    value = (value * (1.0 + dot(pick, tables[1])) + dot(pick, tables[0])).astype(jnp.bfloat16)
    out[...] = value
    if turned:
        turn(order, value, *turned)


def gate_kernel(order, picks, tables, grad, out, bias, *turned):
    value = (wide(grad[...]) * dot(picks[...], tables[5])).astype(jnp.bfloat16)
    out[...] = value
    accumulate(bias, jnp.sum(wide(value), axis=0, keepdims=True))
    if turned:
        turn(order, value, *turned)


def middle_of(pick, tables, tokens, part, other, bias):
    attn_out = wide(part[...]) + wide(other[...]) + bias[...]
    return attn_out, wide(tokens[...]) + dot(pick, tables[2]) * attn_out


def middle_kernel(order, picks, tables, tokens, part, other, bias, out, mean, inverse, *turned):
    pick = picks[...]
    value = middle_of(pick, tables, tokens, part, other, bias)[1]
    middle, center, scale = norm_parts(value)
    mean[...] = middle
    inverse[...] = scale
    value = center * scale * (1.0 + dot(pick, tables[4])) + dot(pick, tables[3])
    value = value.astype(jnp.bfloat16)
    out[...] = value
    if turned:
        turn(order, value, *turned)


def middle_grad_kernel(
    order, side, picks, marks, seg, tables, tokens, part, other, bias, mean, inverse, mlp, mlp_other, grad,
    out, bias_sum, grad_mine, totals, *turned
):
    pick = picks[...]
    width = grad.shape[1]
    attn_out, value = middle_of(pick, tables, tokens, part, other, bias)
    norm = (value - mean[...]) * inverse[...]
    in_grad = wide(mlp[...]) + wide(mlp_other[...])
    value = in_grad * (1.0 + dot(pick, tables[4]))
    plain = jnp.sum(value, axis=1, keepdims=True) / width
    cross = jnp.sum(value * norm, axis=1, keepdims=True) / width
    value = wide(grad[...]) + inverse[...] * (value - plain - norm * cross)
    grad_mine[...] = own_part(side[0], value, grad_mine.shape[1])
    accumulate(totals, segment_sums(marks, seg, value * attn_out, in_grad, in_grad * norm))
    value = (value * dot(pick, tables[2])).astype(jnp.bfloat16)
    out[...] = value
    accumulate(bias_sum, jnp.sum(wide(value), axis=0, keepdims=True))
    if turned:
        turn(order, value, *turned)


def halves_kernel(side, picks, tables, part, tokens, mean, inverse, kept, sent, sums):
    value = part[...]
    width = kept.shape[1]
    kept[...] = own_part(side[0], value, width)
    sent[:, :width] = own_part(1 - side[0], value, width)
    value = wide(value) * (1.0 + dot(picks[...], tables[1]))
    norm = (wide(tokens[...]) - mean[...]) * inverse[...]
    for at, term in enumerate((value, value * norm)):
        total = jnp.sum(term, axis=1, keepdims=True)
        high = total.astype(jnp.bfloat16)
        sums[:, at : at + 1] = total
        sent[:, width + 2 * at : width + 2 * at + 1] = high
        sent[:, width + 2 * at + 1 : width + 2 * at + 2] = (total - wide(high)).astype(jnp.bfloat16)


def token_grad_kernel(
    width, picks, marks, seg, tables, kept, other, sums, normed, inverse, grad, out_t, totals
):
    mine = kept.shape[1]
    value = wide(kept[...]) + wide(other[:, :mine])
    norm = normed[...]
    accumulate(totals, segment_sums(marks, seg, value, value * norm))
    value = value * (1.0 + dot(picks[...], tables[1]))
    for at, factor in enumerate((1.0, norm)):
        rest = wide(other[:, mine + 2 * at : mine + 2 * at + 1])
        rest = rest + wide(other[:, mine + 2 * at + 1 : mine + 2 * at + 2])
        value = value - factor * ((sums[:, at : at + 1] + rest) / width)
    out_t[...] = (grad[...] + inverse[...] * value).T


def layer_kernel(
    picks, marks, seg, tables, tokens, part, other, bias, down, down_other, down_bias, grad, out, totals
):
    pick = picks[...]
    mlp_out = wide(down[...]) + wide(down_other[...]) + down_bias[...]
    middle = middle_of(pick, tables, tokens, part, other, bias)[1]
    out[...] = (middle + dot(pick, tables[5]) * mlp_out).astype(jnp.bfloat16)
    accumulate(totals, segment_sums(marks, seg, wide(grad[...]) * mlp_out))


def row_parts(sent, first):
    if first:
        return (2, 3) if sent else (0, 1)
    return (1, 3) if sent else (0, 2)


def put_rows(left, right, out, parts, product, begin=0):
    quarter = left.shape[0] // 4
    columns = slice(begin, begin + (right.shape[0] if product is dot_nt else right.shape[1]))
    if parts[1] == parts[0] + 1:
        rows = slice(parts[0] * quarter, (parts[1] + 1) * quarter)
        out[:, columns] = product(left[rows, :], right[...]).astype(jnp.bfloat16)
        return
    for at, part in enumerate(parts):
        rows = slice(part * quarter, (part + 1) * quarter)
        value = product(left[rows, :], right[...]).astype(jnp.bfloat16)
        out[at * quarter : (at + 1) * quarter, columns] = value


def mlp_grads_kernel(sent, summed, fetched, left, right, *refs):
    sources, (first, second), rest = refs[:fetched], refs[fetched : fetched + 2], refs[fetched + 2 :]
    step = pl.program_id(0)
    copies = []
    if fetched:
        copies = [
            pltpu.make_async_copy(source, target, rest[-1].at[at])
            for at, (source, target) in enumerate(zip(sources, rest[:fetched]))
        ]

    @pl.when(step == 0)
    def _():
        for copy in copies:
            copy.start()
        put_rows(left, right, first, row_parts(sent, True), dot)

    @pl.when(step == 1)
    def _():
        put_rows(left, right, second, row_parts(sent, False), dot)
        for copy in copies:
            copy.wait()

    if summed:
        rest[0][...] = jnp.sum(wide(right[...]), axis=0, keepdims=True)


def qkv_grads_kernel(sent, left, proj_left, both, value, attended, first, second, *sums):
    step = pl.program_id(0)

    def column_sums(array):
        ones = jnp.ones((8, array.shape[1]), jnp.bfloat16)
        return dot_nt(ones, array[...])

    @pl.when(step == 0)
    def _():
        put_rows(left, both, first, row_parts(sent, True), dot_nt)
        if sums:
            sums[0][...] = column_sums(both)
            sums[1][...] = column_sums(value)

    @pl.when(step == 1)
    def _():
        second[...] = jnp.zeros_like(second)
        put_rows(left, value, second, row_parts(sent, False), dot_nt)

    @pl.when(step == 2)
    def _():
        begin = second.shape[1] - attended.shape[0]
        put_rows(proj_left, attended, second, row_parts(sent, False), dot_nt, begin)


SMEM = pl.BlockSpec(memory_space=pltpu.SMEM)
GRADS = 10
FREE = pl.CostEstimate(flops=1, bytes_accessed=1, transcendentals=0)


def micros(time):
    if time == 0:
        return FREE
    return pl.CostEstimate(flops=time * 10**9, bytes_accessed=time * 10**6, transcendentals=0)


def shape(dims, dtype=jnp.bfloat16):
    return jax.ShapeDtypeStruct(dims, dtype)


def room(mib):
    return pltpu.CompilerParams(vmem_limit_bytes=mib << 20)


def spec(dims, kind):
    if kind == "v":
        return VMEM
    if kind == "r":
        return pl.BlockSpec((CHUNK, dims[1]), lambda i: (i, 0))
    if kind == "c":
        return pl.BlockSpec((dims[0], CHUNK), lambda i: (0, i))
    return pl.BlockSpec(tuple(dims), lambda i: (0,) * len(dims))


def sweep(kernel, length, scalars, arrays, outs, work=(), mib=40, cost=200):
    return pl.pallas_call(
        kernel,
        grid=(length // CHUNK,),
        in_specs=[SMEM] * len(scalars) + [spec(a.shape, kind) for a, kind in arrays],
        out_specs=[spec(o.shape, kind) for o, kind in outs],
        out_shape=[o for o, _ in outs],
        scratch_shapes=[pltpu.VMEM(dims, jnp.float32) for dims in work],
        compiler_params=room(mib),
        cost_estimate=micros(cost),
    )(*scalars, *[a for a, _ in arrays])


def mlp_grads(sent, left, right, summed=False, fetch=()):
    width, length = left.shape
    hidden = right.shape[1]
    half = hidden // 2
    out = pl.BlockSpec((width // 2, half), lambda j: (0, 0))
    sums = [pl.BlockSpec((1, half), lambda j: (0, j))] if summed else []
    sums_shape = [shape((1, hidden), jnp.float32)] if summed else []
    return pl.pallas_call(
        functools.partial(mlp_grads_kernel, sent, summed, len(fetch)),
        grid=(2,),
        in_specs=[spec(left.shape, "w"), pl.BlockSpec((length, half), lambda j: (0, j))]
        + [pl.BlockSpec(memory_space=pl.ANY)] * len(fetch),
        out_specs=[out, out] + sums + [VMEM] * len(fetch),
        out_shape=[shape((width // 2, half))] * 2
        + sums_shape
        + [pltpu.VMEM(a.shape, a.dtype) for a in fetch],
        scratch_shapes=[pltpu.SemaphoreType.DMA((len(fetch),))] if fetch else [],
        compiler_params=room(24),
        cost_estimate=micros(GRADS),
    )(left, right, *fetch)


def sum_kernel(counts, splits, *refs):
    halves, at = [], 0
    for count in counts[:2]:
        total = wide(refs[at][...])
        for ref in refs[at + 1 : at + count]:
            total += wide(ref[...])
        halves.append(total)
        at += count
    outs = refs[at + counts[2] :]
    for half in range(2):
        begin = 0 if half == 0 else halves[0].shape[1]
        columns = slice(begin, begin + halves[half].shape[1])
        for ref in refs[at : at + counts[2]]:
            halves[half] += wide(ref[:, columns])
    if splits is None:
        for out, total in zip(outs, halves):
            out[...] = total.astype(out.dtype)
    elif splits == ():
        for total, begin in zip(halves, (0, halves[0].shape[1])):
            outs[0][:, begin : begin + total.shape[1]] = total.astype(outs[0].dtype)
    else:
        for at, (half, begin, end) in enumerate(splits):
            if at < 3:
                outs[0][at] = halves[half][:, begin:end]
            else:
                outs[1][...] = halves[half][:, begin:end]


def sum_rows(halves, joined, at, count, outs, splits=None):
    arrays = halves[0] + halves[1] + joined
    arrays = [pltpu.with_memory_space_constraint(a, pltpu.HBM) for a in arrays]

    def rows(width):
        return pl.BlockSpec((count, width), lambda i: (at, 0))

    return pl.pallas_call(
        functools.partial(sum_kernel, (len(halves[0]), len(halves[1]), len(joined)), splits),
        grid=(1,),
        in_specs=[rows(a.shape[1]) for a in arrays],
        out_specs=[pl.BlockSpec(o.shape, lambda i, n=len(o.shape): (0,) * n) for o in outs],
        out_shape=outs,
        compiler_params=room(16),
        cost_estimate=FREE,
    )(*arrays)


def pack_kernel(
    side, middle, late, gate, cond, proj_bias, down_bias, up_bias, qk_bias, value_bias, out, work
):
    width = out.shape[1]
    segs = cond.shape[0]
    own = [late[:segs, :], late[2 * segs : 3 * segs, :]]
    for source, at in ((middle, 0), (middle, 1), (middle, 2), (gate, 0)):
        own.append(own_part(side[0], source[2 * at * segs : (2 * at + 1) * segs, :], width))
    own += [wide(cond[:, at : at + width]) for at in range(0, cond.shape[1], width)]
    for at, value in enumerate(own):
        work[at * segs : (at + 1) * segs, :] = value
    rows = []
    for source in (proj_bias, down_bias, up_bias):
        rows += [source[0:1, at : at + width] for at in range(0, source.shape[1], width)]
    rows += [qk_bias[0:1, :width], value_bias[0:1, :]]
    first = len(own) * segs
    for at, value in enumerate(rows):
        work[first + at : first + at + 1, :] = value
    out[...] = work[: out.shape[0], :].astype(jnp.bfloat16)


def finish_kernel(segs, first, held, other, cond, other_cond, mod, modbias, bias, work):
    value = jnp.concatenate([wide(held[...]), wide(other[...])], axis=0)
    left = jnp.concatenate([wide(cond[...]), wide(other_cond[...])], axis=0)
    devices, rows, width = value.shape
    left = left.reshape((devices * segs, left.shape[2])).T.astype(jnp.bfloat16)
    for at in range(mod.shape[0]):
        part = value[:, at * segs : (at + 1) * segs, :].reshape((devices * segs, width))
        mod[at] = dot(left, part.astype(jnp.bfloat16))
        modbias[at : at + 1, :] = jnp.sum(part, axis=0, keepdims=True)
    work[:rows, :] = jnp.sum(value, axis=0)
    count = bias.shape[0]
    bias[...] = work[first : first + count, :]


def padded(width):
    return -(-width // 128) * 128


def qkv_grads(sent, left, proj_left, triple, attended):
    width, length = left.shape
    local = attended.shape[0]
    wide_block = padded(local)
    sums_spec = [pl.BlockSpec((8, 2 * local), lambda j: (0, 0)), pl.BlockSpec((8, local), lambda j: (0, 0))]
    sums_shape = [shape((8, 2 * local), jnp.float32), shape((8, local), jnp.float32)]
    return pl.pallas_call(
        functools.partial(qkv_grads_kernel, sent),
        grid=(3,),
        in_specs=[
            spec(left.shape, "w"),
            spec(left.shape, "w"),
            pl.BlockSpec((2 * local, length), lambda j: (0, 0)),
            pl.BlockSpec((local, length), lambda j: (2, 0)),
            spec(attended.shape, "w"),
        ],
        out_specs=[
            pl.BlockSpec((width // 2, 2 * local), lambda j: (0, 0)),
            pl.BlockSpec((width // 2, wide_block + local), lambda j: (0, 0)),
        ]
        + sums_spec * sent,
        out_shape=[shape((width // 2, 2 * local)), shape((width // 2, wide_block + local))]
        + sums_shape * sent,
        compiler_params=room(32),
        cost_estimate=FREE,
    )(left, proj_left, triple, triple, attended)


def attention_forward(segments, qkv, width=256):
    heads, length = qkv.shape[1], qkv.shape[3]
    return pl.pallas_call(
        functools.partial(attention_forward_kernel, width),
        in_specs=[VMEM] * 2,
        out_specs=[VMEM] * 2,
        out_shape=[shape((heads, HEAD_DIM, length)), shape((heads, 1, length), jnp.float32)],
        scratch_shapes=[
            pltpu.VMEM((HEAD_DIM + SEGS, length), jnp.bfloat16),
            pltpu.VMEM((length, HEAD_DIM + SEGS), jnp.bfloat16),
        ],
        compiler_params=room(12),
        cost_estimate=micros(15),
    )(segments, qkv)


def attention_backward(segments, qkv, stat, grad, width=256):
    heads, length = qkv.shape[1], qkv.shape[3]
    return pl.pallas_call(
        functools.partial(attention_backward_kernel, width),
        in_specs=[VMEM] * 4,
        out_specs=VMEM,
        out_shape=shape(qkv.shape),
        scratch_shapes=[
            pltpu.VMEM((HEAD_DIM + SEGS, length), jnp.bfloat16),
            pltpu.VMEM((length, HEAD_DIM + SEGS), jnp.bfloat16),
        ]
        + [pltpu.VMEM((length, HEAD_DIM), jnp.bfloat16)] * 3
        + [pltpu.VMEM((length, length), jnp.bfloat16)] * 2,
        compiler_params=room(16),
        cost_estimate=micros(15),
    )(segments, qkv, stat, grad)


def silu(array):
    return array / (1.0 + jnp.exp(-array))


def product(spec, left, right):
    return jnp.einsum(spec, left, right, preferred_element_type=jnp.float32)


def exchange(array):
    return lax.ppermute(array, "tensor", [(0, 1), (1, 0)])


def summands(part, size):
    if size == 2:
        return part, exchange(part)
    return lax.psum(part, "tensor"), jnp.zeros_like(part)


def tensor_join(array, size):
    if size == 2:
        other = exchange(array)
        first = lax.axis_index("tensor") == 0
        return jnp.concatenate(
            [jnp.where(first, array, other), jnp.where(first, other, array)], axis=-1
        )
    return lax.all_gather(array, "tensor", axis=array.ndim - 1, tiled=True)


def partners(size, bit):
    return [(i, i ^ (1 << bit)) for i in range(size)]


def tie(*values):
    return lax.optimization_barrier(values)


def after(value, *others):
    return tie(value, *others)[0]


class Gather:
    def __init__(self, array, size, order):
        self.held, self.size, self.order = array[None], size, list(order)

    def last(self):
        bit = self.order.pop(0)
        return self.held, lax.ppermute(self.held, "batch", partners(self.size, bit))

    def step(self, *others):
        if self.order:
            bit = self.order.pop(0)
            self.held = after(self.held, *others)
            other = lax.ppermute(self.held, "batch", partners(self.size, bit))
            self.held = jnp.concatenate([self.held, other], axis=0)


class Sum:
    def __init__(self, sends, size, kernels):
        self.kernels = kernels
        self.sends, self.size, self.bits = sends, size, size.bit_length() - 1
        self.keeps, self.got = None, []

    def pieces(self, at, count, dtype, splits=None, outs=None):
        halves = [[self.keeps[h]] + [stage[h] for stage in self.got[:2]] for h in range(2)]
        joined = [new for (new,) in self.got[2:]]
        widths = [half[0].shape[1] for half in halves]
        if self.kernels:
            if outs is None:
                outs = [shape((count, width), dtype) for width in widths]
                if len(self.got) > 1:
                    outs, splits = [shape((count, sum(widths)), dtype)], ()
            return list(sum_rows(halves, joined, at, count, outs, splits))
        window = slice(at * count, (at + 1) * count)
        totals = [sum(a[window].astype(jnp.float32) for a in half) for half in halves]
        if len(self.got) < 2:
            return [total.astype(dtype) for total in totals]
        total = jnp.concatenate(totals, axis=1)
        total = sum((a[window].astype(jnp.float32) for a in joined), total)
        if outs is None:
            return [total.astype(dtype)]
        if splits == ():
            return [total.astype(dtype)]
        totals = [total[:, : widths[0]], total[:, widths[0] :]]
        parts = [totals[half][:, begin:end] for half, begin, end in splits]
        return [jnp.stack(parts[:3]), parts[3]]

    def send(self, *others):
        stage = len(self.got)
        sends, bits = self.sends, [stage]
        if stage > 0:
            left = self.keeps[0].shape[0] >> stage
            sends = self.pieces(1, left, jnp.bfloat16)
        if stage < 2:
            bits = [stage, 1 - stage]
        tied = tie(*sends, *others)
        self.sent = tied[: len(sends)]
        self.flying = [
            lax.ppermute(piece, "batch", partners(self.size, bit))
            for piece, bit in zip(tied, bits)
        ]
        return tied[len(sends) :]

    def take(self, *others):
        tied = tie(*self.flying, *others)
        self.got.append(tied[: len(self.flying)])
        return tied[len(self.flying) :]

    def settle(self, other):
        if len(self.got) == self.bits:
            self.keeps = list(tie(*self.keeps, other)[:2])

    def result(self, splits=()):
        while len(self.got) < self.bits:
            self.send()
            self.take()
        count = 2 * self.keeps[0].shape[0] // self.size
        if splits:
            width = splits[0][2] - splits[0][1]
            outs = [shape((3, count, width), jnp.float32), shape((count, width), jnp.float32)]
        else:
            outs = [shape((count, sum(keep.shape[1] for keep in self.keeps)), jnp.float32)]
        return self.pieces(0, count, jnp.float32, splits, outs)


def gelu_and_slope(array):
    square = array * array
    bent = jnp.tanh(0.7978845608028654 * (array + 0.044715 * array * square))
    half = 0.5 * (1.0 + bent)
    inner = 0.7978845608028654 * (1.0 + 3.0 * 0.044715 * square)
    return array * half, half + 0.5 * array * (1.0 - bent * bent) * inner


def in_three(array):
    high = lax.reduce_precision(array, 8, 7)
    middle = lax.reduce_precision(array - high, 8, 7)
    return [high, middle, array - high - middle]


def on_device(
    n_batch,
    tokens,
    segment_ids,
    conditions,
    condition_segment,
    qkv_weight,
    qv_bias,
    proj_weight,
    proj_bias,
    up_weight,
    up_bias,
    down_weight,
    down_bias,
    mod_weight,
    mod_bias,
    out_grad,
):
    bf16, f32 = jnp.bfloat16, jnp.float32
    tokens, out_grad = tokens[0], out_grad[0]
    length, model_width = tokens.shape
    local_width = qkv_weight.shape[2]
    hidden_width = up_weight.shape[1]
    heads = local_width // HEAD_DIM
    n_tensor = model_width // local_width
    bits = list(range(n_batch.bit_length() - 1))
    block = model_width // n_batch
    in_kernel = block % 8 == 0
    index = lax.axis_index("batch")
    order = jnp.array(
        [sum((p >> bit & 1) << (bits[-1] - bit) for bit in bits) for p in range(n_batch)], jnp.int32
    )
    order = order ^ index
    side = lax.axis_index("tensor")[None]

    def run(kernel, scalars, arrays, outs):
        turned = shape((model_width, length))
        if in_kernel:
            chunk = (model_width, CHUNK)
            return sweep(kernel, length, scalars, arrays, outs + [(turned, "c")], [chunk])
        got = sweep(kernel, length, scalars, arrays, outs)
        return list(got) + [got[0].T.reshape((n_batch, block, length))[order].reshape(turned.shape)]

    def part_rows(left, sent, first):
        quarter = model_width // 4
        rows = [left[at * quarter : (at + 1) * quarter] for at in row_parts(sent, first)]
        return jnp.concatenate(rows)

    def hidden_grads(sent, left, right, summed=False, fetch=()):
        if in_kernel:
            first, second, *rest = mlp_grads(sent, left, right, summed, fetch)
            return [first, second], rest
        rest = [jnp.sum(right.astype(f32), axis=0)[None]] if summed else fetch
        cut = right.shape[1] // 2
        return [
            product("dl,lc->dc", part_rows(left, sent, True), right[:, :cut]).astype(bf16),
            product("dl,lc->dc", part_rows(left, sent, False), right[:, cut:]).astype(bf16),
        ], rest

    def attention_grads(sent, left, proj_left, triple, attended):
        if in_kernel:
            first, second, *sums = qkv_grads(sent, left, proj_left, triple, attended)
            return [first, second], sums
        sums = jnp.sum(triple.astype(f32), axis=1)[None]
        sums = (sums[:, : 2 * local_width], sums[:, 2 * local_width :])
        cut, extra = 2 * local_width, ((0, 0), (0, padded(local_width) - local_width))
        halves = [
            (part_rows(left, sent, True), triple[:cut]),
            (part_rows(left, sent, False), triple[cut:]),
            (part_rows(proj_left, sent, False), attended),
        ]
        first, value, proj = [product("dl,cl->dc", *pair).astype(bf16) for pair in halves]
        return [first, jnp.concatenate([jnp.pad(value, extra), proj], axis=1)], sums

    cond_float = conditions[0].astype(f32)
    cond_act = silu(cond_float).astype(bf16)
    mod_local = product("sd,djc->jsc", cond_act, mod_weight) + mod_bias[:, None]
    modulation = tensor_join(mod_local, n_tensor)
    segs = modulation.shape[1]
    tables = jnp.concatenate(in_three(modulation) + [jnp.zeros_like(modulation)], axis=1).astype(bf16)
    marks = jnp.concatenate([condition_segment[0], jnp.full((segs,), -1, jnp.int32)])[:, None]
    full, column = (length, model_width), shape((length, 1), f32)
    mine = (length, local_width)
    row = shape((1, model_width), f32)

    qkv_weight = qkv_weight.transpose((1, 2, 0))
    attn_in, mean_one, inverse_one, normed_mine, picks, biases, in_t = run(
        entry_kernel,
        [order, side],
        [(marks, "v"), (segment_ids, "c"), (tables, "v"), (qv_bias, "v"), (tokens, "r")],
        [
            (shape(full), "r"),
            (column, "r"),
            (column, "r"),
            (shape(mine, f32), "r"),
            (shape((length, 4 * segs)), "r"),
            (shape((3, local_width), f32), "w"),
        ],
    )
    qkv = product("jcd,ld->jcl", qkv_weight, attn_in) + biases[:, :, None]
    qkv = qkv.astype(bf16).reshape((3, heads, HEAD_DIM, length))
    attended, stat = attention_forward(segment_ids, qkv)
    attended = attended.reshape((local_width, length))
    proj_part = product("cl,cd->ld", attended, proj_weight).astype(bf16)
    proj_part, proj_other = summands(proj_part, n_tensor)
    out_grad, proj_tied = tie(out_grad, proj_part)
    mlp_grad, down_bias_grad, grad_t = run(
        gate_kernel,
        [order],
        [(picks, "r"), (tables, "v"), (out_grad, "r")],
        [(shape(full), "r"), (row, "w")],
    )
    proj_other, mlp_grad = tie(proj_other, mlp_grad)
    middle_args = [
        (tables, "v"), (tokens, "r"), (proj_tied, "r"), (proj_other, "r"), (proj_bias[None], "v")
    ]
    mlp_in, mean_two, inverse_two, mlp_t = run(
        middle_kernel,
        [order],
        [(picks, "r")] + middle_args,
        [(shape(full), "r"), (column, "r"), (column, "r")],
    )
    hidden = product("ld,df->lf", mlp_in, up_weight) + up_bias
    active, slope = gelu_and_slope(hidden)
    active, slope = tie(active.astype(bf16), slope.astype(bf16))

    sends, _ = hidden_grads(True, grad_t, active)
    down_sum = Sum(sends, n_batch, in_kernel)
    (mlp_grad_then, active_then) = down_sum.send(mlp_grad, active)
    active_grad = product("ld,fd->lf", mlp_grad_then, down_weight)
    hidden_grad = (active_grad * slope.astype(f32)).astype(bf16)
    mlp_part = product("lf,df->ld", hidden_grad, up_weight).astype(bf16)
    mlp_part, mlp_other = summands(mlp_part, n_tensor)
    (hidden_then, mlp_tied) = tie(hidden_grad, mlp_part)
    sends, (up_bias_grad,) = hidden_grads(True, mlp_t, hidden_then, summed=True)
    up_sum = Sum(sends, n_batch, in_kernel)
    down_sum.keeps, _ = hidden_grads(False, grad_t, active_then)
    first, second, *down_sum.keeps = down_sum.take(*up_sum.sends, *down_sum.keeps)
    up_sum.sends = [first, second]
    (mlp_other, hidden_then) = down_sum.send(mlp_other, hidden_then)
    (mlp_other, hidden_then) = up_sum.send(mlp_other, hidden_then)
    attn_grad, proj_bias_grad, grad_mine, early_totals, attn_t = run(
        middle_grad_kernel,
        [order, side],
        [(picks, "r"), (marks, "v"), (segment_ids, "c")]
        + middle_args
        + [(mean_two, "r"), (inverse_two, "r"), (mlp_tied, "r"), (mlp_other, "r"), (out_grad, "r")],
        [
            (shape(full), "r"),
            (row, "w"),
            (shape(mine, f32), "r"),
            (shape((6 * segs, model_width), f32), "w"),
        ],
    )
    attended_grad = product("cd,ld->cl", proj_weight, attn_grad).astype(bf16)

    triple = attention_backward(
        segment_ids, qkv, stat, attended_grad.reshape((heads, HEAD_DIM, length))
    ).reshape((3 * local_width, length))
    up_sum.keeps, _ = hidden_grads(False, mlp_t, hidden_then)
    sends, (qk_bias_grad, value_bias_grad) = attention_grads(True, in_t, attn_t, triple, attended)
    qkv_sum = Sum(sends, n_batch, in_kernel)
    first, second, *up_sum.keeps = up_sum.take(*qkv_sum.sends, *up_sum.keeps)
    qkv_sum.sends = [first, second]
    (triple,) = down_sum.take(triple)
    (triple,) = up_sum.send(triple)
    (triple,) = qkv_sum.send(triple)
    (triple,) = down_sum.send(triple)
    attn_part = product(
        "jcl,jcd->ld", triple.reshape((3, local_width, length)), qkv_weight
    ).astype(bf16)
    kept, sent, sums = sweep(
        halves_kernel,
        length,
        [side],
        [
            (picks, "r"),
            (tables, "v"),
            (attn_part, "r"),
            (tokens, "r"),
            (mean_one, "r"),
            (inverse_one, "r"),
        ],
        [
            (shape(mine), "r"),
            (shape((length, padded(local_width + 4))), "r"),
            (shape((length, 2), f32), "r"),
        ],
        cost=0,
    )
    down_part = product("lf,fd->ld", after(active, kept), down_weight).astype(bf16)
    (kept, sent, down_part) = up_sum.take(kept, sent, down_part)
    (kept, sent) = down_sum.take(kept, sent)
    (kept, sent, triple) = up_sum.send(kept, sent, triple)
    (kept, sent, triple) = down_sum.send(kept, sent, triple)
    (mod_local, kept) = tie(mod_local, kept)
    tables_mine = jnp.concatenate(in_three(mod_local) + [jnp.zeros_like(mod_local)], axis=1).astype(bf16)
    if n_tensor == 2:
        other = exchange(sent)
    else:
        kept = lax.psum_scatter(attn_part, "tensor", scatter_dimension=1, tiled=True)
        other = jnp.zeros_like(sent)
        sums = lax.psum(sums, "tensor")
    qkv_sum.keeps, _ = attention_grads(False, in_t, attn_t, triple, attended)
    token_t, late_totals = sweep(
        functools.partial(token_grad_kernel, model_width),
        length,
        [],
        [
            (picks, "r"),
            (marks, "v"), (segment_ids, "c"),
            (tables_mine, "v"),
            (kept, "r"),
            (other, "r"),
            (sums, "r"),
            (normed_mine, "r"),
            (inverse_one, "r"),
            (grad_mine, "r"),
        ],
        [(shape((local_width, length), f32), "c"), (shape((4 * segs, local_width), f32), "w")],
        cost=0,
    )
    (late_totals, *qkv_sum.keeps) = qkv_sum.take(late_totals, *qkv_sum.keeps)
    (late_totals,) = up_sum.take(late_totals)
    (down_part, late_totals) = qkv_sum.send(down_part, late_totals)
    (down_part, late_totals) = up_sum.send(down_part, late_totals)
    (down_part,) = down_sum.take(down_part)
    down_part, down_other = summands(down_part, n_tensor)
    layer_out, gate_total = sweep(
        layer_kernel,
        length,
        [],
        [(picks, "r"), (marks, "v"), (segment_ids, "c")]
        + middle_args
        + [(down_part, "r"), (down_other, "r"), (down_bias[None], "v"), (out_grad, "r")],
        [(shape(full), "r"), (shape((2 * segs, model_width), f32), "w")],
        cost=0,
    )
    (gate_total,) = up_sum.take(gate_total)
    bias_rows = 2 * n_tensor + hidden_width // local_width + 2
    rows = (6 + n_tensor) * segs + bias_rows
    (packed,) = pl.pallas_call(
        pack_kernel,
        in_specs=[SMEM] + [VMEM] * 9,
        out_specs=[VMEM],
        out_shape=[shape((rows, local_width))],
        scratch_shapes=[pltpu.VMEM((-(-rows // 16) * 16, local_width), f32)],
        compiler_params=room(16),
        cost_estimate=FREE,
    )(
        side,
        early_totals,
        late_totals,
        gate_total,
        cond_act,
        proj_bias_grad,
        down_bias_grad,
        up_bias_grad,
        qk_bias_grad,
        value_bias_grad,
    )
    gathered = Gather(packed, n_batch, bits[:1:-1] + bits[1::-1])
    gathered.step()
    (packed, gathered.held) = qkv_sum.take(packed, gathered.held)
    (packed,) = qkv_sum.send(packed)
    gathered.step()
    tgrad = packed[: 6 * segs].reshape((6, segs, local_width))
    gathered.step()
    (gathered.held,) = qkv_sum.take(gathered.held)
    qkv_sum.send()
    while len(gathered.order) > 1:
        gathered.step()
    halves = gathered.last()
    down_sum.settle(qkv_sum.sent[0])
    up_sum.settle(qkv_sum.sent[0])
    (down,), (up,) = down_sum.result(), up_sum.result()
    (up, down) = qkv_sum.take(up, down)
    cond_then = after(tgrad, *qkv_sum.sent)
    cond_part = product("jsc,djc->sd", cond_then, mod_weight)
    cond_part, cond_other = summands(cond_part.astype(bf16), n_tensor)
    cond_act_grad = cond_part.astype(f32) + cond_other.astype(f32)
    condition_grad = jax.vjp(silu, cond_float)[1](cond_act_grad)[0]

    part = index * block // local_width
    cond_blocks = [
        lax.dynamic_slice(
            half,
            (0, (6 + part) * segs, index * block % local_width),
            (half.shape[0], segs, block),
        )
        for half in halves
    ]
    mod_sum, modbias_sum, bias_all = pl.pallas_call(
        functools.partial(finish_kernel, segs, (6 + n_tensor) * segs),
        in_specs=[VMEM] * 4,
        out_specs=[VMEM] * 3,
        out_shape=[
            shape((6, block, local_width), f32),
            shape((6, local_width), f32),
            shape((bias_rows, local_width), f32),
        ],
        scratch_shapes=[pltpu.VMEM((-(-rows // 8) * 8, local_width), f32)],
        compiler_params=room(24),
        cost_estimate=FREE,
    )(*halves, *cond_blocks)
    qv_sum = bias_all[-2:]
    bias_all = bias_all[:-2].reshape(-1)
    projbias_sum = bias_all[:model_width]
    downbias_sum = bias_all[model_width : 2 * model_width]
    upbias_sum = bias_all[2 * model_width :]
    mod_sum = mod_sum.transpose((1, 0, 2))
    begin = padded(local_width)
    last, proj_last = qkv_sum.result(
        [
            (0, 0, local_width),
            (0, local_width, 2 * local_width),
            (1, 0, local_width),
            (1, begin, begin + local_width),
        ]
    )
    last = last.transpose((1, 0, 2))
    return (
        layer_out[None],
        token_t.T[None],
        condition_grad[None],
        last,
        qv_sum,
        proj_last.T,
        projbias_sum,
        up,
        upbias_sum,
        down.T,
        downbias_sum,
        mod_sum,
        modbias_sum,
    )


def solution(mesh):
    return jax.shard_map(
        functools.partial(on_device, mesh.shape["batch"]),
        mesh=mesh,
        in_specs=(
            P("batch", None, None),
            P("batch", None),
            P("batch", None, None),
            P("batch", None),
            P(None, None, "tensor"),
            P(None, "tensor"),
            P("tensor", None),
            P(),
            P(None, "tensor"),
            P("tensor"),
            P("tensor", None),
            P(),
            P(None, None, "tensor"),
            P(None, "tensor"),
            P("batch", None, None),
        ),
        out_specs=(
            P("batch", None, None),
            P("batch", None, "tensor"),
            P("batch", None, None),
            P("batch", None, "tensor"),
            P(None, "tensor"),
            P("tensor", "batch"),
            P(),
            P("batch", "tensor"),
            P("tensor"),
            P("tensor", "batch"),
            P(),
            P("batch", None, "tensor"),
            P(None, "tensor"),
        ),
        check_vma=False,
    )
```
